32 devices in a mesh: gx: 2 (over x), gy: 4 (over z), gz: 4 (over y, core).
Axes of the slice: x: 2, y: 2, z: 4, core: 2. Of those that a mesh axis runs over, the one named last changes fastest.
Arguments:
- a_blocks: bfloat16 [8, 16, 8, 7, 4096], P('gx', 'gy', 'gz'), may hold values from -6 to 6
- prolong: bfloat16 [8, 16, 8, 4096], P('gx', 'gy', 'gz'), may hold values from -0.75 to 0.75
- pairing: int32 [4, 8, 8], P('gx', 'gy', 'gz'), may hold values 0 or 1
- route: int32 [512, 1], P(('gx', 'gy', 'gz')), may hold values from 0 to 1; in each aligned block of 16 rows (0 to 15, 16 to 31, ...) at most 12 rows name the same one
Outputs:
- coarse_rows: bfloat16 [768, 11, 4096], P(('gx', 'gy', 'gz'))
The draws below stay inside these ranges and needn't reach their ends.
Inputs may be any that keep to these rules, and one draw needn't show every extreme that they name: `pairing`: 0 pairs each patch's elements along the first direction, 1 along the second. `route`: among the 16 aggregates of one device no destination is named more than 12 times, and in every draw some device names one destination exactly 12 times.
All inputs are finite; a program needn't handle non-finite values. No bound on the sum of `pairing` on one device may be relied on, other than what follows from the above.
Results may differ from the reference program's by a relative error of at most 0.0049.
Values may be sent and summed in bfloat16 or wider, within the bound.
No kernel may reach another device: no remote copies, remote signals or barrier semaphores. Data moves between devices by JAX's collectives and lax.ppermute only.
A program may use at most 128 MiB of HBM per device.

```python
import math
import jax
import jax.numpy as jnp
import numpy as np
from jax import lax

BLK = 64
FACES = 7
COARSE = 11
CX = 4
CY = 4
CZ = 2
NX = 8
NY = 16
NZ = 8
AGG_DEV = 16
NAGG = 512
CAP = 12
N_GX = 2
N_GY = 4
N_GZ = 4
DEVICES = 32


def touch_ends(values, own_key, smallest, high):
    shape = values.shape
    index_at = [jax.random.randint(jax.random.fold_in(own_key, axis), (), 0, shape[axis]) for axis in range(len(shape))]
    values = values.at[tuple(index_at)].set(smallest)
    longest = shape.index(max(shape))
    index_at[longest] = (index_at[longest] + 1) % shape[longest]
    return values.at[tuple(index_at)].set(high)


def level_of(own_key, dims, cuts, smallest, largest):
    factor_of, own = 1.0, jax.random.fold_in(own_key, 6)
    for axis_at, parts in cuts:
        heights = jnp.exp(jax.random.uniform(jax.random.fold_in(own, axis_at), (parts,), jnp.float32, smallest / len(cuts), largest / len(cuts)))
        factor_of = factor_of * jnp.repeat(heights, dims[axis_at] // parts).reshape([-1 if axis == axis_at else 1 for axis in range(len(dims))])
    return factor_of


def routed_block(stream_key, own, number, rows, count, top, reach, lean):
    order = jax.random.permutation(stream_key, count)
    packed, common = load_shares(count, rows * top, reach, lean, True), load_shares(count, rows * top, reach, lean, False)
    places = jnp.arange(count)

    def named(lengths, rotation):
        used = int((lengths > 0).sum())
        fixed = max(1, used // 4)
        moved = fixed + (places - fixed + rotation * (used - fixed)) % max(1, count - fixed)
        return jnp.zeros((count,), jnp.int32).at[order[jnp.where(places < fixed, places, moved)]].set(jnp.asarray(lengths, jnp.int32))

    lengths = jnp.where(number % 4 == 0, named(packed, number // 4), named(common, number - number // 4 - 1))
    mixed = jax.random.permutation(jax.random.fold_in(own, 3), count)
    giver, receiver = mixed[0:count // 2 * 2:2], mixed[1:count // 2 * 2:2]
    room = jnp.minimum(lengths[giver] - 1, reach - lengths[receiver]) // 2
    room = jnp.where((giver == order[0]) | (receiver == order[0]) | (lengths[receiver] == 0), 0, jnp.maximum(room, 0))
    moved = jax.random.randint(jax.random.fold_in(own, 4), (count // 2,), 0, 1 << 20) % (room + 1)
    lengths = lengths.at[giver].add(-moved).at[receiver].add(moved)
    labels = jnp.searchsorted(jnp.cumsum(lengths), jnp.arange(rows * top), side="right").astype(jnp.int32)
    listing = labels.reshape(top, rows).T
    listing = listing[jax.random.permutation(jax.random.fold_in(own, 1), rows)]
    rotation = jax.random.randint(jax.random.fold_in(own, 2), (rows, 1), 0, top)
    return jnp.take_along_axis(listing, (jnp.arange(top)[None, :] + rotation) % top, axis=1)


def load_shares(amount, total, most, skew, full):
    loads = [(1 << 20) // math.isqrt(rank ** skew) + 1 for rank in range(1, amount + 1)]
    largest = most if full else min(most, max(-(-total // amount), total * loads[0] // sum(loads)))
    least = 1 if total - largest >= amount - 1 else 0
    given, surplus = [largest] + [least] * (amount - 1), total - largest - least * (amount - 1)
    while surplus > 0:
        free = [i for i in range(1, amount) if given[i] < largest] or [i for i in range(1, amount) if given[i] < most]
        mass, left = sum([loads[i] for i in free]), surplus
        for i in free:
            extra = min(most - given[i], max(1, left * loads[i] // mass), surplus)
            given[i] = given[i] + extra
            surplus = surplus - extra
    return np.array(given)


def scatter_about(own_key, shape, width, reach, pieces=(), held_as=jnp.bfloat16):
    values = width * jax.random.normal(own_key, shape, jnp.float32)
    if pieces:
        values = values * level_of(own_key, shape, pieces, -0.22, 0.18)
    return jnp.clip(values, -reach, reach).astype(held_as)


def setup_inputs(seed: int = 0) -> dict:
    key_list = jax.random.split(jax.random.key(seed), 5)
    a_blocks = scatter_about(key_list[0], (NX, NY, NZ, FACES, BLK * BLK), 1.0, 6.0, ((0, 2), (1, 4), (2, 4)))
    prolong = scatter_about(key_list[1], (NX, NY, NZ, BLK * BLK), BLK ** -0.5, 0.75, ((0, 2), (1, 4), (2, 4)))
    pairing = touch_ends((jax.random.randint(key_list[2], (NX // 2, NY // 2, NZ), 0, 2) < 1).astype(jnp.int32), jax.random.fold_in(key_list[2], 1), 0, 1)
    route_keys = jax.random.split(jax.random.fold_in(key_list[3], 1), NAGG // AGG_DEV)
    route_turns = jax.random.permutation(jax.random.fold_in(key_list[3], 3), NAGG // AGG_DEV)
    route = jax.vmap(lambda own, number: routed_block(jax.random.fold_in(key_list[3], 2), own, number, AGG_DEV, N_GX, 1, CAP, 2))(route_keys, route_turns).reshape((NAGG, 1))
    return {"a_blocks": a_blocks, "prolong": prolong, "pairing": pairing, "route": route}


x_first_order = [0, 2, 1, 3, 4, 5, 6]
x_second_order = [0, 1, 2, 3, 4, 5, 6]
y_first_order = [0, 4, 1, 2, 3, 5, 6]
y_second_order = [0, 3, 1, 2, 4, 5, 6]


def neighbours(padded):
    shifted = [padded[1:-1, 1:-1, 1:-1], padded[:-2, 1:-1, 1:-1], padded[2:, 1:-1, 1:-1],
               padded[1:-1, :-2, 1:-1], padded[1:-1, 2:, 1:-1], padded[1:-1, 1:-1, :-2],
               padded[1:-1, 1:-1, 2:]]
    return jnp.stack(shifted, axis=3)


def triple(blocks, nearby):
    leading = blocks.shape[:-1]
    left_mat = blocks.reshape(leading + (BLK, BLK)).astype(jnp.float32)
    right_mat = nearby.reshape(leading + (BLK, BLK)).astype(jnp.float32)
    own_block = jnp.swapaxes(right_mat[..., :1, :, :], -1, -2)
    product = jnp.matmul(left_mat, right_mat, precision=lax.Precision.HIGHEST)
    product = lax.optimization_barrier(product.astype(jnp.bfloat16)).astype(jnp.float32)
    result = jnp.matmul(own_block, product, precision=lax.Precision.HIGHEST)
    return result.reshape(leading + (BLK * BLK,))


def members(element_grid, pairs):
    size_x, size_y, size_z = element_grid.shape[:3]
    trailing = element_grid.shape[3:]
    patches = element_grid.reshape((size_x // 2, 2, size_y // 2, 2, size_z) + trailing)

    def pick(upper, lower, slot_order):
        return jnp.take(patches[:, upper, :, lower], jnp.array(slot_order, dtype=jnp.int32), axis=3)

    x_one = jnp.stack([pick(0, 0, x_first_order), pick(0, 1, x_first_order)], axis=3)
    x_two = jnp.stack([pick(1, 0, x_second_order), pick(1, 1, x_second_order)], axis=3)
    y_one = jnp.stack([pick(0, 0, y_first_order), pick(1, 0, y_first_order)], axis=3)
    y_two = jnp.stack([pick(0, 1, y_second_order), pick(1, 1, y_second_order)], axis=3)
    along_x = (pairs == 0).reshape(pairs.shape + (1,) * (x_one.ndim - 3))
    member_one = jnp.where(along_x, x_one, y_one)
    member_two = jnp.where(along_x, x_two, y_two)
    return member_one.reshape((-1,) + member_one.shape[4:]), member_two.reshape((-1,) + member_two.shape[4:])


def arrange(member_one, member_two):
    diagonal = member_one[..., 0, :] + member_two[..., 0, :] + member_one[..., 1, :] + member_two[..., 1, :]
    return jnp.concatenate([diagonal[..., None, :], member_one[..., 2:, :], member_two[..., 2:, :]], axis=-2)


def slot_sources(routes, n_dest, capacity):
    total = routes.shape[0]
    chosen = (routes[:, None] == jnp.arange(n_dest, dtype=jnp.int32)[None, :]).astype(jnp.int32)
    before = (jnp.cumsum(chosen, axis=0) - chosen).astype(jnp.int32)
    ranking = jnp.sum(before * chosen, axis=1).astype(jnp.int32)
    position = routes * capacity + ranking
    targets = jnp.arange(n_dest * capacity, dtype=jnp.int32)
    matches = position[None, :] == targets[:, None]
    anchor = jnp.sum(jnp.where(matches, jnp.arange(total, dtype=jnp.int32)[None, :], 0), axis=1).astype(jnp.int32)
    filled = jnp.any(matches, axis=1)
    return anchor, filled


def pack_slots(payload, anchor, filled):
    taken = jnp.take(payload, anchor, axis=0)
    keep_row = filled.reshape(filled.shape + (1,) * (payload.ndim - 1))
    return jnp.where(keep_row, taken, jnp.zeros_like(taken))


def reference(a_blocks, prolong, pairing, route):
    padded = jnp.pad(prolong, ((1, 1), (1, 1), (1, 1), (0, 0)))
    routes_all = route[:, 0].reshape(N_GX, N_GY * N_GZ, AGG_DEV)

    def one_slab(inputs):
        slab_index, slab_dest = inputs
        first_row = (slab_index * CX).astype(jnp.int32)
        blocks = lax.dynamic_slice_in_dim(a_blocks, first_row, CX, 0)
        beside_all = lax.dynamic_slice_in_dim(padded, first_row, CX + 2, 0)
        slab_pairs = lax.dynamic_slice_in_dim(pairing, (slab_index * (CX // 2)).astype(jnp.int32), CX // 2, 0)
        galerkin = triple(blocks, neighbours(beside_all))
        member_one, member_two = members(galerkin, slab_pairs)
        coarse = arrange(member_one, member_two).astype(jnp.bfloat16)
        coarse = coarse.reshape(CX // 2, N_GY, CY // 2, N_GZ, CZ, 2, COARSE, BLK * BLK)
        coarse = coarse.transpose(1, 3, 0, 2, 4, 5, 6, 7).reshape(N_GY * N_GZ, AGG_DEV, COARSE, BLK * BLK)

        def send_one(device_rows, device_dest):
            anchor, filled = slot_sources(device_dest, N_GX, CAP)
            return pack_slots(device_rows, anchor, filled)

        return jax.vmap(send_one)(coarse, slab_dest)

    buffers = lax.map(one_slab, (jnp.arange(N_GX, dtype=jnp.int32), routes_all))
    buffers = buffers.reshape(N_GX, N_GY * N_GZ, N_GX, CAP, COARSE, BLK * BLK)
    return buffers.transpose(2, 1, 0, 3, 4, 5).reshape(DEVICES * N_GX * CAP, COARSE, BLK * BLK)
```

```python
import functools
import math

import jax
import jax.numpy as jnp
from jax import lax
from jax.experimental import pallas as pl
from jax.experimental.pallas import tpu as pltpu
from jax.sharding import PartitionSpec as P


x_first_order = [0, 2, 1, 3, 4, 5, 6]
x_second_order = [0, 1, 2, 3, 4, 5, 6]
y_first_order = [0, 4, 1, 2, 3, 5, 6]
y_second_order = [0, 3, 1, 2, 4, 5, 6]

LANES = 128
SUB = 8


def padded_2(array, sides, width):
    for axis, dim in sides:
        devices, length = (lax.axis_size(axis), array.shape[dim])
        up = [(i, (i + 1) % devices) for i in range(devices - 1)]
        down = [(j, i) for i, j in up]
        last = lax.slice_in_dim(array, length - width, length, axis=dim)
        initial = lax.slice_in_dim(array, 0, width, axis=dim)
        before = lax.ppermute(last, axis, up)
        after = lax.ppermute(initial, axis, down)
        array = jnp.concatenate([before, array, after], axis=dim)
    return array


def neighbours(padded):
    shifted = [
        padded[1:-1, 1:-1, 1:-1],
        padded[:-2, 1:-1, 1:-1],
        padded[2:, 1:-1, 1:-1],
        padded[1:-1, :-2, 1:-1],
        padded[1:-1, 2:, 1:-1],
        padded[1:-1, 1:-1, :-2],
        padded[1:-1, 1:-1, 2:],
    ]
    return jnp.stack(shifted, axis=3)


def triple(blocks, nearby):
    block_side = math.isqrt(blocks.shape[-1])
    leading = blocks.shape[:-1]
    left_mat = blocks.reshape(leading + (block_side, block_side))
    right_mat = nearby.reshape(leading + (block_side, block_side))
    own_block = jnp.swapaxes(right_mat[..., :1, :, :], -1, -2)
    product = jnp.matmul(left_mat, right_mat, preferred_element_type=jnp.float32).astype(
        jnp.bfloat16
    )
    result = jnp.matmul(own_block, product, preferred_element_type=jnp.float32)
    return result.reshape(leading + (block_side * block_side,))


def members(element_grid, pairs):
    size_x, size_y, size_z = element_grid.shape[:3]
    trailing = element_grid.shape[3:]
    patches = element_grid.reshape((size_x // 2, 2, size_y // 2, 2, size_z) + trailing)

    def pick(upper, lower, slot_order):
        return jnp.take(patches[:, upper, :, lower], jnp.array(slot_order, dtype=jnp.int32), axis=3)

    x_one = jnp.stack([pick(0, 0, x_first_order), pick(0, 1, x_first_order)], axis=3)
    x_two = jnp.stack([pick(1, 0, x_second_order), pick(1, 1, x_second_order)], axis=3)
    y_one = jnp.stack([pick(0, 0, y_first_order), pick(1, 0, y_first_order)], axis=3)
    y_two = jnp.stack([pick(0, 1, y_second_order), pick(1, 1, y_second_order)], axis=3)
    along_x = (pairs == 0).reshape(pairs.shape + (1,) * (x_one.ndim - 3))
    member_one = jnp.where(along_x, x_one, y_one)
    member_two = jnp.where(along_x, x_two, y_two)
    return (
        member_one.reshape((-1,) + member_one.shape[4:]),
        member_two.reshape((-1,) + member_two.shape[4:]),
    )


def arrange(member_one, member_two):
    diagonal = (
        member_one[..., 0, :]
        + member_two[..., 0, :]
        + member_one[..., 1, :]
        + member_two[..., 1, :]
    )
    return jnp.concatenate(
        [diagonal[..., None, :], member_one[..., 2:, :], member_two[..., 2:, :]], axis=-2
    )


def slot_sources(routes, n_dest, capacity):
    total = routes.shape[0]
    chosen = (routes[:, None] == jnp.arange(n_dest, dtype=jnp.int32)[None, :]).astype(jnp.int32)
    before = jnp.cumsum(chosen, axis=0) - chosen
    ranking = jnp.sum(before * chosen, axis=1)
    position = routes * capacity + ranking
    targets = jnp.arange(n_dest * capacity, dtype=jnp.int32)
    matches = position[None, :] == targets[:, None]
    anchor = jnp.sum(jnp.where(matches, jnp.arange(total, dtype=jnp.int32)[None, :], 0), axis=1)
    filled = jnp.any(matches, axis=1)
    return (anchor, filled)


def pack_slots(payload, anchor, filled):
    taken = jnp.take(payload, anchor, axis=0)
    keep_row = filled.reshape(filled.shape + (1,) * (payload.ndim - 1))
    return jnp.where(keep_row, taken, jnp.zeros_like(taken))


def general(a_blocks, prolong, pairing, route, capacity):
    padded = padded_2(prolong, (("gx", 0), ("gy", 1), ("gz", 2)), 1)
    nearby = neighbours(padded)
    anchor, filled = slot_sources(route[:, 0], lax.axis_size("gx"), capacity)
    galerkin = triple(a_blocks, nearby)
    member_one, member_two = members(galerkin, pairing)
    coarse = arrange(member_one, member_two).astype(jnp.bfloat16)
    return lax.all_to_all(
        pack_slots(coarse, anchor, filled), "gx", split_axis=0, concat_axis=0, tiled=True
    )


def dot(left, right):
    return jnp.dot(left, right, preferred_element_type=jnp.float32)


def iota(shape, axis):
    return lax.broadcasted_iota(jnp.int32, shape, axis)


def as_bf16(mask):
    return mask.astype(jnp.float32).astype(jnp.bfloat16)


def pair(one, two):
    h = one.shape[1] // 2
    low = jnp.concatenate([one[:, :h], two[:, :h]], axis=1)
    high = jnp.concatenate([one[:, h:], two[:, h:]], axis=1)
    return jnp.concatenate([low, high], axis=0)


def unpair(both):
    rows, h = both.shape[0] // 2, both.shape[1] // 2
    even, odd = both[:rows], both[rows:]
    return (
        jnp.concatenate([even[:, :h], odd[:, :h]], axis=1),
        jnp.concatenate([even[:, h:], odd[:, h:]], axis=1),
    )


def constants(blk):
    n = 2 * blk
    row, col = iota((n, n), 0), iota((n, n), 1)
    c, z = row % blk, row // blk
    clean = as_bf16(col == (c % 2) * blk + (c // 2) * 2 + z)
    row, col = iota((2 * n, n), 0), iota((2 * n, n), 1)
    k, p, q = row // n, (row // blk) % 2, row % (blk // 2)
    spread = as_bf16(col == k * blk + 2 * q + p)
    same = (((row // (blk // 2)) % 2) == (col % 2)).astype(jnp.float32)
    return clean, spread, same


def clean_pair(clean, both):
    return dot(clean, both).astype(jnp.bfloat16)


def left_factors(spread, same, both):
    out = lax.dot_general(
        spread, both, (((1,), (1,)), ((), ())), preferred_element_type=jnp.float32
    )
    return (out * same).astype(jnp.bfloat16)


def diagonal_blocks(part):
    h = part.shape[1] // 2
    none = jnp.zeros((part.shape[0], h), part.dtype)
    made = []
    for k in range(2):
        one = part[:, k * h : (k + 1) * h]
        made.append(
            jnp.concatenate(
                [jnp.concatenate([one, none], axis=1), jnp.concatenate([none, one], axis=1)], axis=0
            )
        )
    return made


def places(route_ref, pair_ref, where_ref, dims, blocks, codes_ref=None):
    px, py, nz, cap, rows = dims
    me = lax.axis_index("gx")
    half = (cap // SUB) * (rows // cap) * SUB
    sent, kept = jnp.int32(0), jnp.int32(0)
    for i in range(px * py * nz * 2):
        away = route_ref[0, i] != me
        c = jnp.where(away, sent, kept)
        sent = sent + away.astype(jnp.int32)
        kept = kept + 1 - away.astype(jnp.int32)
        kind = 1 - away.astype(jnp.int32)
        rest = cap % SUB
        f = jnp.where(me == 0, c, c - rest)
        h = jnp.where(me == 0, c - (cap - rest), c)
        in_full = jnp.where(me == 0, c < cap - rest, c >= rest)
        swap = jnp.where(me == 0, 0, rest)
        one = jnp.where(in_full, f, half + h + swap)
        two = jnp.where(in_full, f + half // 2, half + h + rest - swap)
        base = kind * (blocks * rows)
        where_ref[0, i] = base + one
        where_ref[1, i] = base + two
        if codes_ref is not None:
            a, b, z, t = i // (py * nz * 2), (i // (nz * 2)) % py, (i // 2) % nz, i % 2
            code = (2 * (jnp.where(pair_ref[a, b, z] == 0, 2, 1) - t) + z).astype(jnp.float32)
            line = jnp.full((1, LANES), code, jnp.float32)
            codes_ref[pl.ds(kind * 2 * SUB + jnp.where(in_full, f, SUB + h), 1), :] = line
            codes_ref[pl.ds(kind * 2 * SUB + jnp.where(in_full, f, SUB + h + rest), 1), :] = line


def put(total_ref, where_ref, i, block, rows, value):
    n = value.shape[0] // 2
    one = where_ref[0, i] + block * rows
    two = where_ref[1, i] + block * rows
    total_ref[pl.ds(one, n, stride=SUB), :] = value[:n]
    total_ref[pl.ds(two, n, stride=SUB), :] = value[n:]


def inner_kernel(
    dims, route_ref, pair_ref, p_ref, a_hbm, send_ref, keep_ref, xface_ref, yup_ref, ydn_ref, zup_ref, zdn_ref,
    a_ref, total_ref, codes_ref, where_ref, sems,
):
    px, py, nz, cap, rows = dims
    blk = p_ref.shape[2]
    q = blk // 2
    nb = 5

    def fetch(n):
        a, b = n // py, n % py
        at = (pl.ds(2 * a, 2), pl.ds(2 * b, 2))
        return pltpu.make_async_copy(a_hbm.at[at], a_ref.at[at], sems.at[n])

    for n in range(px * py):
        fetch(n).start()
    total_ref[...] = jnp.zeros_like(total_ref)
    codes_ref[...] = jnp.zeros_like(codes_ref)
    places(route_ref, pair_ref, where_ref, dims, nb, codes_ref)
    me = lax.axis_index("gx")
    xface_ref[...] = p_ref[jnp.where(me == 0, 2 * px - 1, 0)]
    for x in range(2 * px):
        yup_ref[x] = p_ref[x, 2 * py - 1]
        ydn_ref[x] = p_ref[x, 0]
    clean, spread, same = constants(blk)
    first = as_bf16(iota((blk, LANES), 0) % 2 == 0)
    second = as_bf16(iota((blk, LANES), 0) % 2 == 1)

    def patch(n, carry):
        a, b = n // py, n % py
        fetch(n).wait()
        weight, inner = {}, {}
        for u in range(2):
            both = pair(p_ref[2 * a + u, 2 * b], p_ref[2 * a + u, 2 * b + 1])
            tidy = clean_pair(clean, both)
            left = left_factors(spread, same, both)
            at = (2 * a + u) * py + b
            zdn_ref[at] = tidy[:blk]
            zup_ref[at] = tidy[blk:]
            for z in range(2):
                weight[u, 0, z], weight[u, 1, z] = diagonal_blocks(tidy[z * blk : (z + 1) * blk])
            for v in range(2):
                here = a_ref.at[2 * a + u, 2 * b + v]
                along_z = here[6] * first + here[5] * second
                right = jnp.concatenate(
                    [pair(here[0], here[2 - u]), pair(here[4 - v], along_z)], axis=1
                )
                got = dot(left[v * 2 * blk : (v + 1) * 2 * blk], right).astype(jnp.bfloat16)
                inner[u, v] = unpair(got[:, : 2 * blk]) + unpair(got[:, 2 * blk :])
        for z in range(2):
            own, with_x, with_y, with_z = {}, {}, {}, {}
            zs, zo = slice(z * q, (z + 1) * q), slice((1 - z) * q, (2 - z) * q)
            for u in range(2):
                for v in range(2):
                    stack = jnp.concatenate(
                        [
                            inner[u, v][0][zs],
                            inner[1 - u, v][1][zs],
                            inner[u, 1 - v][2][zs],
                            inner[u, v][3][zo],
                        ],
                        axis=0,
                    )
                    got = dot(stack, weight[u, v, z])
                    own[u, v] = got[:q]
                    with_x[1 - u, v] = got[q : 2 * q]
                    with_y[u, 1 - v] = got[2 * q : 3 * q]
                    with_z[u, v] = got[3 * q :]
            flat = pair_ref[a, b, z] == 0
            flat_o = pair_ref[a, b, 1 - z] == 0
            i = ((a * py + b) * nz + z) * 2
            io = ((a * py + b) * nz + 1 - z) * 2
            sums = {}
            for u in range(2):
                for v in range(2):
                    t = u if u == v else jnp.where(flat, v, u)
                    m = u if u == v else jnp.where(flat, u, v)
                    sums[u, v] = own[u, v] + jnp.where(flat, with_x[u, v], with_y[u, v])
                    put(total_ref, where_ref, i + t, 1 + 2 * m, rows, jnp.where(flat, with_y[u, v], with_x[u, v]))
                    t = u if u == v else jnp.where(flat_o, v, u)
                    m = u if u == v else jnp.where(flat_o, u, v)
                    put(total_ref, where_ref, io + t, 2 + 2 * m, rows, with_z[u, v])
            put(total_ref, where_ref, i, 0, rows, sums[0, 0] + jnp.where(flat, sums[1, 0], sums[0, 1]))
            put(total_ref, where_ref, i + 1, 0, rows, sums[1, 1] + jnp.where(flat, sums[0, 1], sums[1, 0]))
        return carry

    lax.fori_loop(0, px * py, patch, 0)
    for kind, out in enumerate((send_ref, keep_ref)):
        for k in range(nb):
            out[k * rows : (k + 1) * rows] = total_ref[
                (kind * nb + k) * rows : (kind * nb + k + 1) * rows
            ].astype(jnp.bfloat16)
        out[nb * rows :] = codes_ref[kind * 2 * SUB : (kind + 1) * 2 * SUB].astype(jnp.bfloat16)


def outer_kernel(
    dims, route_ref, pair_ref, p_ref, a_ref, xface_ref, ylow_ref, yhigh_ref, zlow_ref, zhigh_ref, send_ref, keep_ref,
    weight_ref, zweight_ref, left_ref, total_ref, where_ref,
):
    px, py, nz, cap, rows = dims
    nx, ny = 2 * px, 2 * py
    blk = p_ref.shape[2]
    q = blk // 2
    nb = 6
    total_ref[...] = jnp.zeros_like(total_ref)
    places(route_ref, pair_ref, where_ref, dims, nb)
    me = lax.axis_index("gx")
    clean, spread, same = constants(blk)
    first = as_bf16(iota((blk, LANES), 0) % 2 == 0)
    second = as_bf16(iota((blk, LANES), 0) % 2 == 1)

    def weights(tidy):
        return [diagonal_blocks(tidy[z * blk : (z + 1) * blk]) for z in range(2)]

    def local(n, carry):
        x, b = n // py, n % py
        both = pair(p_ref[x, 2 * b], p_ref[x, 2 * b + 1])
        made = weights(clean_pair(clean, both))
        left = left_factors(spread, same, both)
        low, high = diagonal_blocks(zlow_ref[n]), diagonal_blocks(zhigh_ref[n])
        for v in range(2):
            left_ref[x, 2 * b + v] = left[v * 2 * blk : (v + 1) * 2 * blk]
            zweight_ref[0, x, 2 * b + v] = low[v]
            zweight_ref[1, x, 2 * b + v] = high[v]
            for z in range(2):
                weight_ref[x + 1, 2 * b + v + 1, z] = made[z][v]
        return carry

    lax.fori_loop(0, nx * py, local, 0)
    above = jnp.where(me == 0, 0.0, 1.0)
    for b in range(py):
        tidy = clean_pair(clean, pair(xface_ref[2 * b], xface_ref[2 * b + 1]))
        low = (tidy.astype(jnp.float32) * above).astype(jnp.bfloat16)
        high = (tidy.astype(jnp.float32) * (1.0 - above)).astype(jnp.bfloat16)
        for at, part in ((0, low), (nx + 1, high)):
            made = weights(part)
            for v in range(2):
                for z in range(2):
                    weight_ref[at, 2 * b + v + 1, z] = made[z][v]
    for a in range(px):
        for at, ref in ((0, ylow_ref), (ny + 1, yhigh_ref)):
            made = weights(clean_pair(clean, pair(ref[2 * a], ref[2 * a + 1])))
            for u in range(2):
                for z in range(2):
                    weight_ref[2 * a + u + 1, at, z] = made[z][u]

    def patch(n, carry):
        a, b = n // py, n % py
        for u in range(2):
            for v in range(2):
                x, y = 2 * a + u, 2 * b + v
                here = a_ref.at[x, y]
                along_z = here[5] * first + here[6] * second
                right = jnp.concatenate(
                    [pair(here[1 + u], here[3 + v]), pair(along_z, along_z)], axis=1
                )
                got = dot(left_ref[x, y], right).astype(jnp.bfloat16)
                with_x, with_y = unpair(got[:, : 2 * blk])
                with_z = unpair(got[:, 2 * blk :])[0]
                for z in range(2):
                    zs = slice(z * q, (z + 1) * q)
                    flat = pair_ref[a, b, z] == 0
                    t = u if u == v else jnp.where(flat, v, u)
                    m = u if u == v else jnp.where(flat, u, v)
                    i = ((a * py + b) * nz + z) * 2 + t
                    for k, (left, weight) in enumerate((
                        (with_x, weight_ref[x + 2 * u, y + 1, z]),
                        (with_y, weight_ref[x + 1, y + 2 * v, z]),
                        (with_z, zweight_ref[z, x, y]),
                    )):
                        put(total_ref, where_ref, i, 3 * m + k, rows, dot(left[zs], weight))
        return carry

    lax.fori_loop(0, px * py, patch, 0)
    for kind, out in enumerate((send_ref, keep_ref)):
        for k in range(nb):
            out[k * rows : (k + 1) * rows] = total_ref[
                (kind * nb + k) * rows : (kind * nb + k + 1) * rows
            ].astype(jnp.bfloat16)


def placed_blocks(early_ref, late_ref, rows, at, size, code):
    near_low, near_high = (code < 1.5)[None], (code > 3.5)[None]
    upper = ((code == 1.0) | (code == 3.0) | (code == 5.0))[None]

    def early(k):
        return early_ref[k * rows + at : k * rows + at + size].astype(jnp.float32).reshape(-1, SUB, LANES)

    def late(k):
        return late_ref[k * rows + at : k * rows + at + size].astype(jnp.float32).reshape(-1, SUB, LANES)

    yield early(0)
    for m in range(2):
        cross, z_in = early(1 + 2 * m), early(2 + 2 * m)
        x_out, y_out, z_out = late(3 * m), late(3 * m + 1), late(3 * m + 2)
        yield jnp.where(near_low, cross, x_out)
        yield jnp.where(near_low, x_out, jnp.where(near_high, y_out, cross))
        yield jnp.where(near_high, cross, y_out)
        yield jnp.where(upper, z_in, z_out)
        yield jnp.where(upper, z_out, z_in)


def keep_kernel(dims, early_ref, late_ref, half_ref, out_hbm, full_ref, sem):
    cap, rows = dims
    full = (cap // SUB) * (rows // cap) * SUB
    me = lax.axis_index("gx")
    nb = out_hbm.shape[0]
    codes = early_ref[5 * rows :].astype(jnp.float32)
    copies = []
    for k, value in enumerate(placed_blocks(early_ref, late_ref, rows, 0, full, codes[:SUB])):
        full_ref[k] = value.reshape(full, LANES).astype(jnp.bfloat16)
        to = out_hbm.at[k, pl.ds(me * (2 * full), full), :]
        copies.append(pltpu.make_async_copy(full_ref.at[k], to, sem.at[k]))
        copies[-1].start()
    for k, value in enumerate(placed_blocks(early_ref, late_ref, rows, full, rows - full, codes[SUB:])):
        half_ref[k] = value.reshape(rows - full, LANES).astype(jnp.bfloat16)
    for copy in copies:
        copy.wait()


def take_kernel(dims, early_ref, late_ref, half_ref, _, out_hbm, full_ref, mixed_ref, sem):
    cap, rows = dims
    full = (cap // SUB) * (rows // cap) * SUB
    me = lax.axis_index("gx")
    codes = early_ref[5 * rows :].astype(jnp.float32)
    copies = []
    for k, value in enumerate(placed_blocks(early_ref, late_ref, rows, 0, full, codes[:SUB])):
        full_ref[k] = value.reshape(full, LANES).astype(jnp.bfloat16)
        to = out_hbm.at[k, pl.ds((1 - me) * (2 * full), full), :]
        copies.append(pltpu.make_async_copy(full_ref.at[k], to, sem.at[0, k]))
        copies[-1].start()
    first_half = (iota((SUB, LANES), 0) < SUB // 2)[None]
    for k, value in enumerate(placed_blocks(early_ref, late_ref, rows, full, rows - full, codes[SUB:])):
        mine = half_ref[k].astype(jnp.float32).reshape(-1, SUB, LANES)
        zero = jnp.where(me == 0, mine, value)
        one = jnp.where(me == 0, value, mine)
        low = jnp.where(first_half, zero, one)
        high = pltpu.roll(jnp.where(first_half, one, zero), SUB // 2, 1)
        mixed_ref[k, : rows - full] = low.reshape(rows - full, LANES).astype(jnp.bfloat16)
        mixed_ref[k, rows - full :] = high.reshape(rows - full, LANES).astype(jnp.bfloat16)
        to = out_hbm.at[k, full : 2 * full, :]
        copies.append(pltpu.make_async_copy(mixed_ref.at[k], to, sem.at[1, k]))
        copies[-1].start()
    for copy in copies:
        copy.wait()


SMEM = pl.BlockSpec(memory_space=pltpu.SMEM)
VMEM = pl.BlockSpec(memory_space=pltpu.VMEM)
ANY = pl.BlockSpec(memory_space=pl.ANY)


def bf16(*shape):
    return jax.ShapeDtypeStruct(shape, jnp.bfloat16)


def local(a_blocks, prolong, pairing, route):
    devices_gx = lax.axis_size("gx")
    aggregates = route.shape[0]
    capacity = max(2, 3 * aggregates // (2 * devices_gx))
    nx, ny, nz, faces, entries = a_blocks.shape
    fits = (
        devices_gx == 2
        and nz == 2
        and nx % 2 == 0
        and ny % 2 == 0
        and faces == 7
        and entries == (LANES // 2) ** 2
        and capacity // SUB == 1
        and capacity % SUB == SUB // 2
    )
    if not fits:
        return general(a_blocks, prolong, pairing, route, capacity)
    px, py = nx // 2, ny // 2
    blk = math.isqrt(entries)
    lines = entries // LANES
    a_view = a_blocks.transpose(0, 1, 3, 2, 4).reshape(nx, ny, faces, nz, lines, LANES)
    a_view = a_view.transpose(0, 1, 2, 4, 3, 5).reshape(nx, ny, faces, nz * lines, LANES)
    p_view = prolong.reshape(nx, ny, nz, lines, LANES).transpose(0, 1, 3, 2, 4)
    p_view = p_view.reshape(nx, ny, nz * lines, LANES)
    route_row = route.reshape(1, aggregates)
    rows = capacity * lines
    dims = (px, py, nz, capacity, rows)
    f32 = jnp.float32

    send_0, keep_0, xface, yup, ydn, zup, zdn = pl.pallas_call(
        functools.partial(inner_kernel, dims),
        out_shape=(
            bf16(5 * rows + 2 * SUB, LANES),
            bf16(5 * rows + 2 * SUB, LANES),
            bf16(ny, blk, LANES),
            bf16(nx, blk, LANES),
            bf16(nx, blk, LANES),
            bf16(nx * py, blk, LANES),
            bf16(nx * py, blk, LANES),
        ),
        in_specs=[SMEM, SMEM, VMEM, ANY],
        out_specs=[VMEM] * 7,
        scratch_shapes=[
            pltpu.VMEM(a_view.shape, jnp.bfloat16),
            pltpu.VMEM((10 * rows, LANES), f32),
            pltpu.VMEM((4 * SUB, LANES), f32),
            pltpu.SMEM((2, aggregates), jnp.int32),
            pltpu.SemaphoreType.DMA((px * py,)),
        ],
        cost_estimate=pl.CostEstimate(flops=10**9, bytes_accessed=4 * 10**6, transcendentals=0),
        name="inner_blocks",
    )(route_row, pairing, p_view, a_view)

    def chain(axis):
        n = lax.axis_size(axis)
        up = [(i, i + 1) for i in range(n - 1)]
        return up, [(j, i) for i, j in up]

    swap = [(0, 1), (1, 0)]
    xface = lax.ppermute(xface, "gx", swap)
    got_0 = lax.ppermute(send_0, "gx", swap)
    up, down = chain("gy")
    ylow, yhigh = lax.ppermute(yup, "gy", up), lax.ppermute(ydn, "gy", down)
    up, down = chain("gz")
    zlow, zhigh = lax.ppermute(zup, "gz", up), lax.ppermute(zdn, "gz", down)

    send_1, keep_1 = pl.pallas_call(
        functools.partial(outer_kernel, dims),
        out_shape=(bf16(6 * rows, LANES), bf16(6 * rows, LANES)),
        in_specs=[SMEM, SMEM] + [VMEM] * 7,
        out_specs=[VMEM] * 2,
        scratch_shapes=[
            pltpu.VMEM((nx + 2, ny + 2, nz, 2 * blk, LANES), jnp.bfloat16),
            pltpu.VMEM((2, nx, ny, 2 * blk, LANES), jnp.bfloat16),
            pltpu.VMEM((nx, ny, 2 * blk, LANES), jnp.bfloat16),
            pltpu.VMEM((12 * rows, LANES), f32),
            pltpu.SMEM((2, aggregates), jnp.int32),
        ],
        cost_estimate=pl.CostEstimate(flops=10**9, bytes_accessed=4 * 10**6, transcendentals=0),
        name="outer_blocks",
    )(route_row, pairing, p_view, a_view, xface, ylow, yhigh, zlow, zhigh)
    got_1 = lax.ppermute(send_1, "gx", swap)

    full = (capacity // SUB) * SUB * lines
    whole = 2 * rows
    half, out = pl.pallas_call(
        functools.partial(keep_kernel, (capacity, rows)),
        out_shape=(bf16(11, rows - full, LANES), bf16(11, whole, LANES)),
        in_specs=[VMEM] * 2,
        out_specs=[VMEM, ANY],
        scratch_shapes=[pltpu.VMEM((11, full, LANES), jnp.bfloat16), pltpu.SemaphoreType.DMA((11,))],
        cost_estimate=pl.CostEstimate(flops=10**7, bytes_accessed=4 * 10**6, transcendentals=0),
        name="place_kept",
    )(keep_0, keep_1)
    out = pl.pallas_call(
        functools.partial(take_kernel, (capacity, rows)),
        out_shape=bf16(11, whole, LANES),
        in_specs=[VMEM] * 3 + [ANY],
        out_specs=ANY,
        input_output_aliases={3: 0},
        scratch_shapes=[
            pltpu.VMEM((11, full, LANES), jnp.bfloat16),
            pltpu.VMEM((11, full, LANES), jnp.bfloat16),
            pltpu.SemaphoreType.DMA((2, 11)),
        ],
        cost_estimate=pl.CostEstimate(flops=10**7, bytes_accessed=4 * 10**6, transcendentals=0),
        name="place_received",
    )(got_0, got_1, half, out)
    out = out.reshape(11, whole // (SUB * lines), lines, SUB, LANES).transpose(1, 3, 0, 2, 4)
    return out.reshape(2 * capacity, 11, entries)


def solution(mesh):
    placed = (
        P("gx", "gy", "gz", None, None),
        P("gx", "gy", "gz", None),
        P("gx", "gy", "gz"),
        P(("gx", "gy", "gz"), None),
    )
    return jax.shard_map(
        local,
        mesh=mesh,
        in_specs=placed,
        out_specs=P(("gx", "gy", "gz"), None, None),
        check_vma=False,
    )
```

```python
import functools
import math

import jax
import jax.numpy as jnp
from jax import lax
from jax.experimental import pallas as pl
from jax.experimental.pallas import tpu as pltpu
from jax.sharding import PartitionSpec as P


x_first_order = [0, 2, 1, 3, 4, 5, 6]
x_second_order = [0, 1, 2, 3, 4, 5, 6]
y_first_order = [0, 4, 1, 2, 3, 5, 6]
y_second_order = [0, 3, 1, 2, 4, 5, 6]

LANES = 128
SUB = 8


def padded_2(array, sides, width):
    for axis, dim in sides:
        devices, length = (lax.axis_size(axis), array.shape[dim])
        up = [(i, (i + 1) % devices) for i in range(devices - 1)]
        down = [(j, i) for i, j in up]
        last = lax.slice_in_dim(array, length - width, length, axis=dim)
        initial = lax.slice_in_dim(array, 0, width, axis=dim)
        before = lax.ppermute(last, axis, up)
        after = lax.ppermute(initial, axis, down)
        array = jnp.concatenate([before, array, after], axis=dim)
    return array


def neighbours(padded):
    shifted = [
        padded[1:-1, 1:-1, 1:-1],
        padded[:-2, 1:-1, 1:-1],
        padded[2:, 1:-1, 1:-1],
        padded[1:-1, :-2, 1:-1],
        padded[1:-1, 2:, 1:-1],
        padded[1:-1, 1:-1, :-2],
        padded[1:-1, 1:-1, 2:],
    ]
    return jnp.stack(shifted, axis=3)


def triple(blocks, nearby):
    block_side = math.isqrt(blocks.shape[-1])
    leading = blocks.shape[:-1]
    left_mat = blocks.reshape(leading + (block_side, block_side))
    right_mat = nearby.reshape(leading + (block_side, block_side))
    own_block = jnp.swapaxes(right_mat[..., :1, :, :], -1, -2)
    product = jnp.matmul(left_mat, right_mat, preferred_element_type=jnp.float32).astype(
        jnp.bfloat16
    )
    result = jnp.matmul(own_block, product, preferred_element_type=jnp.float32)
    return result.reshape(leading + (block_side * block_side,))


def members(element_grid, pairs):
    size_x, size_y, size_z = element_grid.shape[:3]
    trailing = element_grid.shape[3:]
    patches = element_grid.reshape((size_x // 2, 2, size_y // 2, 2, size_z) + trailing)

    def pick(upper, lower, slot_order):
        return jnp.take(patches[:, upper, :, lower], jnp.array(slot_order, dtype=jnp.int32), axis=3)

    x_one = jnp.stack([pick(0, 0, x_first_order), pick(0, 1, x_first_order)], axis=3)
    x_two = jnp.stack([pick(1, 0, x_second_order), pick(1, 1, x_second_order)], axis=3)
    y_one = jnp.stack([pick(0, 0, y_first_order), pick(1, 0, y_first_order)], axis=3)
    y_two = jnp.stack([pick(0, 1, y_second_order), pick(1, 1, y_second_order)], axis=3)
    along_x = (pairs == 0).reshape(pairs.shape + (1,) * (x_one.ndim - 3))
    member_one = jnp.where(along_x, x_one, y_one)
    member_two = jnp.where(along_x, x_two, y_two)
    return (
        member_one.reshape((-1,) + member_one.shape[4:]),
        member_two.reshape((-1,) + member_two.shape[4:]),
    )


def arrange(member_one, member_two):
    diagonal = (
        member_one[..., 0, :]
        + member_two[..., 0, :]
        + member_one[..., 1, :]
        + member_two[..., 1, :]
    )
    return jnp.concatenate(
        [diagonal[..., None, :], member_one[..., 2:, :], member_two[..., 2:, :]], axis=-2
    )


def slot_sources(routes, n_dest, capacity):
    total = routes.shape[0]
    chosen = (routes[:, None] == jnp.arange(n_dest, dtype=jnp.int32)[None, :]).astype(jnp.int32)
    before = jnp.cumsum(chosen, axis=0) - chosen
    ranking = jnp.sum(before * chosen, axis=1)
    position = routes * capacity + ranking
    targets = jnp.arange(n_dest * capacity, dtype=jnp.int32)
    matches = position[None, :] == targets[:, None]
    anchor = jnp.sum(jnp.where(matches, jnp.arange(total, dtype=jnp.int32)[None, :], 0), axis=1)
    filled = jnp.any(matches, axis=1)
    return (anchor, filled)


def pack_slots(payload, anchor, filled):
    taken = jnp.take(payload, anchor, axis=0)
    keep_row = filled.reshape(filled.shape + (1,) * (payload.ndim - 1))
    return jnp.where(keep_row, taken, jnp.zeros_like(taken))


def general(a_blocks, prolong, pairing, route, capacity):
    padded = padded_2(prolong, (("gx", 0), ("gy", 1), ("gz", 2)), 1)
    nearby = neighbours(padded)
    anchor, filled = slot_sources(route[:, 0], lax.axis_size("gx"), capacity)
    galerkin = triple(a_blocks, nearby)
    member_one, member_two = members(galerkin, pairing)
    coarse = arrange(member_one, member_two).astype(jnp.bfloat16)
    return lax.all_to_all(
        pack_slots(coarse, anchor, filled), "gx", split_axis=0, concat_axis=0, tiled=True
    )


def dot(left, right):
    return jnp.dot(left, right, preferred_element_type=jnp.float32)


def iota(shape, axis):
    return lax.broadcasted_iota(jnp.int32, shape, axis)


def as_bf16(mask):
    return mask.astype(jnp.float32).astype(jnp.bfloat16)


def pair(one, two):
    h = one.shape[1] // 2
    low = jnp.concatenate([one[:, :h], two[:, :h]], axis=1)
    high = jnp.concatenate([one[:, h:], two[:, h:]], axis=1)
    return jnp.concatenate([low, high], axis=0)


def unpair(both):
    rows, h = both.shape[0] // 2, both.shape[1] // 2
    even, odd = both[:rows], both[rows:]
    return (
        jnp.concatenate([even[:, :h], odd[:, :h]], axis=1),
        jnp.concatenate([even[:, h:], odd[:, h:]], axis=1),
    )


def constants(blk):
    n = 2 * blk
    row, col = iota((n, n), 0), iota((n, n), 1)
    c, z = row % blk, row // blk
    clean = as_bf16(col == (c % 2) * blk + (c // 2) * 2 + z)
    q = blk // 2
    k, p = row // blk, (row // q) % 2
    spread = as_bf16(col == k * blk + 2 * (row % q) + p)
    return clean, spread


def even_lanes(rows):
    return as_bf16(iota((rows, LANES), 1) % 2 == 0), as_bf16(iota((rows, LANES), 1) % 2 == 1)


def even_rows(rows):
    return as_bf16(iota((rows, LANES), 0) % 2 == 0), as_bf16(iota((rows, LANES), 0) % 2 == 1)


def transposed_dot(left, right):
    return lax.dot_general(
        left, right, (((1,), (1,)), ((), ())), preferred_element_type=jnp.float32
    )


def store_left(left_ref, x, b, both_t, masks):
    q = masks[0].shape[0]
    for k in range(2):
        for p in range(2):
            part = both_t[(2 * k + p) * q : (2 * k + p + 1) * q]
            for z in range(2):
                left_ref[x, 2 * b + k, (2 * p + z) * q : (2 * p + z + 1) * q] = part * masks[z]


def store_weight(ref, one):
    none = jnp.zeros_like(one)
    rows = one.shape[0]
    ref[:rows] = jnp.concatenate([one, none], axis=1)
    ref[rows:] = jnp.concatenate([none, one], axis=1)


def halves(part):
    h = part.shape[1] // 2
    return part[:, :h], part[:, h:]


def places(route_ref, where_ref, table_ref, dims, blocks):
    aggregates, cap, rows = dims
    me = lax.axis_index("gx")
    lines = rows // cap
    rest = cap % SUB
    half = (cap - rest) * lines
    at_zero = me == 0
    for c in range(cap):
        if c < cap - rest:
            zero = (c, c + half // 2, c, c)
        else:
            h = c - (cap - rest)
            zero = (half + h, half + h + rest, SUB + h, SUB + h + rest)
        if c < rest:
            one = (half + c + rest, half + c, SUB + c, SUB + c + rest)
        else:
            h = c - rest
            one = (h, h + half // 2, h, h)
        for k in range(4):
            table_ref[k, c] = jnp.where(at_zero, zero[k], one[k])
    sent, kept = jnp.int32(0), jnp.int32(0)
    for i in range(aggregates):
        away = route_ref[0, i] != me
        one = away.astype(jnp.int32)
        c = jnp.where(away, sent, kept)
        sent = sent + one
        kept = kept + (1 - one)
        base = jnp.where(away, 0, blocks * rows)
        where_ref[0, i] = base + table_ref[0, c]
        where_ref[1, i] = base + table_ref[1, c]
        where_ref[2, i] = jnp.where(away, 0, 2 * SUB) + table_ref[2, c]
        where_ref[3, i] = jnp.where(away, 0, 2 * SUB) + table_ref[3, c]
    return sent, kept


def put(total_ref, where_ref, i, block, rows, value):
    n = value.shape[0] // 2
    one = where_ref[0, i] + block * rows
    two = where_ref[1, i] + block * rows
    total_ref[pl.ds(one, n, stride=SUB), :] = value[:n]
    total_ref[pl.ds(two, n, stride=SUB), :] = value[n:]


def finish(out, total_ref, kind, blocks, dims, count):
    _, cap, rows = dims
    rest = cap % SUB
    full = (cap - rest) * (rows // cap)
    me = lax.axis_index("gx")
    line = iota((SUB, LANES), 0)
    in_full = (line + jnp.where(me == 0, 0, rest) < count)[None]
    in_half = (line % rest + jnp.where(me == 0, cap - rest, 0) < count)[None]
    for k in range(blocks):
        for at, size, filled in ((0, full, in_full), (full, rows - full, in_half)):
            value = total_ref[pl.ds((kind * blocks + k) * rows + at, size), :].reshape(-1, SUB, LANES)
            value = jnp.where(filled, value, 0.0).reshape(size, LANES)
            out[k * rows + at : k * rows + at + size] = value.astype(jnp.bfloat16)


GROUP = 4


def in_groups(items, size):
    items = list(items)
    return [items[k : k + size] for k in range(0, len(items), size)]


def inner_kernel(
    dims, grid, route_ref, pair_ref, p_ref, a_hbm, send_ref, keep_ref, xface_ref, yup_ref, ydn_ref, zup_ref, zdn_ref,
    a_ref, left_ref, weight_ref, part_ref, total_ref, codes_ref, where_ref, table_ref, sems,
):
    px, py, nz = grid
    aggregates, _, rows = dims
    blk = p_ref.shape[2]
    q = blk // 2
    nb = 5
    patches = [(a, b) for a in range(px) for b in range(py)]

    def fetch(n):
        a, b = patches[n]
        at = (pl.ds(2 * a, 2), pl.ds(2 * b, 2))
        return pltpu.make_async_copy(a_hbm.at[at], a_ref.at[at], sems.at[n])

    for n in range(len(patches)):
        fetch(n).start()
    clean, spread = constants(blk)
    lanes_of = even_lanes(q)
    sent, kept = places(route_ref, where_ref, table_ref, dims, nb)
    codes_ref[...] = jnp.zeros_like(codes_ref)
    for i in range(aggregates):
        a, b, z, t = i // (py * nz * 2), (i // (nz * 2)) % py, (i // 2) % nz, i % 2
        code = (2 * (jnp.where(pair_ref[a, b, z] == 0, 2, 1) - t) + z).astype(jnp.float32)
        line = jnp.full((1, LANES), code, jnp.float32)
        codes_ref[pl.ds(where_ref[2, i], 1), :] = line
        codes_ref[pl.ds(where_ref[3, i], 1), :] = line
    me = lax.axis_index("gx")
    xface_ref[...] = p_ref[jnp.where(me == 0, 2 * px - 1, 0)]
    for x in range(2 * px):
        yup_ref[x] = p_ref[x, 2 * py - 1]
        ydn_ref[x] = p_ref[x, 0]

    for group in in_groups([(x, b) for x in range(2 * px) for b in range(py)], GROUP):
        both = [pair(p_ref[x, 2 * b], p_ref[x, 2 * b + 1]) for x, b in group]
        tidy = [dot(clean, one).astype(jnp.bfloat16) for one in both]
        left = [transposed_dot(spread, one).astype(jnp.bfloat16) for one in both]
        for (x, b), one in zip(group, tidy):
            zdn_ref[x * py + b] = one[:blk]
            zup_ref[x * py + b] = one[blk:]
            for z in range(nz):
                for v, part in enumerate(halves(one[z * blk : (z + 1) * blk])):
                    store_weight(weight_ref.at[x, 2 * b + v, z], part)
        for (x, b), one in zip(group, left):
            store_left(left_ref, x, b, one, lanes_of)

    first, second = even_rows(blk)
    for n, (a, b) in enumerate(patches):
        fetch(n).wait()
        group = [(2 * a + u, 2 * b + v) for u in range(2) for v in range(2)]
        right = []
        for x, y in group:
            here = a_ref.at[x, y]
            along_z = here[6] * first + here[5] * second
            right.append(
                jnp.concatenate(
                    [pair(here[0], here[2 - x % 2]), pair(here[4 - y % 2], along_z)], axis=1
                )
            )
        got = [dot(left_ref[x, y], one).astype(jnp.bfloat16) for (x, y), one in zip(group, right)]
        for (x, y), one in zip(group, got):
            parts = unpair(one[:, : 2 * blk]) + unpair(one[:, 2 * blk :])
            for k in range(4):
                part_ref[x, y, k] = parts[k]

    for a, b in patches:
        own, with_x, with_y, with_z = {}, {}, {}, {}
        group = [(u, v, z) for z in range(nz) for u in range(2) for v in range(2)]
        stacks = []
        for u, v, z in group:
            x, y = 2 * a + u, 2 * b + v
            zs, zo = pl.ds(z * q, q), pl.ds((1 - z) * q, q)
            stacks.append(
                jnp.concatenate(
                    [
                        part_ref[x, y, 0, zs],
                        part_ref[2 * a + 1 - u, y, 1, zs],
                        part_ref[x, 2 * b + 1 - v, 2, zs],
                        part_ref[x, y, 3, zo],
                    ],
                    axis=0,
                )
            )
        made = [
            dot(one, weight_ref[2 * a + u, 2 * b + v, z]) for (u, v, z), one in zip(group, stacks)
        ]
        for (u, v, z), got in zip(group, made):
            own[u, v, z] = got[:q]
            with_x[1 - u, v, z] = got[q : 2 * q]
            with_y[u, 1 - v, z] = got[2 * q : 3 * q]
            with_z[u, v, 1 - z] = got[3 * q :]
        for z in range(nz):
            flat = pair_ref[a, b, z] == 0
            i = ((a * py + b) * nz + z) * 2
            sums = {}
            for u in range(2):
                for v in range(2):
                    t = u if u == v else jnp.where(flat, v, u)
                    m = u if u == v else jnp.where(flat, u, v)
                    e = (u, v, z)
                    sums[u, v] = own[e] + jnp.where(flat, with_x[e], with_y[e])
                    cross = jnp.where(flat, with_y[e], with_x[e])
                    put(total_ref, where_ref, i + t, 1 + 2 * m, rows, cross)
                    put(total_ref, where_ref, i + t, 2 + 2 * m, rows, with_z[e])
            put(total_ref, where_ref, i, 0, rows, sums[0, 0] + jnp.where(flat, sums[1, 0], sums[0, 1]))
            put(total_ref, where_ref, i + 1, 0, rows, sums[1, 1] + jnp.where(flat, sums[0, 1], sums[1, 0]))

    for kind, (out, count) in enumerate(((send_ref, sent), (keep_ref, kept))):
        finish(out, total_ref, kind, nb, dims, count)
        out[nb * rows :] = codes_ref[kind * 2 * SUB : (kind + 1) * 2 * SUB].astype(jnp.bfloat16)


def outer_kernel(
    dims, grid, route_ref, pair_ref, p_ref, a_hbm, zup_ref, zdn_ref, xface_hbm, ylow_hbm, yhigh_hbm, zlow_hbm, zhigh_hbm,
    send_ref, keep_ref,
    a_ref, xface_ref, ylow_ref, yhigh_ref, zlow_ref, zhigh_ref,
    weight_ref, zweight_ref, left_ref, part_ref, total_ref, where_ref, table_ref, sems,
):
    px, py, nz = grid
    _, _, rows = dims
    nx, ny = 2 * px, 2 * py
    blk = p_ref.shape[2]
    q = blk // 2
    nb = 6
    copies = [
        pltpu.make_async_copy(one, two, sems.at[k])
        for k, (one, two) in enumerate((
            (a_hbm, a_ref), (xface_hbm, xface_ref), (ylow_hbm, ylow_ref), (yhigh_hbm, yhigh_ref),
            (zlow_hbm, zlow_ref), (zhigh_hbm, zhigh_ref),
        ))
    ]
    for copy in copies:
        copy.start()
    sent, kept = places(route_ref, where_ref, table_ref, dims, nb)
    me = lax.axis_index("gx")
    clean, spread = constants(blk)
    lanes_of = even_lanes(q)
    first, second = even_rows(blk)

    for group in in_groups([(x, b) for x in range(nx) for b in range(py)], GROUP):
        both = [pair(p_ref[x, 2 * b], p_ref[x, 2 * b + 1]) for x, b in group]
        left = [transposed_dot(spread, one).astype(jnp.bfloat16) for one in both]
        for x, b in group:
            for z, ref in enumerate((zdn_ref, zup_ref)):
                for v, part in enumerate(halves(ref[x * py + b])):
                    store_weight(weight_ref.at[x + 1, 2 * b + v + 1, z], part)
        for (x, b), one in zip(group, left):
            store_left(left_ref, x, b, one, lanes_of)
    copies[0].wait()
    for group in in_groups([(x, y) for x in range(nx) for y in range(ny)], GROUP):
        right = []
        for x, y in group:
            here = a_ref.at[x, y]
            along_z = here[5] * first + here[6] * second
            low, high = halves(along_z)
            right.append(
                jnp.concatenate(
                    [pair(here[1 + x % 2], here[3 + y % 2]), jnp.concatenate([low, high], axis=0)],
                    axis=1,
                )
            )
        got = [dot(left_ref[x, y], one).astype(jnp.bfloat16) for (x, y), one in zip(group, right)]
        for (x, y), one in zip(group, got):
            part_ref[x, y, 0], part_ref[x, y, 1] = unpair(one[:, : 2 * blk])
            along = one[:, 2 * blk :]
            part_ref[x, y, 2] = jnp.concatenate([along[:blk], along[blk:]], axis=1)

    for copy in copies[1:]:
        copy.wait()
    above = jnp.where(me == 0, 0.0, 1.0)
    sides = [xface_ref[y] for y in range(ny)], [ylow_ref[x] for x in range(nx)], [yhigh_ref[x] for x in range(nx)]
    both = [[pair(one[k], one[k + 1]) for k in range(0, len(one), 2)] for one in sides]
    tidy = [[dot(clean, one) for one in some] for some in both]
    for b in range(py):
        for at, scale in ((0, above), (nx + 1, 1.0 - above)):
            one = (tidy[0][b] * scale).astype(jnp.bfloat16)
            for z in range(nz):
                for v, part in enumerate(halves(one[z * blk : (z + 1) * blk])):
                    store_weight(weight_ref.at[at, 2 * b + v + 1, z], part)
    for at, some in ((0, tidy[1]), (ny + 1, tidy[2])):
        for a in range(px):
            one = some[a].astype(jnp.bfloat16)
            for z in range(nz):
                for u, part in enumerate(halves(one[z * blk : (z + 1) * blk])):
                    store_weight(weight_ref.at[2 * a + u + 1, at, z], part)
    for side, ref in enumerate((zlow_ref, zhigh_ref)):
        for x in range(nx):
            for b in range(py):
                for v, part in enumerate(halves(ref[x * py + b])):
                    store_weight(zweight_ref.at[side, x, 2 * b + v], part)

    for group in in_groups([(x, y) for x in range(nx) for y in range(ny)], 2):
        work = []
        for x, y in group:
            for z in range(nz):
                zs = pl.ds(z * q, q)
                a, b, u, v = x // 2, y // 2, x % 2, y % 2
                flat = pair_ref[a, b, z] == 0
                t = u if u == v else jnp.where(flat, v, u)
                m = u if u == v else jnp.where(flat, u, v)
                i = ((a * py + b) * nz + z) * 2 + t
                for k, weight in enumerate((
                    weight_ref.at[x + 2 * u, y + 1, z],
                    weight_ref.at[x + 1, y + 2 * v, z],
                    zweight_ref.at[z, x, y],
                )):
                    work.append((i, 3 * m + k, part_ref[x, y, k, zs], weight))
        made = [dot(left, weight[...]) for _, _, left, weight in work]
        for (i, block, _, _), got in zip(work, made):
            put(total_ref, where_ref, i, block, rows, got)

    for kind, (out, count) in enumerate(((send_ref, sent), (keep_ref, kept))):
        finish(out, total_ref, kind, nb, dims, count)


def placed_blocks(early_ref, late_ref, rows, at, size, codes):
    code = jnp.concatenate([codes, codes], axis=0)
    near_low, near_high = (code < 1.5)[None], (code > 3.5)[None]
    upper = ((code == 1.0) | (code == 3.0) | (code == 5.0))[None]

    def tiles(ref, k):
        return ref[k * rows + at : k * rows + at + size].reshape(-1, 2 * SUB, LANES)

    yield tiles(early_ref, 0)
    for m in range(2):
        cross, z_in = tiles(early_ref, 1 + 2 * m), tiles(early_ref, 2 + 2 * m)
        x_out, y_out, z_out = (tiles(late_ref, 3 * m + k) for k in range(3))
        yield jnp.where(near_low, cross, x_out)
        yield jnp.where(near_low, x_out, jnp.where(near_high, y_out, cross))
        yield jnp.where(near_high, cross, y_out)
        yield jnp.where(upper, z_in, z_out)
        yield jnp.where(upper, z_out, z_in)


def keep_kernel(dims, early_ref, late_ref, half_ref, out_hbm, full_ref, sem):
    cap, rows = dims
    full = (cap - cap % SUB) * (rows // cap)
    me = lax.axis_index("gx")
    codes = early_ref[5 * rows :]
    copies = []
    for k, value in enumerate(placed_blocks(early_ref, late_ref, rows, 0, full, codes[:SUB])):
        full_ref[k] = value.reshape(full, LANES)
        to = out_hbm.at[k, pl.ds(me * (2 * full), full), :]
        copies.append(pltpu.make_async_copy(full_ref.at[k], to, sem.at[k]))
        copies[-1].start()
    for k, value in enumerate(placed_blocks(early_ref, late_ref, rows, full, rows - full, codes[SUB:])):
        half_ref[k] = value.reshape(rows - full, LANES)
    for copy in copies:
        copy.wait()


def take_kernel(dims, early_ref, late_ref, half_ref, _, out_hbm, full_ref, mixed_ref, sem):
    cap, rows = dims
    full = (cap - cap % SUB) * (rows // cap)
    me = lax.axis_index("gx")
    codes = early_ref[5 * rows :]
    copies = []
    for k, value in enumerate(placed_blocks(early_ref, late_ref, rows, 0, full, codes[:SUB])):
        full_ref[k] = value.reshape(full, LANES)
        to = out_hbm.at[k, pl.ds((1 - me) * (2 * full), full), :]
        copies.append(pltpu.make_async_copy(full_ref.at[k], to, sem.at[0, k]))
        copies[-1].start()
    first_half = (iota((SUB, LANES), 0) < SUB // 2)[None]
    pick = first_half == (me == 0)
    for k, value in enumerate(placed_blocks(early_ref, late_ref, rows, full, rows - full, codes[SUB:])):
        theirs = value.reshape(rows - full, LANES).astype(jnp.float32).reshape(-1, SUB, LANES)
        mine = half_ref[k].astype(jnp.float32).reshape(-1, SUB, LANES)
        low = jnp.where(pick, mine, theirs)
        high = pltpu.roll(jnp.where(pick, theirs, mine), SUB // 2, 1)
        mixed_ref[k, : rows - full] = low.reshape(rows - full, LANES).astype(jnp.bfloat16)
        mixed_ref[k, rows - full :] = high.reshape(rows - full, LANES).astype(jnp.bfloat16)
        to = out_hbm.at[k, full : 2 * full, :]
        copies.append(pltpu.make_async_copy(mixed_ref.at[k], to, sem.at[1, k]))
        copies[-1].start()
    for copy in copies:
        copy.wait()


SMEM = pl.BlockSpec(memory_space=pltpu.SMEM)
VMEM = pl.BlockSpec(memory_space=pltpu.VMEM)
ANY = pl.BlockSpec(memory_space=pl.ANY)


def bf16(*shape):
    return jax.ShapeDtypeStruct(shape, jnp.bfloat16)


def local(a_blocks, prolong, pairing, route):
    devices_gx = lax.axis_size("gx")
    aggregates = route.shape[0]
    capacity = max(2, 3 * aggregates // (2 * devices_gx))
    nx, ny, nz, faces, entries = a_blocks.shape
    fits = (
        devices_gx == 2
        and nz == 2
        and nx % 2 == 0
        and ny % 2 == 0
        and faces == 7
        and entries == (LANES // 2) ** 2
        and capacity // SUB == 1
        and capacity % SUB == SUB // 2
    )
    if not fits:
        return general(a_blocks, prolong, pairing, route, capacity)
    px, py = nx // 2, ny // 2
    blk = math.isqrt(entries)
    lines = entries // LANES
    a_view = a_blocks.transpose(0, 1, 3, 2, 4).reshape(nx, ny, faces, nz, lines, LANES)
    a_view = a_view.transpose(0, 1, 2, 4, 3, 5).reshape(nx, ny, faces, nz * lines, LANES)
    p_view = prolong.reshape(nx, ny, nz, lines, LANES).transpose(0, 1, 3, 2, 4)
    p_view = p_view.reshape(nx, ny, nz * lines, LANES)
    route_row = route.reshape(1, aggregates)
    rows = capacity * lines
    dims, grid = (aggregates, capacity, rows), (px, py, nz)
    f32 = jnp.float32
    half_type = jnp.bfloat16
    face_x, face_y, face_z = (ny, blk, LANES), (nx, blk, LANES), (nx * py, blk, LANES)
    room = pltpu.CompilerParams(vmem_limit_bytes=67_043_328)
    cost = pl.CostEstimate(flops=10**9, bytes_accessed=4 * 10**6, transcendentals=0)

    send_0, keep_0, xface, yup, ydn, zup, zdn = pl.pallas_call(
        functools.partial(inner_kernel, dims, grid),
        out_shape=(
            bf16(5 * rows + 2 * SUB, LANES),
            bf16(5 * rows + 2 * SUB, LANES),
            bf16(*face_x),
            bf16(*face_y),
            bf16(*face_y),
            bf16(*face_z),
            bf16(*face_z),
        ),
        in_specs=[SMEM, SMEM, VMEM, ANY],
        out_specs=[VMEM] * 7,
        scratch_shapes=[
            pltpu.VMEM(a_view.shape, half_type),
            pltpu.VMEM((nx, ny, 2 * blk, LANES), half_type),
            pltpu.VMEM((nx, ny, nz, 2 * blk, LANES), half_type),
            pltpu.VMEM((nx, ny, 4, blk, LANES), half_type),
            pltpu.VMEM((10 * rows, LANES), f32),
            pltpu.VMEM((4 * SUB, LANES), f32),
            pltpu.SMEM((4, aggregates), jnp.int32),
            pltpu.SMEM((4, capacity), jnp.int32),
            pltpu.SemaphoreType.DMA((px * py,)),
        ],
        compiler_params=room,
        cost_estimate=cost,
        name="inner_blocks",
    )(route_row, pairing, p_view, a_view)

    def chain(axis):
        n = lax.axis_size(axis)
        up = [(i, i + 1) for i in range(n - 1)]
        return up, [(j, i) for i, j in up]

    swap = [(0, 1), (1, 0)]
    xface = lax.ppermute(xface, "gx", swap)
    got_0 = lax.ppermute(send_0, "gx", swap)
    up, down = chain("gy")
    ylow = lax.ppermute(yup, "gy", up)
    yhigh = lax.ppermute(ydn, "gy", down)
    up, down = chain("gz")
    zlow = lax.ppermute(zup, "gz", up)
    zhigh = lax.ppermute(zdn, "gz", down)

    send_1, keep_1 = pl.pallas_call(
        functools.partial(outer_kernel, dims, grid),
        out_shape=(bf16(6 * rows, LANES), bf16(6 * rows, LANES)),
        in_specs=[SMEM, SMEM, VMEM, ANY, VMEM, VMEM] + [ANY] * 5,
        out_specs=[VMEM] * 2,
        scratch_shapes=[
            pltpu.VMEM(a_view.shape, half_type),
            pltpu.VMEM(face_x, half_type),
            pltpu.VMEM(face_y, half_type),
            pltpu.VMEM(face_y, half_type),
            pltpu.VMEM(face_z, half_type),
            pltpu.VMEM(face_z, half_type),
            pltpu.VMEM((nx + 2, ny + 2, nz, 2 * blk, LANES), half_type),
            pltpu.VMEM((2, nx, ny, 2 * blk, LANES), half_type),
            pltpu.VMEM((nx, ny, 2 * blk, LANES), half_type),
            pltpu.VMEM((nx, ny, 3, blk, LANES), half_type),
            pltpu.VMEM((12 * rows, LANES), f32),
            pltpu.SMEM((4, aggregates), jnp.int32),
            pltpu.SMEM((4, capacity), jnp.int32),
            pltpu.SemaphoreType.DMA((6,)),
        ],
        compiler_params=pltpu.CompilerParams(vmem_limit_bytes=67_043_328 - 1400 * 1024),
        cost_estimate=cost,
        name="outer_blocks",
    )(route_row, pairing, p_view, a_view, zup, zdn, xface, ylow, yhigh, zlow, zhigh)
    got_1 = lax.ppermute(send_1, "gx", swap)

    full = (capacity // SUB) * SUB * lines
    whole = 2 * rows
    half, out = pl.pallas_call(
        functools.partial(keep_kernel, (capacity, rows)),
        out_shape=(bf16(11, rows - full, LANES), bf16(11, whole, LANES)),
        in_specs=[VMEM] * 2,
        out_specs=[VMEM, ANY],
        scratch_shapes=[pltpu.VMEM((11, full, LANES), half_type), pltpu.SemaphoreType.DMA((11,))],
        compiler_params=room,
        cost_estimate=cost,
        name="place_kept",
    )(keep_0, keep_1)
    out = pl.pallas_call(
        functools.partial(take_kernel, (capacity, rows)),
        out_shape=bf16(11, whole, LANES),
        in_specs=[VMEM] * 3 + [ANY],
        out_specs=ANY,
        input_output_aliases={3: 0},
        scratch_shapes=[
            pltpu.VMEM((11, full, LANES), half_type),
            pltpu.VMEM((11, full, LANES), half_type),
            pltpu.SemaphoreType.DMA((2, 11)),
        ],
        compiler_params=room,
        cost_estimate=cost,
        name="place_received",
    )(got_0, got_1, half, out)
    out = out.reshape(11, whole // (SUB * lines), lines, SUB, LANES).transpose(1, 3, 0, 2, 4)
    return out.reshape(2 * capacity, 11, entries)


def solution(mesh):
    placed = (
        P("gx", "gy", "gz", None, None),
        P("gx", "gy", "gz", None),
        P("gx", "gy", "gz"),
        P(("gx", "gy", "gz"), None),
    )
    return jax.shard_map(
        local,
        mesh=mesh,
        in_specs=placed,
        out_specs=P(("gx", "gy", "gz"), None, None),
        check_vma=False,
    )
```

```python
import functools
import math

import jax
import jax.numpy as jnp
from jax import lax
from jax.experimental import pallas as pl
from jax.experimental.pallas import tpu as pltpu
from jax.sharding import PartitionSpec as P


x_first_order = [0, 2, 1, 3, 4, 5, 6]
x_second_order = [0, 1, 2, 3, 4, 5, 6]
y_first_order = [0, 4, 1, 2, 3, 5, 6]
y_second_order = [0, 3, 1, 2, 4, 5, 6]

LANES = 128
SUB = 8


def padded_2(array, sides, width):
    for axis, dim in sides:
        devices, length = (lax.axis_size(axis), array.shape[dim])
        up = [(i, (i + 1) % devices) for i in range(devices - 1)]
        down = [(j, i) for i, j in up]
        last = lax.slice_in_dim(array, length - width, length, axis=dim)
        initial = lax.slice_in_dim(array, 0, width, axis=dim)
        before = lax.ppermute(last, axis, up)
        after = lax.ppermute(initial, axis, down)
        array = jnp.concatenate([before, array, after], axis=dim)
    return array


def neighbours(padded):
    shifted = [
        padded[1:-1, 1:-1, 1:-1],
        padded[:-2, 1:-1, 1:-1],
        padded[2:, 1:-1, 1:-1],
        padded[1:-1, :-2, 1:-1],
        padded[1:-1, 2:, 1:-1],
        padded[1:-1, 1:-1, :-2],
        padded[1:-1, 1:-1, 2:],
    ]
    return jnp.stack(shifted, axis=3)


def triple(blocks, nearby):
    block_side = math.isqrt(blocks.shape[-1])
    leading = blocks.shape[:-1]
    left_mat = blocks.reshape(leading + (block_side, block_side))
    right_mat = nearby.reshape(leading + (block_side, block_side))
    own_block = jnp.swapaxes(right_mat[..., :1, :, :], -1, -2)
    product = jnp.matmul(left_mat, right_mat, preferred_element_type=jnp.float32).astype(
        jnp.bfloat16
    )
    result = jnp.matmul(own_block, product, preferred_element_type=jnp.float32)
    return result.reshape(leading + (block_side * block_side,))


def members(element_grid, pairs):
    size_x, size_y, size_z = element_grid.shape[:3]
    trailing = element_grid.shape[3:]
    patches = element_grid.reshape((size_x // 2, 2, size_y // 2, 2, size_z) + trailing)

    def pick(upper, lower, slot_order):
        return jnp.take(patches[:, upper, :, lower], jnp.array(slot_order, dtype=jnp.int32), axis=3)

    x_one = jnp.stack([pick(0, 0, x_first_order), pick(0, 1, x_first_order)], axis=3)
    x_two = jnp.stack([pick(1, 0, x_second_order), pick(1, 1, x_second_order)], axis=3)
    y_one = jnp.stack([pick(0, 0, y_first_order), pick(1, 0, y_first_order)], axis=3)
    y_two = jnp.stack([pick(0, 1, y_second_order), pick(1, 1, y_second_order)], axis=3)
    along_x = (pairs == 0).reshape(pairs.shape + (1,) * (x_one.ndim - 3))
    member_one = jnp.where(along_x, x_one, y_one)
    member_two = jnp.where(along_x, x_two, y_two)
    return (
        member_one.reshape((-1,) + member_one.shape[4:]),
        member_two.reshape((-1,) + member_two.shape[4:]),
    )


def arrange(member_one, member_two):
    diagonal = (
        member_one[..., 0, :]
        + member_two[..., 0, :]
        + member_one[..., 1, :]
        + member_two[..., 1, :]
    )
    return jnp.concatenate(
        [diagonal[..., None, :], member_one[..., 2:, :], member_two[..., 2:, :]], axis=-2
    )


def slot_sources(routes, n_dest, capacity):
    total = routes.shape[0]
    chosen = (routes[:, None] == jnp.arange(n_dest, dtype=jnp.int32)[None, :]).astype(jnp.int32)
    before = jnp.cumsum(chosen, axis=0) - chosen
    ranking = jnp.sum(before * chosen, axis=1)
    position = routes * capacity + ranking
    targets = jnp.arange(n_dest * capacity, dtype=jnp.int32)
    matches = position[None, :] == targets[:, None]
    anchor = jnp.sum(jnp.where(matches, jnp.arange(total, dtype=jnp.int32)[None, :], 0), axis=1)
    filled = jnp.any(matches, axis=1)
    return (anchor, filled)


def pack_slots(payload, anchor, filled):
    taken = jnp.take(payload, anchor, axis=0)
    keep_row = filled.reshape(filled.shape + (1,) * (payload.ndim - 1))
    return jnp.where(keep_row, taken, jnp.zeros_like(taken))


def general(a_blocks, prolong, pairing, route, capacity):
    padded = padded_2(prolong, (("gx", 0), ("gy", 1), ("gz", 2)), 1)
    nearby = neighbours(padded)
    anchor, filled = slot_sources(route[:, 0], lax.axis_size("gx"), capacity)
    galerkin = triple(a_blocks, nearby)
    member_one, member_two = members(galerkin, pairing)
    coarse = arrange(member_one, member_two).astype(jnp.bfloat16)
    return lax.all_to_all(
        pack_slots(coarse, anchor, filled), "gx", split_axis=0, concat_axis=0, tiled=True
    )


def dot(left, right):
    return jnp.dot(left, right, preferred_element_type=jnp.float32)


def iota(shape, axis):
    return lax.broadcasted_iota(jnp.int32, shape, axis)


def as_bf16(mask):
    return mask.astype(jnp.float32).astype(jnp.bfloat16)


def pair(one, two):
    h = one.shape[1] // 2
    low = jnp.concatenate([one[:, :h], two[:, :h]], axis=1)
    high = jnp.concatenate([one[:, h:], two[:, h:]], axis=1)
    return jnp.concatenate([low, high], axis=0)


def unpair(both):
    rows, h = both.shape[0] // 2, both.shape[1] // 2
    even, odd = both[:rows], both[rows:]
    return (
        jnp.concatenate([even[:, :h], odd[:, :h]], axis=1),
        jnp.concatenate([even[:, h:], odd[:, h:]], axis=1),
    )


def constants(blk):
    n = 2 * blk
    row, col = iota((n, n), 0), iota((n, n), 1)
    c, z = row % blk, row // blk
    clean = as_bf16(col == (c % 2) * blk + (c // 2) * 2 + z)
    q = blk // 2
    k, p = row // blk, (row // q) % 2
    spread = as_bf16(col == k * blk + 2 * (row % q) + p)
    return clean, spread


def even_lanes(rows):
    return as_bf16(iota((rows, LANES), 1) % 2 == 0), as_bf16(iota((rows, LANES), 1) % 2 == 1)


def even_rows(rows):
    return as_bf16(iota((rows, LANES), 0) % 2 == 0), as_bf16(iota((rows, LANES), 0) % 2 == 1)


def transposed_dot(left, right):
    return lax.dot_general(
        left, right, (((1,), (1,)), ((), ())), preferred_element_type=jnp.float32
    )


def left_factors(both_t, k, masks):
    q = masks[0].shape[0]
    parts = [both_t[(2 * k + p) * q : (2 * k + p + 1) * q] for p in range(2)]
    return jnp.concatenate([part * mask for part in parts for mask in masks], axis=0)


def weights_of(part):
    h = part.shape[1] // 2
    none = jnp.zeros((part.shape[0], h), part.dtype)
    made = []
    for k in range(2):
        one = part[:, k * h : (k + 1) * h]
        made.append(
            jnp.concatenate(
                [jnp.concatenate([one, none], axis=1), jnp.concatenate([none, one], axis=1)], axis=0
            )
        )
    return made


def halves(part):
    h = part.shape[1] // 2
    return part[:, :h], part[:, h:]


def places(route_ref, where_ref, table_ref, dims, blocks):
    aggregates, cap, rows = dims
    me = lax.axis_index("gx")
    lines = rows // cap
    rest = cap % SUB
    half = (cap - rest) * lines
    at_zero = me == 0
    for c in range(cap):
        if c < cap - rest:
            zero = (c, c + half // 2, c, c)
        else:
            h = c - (cap - rest)
            zero = (half + h, half + h + rest, SUB + h, SUB + h + rest)
        if c < rest:
            one = (half + c + rest, half + c, SUB + c, SUB + c + rest)
        else:
            h = c - rest
            one = (h, h + half // 2, h, h)
        for k in range(4):
            table_ref[k, c] = jnp.where(at_zero, zero[k], one[k])
    sent, kept = jnp.int32(0), jnp.int32(0)
    for i in range(aggregates):
        away = route_ref[0, i] != me
        one = away.astype(jnp.int32)
        c = jnp.where(away, sent, kept)
        sent = sent + one
        kept = kept + (1 - one)
        base = jnp.where(away, 0, blocks * rows)
        where_ref[0, i] = base + table_ref[0, c]
        where_ref[1, i] = base + table_ref[1, c]
        where_ref[2, i] = jnp.where(away, 0, 2 * SUB) + table_ref[2, c]
        where_ref[3, i] = jnp.where(away, 0, 2 * SUB) + table_ref[3, c]
    return sent, kept


def put(total_ref, where_ref, i, block, rows, value):
    n = value.shape[0] // 2
    one = where_ref[0, i] + block * rows
    two = where_ref[1, i] + block * rows
    total_ref[pl.ds(one, n, stride=SUB), :] = value[:n]
    total_ref[pl.ds(two, n, stride=SUB), :] = value[n:]


def finish(outs, total_ref, kind, dims, count):
    _, cap, rows = dims
    rest = cap % SUB
    full = (cap - rest) * (rows // cap)
    me = lax.axis_index("gx")
    line = iota((2 * SUB, LANES), 0)
    in_full = as_bf16(line % SUB + jnp.where(me == 0, 0, rest) < count) > 0.5
    in_half = as_bf16(line % rest + jnp.where(me == 0, cap - rest, 0) < count) > 0.5
    blocks = sum(n for _, n in outs)
    done = 0
    for out, n in outs:
        for k in range(n):
            for at, size, filled in ((0, full, in_full), (full, rows - full, in_half)):
                value = total_ref[pl.ds((kind * blocks + done + k) * rows + at, size), :]
                value = value.astype(jnp.bfloat16).reshape(-1, 2 * SUB, LANES)
                value = jnp.where(filled[None], value, jnp.zeros_like(value))
                out[k * rows + at : k * rows + at + size] = value.reshape(size, LANES)
        done += n


def inner_kernel(
    dims, grid, route_ref, pair_ref, p_ref, a_hbm,
    send_ref, keep_ref, xface_ref, yup_ref, ydn_ref, zup_ref, zdn_ref, left_ref,
    a_ref, part_ref, total_ref, codes_ref, where_ref, table_ref, sems,
):
    px, py, nz = grid
    aggregates, _, rows = dims
    nx, ny = 2 * px, 2 * py
    blk = p_ref.shape[2]
    q = blk // 2
    nb = 5
    copy = pltpu.make_async_copy(a_hbm, a_ref, sems.at[0])
    copy.start()
    clean, spread = constants(blk)
    masks = even_lanes(q)
    first, second = even_rows(blk)
    me = lax.axis_index("gx")

    pairs = [(x, b) for x in range(nx) for b in range(py)]
    both = {e: pair(p_ref[e[0], 2 * e[1]], p_ref[e[0], 2 * e[1] + 1]) for e in pairs}
    tidy = {e: dot(clean, both[e]).astype(jnp.bfloat16) for e in pairs}
    for x, b in pairs:
        left_ref[x * py + b] = transposed_dot(spread, both[x, b]).astype(jnp.bfloat16)
        zdn_ref[x * py + b] = tidy[x, b][:blk]
        zup_ref[x * py + b] = tidy[x, b][blk:]
    for a in range(px):
        one, two = tidy[2 * a, 0], tidy[2 * a + 1, 0]
        ydn_ref[a] = jnp.concatenate([one[:, :blk], two[:, :blk]], axis=1)
        one, two = tidy[2 * a, py - 1], tidy[2 * a + 1, py - 1]
        yup_ref[a] = jnp.concatenate([one[:, blk:], two[:, blk:]], axis=1)
    for b in range(py):
        for z, ref in enumerate((zdn_ref, zup_ref)):
            xface_ref[b, z * blk : (z + 1) * blk] = ref[jnp.where(me == 0, nx - 1, 0) * py + b]
    copy.wait()

    for x, y in [(x, y) for x in range(nx) for y in range(ny)]:
        here = a_ref.at[x, y]
        along_z = here[6] * first + here[5] * second
        right = jnp.concatenate(
            [pair(here[0], here[2 - x % 2]), pair(here[4 - y % 2], along_z)], axis=1
        )
        left = left_factors(left_ref[x * py + y // 2], y % 2, masks)
        got = dot(left, right).astype(jnp.bfloat16)
        parts = unpair(got[:, : 2 * blk]) + unpair(got[:, 2 * blk :])
        for k in range(4):
            part_ref[x, y, k] = parts[k]

    sent, kept = places(route_ref, where_ref, table_ref, dims, nb)
    codes_ref[...] = jnp.zeros_like(codes_ref)
    for i in range(aggregates):
        a, b, z, t = i // (py * nz * 2), (i // (nz * 2)) % py, (i // 2) % nz, i % 2
        code = (2 * (jnp.where(pair_ref[a, b, z] == 0, 2, 1) - t) + z).astype(jnp.float32)
        line = jnp.full((1, LANES), code, jnp.float32)
        codes_ref[pl.ds(where_ref[2, i], 1), :] = line
        codes_ref[pl.ds(where_ref[3, i], 1), :] = line

    for a, b in [(a, b) for a in range(px) for b in range(py)]:
        own, with_x, with_y, with_z = {}, {}, {}, {}
        for z, ref in enumerate((zdn_ref, zup_ref)):
            zs, zo = pl.ds(z * q, q), pl.ds((1 - z) * q, q)
            for u in range(2):
                x = 2 * a + u
                weight = weights_of(ref[x * py + b])
                for v in range(2):
                    y = 2 * b + v
                    stack = jnp.concatenate(
                        [
                            part_ref[x, y, 0, zs],
                            part_ref[2 * a + 1 - u, y, 1, zs],
                            part_ref[x, 2 * b + 1 - v, 2, zs],
                            part_ref[x, y, 3, zo],
                        ],
                        axis=0,
                    )
                    got = dot(stack, weight[v])
                    own[u, v, z] = got[:q]
                    with_x[1 - u, v, z] = got[q : 2 * q]
                    with_y[u, 1 - v, z] = got[2 * q : 3 * q]
                    with_z[u, v, 1 - z] = got[3 * q :]
        for z in range(nz):
            flat = pair_ref[a, b, z] == 0
            i = ((a * py + b) * nz + z) * 2
            sums = {}
            for u in range(2):
                for v in range(2):
                    t = u if u == v else jnp.where(flat, v, u)
                    m = u if u == v else jnp.where(flat, u, v)
                    e = (u, v, z)
                    sums[u, v] = own[e] + jnp.where(flat, with_x[e], with_y[e])
                    cross = jnp.where(flat, with_y[e], with_x[e])
                    put(total_ref, where_ref, i + t, 1 + m, rows, cross)
                    put(total_ref, where_ref, i + t, 3 + m, rows, with_z[e])
            put(total_ref, where_ref, i, 0, rows, sums[0, 0] + jnp.where(flat, sums[1, 0], sums[0, 1]))
            put(total_ref, where_ref, i + 1, 0, rows, sums[1, 1] + jnp.where(flat, sums[0, 1], sums[1, 0]))

    for kind, (out, count) in enumerate(((send_ref, sent), (keep_ref, kept))):
        finish(((out, nb),), total_ref, kind, dims, count)
        out[nb * rows :] = codes_ref[kind * 2 * SUB : (kind + 1) * 2 * SUB].astype(jnp.bfloat16)


def outer_left_kernel(grid, left_ref, a_hbm, part_ref, a_ref, sems):
    px, py, _ = grid
    nx, ny = 2 * px, 2 * py
    blk = a_ref.shape[3]
    copy = pltpu.make_async_copy(a_hbm, a_ref, sems.at[0])
    copy.start()
    masks = even_lanes(blk // 2)
    first, second = even_rows(blk)
    copy.wait()
    for x, y in [(x, y) for x in range(nx) for y in range(ny)]:
        here = a_ref.at[x, y]
        along_z = here[5] * first + here[6] * second
        low, high = halves(along_z)
        right = jnp.concatenate(
            [pair(here[1 + x % 2], here[3 + y % 2]), jnp.concatenate([low, high], axis=0)], axis=1
        )
        left = left_factors(left_ref[x * py + y // 2], y % 2, masks)
        got = dot(left, right).astype(jnp.bfloat16)
        part_ref[x, y, 0], part_ref[x, y, 1] = unpair(got[:, : 2 * blk])
        along = got[:, 2 * blk :]
        part_ref[x, y, 2] = jnp.concatenate([along[:blk], along[blk:]], axis=1)


def outer_kernel(
    dims, grid, route_ref, pair_ref, part_ref, zup_ref, zdn_ref,
    xface_hbm, ylow_hbm, yhigh_hbm, zlow_hbm, zhigh_hbm,
    send_xy_ref, send_z_ref, keep_xy_ref, keep_z_ref,
    xface_ref, ylow_ref, yhigh_ref, zlow_ref, zhigh_ref, total_ref, where_ref, table_ref, sems,
):
    px, py, nz = grid
    _, _, rows = dims
    nx, ny = 2 * px, 2 * py
    blk = part_ref.shape[3]
    q = blk // 2
    nb = 6
    copies = [
        pltpu.make_async_copy(one, two, sems.at[k])
        for k, (one, two) in enumerate((
            (xface_hbm, xface_ref), (ylow_hbm, ylow_ref), (yhigh_hbm, yhigh_ref),
            (zlow_hbm, zlow_ref), (zhigh_hbm, zhigh_ref),
        ))
    ]
    for copy in copies:
        copy.start()
    sent, kept = places(route_ref, where_ref, table_ref, dims, nb)
    me = lax.axis_index("gx")
    above = (iota((blk, LANES), 0) * 0 + me) > 0
    for copy in copies:
        copy.wait()

    def beside_x(x, b, z, u):
        to = x - 1 if u == 0 else x + 1
        if 0 <= to < nx:
            return (zdn_ref, zup_ref)[z][to * py + b]
        part = xface_ref[b, z * blk : (z + 1) * blk].astype(jnp.float32)
        part = jnp.where(above, part, 0.0) if u == 0 else jnp.where(above, 0.0, part)
        return part.astype(jnp.bfloat16)

    def beside_y(x, y, z, v):
        to = y - 1 if v == 0 else y + 1
        if 0 <= to < ny:
            return (zdn_ref, zup_ref)[z][x * py + to // 2], to % 2
        ref = ylow_ref if v == 0 else yhigh_ref
        return ref[x // 2, z * blk : (z + 1) * blk], x % 2

    for x in range(nx):
        made = []
        for b, z in [(b, z) for b in range(py) for z in range(nz)]:
            zs = pl.ds(z * q, q)
            u, a = x % 2, x // 2
            along_x = weights_of(beside_x(x, b, z, u))
            along_z = weights_of((zlow_ref, zhigh_ref)[z][x * py + b])
            flat = pair_ref[a, b, z] == 0
            for v in range(2):
                y = 2 * b + v
                t = u if u == v else jnp.where(flat, v, u)
                m = u if u == v else jnp.where(flat, u, v)
                i = ((a * py + b) * nz + z) * 2 + t
                other, k = beside_y(x, y, z, v)
                along_y = weights_of(other)[k]
                made.append((i, 2 * m, dot(part_ref[x, y, 0, zs], along_x[v])))
                made.append((i, 2 * m + 1, dot(part_ref[x, y, 1, zs], along_y)))
                made.append((i, 4 + m, dot(part_ref[x, y, 2, zs], along_z[v])))
        for i, block, got in made:
            put(total_ref, where_ref, i, block, rows, got)

    for kind, (xy, along, count) in enumerate((
        (send_xy_ref, send_z_ref, sent), (keep_xy_ref, keep_z_ref, kept),
    )):
        finish(((xy, 4), (along, 2)), total_ref, kind, dims, count)


def placed_blocks(early_ref, xy_ref, z_ref, codes, rows, at, size):
    code = jnp.concatenate([codes, codes], axis=0)
    near_low, near_high = (code < 1.5)[None], (code > 3.5)[None]
    upper = ((code == 1.0) | (code == 3.0) | (code == 5.0))[None]

    def tiles(ref, k):
        return ref[k * rows + at : k * rows + at + size].reshape(-1, 2 * SUB, LANES)

    if xy_ref is not None:
        yield 0, tiles(early_ref, 0)
        for m in range(2):
            cross, x_out, y_out = tiles(early_ref, 1 + m), tiles(xy_ref, 2 * m), tiles(xy_ref, 2 * m + 1)
            yield 1 + 5 * m, jnp.where(near_low, cross, x_out)
            yield 2 + 5 * m, jnp.where(near_low, x_out, jnp.where(near_high, y_out, cross))
            yield 3 + 5 * m, jnp.where(near_high, cross, y_out)
    if z_ref is not None:
        for m in range(2):
            z_in, z_out = tiles(early_ref, 3 + m), tiles(z_ref, m)
            yield 4 + 5 * m, jnp.where(upper, z_in, z_out)
            yield 5 + 5 * m, jnp.where(upper, z_out, z_in)


def keep_kernel(dims, early_ref, xy_ref, z_ref, half_ref, out_hbm, full_ref, sem):
    cap, rows = dims
    full = (cap - cap % SUB) * (rows // cap)
    me = lax.axis_index("gx")
    codes = early_ref[5 * rows :]
    copies = []
    for k, value in placed_blocks(early_ref, xy_ref, z_ref, codes[:SUB], rows, 0, full):
        full_ref[k] = value.reshape(full, LANES)
        to = out_hbm.at[k, pl.ds(me * (2 * full), full), :]
        copies.append(pltpu.make_async_copy(full_ref.at[k], to, sem.at[k]))
        copies[-1].start()
    for k, value in placed_blocks(early_ref, xy_ref, z_ref, codes[SUB:], rows, full, rows - full):
        half_ref[k] = value.reshape(rows - full, LANES)
    for copy in copies:
        copy.wait()


def take_kernel(dims, with_xy, early_ref, late_ref, half_ref, _, out_hbm, full_ref, mixed_ref, sem):
    cap, rows = dims
    full = (cap - cap % SUB) * (rows // cap)
    me = lax.axis_index("gx")
    codes = early_ref[5 * rows :]
    xy_ref, z_ref = (late_ref, None) if with_xy else (None, late_ref)
    copies = []
    for k, value in placed_blocks(early_ref, xy_ref, z_ref, codes[:SUB], rows, 0, full):
        full_ref[k] = value.reshape(full, LANES)
        to = out_hbm.at[k, pl.ds((1 - me) * (2 * full), full), :]
        copies.append(pltpu.make_async_copy(full_ref.at[k], to, sem.at[0, k]))
        copies[-1].start()
    first_half = (iota((SUB, LANES), 0) < SUB // 2)[None]
    pick = first_half == (me == 0)
    for k, value in placed_blocks(early_ref, xy_ref, z_ref, codes[SUB:], rows, full, rows - full):
        theirs = value.reshape(rows - full, LANES).astype(jnp.float32).reshape(-1, SUB, LANES)
        mine = half_ref[k].astype(jnp.float32).reshape(-1, SUB, LANES)
        low = jnp.where(pick, mine, theirs)
        high = pltpu.roll(jnp.where(pick, theirs, mine), SUB // 2, 1)
        mixed_ref[k, : rows - full] = low.reshape(rows - full, LANES).astype(jnp.bfloat16)
        mixed_ref[k, rows - full :] = high.reshape(rows - full, LANES).astype(jnp.bfloat16)
        to = out_hbm.at[k, full : 2 * full, :]
        copies.append(pltpu.make_async_copy(mixed_ref.at[k], to, sem.at[1, k]))
        copies[-1].start()
    for copy in copies:
        copy.wait()


SMEM = pl.BlockSpec(memory_space=pltpu.SMEM)
VMEM = pl.BlockSpec(memory_space=pltpu.VMEM)
ANY = pl.BlockSpec(memory_space=pl.ANY)


def bf16(*shape):
    return jax.ShapeDtypeStruct(shape, jnp.bfloat16)


def local(a_blocks, prolong, pairing, route):
    devices_gx = lax.axis_size("gx")
    aggregates = route.shape[0]
    capacity = max(2, 3 * aggregates // (2 * devices_gx))
    nx, ny, nz, faces, entries = a_blocks.shape
    fits = (
        devices_gx == 2
        and nz == 2
        and nx % 2 == 0
        and ny % 2 == 0
        and faces == 7
        and entries == (LANES // 2) ** 2
        and capacity // SUB == 1
        and capacity % SUB == SUB // 2
    )
    if not fits:
        return general(a_blocks, prolong, pairing, route, capacity)
    px, py = nx // 2, ny // 2
    blk = math.isqrt(entries)
    lines = entries // LANES
    a_view = a_blocks.transpose(0, 1, 3, 2, 4).reshape(nx, ny, faces, nz, lines, LANES)
    a_view = a_view.transpose(0, 1, 2, 4, 3, 5).reshape(nx, ny, faces, nz * lines, LANES)
    p_view = prolong.reshape(nx, ny, nz, lines, LANES).transpose(0, 1, 3, 2, 4)
    p_view = p_view.reshape(nx, ny, nz * lines, LANES)
    route_row = route.reshape(1, aggregates)
    rows = capacity * lines
    dims, grid = (aggregates, capacity, rows), (px, py, nz)
    f32 = jnp.float32
    half_type = jnp.bfloat16
    face_x, face_y, face_z = (py, 2 * blk, LANES), (px, 2 * blk, LANES), (nx * py, blk, LANES)
    parts = (nx, ny, 3, blk, LANES)
    room = pltpu.CompilerParams(vmem_limit_bytes=67_043_328)
    cost = pl.CostEstimate(flops=10**9, bytes_accessed=4 * 10**6, transcendentals=0)

    send_0, keep_0, xface, yup, ydn, zup, zdn, left = pl.pallas_call(
        functools.partial(inner_kernel, dims, grid),
        out_shape=(
            bf16(5 * rows + 2 * SUB, LANES),
            bf16(5 * rows + 2 * SUB, LANES),
            bf16(*face_x),
            bf16(*face_y),
            bf16(*face_y),
            bf16(*face_z),
            bf16(*face_z),
            bf16(nx * py, 2 * blk, LANES),
        ),
        in_specs=[SMEM, SMEM, VMEM, ANY],
        out_specs=[VMEM] * 8,
        scratch_shapes=[
            pltpu.VMEM(a_view.shape, half_type),
            pltpu.VMEM((nx, ny, 4, blk, LANES), half_type),
            pltpu.VMEM((10 * rows, LANES), f32),
            pltpu.VMEM((4 * SUB, LANES), f32),
            pltpu.SMEM((4, aggregates), jnp.int32),
            pltpu.SMEM((4, capacity), jnp.int32),
            pltpu.SemaphoreType.DMA((1,)),
        ],
        compiler_params=room,
        cost_estimate=cost,
        name="inner_blocks",
    )(route_row, pairing, p_view, a_view)

    def chain(axis):
        n = lax.axis_size(axis)
        up = [(i, i + 1) for i in range(n - 1)]
        return up, [(j, i) for i, j in up]

    swap = [(0, 1), (1, 0)]
    xface = lax.ppermute(xface, "gx", swap)
    got_0 = lax.ppermute(send_0, "gx", swap)
    up, down = chain("gy")
    ylow = lax.ppermute(yup, "gy", up)
    yhigh = lax.ppermute(ydn, "gy", down)
    up, down = chain("gz")
    zlow = lax.ppermute(zup, "gz", up)
    zhigh = lax.ppermute(zdn, "gz", down)

    part = pl.pallas_call(
        functools.partial(outer_left_kernel, grid),
        out_shape=bf16(*parts),
        in_specs=[VMEM, ANY],
        out_specs=VMEM,
        scratch_shapes=[pltpu.VMEM(a_view.shape, half_type), pltpu.SemaphoreType.DMA((1,))],
        compiler_params=room,
        cost_estimate=cost,
        name="outer_left",
    )(left, a_view)
    send_xy, send_z, keep_xy, keep_z = pl.pallas_call(
        functools.partial(outer_kernel, dims, grid),
        out_shape=(bf16(4 * rows, LANES), bf16(2 * rows, LANES)) * 2,
        in_specs=[SMEM, SMEM, VMEM, VMEM, VMEM] + [ANY] * 5,
        out_specs=[VMEM] * 4,
        scratch_shapes=[
            pltpu.VMEM(face_x, half_type),
            pltpu.VMEM(face_y, half_type),
            pltpu.VMEM(face_y, half_type),
            pltpu.VMEM(face_z, half_type),
            pltpu.VMEM(face_z, half_type),
            pltpu.VMEM((12 * rows, LANES), f32),
            pltpu.SMEM((4, aggregates), jnp.int32),
            pltpu.SMEM((4, capacity), jnp.int32),
            pltpu.SemaphoreType.DMA((5,)),
        ],
        compiler_params=pltpu.CompilerParams(vmem_limit_bytes=67_043_328 - 1400 * 1024),
        cost_estimate=cost,
        name="outer_blocks",
    )(route_row, pairing, part, zup, zdn, xface, ylow, yhigh, zlow, zhigh)
    got_xy = lax.ppermute(send_xy, "gx", swap)
    got_z = lax.ppermute(send_z, "gx", swap)

    full = (capacity // SUB) * SUB * lines
    whole = 2 * rows
    half, out = pl.pallas_call(
        functools.partial(keep_kernel, (capacity, rows)),
        out_shape=(bf16(11, rows - full, LANES), bf16(11, whole, LANES)),
        in_specs=[VMEM] * 3,
        out_specs=[VMEM, ANY],
        scratch_shapes=[pltpu.VMEM((11, full, LANES), half_type), pltpu.SemaphoreType.DMA((11,))],
        compiler_params=room,
        cost_estimate=cost,
        name="place_kept",
    )(keep_0, keep_xy, keep_z)
    for with_xy, late in ((True, got_xy), (False, got_z)):
        out = pl.pallas_call(
            functools.partial(take_kernel, (capacity, rows), with_xy),
            out_shape=bf16(11, whole, LANES),
            in_specs=[VMEM] * 3 + [ANY],
            out_specs=ANY,
            input_output_aliases={3: 0},
            scratch_shapes=[
                pltpu.VMEM((11, full, LANES), half_type),
                pltpu.VMEM((11, full, LANES), half_type),
                pltpu.SemaphoreType.DMA((2, 11)),
            ],
            compiler_params=room,
            cost_estimate=cost,
            name="place_xy" if with_xy else "place_z",
        )(got_0, late, half, out)
    out = out.reshape(11, whole // (SUB * lines), lines, SUB, LANES).transpose(1, 3, 0, 2, 4)
    return out.reshape(2 * capacity, 11, entries)


def solution(mesh):
    placed = (
        P("gx", "gy", "gz", None, None),
        P("gx", "gy", "gz", None),
        P("gx", "gy", "gz"),
        P(("gx", "gy", "gz"), None),
    )
    return jax.shard_map(
        local,
        mesh=mesh,
        in_specs=placed,
        out_specs=P(("gx", "gy", "gz"), None, None),
        check_vma=False,
    )
```

```python
import functools
import math

import jax
import jax.numpy as jnp
from jax import lax
from jax.experimental import pallas as pl
from jax.experimental.pallas import tpu as pltpu
from jax.sharding import PartitionSpec as P


x_first_order = [0, 2, 1, 3, 4, 5, 6]
x_second_order = [0, 1, 2, 3, 4, 5, 6]
y_first_order = [0, 4, 1, 2, 3, 5, 6]
y_second_order = [0, 3, 1, 2, 4, 5, 6]

LANES = 128
SUB = 8


def padded_2(array, sides, width):
    for axis, dim in sides:
        devices, length = (lax.axis_size(axis), array.shape[dim])
        up = [(i, (i + 1) % devices) for i in range(devices - 1)]
        down = [(j, i) for i, j in up]
        last = lax.slice_in_dim(array, length - width, length, axis=dim)
        initial = lax.slice_in_dim(array, 0, width, axis=dim)
        before = lax.ppermute(last, axis, up)
        after = lax.ppermute(initial, axis, down)
        array = jnp.concatenate([before, array, after], axis=dim)
    return array


def neighbours(padded):
    shifted = [
        padded[1:-1, 1:-1, 1:-1],
        padded[:-2, 1:-1, 1:-1],
        padded[2:, 1:-1, 1:-1],
        padded[1:-1, :-2, 1:-1],
        padded[1:-1, 2:, 1:-1],
        padded[1:-1, 1:-1, :-2],
        padded[1:-1, 1:-1, 2:],
    ]
    return jnp.stack(shifted, axis=3)


def triple(blocks, nearby):
    block_side = math.isqrt(blocks.shape[-1])
    leading = blocks.shape[:-1]
    left_mat = blocks.reshape(leading + (block_side, block_side))
    right_mat = nearby.reshape(leading + (block_side, block_side))
    own_block = jnp.swapaxes(right_mat[..., :1, :, :], -1, -2)
    product = jnp.matmul(left_mat, right_mat, preferred_element_type=jnp.float32).astype(
        jnp.bfloat16
    )
    result = jnp.matmul(own_block, product, preferred_element_type=jnp.float32)
    return result.reshape(leading + (block_side * block_side,))


def members(element_grid, pairs):
    size_x, size_y, size_z = element_grid.shape[:3]
    trailing = element_grid.shape[3:]
    patches = element_grid.reshape((size_x // 2, 2, size_y // 2, 2, size_z) + trailing)

    def pick(upper, lower, slot_order):
        return jnp.take(patches[:, upper, :, lower], jnp.array(slot_order, dtype=jnp.int32), axis=3)

    x_one = jnp.stack([pick(0, 0, x_first_order), pick(0, 1, x_first_order)], axis=3)
    x_two = jnp.stack([pick(1, 0, x_second_order), pick(1, 1, x_second_order)], axis=3)
    y_one = jnp.stack([pick(0, 0, y_first_order), pick(1, 0, y_first_order)], axis=3)
    y_two = jnp.stack([pick(0, 1, y_second_order), pick(1, 1, y_second_order)], axis=3)
    along_x = (pairs == 0).reshape(pairs.shape + (1,) * (x_one.ndim - 3))
    member_one = jnp.where(along_x, x_one, y_one)
    member_two = jnp.where(along_x, x_two, y_two)
    return (
        member_one.reshape((-1,) + member_one.shape[4:]),
        member_two.reshape((-1,) + member_two.shape[4:]),
    )


def arrange(member_one, member_two):
    diagonal = (
        member_one[..., 0, :]
        + member_two[..., 0, :]
        + member_one[..., 1, :]
        + member_two[..., 1, :]
    )
    return jnp.concatenate(
        [diagonal[..., None, :], member_one[..., 2:, :], member_two[..., 2:, :]], axis=-2
    )


def slot_sources(routes, n_dest, capacity):
    total = routes.shape[0]
    chosen = (routes[:, None] == jnp.arange(n_dest, dtype=jnp.int32)[None, :]).astype(jnp.int32)
    before = jnp.cumsum(chosen, axis=0) - chosen
    ranking = jnp.sum(before * chosen, axis=1)
    position = routes * capacity + ranking
    targets = jnp.arange(n_dest * capacity, dtype=jnp.int32)
    matches = position[None, :] == targets[:, None]
    anchor = jnp.sum(jnp.where(matches, jnp.arange(total, dtype=jnp.int32)[None, :], 0), axis=1)
    filled = jnp.any(matches, axis=1)
    return (anchor, filled)


def pack_slots(payload, anchor, filled):
    taken = jnp.take(payload, anchor, axis=0)
    keep_row = filled.reshape(filled.shape + (1,) * (payload.ndim - 1))
    return jnp.where(keep_row, taken, jnp.zeros_like(taken))


def general(a_blocks, prolong, pairing, route, capacity):
    padded = padded_2(prolong, (("gx", 0), ("gy", 1), ("gz", 2)), 1)
    nearby = neighbours(padded)
    anchor, filled = slot_sources(route[:, 0], lax.axis_size("gx"), capacity)
    galerkin = triple(a_blocks, nearby)
    member_one, member_two = members(galerkin, pairing)
    coarse = arrange(member_one, member_two).astype(jnp.bfloat16)
    return lax.all_to_all(
        pack_slots(coarse, anchor, filled), "gx", split_axis=0, concat_axis=0, tiled=True
    )


def dot(left, right):
    return jnp.dot(left, right, preferred_element_type=jnp.float32)


def iota(shape, axis):
    return lax.broadcasted_iota(jnp.int32, shape, axis)


def as_bf16(mask):
    return mask.astype(jnp.float32).astype(jnp.bfloat16)


def pair(one, two):
    h = one.shape[1] // 2
    low = jnp.concatenate([one[:, :h], two[:, :h]], axis=1)
    high = jnp.concatenate([one[:, h:], two[:, h:]], axis=1)
    return jnp.concatenate([low, high], axis=0)


def unpair(both):
    rows, h = both.shape[0] // 2, both.shape[1] // 2
    even, odd = both[:rows], both[rows:]
    return (
        jnp.concatenate([even[:, :h], odd[:, :h]], axis=1),
        jnp.concatenate([even[:, h:], odd[:, h:]], axis=1),
    )


def constants(blk):
    n = 2 * blk
    row, col = iota((n, n), 0), iota((n, n), 1)
    c, z = row % blk, row // blk
    clean = as_bf16(col == (c % 2) * blk + (c // 2) * 2 + z)
    q = blk // 2
    k, p = row // blk, (row // q) % 2
    spread = as_bf16(col == k * blk + 2 * (row % q) + p)
    return clean, spread


def even_lanes(rows):
    return as_bf16(iota((rows, LANES), 1) % 2 == 0), as_bf16(iota((rows, LANES), 1) % 2 == 1)


def even_rows(rows):
    return as_bf16(iota((rows, LANES), 0) % 2 == 0), as_bf16(iota((rows, LANES), 0) % 2 == 1)


def transposed_dot(left, right):
    return lax.dot_general(
        left, right, (((1,), (1,)), ((), ())), preferred_element_type=jnp.float32
    )


def left_factors(both_t, k, masks):
    q = masks[0].shape[0]
    parts = [both_t[(2 * k + p) * q : (2 * k + p + 1) * q] for p in range(2)]
    return jnp.concatenate([part * mask for part in parts for mask in masks], axis=0)


def weights_of(part):
    h = part.shape[1] // 2
    none = jnp.zeros((part.shape[0], h), part.dtype)
    made = []
    for k in range(2):
        one = part[:, k * h : (k + 1) * h]
        made.append(
            jnp.concatenate(
                [jnp.concatenate([one, none], axis=1), jnp.concatenate([none, one], axis=1)], axis=0
            )
        )
    return made


def halves(part):
    h = part.shape[1] // 2
    return part[:, :h], part[:, h:]


def places(route_ref, where_ref, table_ref, dims, blocks):
    aggregates, cap, rows = dims
    me = lax.axis_index("gx")
    lines = rows // cap
    rest = cap % SUB
    half = (cap - rest) * lines
    at_zero = me == 0
    for c in range(cap):
        if c < cap - rest:
            zero = (c, c + half // 2, c, c)
        else:
            h = c - (cap - rest)
            zero = (half + h, half + h + rest, SUB + h, SUB + h + rest)
        if c < rest:
            one = (half + c + rest, half + c, SUB + c, SUB + c + rest)
        else:
            h = c - rest
            one = (h, h + half // 2, h, h)
        for k in range(4):
            table_ref[k, c] = jnp.where(at_zero, zero[k], one[k])
    sent, kept = jnp.int32(0), jnp.int32(0)
    for i in range(aggregates):
        away = route_ref[0, i] != me
        one = away.astype(jnp.int32)
        c = jnp.where(away, sent, kept)
        sent = sent + one
        kept = kept + (1 - one)
        base = jnp.where(away, 0, blocks * rows)
        where_ref[0, i] = base + table_ref[0, c]
        where_ref[1, i] = base + table_ref[1, c]
        where_ref[2, i] = jnp.where(away, 0, 2 * SUB) + table_ref[2, c]
        where_ref[3, i] = jnp.where(away, 0, 2 * SUB) + table_ref[3, c]
    return sent, kept


def put(total_ref, where_ref, i, block, rows, value):
    n = value.shape[0] // 2
    one = where_ref[0, i] + block * rows
    two = where_ref[1, i] + block * rows
    total_ref[pl.ds(one, n, stride=SUB), :] = value[:n]
    total_ref[pl.ds(two, n, stride=SUB), :] = value[n:]


def finish(outs, total_ref, kind, dims, count):
    _, cap, rows = dims
    rest = cap % SUB
    full = (cap - rest) * (rows // cap)
    me = lax.axis_index("gx")
    line = iota((2 * SUB, LANES), 0)
    in_full = as_bf16(line % SUB + jnp.where(me == 0, 0, rest) < count) > 0.5
    in_half = as_bf16(line % rest + jnp.where(me == 0, cap - rest, 0) < count) > 0.5
    blocks = sum(n for _, n in outs)
    done = 0
    for out, n in outs:
        for k in range(n):
            for at, size, filled in ((0, full, in_full), (full, rows - full, in_half)):
                value = total_ref[pl.ds((kind * blocks + done + k) * rows + at, size), :]
                value = value.astype(jnp.bfloat16).reshape(-1, 2 * SUB, LANES)
                value = jnp.where(filled[None], value, jnp.zeros_like(value))
                out[k * rows + at : k * rows + at + size] = value.reshape(size, LANES)
        done += n


def inner_kernel(
    dims, grid, route_hbm, pair_hbm, p_hbm, a_hbm,
    send_ref, keep_ref, xface_ref, yup_ref, ydn_ref, zup_ref, zdn_ref, left_ref, a_ref,
    p_ref, route_ref, pair_ref, part_ref, total_ref, codes_ref, where_ref, table_ref, sems,
):
    px, py, nz = grid
    aggregates, _, rows = dims
    nx, ny = 2 * px, 2 * py
    blk = p_ref.shape[2]
    q = blk // 2
    nb = 5
    copies = [
        pltpu.make_async_copy(one, two, sems.at[k])
        for k, (one, two) in enumerate((
            (p_hbm, p_ref), (route_hbm, route_ref), (pair_hbm, pair_ref), (a_hbm, a_ref),
        ))
    ]
    for copy in copies:
        copy.start()
    clean, spread = constants(blk)
    masks = even_lanes(q)
    first, second = even_rows(blk)
    me = lax.axis_index("gx")
    for copy in copies[:3]:
        copy.wait()

    pairs = [(x, b) for x in range(nx) for b in range(py)]
    both = {e: pair(p_ref[e[0], 2 * e[1]], p_ref[e[0], 2 * e[1] + 1]) for e in pairs}
    tidy = {e: dot(clean, both[e]).astype(jnp.bfloat16) for e in pairs}
    for x, b in pairs:
        left_ref[x * py + b] = transposed_dot(spread, both[x, b]).astype(jnp.bfloat16)
        zdn_ref[x * py + b] = tidy[x, b][:blk]
        zup_ref[x * py + b] = tidy[x, b][blk:]
    for a in range(px):
        one, two = tidy[2 * a, 0], tidy[2 * a + 1, 0]
        ydn_ref[a] = jnp.concatenate([one[:, :blk], two[:, :blk]], axis=1)
        one, two = tidy[2 * a, py - 1], tidy[2 * a + 1, py - 1]
        yup_ref[a] = jnp.concatenate([one[:, blk:], two[:, blk:]], axis=1)
    for b in range(py):
        for z, ref in enumerate((zdn_ref, zup_ref)):
            xface_ref[b, z * blk : (z + 1) * blk] = ref[jnp.where(me == 0, nx - 1, 0) * py + b]
    copies[3].wait()

    for x, y in [(x, y) for x in range(nx) for y in range(ny)]:
        here = a_ref.at[x, y]
        along_z = here[6] * first + here[5] * second
        right = jnp.concatenate(
            [pair(here[0], here[2 - x % 2]), pair(here[4 - y % 2], along_z)], axis=1
        )
        left = left_factors(left_ref[x * py + y // 2], y % 2, masks)
        got = dot(left, right).astype(jnp.bfloat16)
        parts = unpair(got[:, : 2 * blk]) + unpair(got[:, 2 * blk :])
        for k in range(4):
            part_ref[x, y, k] = parts[k]

    sent, kept = places(route_ref, where_ref, table_ref, dims, nb)
    codes_ref[...] = jnp.zeros_like(codes_ref)
    for i in range(aggregates):
        a, b, z, t = i // (py * nz * 2), (i // (nz * 2)) % py, (i // 2) % nz, i % 2
        code = (2 * (jnp.where(pair_ref[a, b, z] == 0, 2, 1) - t) + z).astype(jnp.float32)
        line = jnp.full((1, LANES), code, jnp.float32)
        codes_ref[pl.ds(where_ref[2, i], 1), :] = line
        codes_ref[pl.ds(where_ref[3, i], 1), :] = line

    for a, b in [(a, b) for a in range(px) for b in range(py)]:
        own, with_x, with_y, with_z = {}, {}, {}, {}
        for z, ref in enumerate((zdn_ref, zup_ref)):
            zs, zo = pl.ds(z * q, q), pl.ds((1 - z) * q, q)
            for u in range(2):
                x = 2 * a + u
                weight = weights_of(ref[x * py + b])
                for v in range(2):
                    y = 2 * b + v
                    stack = jnp.concatenate(
                        [
                            part_ref[x, y, 0, zs],
                            part_ref[2 * a + 1 - u, y, 1, zs],
                            part_ref[x, 2 * b + 1 - v, 2, zs],
                            part_ref[x, y, 3, zo],
                        ],
                        axis=0,
                    )
                    got = dot(stack, weight[v])
                    own[u, v, z] = got[:q]
                    with_x[1 - u, v, z] = got[q : 2 * q]
                    with_y[u, 1 - v, z] = got[2 * q : 3 * q]
                    with_z[u, v, 1 - z] = got[3 * q :]
        for z in range(nz):
            flat = pair_ref[a, b, z] == 0
            i = ((a * py + b) * nz + z) * 2
            sums = {}
            for u in range(2):
                for v in range(2):
                    t = u if u == v else jnp.where(flat, v, u)
                    m = u if u == v else jnp.where(flat, u, v)
                    e = (u, v, z)
                    sums[u, v] = own[e] + jnp.where(flat, with_x[e], with_y[e])
                    cross = jnp.where(flat, with_y[e], with_x[e])
                    put(total_ref, where_ref, i + t, 1 + m, rows, cross)
                    put(total_ref, where_ref, i + t, 3 + m, rows, with_z[e])
            put(total_ref, where_ref, i, 0, rows, sums[0, 0] + jnp.where(flat, sums[1, 0], sums[0, 1]))
            put(total_ref, where_ref, i + 1, 0, rows, sums[1, 1] + jnp.where(flat, sums[0, 1], sums[1, 0]))

    for kind, (out, count) in enumerate(((send_ref, sent), (keep_ref, kept))):
        finish(((out, nb),), total_ref, kind, dims, count)
        out[nb * rows :] = codes_ref[kind * 2 * SUB : (kind + 1) * 2 * SUB].astype(jnp.bfloat16)


def outer_left_kernel(grid, left_ref, a_ref, part_ref):
    px, py, _ = grid
    nx, ny = 2 * px, 2 * py
    blk = a_ref.shape[3]
    masks = even_lanes(blk // 2)
    first, second = even_rows(blk)
    for x, y in [(x, y) for x in range(nx) for y in range(ny)]:
        here = a_ref.at[x, y]
        along_z = here[5] * first + here[6] * second
        low, high = halves(along_z)
        right = jnp.concatenate(
            [pair(here[1 + x % 2], here[3 + y % 2]), jnp.concatenate([low, high], axis=0)], axis=1
        )
        left = left_factors(left_ref[x * py + y // 2], y % 2, masks)
        got = dot(left, right).astype(jnp.bfloat16)
        part_ref[x, y, 0], part_ref[x, y, 1] = unpair(got[:, : 2 * blk])
        along = got[:, 2 * blk :]
        part_ref[x, y, 2] = jnp.concatenate([along[:blk], along[blk:]], axis=1)


def outer_kernel(
    dims, grid, route_ref, pair_ref, part_ref, zup_ref, zdn_ref,
    xface_ref, ylow_ref, yhigh_ref, zlow_ref, zhigh_ref,
    send_xy_ref, send_z_ref, keep_xy_ref, keep_z_ref,
    total_ref, where_ref, table_ref,
):
    px, py, nz = grid
    _, _, rows = dims
    nx, ny = 2 * px, 2 * py
    blk = part_ref.shape[3]
    q = blk // 2
    nb = 6
    sent, kept = places(route_ref, where_ref, table_ref, dims, nb)
    me = lax.axis_index("gx")
    above = (iota((blk, LANES), 0) * 0 + me) > 0

    def beside_x(x, b, z, u):
        to = x - 1 if u == 0 else x + 1
        if 0 <= to < nx:
            return (zdn_ref, zup_ref)[z][to * py + b]
        part = xface_ref[b, z * blk : (z + 1) * blk].astype(jnp.float32)
        part = jnp.where(above, part, 0.0) if u == 0 else jnp.where(above, 0.0, part)
        return part.astype(jnp.bfloat16)

    def beside_y(x, y, z, v):
        to = y - 1 if v == 0 else y + 1
        if 0 <= to < ny:
            return (zdn_ref, zup_ref)[z][x * py + to // 2], to % 2
        ref = ylow_ref if v == 0 else yhigh_ref
        return ref[x // 2, z * blk : (z + 1) * blk], x % 2

    for x in range(nx):
        made = []
        for b, z in [(b, z) for b in range(py) for z in range(nz)]:
            zs = pl.ds(z * q, q)
            u, a = x % 2, x // 2
            along_x = weights_of(beside_x(x, b, z, u))
            along_z = weights_of((zlow_ref, zhigh_ref)[z][x * py + b])
            flat = pair_ref[a, b, z] == 0
            for v in range(2):
                y = 2 * b + v
                t = u if u == v else jnp.where(flat, v, u)
                m = u if u == v else jnp.where(flat, u, v)
                i = ((a * py + b) * nz + z) * 2 + t
                other, k = beside_y(x, y, z, v)
                along_y = weights_of(other)[k]
                made.append((i, 2 * m, dot(part_ref[x, y, 0, zs], along_x[v])))
                made.append((i, 2 * m + 1, dot(part_ref[x, y, 1, zs], along_y)))
                made.append((i, 4 + m, dot(part_ref[x, y, 2, zs], along_z[v])))
        for i, block, got in made:
            put(total_ref, where_ref, i, block, rows, got)

    for kind, (xy, along, count) in enumerate((
        (send_xy_ref, send_z_ref, sent), (keep_xy_ref, keep_z_ref, kept),
    )):
        finish(((xy, 4), (along, 2)), total_ref, kind, dims, count)


def placed_blocks(early_ref, xy_ref, z_ref, codes, rows, at, size):
    code = jnp.concatenate([codes, codes], axis=0)
    near_low, near_high = (code < 1.5)[None], (code > 3.5)[None]
    upper = ((code == 1.0) | (code == 3.0) | (code == 5.0))[None]

    def tiles(ref, k):
        return ref[k * rows + at : k * rows + at + size].reshape(-1, 2 * SUB, LANES)

    if xy_ref is not None:
        yield 0, tiles(early_ref, 0)
        for m in range(2):
            cross, x_out, y_out = tiles(early_ref, 1 + m), tiles(xy_ref, 2 * m), tiles(xy_ref, 2 * m + 1)
            yield 1 + 5 * m, jnp.where(near_low, cross, x_out)
            yield 2 + 5 * m, jnp.where(near_low, x_out, jnp.where(near_high, y_out, cross))
            yield 3 + 5 * m, jnp.where(near_high, cross, y_out)
    if z_ref is not None:
        for m in range(2):
            z_in, z_out = tiles(early_ref, 3 + m), tiles(z_ref, m)
            yield 4 + 5 * m, jnp.where(upper, z_in, z_out)
            yield 5 + 5 * m, jnp.where(upper, z_out, z_in)


def keep_kernel(dims, early_ref, xy_ref, z_ref, half_ref, out_hbm, full_ref, sem):
    cap, rows = dims
    full = (cap - cap % SUB) * (rows // cap)
    me = lax.axis_index("gx")
    codes = early_ref[5 * rows :]
    copies = []
    for k, value in placed_blocks(early_ref, xy_ref, z_ref, codes[:SUB], rows, 0, full):
        full_ref[k] = value.reshape(full, LANES)
        to = out_hbm.at[k, pl.ds(me * (2 * full), full), :]
        copies.append(pltpu.make_async_copy(full_ref.at[k], to, sem.at[k]))
        copies[-1].start()
    for k, value in placed_blocks(early_ref, xy_ref, z_ref, codes[SUB:], rows, full, rows - full):
        half_ref[k] = value.reshape(rows - full, LANES)
    for copy in copies:
        copy.wait()


def take_kernel(dims, with_xy, early_ref, late_ref, half_ref, _, out_hbm, full_ref, mixed_ref, sem):
    cap, rows = dims
    full = (cap - cap % SUB) * (rows // cap)
    me = lax.axis_index("gx")
    codes = early_ref[5 * rows :]
    xy_ref, z_ref = (late_ref, None) if with_xy else (None, late_ref)
    copies = []
    for k, value in placed_blocks(early_ref, xy_ref, z_ref, codes[:SUB], rows, 0, full):
        full_ref[k] = value.reshape(full, LANES)
        to = out_hbm.at[k, pl.ds((1 - me) * (2 * full), full), :]
        copies.append(pltpu.make_async_copy(full_ref.at[k], to, sem.at[0, k]))
        copies[-1].start()
    first_half = (iota((SUB, LANES), 0) < SUB // 2)[None]
    pick = first_half == (me == 0)
    for k, value in placed_blocks(early_ref, xy_ref, z_ref, codes[SUB:], rows, full, rows - full):
        theirs = value.reshape(rows - full, LANES).astype(jnp.float32).reshape(-1, SUB, LANES)
        mine = half_ref[k].astype(jnp.float32).reshape(-1, SUB, LANES)
        low = jnp.where(pick, mine, theirs)
        high = pltpu.roll(jnp.where(pick, theirs, mine), SUB // 2, 1)
        mixed_ref[k, : rows - full] = low.reshape(rows - full, LANES).astype(jnp.bfloat16)
        mixed_ref[k, rows - full :] = high.reshape(rows - full, LANES).astype(jnp.bfloat16)
        to = out_hbm.at[k, full : 2 * full, :]
        copies.append(pltpu.make_async_copy(mixed_ref.at[k], to, sem.at[1, k]))
        copies[-1].start()
    for copy in copies:
        copy.wait()


SMEM = pl.BlockSpec(memory_space=pltpu.SMEM)
VMEM = pl.BlockSpec(memory_space=pltpu.VMEM)
ANY = pl.BlockSpec(memory_space=pl.ANY)


def bf16(*shape):
    return jax.ShapeDtypeStruct(shape, jnp.bfloat16)


def near(*shape):
    return pltpu.VMEM(shape, jnp.bfloat16)


def held(*arrays):
    return [pltpu.with_memory_space_constraint(one, pltpu.VMEM) for one in arrays]


def local(a_blocks, prolong, pairing, route):
    devices_gx = lax.axis_size("gx")
    aggregates = route.shape[0]
    capacity = max(2, 3 * aggregates // (2 * devices_gx))
    nx, ny, nz, faces, entries = a_blocks.shape
    fits = (
        devices_gx == 2
        and nz == 2
        and nx % 2 == 0
        and ny % 2 == 0
        and faces == 7
        and entries == (LANES // 2) ** 2
        and capacity // SUB == 1
        and capacity % SUB == SUB // 2
    )
    if not fits:
        return general(a_blocks, prolong, pairing, route, capacity)
    px, py = nx // 2, ny // 2
    blk = math.isqrt(entries)
    lines = entries // LANES
    a_view = a_blocks.transpose(0, 1, 3, 2, 4).reshape(nx, ny, faces, nz, lines, LANES)
    a_view = a_view.transpose(0, 1, 2, 4, 3, 5).reshape(nx, ny, faces, nz * lines, LANES)
    p_view = prolong.reshape(nx, ny, nz, lines, LANES).transpose(0, 1, 3, 2, 4)
    p_view = p_view.reshape(nx, ny, nz * lines, LANES)
    route_row = route.reshape(1, aggregates)
    rows = capacity * lines
    dims, grid = (aggregates, capacity, rows), (px, py, nz)
    f32 = jnp.float32
    half_type = jnp.bfloat16
    face_x, face_y, face_z = (py, 2 * blk, LANES), (px, 2 * blk, LANES), (nx * py, blk, LANES)
    parts = (nx, ny, 3, blk, LANES)
    room = pltpu.CompilerParams(vmem_limit_bytes=24 * 2**20)
    cost = pl.CostEstimate(flops=10**9, bytes_accessed=4 * 10**6, transcendentals=0)

    send_0, keep_0, xface, yup, ydn, zup, zdn, left, a_near = pl.pallas_call(
        functools.partial(inner_kernel, dims, grid),
        out_shape=(
            near(5 * rows + 2 * SUB, LANES),
            near(5 * rows + 2 * SUB, LANES),
            near(*face_x),
            near(*face_y),
            near(*face_y),
            near(*face_z),
            near(*face_z),
            near(nx * py, 2 * blk, LANES),
            near(*a_view.shape),
        ),
        in_specs=[ANY] * 4,
        out_specs=[VMEM] * 9,
        scratch_shapes=[
            pltpu.VMEM(p_view.shape, half_type),
            pltpu.SMEM(route_row.shape, jnp.int32),
            pltpu.SMEM(pairing.shape, jnp.int32),
            pltpu.VMEM((nx, ny, 4, blk, LANES), half_type),
            pltpu.VMEM((10 * rows, LANES), f32),
            pltpu.VMEM((4 * SUB, LANES), f32),
            pltpu.SMEM((4, aggregates), jnp.int32),
            pltpu.SMEM((4, capacity), jnp.int32),
            pltpu.SemaphoreType.DMA((4,)),
        ],
        compiler_params=room,
        cost_estimate=cost,
        name="inner_blocks",
    )(*[pltpu.with_memory_space_constraint(one, pltpu.HBM) for one in (route_row, pairing, p_view, a_view)])

    def chain(axis):
        n = lax.axis_size(axis)
        up = [(i, i + 1) for i in range(n - 1)]
        return up, [(j, i) for i, j in up]

    swap = [(0, 1), (1, 0)]
    xface = lax.ppermute(xface, "gx", swap)
    got_0 = lax.ppermute(send_0, "gx", swap)
    up, down = chain("gy")
    ylow = lax.ppermute(yup, "gy", up)
    yhigh = lax.ppermute(ydn, "gy", down)
    up, down = chain("gz")
    zlow = lax.ppermute(zup, "gz", up)
    zhigh = lax.ppermute(zdn, "gz", down)

    part = pl.pallas_call(
        functools.partial(outer_left_kernel, grid),
        out_shape=near(*parts),
        in_specs=[VMEM] * 2,
        out_specs=VMEM,
        compiler_params=room,
        cost_estimate=cost,
        name="outer_left",
    )(*held(left, a_near))
    send_xy, send_z, keep_xy, keep_z = pl.pallas_call(
        functools.partial(outer_kernel, dims, grid),
        out_shape=(near(4 * rows, LANES), near(2 * rows, LANES)) * 2,
        in_specs=[SMEM, SMEM] + [VMEM] * 8,
        out_specs=[VMEM] * 4,
        scratch_shapes=[
            pltpu.VMEM((12 * rows, LANES), f32),
            pltpu.SMEM((4, aggregates), jnp.int32),
            pltpu.SMEM((4, capacity), jnp.int32),
        ],
        compiler_params=room,
        cost_estimate=cost,
        name="outer_blocks",
    )(route_row, pairing, *held(part, zup, zdn, xface, ylow, yhigh, zlow, zhigh))
    got_xy = lax.ppermute(send_xy, "gx", swap)
    got_z = lax.ppermute(send_z, "gx", swap)

    full = (capacity // SUB) * SUB * lines
    whole = 2 * rows
    half, out = pl.pallas_call(
        functools.partial(keep_kernel, (capacity, rows)),
        out_shape=(near(11, rows - full, LANES), bf16(11, whole, LANES)),
        in_specs=[VMEM] * 3,
        out_specs=[VMEM, ANY],
        scratch_shapes=[pltpu.VMEM((11, full, LANES), half_type), pltpu.SemaphoreType.DMA((11,))],
        compiler_params=room,
        cost_estimate=cost,
        name="place_kept",
    )(*held(keep_0, keep_xy, keep_z))
    for with_xy, late in ((True, got_xy), (False, got_z)):
        out = pl.pallas_call(
            functools.partial(take_kernel, (capacity, rows), with_xy),
            out_shape=bf16(11, whole, LANES),
            in_specs=[VMEM] * 3 + [ANY],
            out_specs=ANY,
            input_output_aliases={3: 0},
            scratch_shapes=[
                pltpu.VMEM((11, full, LANES), half_type),
                pltpu.VMEM((11, full, LANES), half_type),
                pltpu.SemaphoreType.DMA((2, 11)),
            ],
            compiler_params=room,
            cost_estimate=cost,
            name="place_xy" if with_xy else "place_z",
        )(*held(got_0, late, half), out)
    out = out.reshape(11, whole // (SUB * lines), lines, SUB, LANES).transpose(1, 3, 0, 2, 4)
    return out.reshape(2 * capacity, 11, entries)


def solution(mesh):
    placed = (
        P("gx", "gy", "gz", None, None),
        P("gx", "gy", "gz", None),
        P("gx", "gy", "gz"),
        P(("gx", "gy", "gz"), None),
    )
    return jax.shard_map(
        local,
        mesh=mesh,
        in_specs=placed,
        out_specs=P(("gx", "gy", "gz"), None, None),
        check_vma=False,
    )
```

```python
import functools
import math

import jax
import jax.numpy as jnp
from jax import lax
from jax.experimental import pallas as pl
from jax.experimental.pallas import tpu as pltpu
from jax.sharding import PartitionSpec as P


x_first_order = [0, 2, 1, 3, 4, 5, 6]
x_second_order = [0, 1, 2, 3, 4, 5, 6]
y_first_order = [0, 4, 1, 2, 3, 5, 6]
y_second_order = [0, 3, 1, 2, 4, 5, 6]

LANES = 128
SUB = 8


def padded_2(array, sides, width):
    for axis, dim in sides:
        devices, length = (lax.axis_size(axis), array.shape[dim])
        up = [(i, (i + 1) % devices) for i in range(devices - 1)]
        down = [(j, i) for i, j in up]
        last = lax.slice_in_dim(array, length - width, length, axis=dim)
        initial = lax.slice_in_dim(array, 0, width, axis=dim)
        before = lax.ppermute(last, axis, up)
        after = lax.ppermute(initial, axis, down)
        array = jnp.concatenate([before, array, after], axis=dim)
    return array


def neighbours(padded):
    shifted = [
        padded[1:-1, 1:-1, 1:-1],
        padded[:-2, 1:-1, 1:-1],
        padded[2:, 1:-1, 1:-1],
        padded[1:-1, :-2, 1:-1],
        padded[1:-1, 2:, 1:-1],
        padded[1:-1, 1:-1, :-2],
        padded[1:-1, 1:-1, 2:],
    ]
    return jnp.stack(shifted, axis=3)


def triple(blocks, nearby):
    block_side = math.isqrt(blocks.shape[-1])
    leading = blocks.shape[:-1]
    left_mat = blocks.reshape(leading + (block_side, block_side))
    right_mat = nearby.reshape(leading + (block_side, block_side))
    own_block = jnp.swapaxes(right_mat[..., :1, :, :], -1, -2)
    product = jnp.matmul(left_mat, right_mat, preferred_element_type=jnp.float32).astype(
        jnp.bfloat16
    )
    result = jnp.matmul(own_block, product, preferred_element_type=jnp.float32)
    return result.reshape(leading + (block_side * block_side,))


def members(element_grid, pairs):
    size_x, size_y, size_z = element_grid.shape[:3]
    trailing = element_grid.shape[3:]
    patches = element_grid.reshape((size_x // 2, 2, size_y // 2, 2, size_z) + trailing)

    def pick(upper, lower, slot_order):
        return jnp.take(patches[:, upper, :, lower], jnp.array(slot_order, dtype=jnp.int32), axis=3)

    x_one = jnp.stack([pick(0, 0, x_first_order), pick(0, 1, x_first_order)], axis=3)
    x_two = jnp.stack([pick(1, 0, x_second_order), pick(1, 1, x_second_order)], axis=3)
    y_one = jnp.stack([pick(0, 0, y_first_order), pick(1, 0, y_first_order)], axis=3)
    y_two = jnp.stack([pick(0, 1, y_second_order), pick(1, 1, y_second_order)], axis=3)
    along_x = (pairs == 0).reshape(pairs.shape + (1,) * (x_one.ndim - 3))
    member_one = jnp.where(along_x, x_one, y_one)
    member_two = jnp.where(along_x, x_two, y_two)
    return (
        member_one.reshape((-1,) + member_one.shape[4:]),
        member_two.reshape((-1,) + member_two.shape[4:]),
    )


def arrange(member_one, member_two):
    diagonal = (
        member_one[..., 0, :]
        + member_two[..., 0, :]
        + member_one[..., 1, :]
        + member_two[..., 1, :]
    )
    return jnp.concatenate(
        [diagonal[..., None, :], member_one[..., 2:, :], member_two[..., 2:, :]], axis=-2
    )


def slot_sources(routes, n_dest, capacity):
    total = routes.shape[0]
    chosen = (routes[:, None] == jnp.arange(n_dest, dtype=jnp.int32)[None, :]).astype(jnp.int32)
    before = jnp.cumsum(chosen, axis=0) - chosen
    ranking = jnp.sum(before * chosen, axis=1)
    position = routes * capacity + ranking
    targets = jnp.arange(n_dest * capacity, dtype=jnp.int32)
    matches = position[None, :] == targets[:, None]
    anchor = jnp.sum(jnp.where(matches, jnp.arange(total, dtype=jnp.int32)[None, :], 0), axis=1)
    filled = jnp.any(matches, axis=1)
    return (anchor, filled)


def pack_slots(payload, anchor, filled):
    taken = jnp.take(payload, anchor, axis=0)
    keep_row = filled.reshape(filled.shape + (1,) * (payload.ndim - 1))
    return jnp.where(keep_row, taken, jnp.zeros_like(taken))


def general(a_blocks, prolong, pairing, route, capacity):
    padded = padded_2(prolong, (("gx", 0), ("gy", 1), ("gz", 2)), 1)
    nearby = neighbours(padded)
    anchor, filled = slot_sources(route[:, 0], lax.axis_size("gx"), capacity)
    galerkin = triple(a_blocks, nearby)
    member_one, member_two = members(galerkin, pairing)
    coarse = arrange(member_one, member_two).astype(jnp.bfloat16)
    return lax.all_to_all(
        pack_slots(coarse, anchor, filled), "gx", split_axis=0, concat_axis=0, tiled=True
    )


def dot(left, right):
    return jnp.dot(left, right, preferred_element_type=jnp.float32)


def iota(shape, axis):
    return lax.broadcasted_iota(jnp.int32, shape, axis)


def as_bf16(mask):
    return mask.astype(jnp.float32).astype(jnp.bfloat16)


def pair(one, two):
    h = one.shape[1] // 2
    low = jnp.concatenate([one[:, :h], two[:, :h]], axis=1)
    high = jnp.concatenate([one[:, h:], two[:, h:]], axis=1)
    return jnp.concatenate([low, high], axis=0)


def unpair(both):
    rows, h = both.shape[0] // 2, both.shape[1] // 2
    even, odd = both[:rows], both[rows:]
    return (
        jnp.concatenate([even[:, :h], odd[:, :h]], axis=1),
        jnp.concatenate([even[:, h:], odd[:, h:]], axis=1),
    )


def constants(blk):
    n = 2 * blk
    row, col = iota((n, n), 0), iota((n, n), 1)
    c, z = row % blk, row // blk
    clean = as_bf16(col == (c % 2) * blk + (c // 2) * 2 + z)
    q = blk // 2
    k, p = row // blk, (row // q) % 2
    spread = as_bf16(col == k * blk + 2 * (row % q) + p)
    return clean, spread


def even_lanes(rows):
    return as_bf16(iota((rows, LANES), 1) % 2 == 0), as_bf16(iota((rows, LANES), 1) % 2 == 1)


def even_rows(rows):
    return as_bf16(iota((rows, LANES), 0) % 2 == 0), as_bf16(iota((rows, LANES), 0) % 2 == 1)


def transposed_dot(left, right):
    return lax.dot_general(
        left, right, (((1,), (1,)), ((), ())), preferred_element_type=jnp.float32
    )


def left_factors(both_t, k, masks):
    q = masks[0].shape[0]
    parts = [both_t[(2 * k + p) * q : (2 * k + p + 1) * q] for p in range(2)]
    return jnp.concatenate([part * mask for part in parts for mask in masks], axis=0)


def weights_of(part):
    h = part.shape[1] // 2
    none = jnp.zeros((part.shape[0], h), part.dtype)
    made = []
    for k in range(2):
        one = part[:, k * h : (k + 1) * h]
        made.append(
            jnp.concatenate(
                [jnp.concatenate([one, none], axis=1), jnp.concatenate([none, one], axis=1)], axis=0
            )
        )
    return made


def halves(part):
    h = part.shape[1] // 2
    return part[:, :h], part[:, h:]


def places(route_ref, where_ref, table_ref, dims, blocks):
    aggregates, cap, rows = dims
    me = lax.axis_index("gx")
    lines = rows // cap
    rest = cap % SUB
    half = (cap - rest) * lines
    at_zero = me == 0
    for c in range(cap):
        if c < cap - rest:
            zero = (c, c + half // 2, c, c)
        else:
            h = c - (cap - rest)
            zero = (half + h, half + h + rest, SUB + h, SUB + h + rest)
        if c < rest:
            one = (half + c + rest, half + c, SUB + c, SUB + c + rest)
        else:
            h = c - rest
            one = (h, h + half // 2, h, h)
        for k in range(4):
            table_ref[k, c] = jnp.where(at_zero, zero[k], one[k])
    sent, kept = jnp.int32(0), jnp.int32(0)
    for i in range(aggregates):
        away = route_ref[0, i] != me
        one = away.astype(jnp.int32)
        c = jnp.where(away, sent, kept)
        sent = sent + one
        kept = kept + (1 - one)
        base = jnp.where(away, 0, blocks * rows)
        where_ref[0, i] = base + table_ref[0, c]
        where_ref[1, i] = base + table_ref[1, c]
        where_ref[2, i] = jnp.where(away, 0, 2 * SUB) + table_ref[2, c]
        where_ref[3, i] = jnp.where(away, 0, 2 * SUB) + table_ref[3, c]
    return sent, kept


def put(total_ref, where_ref, i, block, rows, value):
    n = value.shape[0] // 2
    one = where_ref[0, i] + block * rows
    two = where_ref[1, i] + block * rows
    total_ref[pl.ds(one, n, stride=SUB), :] = value[:n]
    total_ref[pl.ds(two, n, stride=SUB), :] = value[n:]


def finish(outs, total_ref, kind, dims, count):
    _, cap, rows = dims
    rest = cap % SUB
    full = (cap - rest) * (rows // cap)
    me = lax.axis_index("gx")
    line = iota((2 * SUB, LANES), 0)
    in_full = as_bf16(line % SUB + jnp.where(me == 0, 0, rest) < count) > 0.5
    in_half = as_bf16(line % rest + jnp.where(me == 0, cap - rest, 0) < count) > 0.5
    blocks = sum(n for _, n in outs)
    done = 0
    for out, n in outs:
        for k in range(n):
            for at, size, filled in ((0, full, in_full), (full, rows - full, in_half)):
                value = total_ref[pl.ds((kind * blocks + done + k) * rows + at, size), :]
                value = value.astype(jnp.bfloat16).reshape(-1, 2 * SUB, LANES)
                value = jnp.where(filled[None], value, jnp.zeros_like(value))
                out[k * rows + at : k * rows + at + size] = value.reshape(size, LANES)
        done += n


def inner_kernel(
    dims, grid, route_hbm, pair_hbm, p_hbm, a_hbm,
    send_ref, keep_ref, xface_ref, ya_ref, yb_ref, za_ref, zb_ref, zup_ref, zdn_ref, left_ref, a_ref,
    p_ref, route_ref, pair_ref, part_ref, total_ref, codes_ref, where_ref, table_ref, sems,
):
    px, py, nz = grid
    aggregates, _, rows = dims
    nx, ny = 2 * px, 2 * py
    blk = p_ref.shape[2]
    q = blk // 2
    nb = 5
    copies = [
        pltpu.make_async_copy(one, two, sems.at[k])
        for k, (one, two) in enumerate((
            (p_hbm, p_ref), (route_hbm, route_ref), (pair_hbm, pair_ref), (a_hbm, a_ref),
        ))
    ]
    for copy in copies:
        copy.start()
    clean, spread = constants(blk)
    masks = even_lanes(q)
    first, second = even_rows(blk)
    me = lax.axis_index("gx")
    for copy in copies[:3]:
        copy.wait()

    pairs = [(x, b) for x in range(nx) for b in range(py)]
    both = {e: pair(p_ref[e[0], 2 * e[1]], p_ref[e[0], 2 * e[1] + 1]) for e in pairs}
    tidy = {e: dot(clean, both[e]).astype(jnp.bfloat16) for e in pairs}
    for x, b in pairs:
        left_ref[x * py + b] = transposed_dot(spread, both[x, b]).astype(jnp.bfloat16)
        zdn_ref[x * py + b] = tidy[x, b][:blk]
        zup_ref[x * py + b] = tidy[x, b][blk:]
    y_even, z_even = lax.axis_index("gy") % 2 == 0, lax.axis_index("gz") % 2 == 0
    for a in range(px):
        one, two = tidy[2 * a, 0], tidy[2 * a + 1, 0]
        down = jnp.concatenate([one[:, :blk], two[:, :blk]], axis=1)
        one, two = tidy[2 * a, py - 1], tidy[2 * a + 1, py - 1]
        up = jnp.concatenate([one[:, blk:], two[:, blk:]], axis=1)
        ya_ref[a], yb_ref[a] = jnp.where(y_even, up, down), jnp.where(y_even, down, up)
    for x, b in pairs:
        down, up = tidy[x, b][:blk], tidy[x, b][blk:]
        za_ref[x * py + b] = jnp.where(z_even, up, down)
        zb_ref[x * py + b] = jnp.where(z_even, down, up)
    for b in range(py):
        for z, ref in enumerate((zdn_ref, zup_ref)):
            xface_ref[b, z * blk : (z + 1) * blk] = ref[jnp.where(me == 0, nx - 1, 0) * py + b]
    copies[3].wait()

    for x, y in [(x, y) for x in range(nx) for y in range(ny)]:
        here = a_ref.at[x, y]
        along_z = here[6] * first + here[5] * second
        right = jnp.concatenate(
            [pair(here[0], here[2 - x % 2]), pair(here[4 - y % 2], along_z)], axis=1
        )
        left = left_factors(left_ref[x * py + y // 2], y % 2, masks)
        got = dot(left, right).astype(jnp.bfloat16)
        parts = unpair(got[:, : 2 * blk]) + unpair(got[:, 2 * blk :])
        for k in range(4):
            part_ref[x, y, k] = parts[k]

    sent, kept = places(route_ref, where_ref, table_ref, dims, nb)
    codes_ref[...] = jnp.zeros_like(codes_ref)
    for i in range(aggregates):
        a, b, z, t = i // (py * nz * 2), (i // (nz * 2)) % py, (i // 2) % nz, i % 2
        code = (2 * (jnp.where(pair_ref[a, b, z] == 0, 2, 1) - t) + z).astype(jnp.float32)
        line = jnp.full((1, LANES), code, jnp.float32)
        codes_ref[pl.ds(where_ref[2, i], 1), :] = line
        codes_ref[pl.ds(where_ref[3, i], 1), :] = line

    for a, b in [(a, b) for a in range(px) for b in range(py)]:
        own, with_x, with_y, with_z = {}, {}, {}, {}
        for z, ref in enumerate((zdn_ref, zup_ref)):
            zs, zo = pl.ds(z * q, q), pl.ds((1 - z) * q, q)
            for u in range(2):
                x = 2 * a + u
                weight = weights_of(ref[x * py + b])
                for v in range(2):
                    y = 2 * b + v
                    stack = jnp.concatenate(
                        [
                            part_ref[x, y, 0, zs],
                            part_ref[2 * a + 1 - u, y, 1, zs],
                            part_ref[x, 2 * b + 1 - v, 2, zs],
                            part_ref[x, y, 3, zo],
                        ],
                        axis=0,
                    )
                    got = dot(stack, weight[v])
                    own[u, v, z] = got[:q]
                    with_x[1 - u, v, z] = got[q : 2 * q]
                    with_y[u, 1 - v, z] = got[2 * q : 3 * q]
                    with_z[u, v, 1 - z] = got[3 * q :]
        for z in range(nz):
            flat = pair_ref[a, b, z] == 0
            i = ((a * py + b) * nz + z) * 2
            sums = {}
            for u in range(2):
                for v in range(2):
                    t = u if u == v else jnp.where(flat, v, u)
                    m = u if u == v else jnp.where(flat, u, v)
                    e = (u, v, z)
                    sums[u, v] = own[e] + jnp.where(flat, with_x[e], with_y[e])
                    cross = jnp.where(flat, with_y[e], with_x[e])
                    put(total_ref, where_ref, i + t, 1 + m, rows, cross)
                    put(total_ref, where_ref, i + t, 3 + m, rows, with_z[e])
            put(total_ref, where_ref, i, 0, rows, sums[0, 0] + jnp.where(flat, sums[1, 0], sums[0, 1]))
            put(total_ref, where_ref, i + 1, 0, rows, sums[1, 1] + jnp.where(flat, sums[0, 1], sums[1, 0]))

    for kind, (out, count) in enumerate(((send_ref, sent), (keep_ref, kept))):
        finish(((out, nb),), total_ref, kind, dims, count)
        out[nb * rows :] = codes_ref[kind * 2 * SUB : (kind + 1) * 2 * SUB].astype(jnp.bfloat16)


def outer_left_kernel(grid, left_ref, a_ref, part_ref):
    px, py, _ = grid
    nx, ny = 2 * px, 2 * py
    blk = a_ref.shape[3]
    masks = even_lanes(blk // 2)
    first, second = even_rows(blk)
    for x, y in [(x, y) for x in range(nx) for y in range(ny)]:
        here = a_ref.at[x, y]
        along_z = here[5] * first + here[6] * second
        low, high = halves(along_z)
        right = jnp.concatenate(
            [pair(here[1 + x % 2], here[3 + y % 2]), jnp.concatenate([low, high], axis=0)], axis=1
        )
        left = left_factors(left_ref[x * py + y // 2], y % 2, masks)
        got = dot(left, right).astype(jnp.bfloat16)
        part_ref[x, y, 0], part_ref[x, y, 1] = unpair(got[:, : 2 * blk])
        along = got[:, 2 * blk :]
        part_ref[x, y, 2] = jnp.concatenate([along[:blk], along[blk:]], axis=1)


def outer_kernel(
    dims, grid, route_ref, pair_ref, part_ref, zup_ref, zdn_ref,
    xface_ref, ya_ref, yb_ref, za_ref, zb_ref,
    send_xy_ref, send_z_ref, keep_xy_ref, keep_z_ref,
    total_ref, where_ref, table_ref,
):
    px, py, nz = grid
    _, _, rows = dims
    nx, ny = 2 * px, 2 * py
    blk = part_ref.shape[3]
    q = blk // 2
    nb = 6
    sent, kept = places(route_ref, where_ref, table_ref, dims, nb)
    me = lax.axis_index("gx")
    line = iota((blk, LANES), 0) * 0
    above = line + me > 0

    def from_sides(axis, first_ref, second_ref, at, high):
        index = lax.axis_index(axis)
        last = index == lax.axis_size(axis) - 1 if high else index == 0
        by_first = index % 2 == (0 if high else 1)
        kept = line + jnp.where(by_first | ~last, 1, 0) > 0
        value = jnp.where(by_first, first_ref[at], second_ref[at]).astype(jnp.float32)
        return jnp.where(kept, value, 0.0).astype(jnp.bfloat16)


    def beside_x(x, b, z, u):
        to = x - 1 if u == 0 else x + 1
        if 0 <= to < nx:
            return (zdn_ref, zup_ref)[z][to * py + b]
        part = xface_ref[b, z * blk : (z + 1) * blk].astype(jnp.float32)
        part = jnp.where(above, part, 0.0) if u == 0 else jnp.where(above, 0.0, part)
        return part.astype(jnp.bfloat16)

    def beside_y(x, y, z, v):
        to = y - 1 if v == 0 else y + 1
        if 0 <= to < ny:
            return (zdn_ref, zup_ref)[z][x * py + to // 2], to % 2
        at = (x // 2, slice(z * blk, (z + 1) * blk))
        return from_sides("gy", ya_ref, yb_ref, at, v == 1), x % 2

    for x in range(nx):
        made = []
        for b, z in [(b, z) for b in range(py) for z in range(nz)]:
            zs = pl.ds(z * q, q)
            u, a = x % 2, x // 2
            along_x = weights_of(beside_x(x, b, z, u))
            along_z = weights_of(from_sides("gz", za_ref, zb_ref, x * py + b, z == 1))
            flat = pair_ref[a, b, z] == 0
            for v in range(2):
                y = 2 * b + v
                t = u if u == v else jnp.where(flat, v, u)
                m = u if u == v else jnp.where(flat, u, v)
                i = ((a * py + b) * nz + z) * 2 + t
                other, k = beside_y(x, y, z, v)
                along_y = weights_of(other)[k]
                made.append((i, 2 * m, dot(part_ref[x, y, 0, zs], along_x[v])))
                made.append((i, 2 * m + 1, dot(part_ref[x, y, 1, zs], along_y)))
                made.append((i, 4 + m, dot(part_ref[x, y, 2, zs], along_z[v])))
        for i, block, got in made:
            put(total_ref, where_ref, i, block, rows, got)

    for kind, (xy, along, count) in enumerate((
        (send_xy_ref, send_z_ref, sent), (keep_xy_ref, keep_z_ref, kept),
    )):
        finish(((xy, 4), (along, 2)), total_ref, kind, dims, count)


def placed_blocks(early_ref, xy_ref, z_ref, codes, rows, at, size):
    code = jnp.concatenate([codes, codes], axis=0)
    near_low, near_high = (code < 1.5)[None], (code > 3.5)[None]
    upper = ((code == 1.0) | (code == 3.0) | (code == 5.0))[None]

    def tiles(ref, k):
        return ref[k * rows + at : k * rows + at + size].reshape(-1, 2 * SUB, LANES)

    if xy_ref is not None:
        yield 0, tiles(early_ref, 0)
        for m in range(2):
            cross, x_out, y_out = tiles(early_ref, 1 + m), tiles(xy_ref, 2 * m), tiles(xy_ref, 2 * m + 1)
            yield 1 + 5 * m, jnp.where(near_low, cross, x_out)
            yield 2 + 5 * m, jnp.where(near_low, x_out, jnp.where(near_high, y_out, cross))
            yield 3 + 5 * m, jnp.where(near_high, cross, y_out)
    if z_ref is not None:
        for m in range(2):
            z_in, z_out = tiles(early_ref, 3 + m), tiles(z_ref, m)
            yield 4 + 5 * m, jnp.where(upper, z_in, z_out)
            yield 5 + 5 * m, jnp.where(upper, z_out, z_in)


def keep_kernel(dims, early_ref, xy_ref, z_ref, half_ref, out_hbm, full_ref, sem):
    cap, rows = dims
    full = (cap - cap % SUB) * (rows // cap)
    me = lax.axis_index("gx")
    codes = early_ref[5 * rows :]
    copies = []
    for k, value in placed_blocks(early_ref, xy_ref, z_ref, codes[:SUB], rows, 0, full):
        full_ref[k] = value.reshape(full, LANES)
        to = out_hbm.at[k, pl.ds(me * (2 * full), full), :]
        copies.append(pltpu.make_async_copy(full_ref.at[k], to, sem.at[k]))
        copies[-1].start()
    for k, value in placed_blocks(early_ref, xy_ref, z_ref, codes[SUB:], rows, full, rows - full):
        half_ref[k] = value.reshape(rows - full, LANES)
    for copy in copies:
        copy.wait()


def take_kernel(dims, with_xy, early_ref, late_ref, half_ref, _, out_hbm, full_ref, mixed_ref, sem):
    cap, rows = dims
    full = (cap - cap % SUB) * (rows // cap)
    me = lax.axis_index("gx")
    codes = early_ref[5 * rows :]
    xy_ref, z_ref = (late_ref, None) if with_xy else (None, late_ref)
    copies = []
    for k, value in placed_blocks(early_ref, xy_ref, z_ref, codes[:SUB], rows, 0, full):
        full_ref[k] = value.reshape(full, LANES)
        to = out_hbm.at[k, pl.ds((1 - me) * (2 * full), full), :]
        copies.append(pltpu.make_async_copy(full_ref.at[k], to, sem.at[0, k]))
        copies[-1].start()
    first_half = (iota((SUB, LANES), 0) < SUB // 2)[None]
    pick = first_half == (me == 0)
    for k, value in placed_blocks(early_ref, xy_ref, z_ref, codes[SUB:], rows, full, rows - full):
        theirs = value.reshape(rows - full, LANES).astype(jnp.float32).reshape(-1, SUB, LANES)
        mine = half_ref[k].astype(jnp.float32).reshape(-1, SUB, LANES)
        low = jnp.where(pick, mine, theirs)
        high = pltpu.roll(jnp.where(pick, theirs, mine), SUB // 2, 1)
        mixed_ref[k, : rows - full] = low.reshape(rows - full, LANES).astype(jnp.bfloat16)
        mixed_ref[k, rows - full :] = high.reshape(rows - full, LANES).astype(jnp.bfloat16)
        to = out_hbm.at[k, full : 2 * full, :]
        copies.append(pltpu.make_async_copy(mixed_ref.at[k], to, sem.at[1, k]))
        copies[-1].start()
    for copy in copies:
        copy.wait()


SMEM = pl.BlockSpec(memory_space=pltpu.SMEM)
VMEM = pl.BlockSpec(memory_space=pltpu.VMEM)
ANY = pl.BlockSpec(memory_space=pl.ANY)


def bf16(*shape):
    return jax.ShapeDtypeStruct(shape, jnp.bfloat16)


def near(*shape):
    return pltpu.VMEM(shape, jnp.bfloat16)


def held(*arrays):
    return [pltpu.with_memory_space_constraint(one, pltpu.VMEM) for one in arrays]


def swaps(ny, nz):
    def first(i):
        return i + 1 if i % 2 == 0 else i - 1

    def second(i, n):
        j = i - 1 if i % 2 == 0 else i + 1
        return j if 0 <= j < n else None

    made = {"y_a": [], "y_b": [], "z_a": [], "z_b": []}
    for j in range(ny):
        for k in range(nz):
            to_y, to_z = second(j, ny), second(k, nz)
            made["y_a"].append((first(j), k))
            made["z_a"].append((j, first(k)))
            made["y_b"].append((j, first(k)) if to_y is None else (to_y, k))
            made["z_b"].append((first(j), k) if to_z is None else (j, to_z))
    return {name: [(i, j * nz + k) for i, (j, k) in enumerate(to)] for name, to in made.items()}


def local(a_blocks, prolong, pairing, route):
    devices_gx = lax.axis_size("gx")
    aggregates = route.shape[0]
    capacity = max(2, 3 * aggregates // (2 * devices_gx))
    nx, ny, nz, faces, entries = a_blocks.shape
    fits = (
        devices_gx == 2
        and lax.axis_size("gy") % 2 == 0
        and lax.axis_size("gz") % 2 == 0
        and nz == 2
        and nx % 2 == 0
        and ny % 2 == 0
        and faces == 7
        and entries == (LANES // 2) ** 2
        and capacity // SUB == 1
        and capacity % SUB == SUB // 2
    )
    if not fits:
        return general(a_blocks, prolong, pairing, route, capacity)
    px, py = nx // 2, ny // 2
    blk = math.isqrt(entries)
    lines = entries // LANES
    a_view = a_blocks.transpose(0, 1, 3, 2, 4).reshape(nx, ny, faces, nz, lines, LANES)
    a_view = a_view.transpose(0, 1, 2, 4, 3, 5).reshape(nx, ny, faces, nz * lines, LANES)
    p_view = prolong.reshape(nx, ny, nz, lines, LANES).transpose(0, 1, 3, 2, 4)
    p_view = p_view.reshape(nx, ny, nz * lines, LANES)
    route_row = route.reshape(1, aggregates)
    rows = capacity * lines
    dims, grid = (aggregates, capacity, rows), (px, py, nz)
    f32 = jnp.float32
    half_type = jnp.bfloat16
    face_x, face_y, face_z = (py, 2 * blk, LANES), (px, 2 * blk, LANES), (nx * py, blk, LANES)
    parts = (nx, ny, 3, blk, LANES)
    room = pltpu.CompilerParams(vmem_limit_bytes=24 * 2**20)
    cost = pl.CostEstimate(flops=10**9, bytes_accessed=4 * 10**6, transcendentals=0)

    send_0, keep_0, xface, ya, yb, za, zb, zup, zdn, left, a_near = pl.pallas_call(
        functools.partial(inner_kernel, dims, grid),
        out_shape=(
            near(5 * rows + 2 * SUB, LANES),
            near(5 * rows + 2 * SUB, LANES),
            near(*face_x),
            near(*face_y),
            near(*face_y),
            near(*face_z),
            near(*face_z),
            near(*face_z),
            near(*face_z),
            near(nx * py, 2 * blk, LANES),
            near(*a_view.shape),
        ),
        in_specs=[ANY] * 4,
        out_specs=[VMEM] * 11,
        scratch_shapes=[
            pltpu.VMEM(p_view.shape, half_type),
            pltpu.SMEM(route_row.shape, jnp.int32),
            pltpu.SMEM(pairing.shape, jnp.int32),
            pltpu.VMEM((nx, ny, 4, blk, LANES), half_type),
            pltpu.VMEM((10 * rows, LANES), f32),
            pltpu.VMEM((4 * SUB, LANES), f32),
            pltpu.SMEM((4, aggregates), jnp.int32),
            pltpu.SMEM((4, capacity), jnp.int32),
            pltpu.SemaphoreType.DMA((4,)),
        ],
        compiler_params=room,
        cost_estimate=cost,
        name="inner_blocks",
    )(*[pltpu.with_memory_space_constraint(one, pltpu.HBM) for one in (route_row, pairing, p_view, a_view)])

    swap = [(0, 1), (1, 0)]
    xface = lax.ppermute(xface, "gx", swap)
    got_0 = lax.ppermute(send_0, "gx", swap)
    rounds = swaps(lax.axis_size("gy"), lax.axis_size("gz"))
    halos = []
    for name, value in (("y_a", ya), ("y_b", yb), ("z_a", za), ("z_b", zb)):
        halos.append(lax.ppermute(value, ("gy", "gz"), rounds[name]))

    part = pl.pallas_call(
        functools.partial(outer_left_kernel, grid),
        out_shape=near(*parts),
        in_specs=[VMEM] * 2,
        out_specs=VMEM,
        compiler_params=room,
        cost_estimate=cost,
        name="outer_left",
    )(*held(left, a_near))
    send_xy, send_z, keep_xy, keep_z = pl.pallas_call(
        functools.partial(outer_kernel, dims, grid),
        out_shape=(near(4 * rows, LANES), near(2 * rows, LANES)) * 2,
        in_specs=[SMEM, SMEM] + [VMEM] * 8,
        out_specs=[VMEM] * 4,
        scratch_shapes=[
            pltpu.VMEM((12 * rows, LANES), f32),
            pltpu.SMEM((4, aggregates), jnp.int32),
            pltpu.SMEM((4, capacity), jnp.int32),
        ],
        compiler_params=room,
        cost_estimate=cost,
        name="outer_blocks",
    )(route_row, pairing, *held(part, zup, zdn, xface, *halos))
    got_xy = lax.ppermute(send_xy, "gx", swap)
    got_z = lax.ppermute(send_z, "gx", swap)

    full = (capacity // SUB) * SUB * lines
    whole = 2 * rows
    half, out = pl.pallas_call(
        functools.partial(keep_kernel, (capacity, rows)),
        out_shape=(near(11, rows - full, LANES), bf16(11, whole, LANES)),
        in_specs=[VMEM] * 3,
        out_specs=[VMEM, ANY],
        scratch_shapes=[pltpu.VMEM((11, full, LANES), half_type), pltpu.SemaphoreType.DMA((11,))],
        compiler_params=room,
        cost_estimate=cost,
        name="place_kept",
    )(*held(keep_0, keep_xy, keep_z))
    for with_xy, late in ((True, got_xy), (False, got_z)):
        out = pl.pallas_call(
            functools.partial(take_kernel, (capacity, rows), with_xy),
            out_shape=bf16(11, whole, LANES),
            in_specs=[VMEM] * 3 + [ANY],
            out_specs=ANY,
            input_output_aliases={3: 0},
            scratch_shapes=[
                pltpu.VMEM((11, full, LANES), half_type),
                pltpu.VMEM((11, full, LANES), half_type),
                pltpu.SemaphoreType.DMA((2, 11)),
            ],
            compiler_params=room,
            cost_estimate=cost,
            name="place_xy" if with_xy else "place_z",
        )(*held(got_0, late, half), out)
    out = out.reshape(11, whole // (SUB * lines), lines, SUB, LANES).transpose(1, 3, 0, 2, 4)
    return out.reshape(2 * capacity, 11, entries)


def solution(mesh):
    placed = (
        P("gx", "gy", "gz", None, None),
        P("gx", "gy", "gz", None),
        P("gx", "gy", "gz"),
        P(("gx", "gy", "gz"), None),
    )
    return jax.shard_map(
        local,
        mesh=mesh,
        in_specs=placed,
        out_specs=P(("gx", "gy", "gz"), None, None),
        check_vma=False,
    )
```

```python
import functools
import math

import jax
import jax.numpy as jnp
from jax import lax
from jax.experimental import pallas as pl
from jax.experimental.pallas import tpu as pltpu
from jax.sharding import PartitionSpec as P


x_first_order = [0, 2, 1, 3, 4, 5, 6]
x_second_order = [0, 1, 2, 3, 4, 5, 6]
y_first_order = [0, 4, 1, 2, 3, 5, 6]
y_second_order = [0, 3, 1, 2, 4, 5, 6]

LANES = 128
SUB = 8


def padded_2(array, sides, width):
    for axis, dim in sides:
        devices, length = (lax.axis_size(axis), array.shape[dim])
        up = [(i, (i + 1) % devices) for i in range(devices - 1)]
        down = [(j, i) for i, j in up]
        last = lax.slice_in_dim(array, length - width, length, axis=dim)
        initial = lax.slice_in_dim(array, 0, width, axis=dim)
        before = lax.ppermute(last, axis, up)
        after = lax.ppermute(initial, axis, down)
        array = jnp.concatenate([before, array, after], axis=dim)
    return array


def neighbours(padded):
    shifted = [
        padded[1:-1, 1:-1, 1:-1],
        padded[:-2, 1:-1, 1:-1],
        padded[2:, 1:-1, 1:-1],
        padded[1:-1, :-2, 1:-1],
        padded[1:-1, 2:, 1:-1],
        padded[1:-1, 1:-1, :-2],
        padded[1:-1, 1:-1, 2:],
    ]
    return jnp.stack(shifted, axis=3)


def triple(blocks, nearby):
    block_side = math.isqrt(blocks.shape[-1])
    leading = blocks.shape[:-1]
    left_mat = blocks.reshape(leading + (block_side, block_side))
    right_mat = nearby.reshape(leading + (block_side, block_side))
    own_block = jnp.swapaxes(right_mat[..., :1, :, :], -1, -2)
    product = jnp.matmul(left_mat, right_mat, preferred_element_type=jnp.float32).astype(
        jnp.bfloat16
    )
    result = jnp.matmul(own_block, product, preferred_element_type=jnp.float32)
    return result.reshape(leading + (block_side * block_side,))


def members(element_grid, pairs):
    size_x, size_y, size_z = element_grid.shape[:3]
    trailing = element_grid.shape[3:]
    patches = element_grid.reshape((size_x // 2, 2, size_y // 2, 2, size_z) + trailing)

    def pick(upper, lower, slot_order):
        return jnp.take(patches[:, upper, :, lower], jnp.array(slot_order, dtype=jnp.int32), axis=3)

    x_one = jnp.stack([pick(0, 0, x_first_order), pick(0, 1, x_first_order)], axis=3)
    x_two = jnp.stack([pick(1, 0, x_second_order), pick(1, 1, x_second_order)], axis=3)
    y_one = jnp.stack([pick(0, 0, y_first_order), pick(1, 0, y_first_order)], axis=3)
    y_two = jnp.stack([pick(0, 1, y_second_order), pick(1, 1, y_second_order)], axis=3)
    along_x = (pairs == 0).reshape(pairs.shape + (1,) * (x_one.ndim - 3))
    member_one = jnp.where(along_x, x_one, y_one)
    member_two = jnp.where(along_x, x_two, y_two)
    return (
        member_one.reshape((-1,) + member_one.shape[4:]),
        member_two.reshape((-1,) + member_two.shape[4:]),
    )


def arrange(member_one, member_two):
    diagonal = (
        member_one[..., 0, :]
        + member_two[..., 0, :]
        + member_one[..., 1, :]
        + member_two[..., 1, :]
    )
    return jnp.concatenate(
        [diagonal[..., None, :], member_one[..., 2:, :], member_two[..., 2:, :]], axis=-2
    )


def slot_sources(routes, n_dest, capacity):
    total = routes.shape[0]
    chosen = (routes[:, None] == jnp.arange(n_dest, dtype=jnp.int32)[None, :]).astype(jnp.int32)
    before = jnp.cumsum(chosen, axis=0) - chosen
    ranking = jnp.sum(before * chosen, axis=1)
    position = routes * capacity + ranking
    targets = jnp.arange(n_dest * capacity, dtype=jnp.int32)
    matches = position[None, :] == targets[:, None]
    anchor = jnp.sum(jnp.where(matches, jnp.arange(total, dtype=jnp.int32)[None, :], 0), axis=1)
    filled = jnp.any(matches, axis=1)
    return (anchor, filled)


def pack_slots(payload, anchor, filled):
    taken = jnp.take(payload, anchor, axis=0)
    keep_row = filled.reshape(filled.shape + (1,) * (payload.ndim - 1))
    return jnp.where(keep_row, taken, jnp.zeros_like(taken))


def general(a_blocks, prolong, pairing, route, capacity):
    padded = padded_2(prolong, (("gx", 0), ("gy", 1), ("gz", 2)), 1)
    nearby = neighbours(padded)
    anchor, filled = slot_sources(route[:, 0], lax.axis_size("gx"), capacity)
    galerkin = triple(a_blocks, nearby)
    member_one, member_two = members(galerkin, pairing)
    coarse = arrange(member_one, member_two).astype(jnp.bfloat16)
    return lax.all_to_all(
        pack_slots(coarse, anchor, filled), "gx", split_axis=0, concat_axis=0, tiled=True
    )


def dot(left, right):
    return jnp.dot(left, right, preferred_element_type=jnp.float32)


def iota(shape, axis):
    return lax.broadcasted_iota(jnp.int32, shape, axis)


def as_bf16(mask):
    return mask.astype(jnp.float32).astype(jnp.bfloat16)


def pair(one, two):
    h = one.shape[1] // 2
    low = jnp.concatenate([one[:, :h], two[:, :h]], axis=1)
    high = jnp.concatenate([one[:, h:], two[:, h:]], axis=1)
    return jnp.concatenate([low, high], axis=0)


def unpair(both):
    rows, h = both.shape[0] // 2, both.shape[1] // 2
    even, odd = both[:rows], both[rows:]
    return (
        jnp.concatenate([even[:, :h], odd[:, :h]], axis=1),
        jnp.concatenate([even[:, h:], odd[:, h:]], axis=1),
    )


def constants(blk):
    n = 2 * blk
    row, col = iota((n, n), 0), iota((n, n), 1)
    c, z = row % blk, row // blk
    clean = as_bf16(col == (c % 2) * blk + (c // 2) * 2 + z)
    q = blk // 2
    k, p = row // blk, (row // q) % 2
    spread = as_bf16(col == k * blk + 2 * (row % q) + p)
    return clean, spread


def even_lanes(rows):
    return as_bf16(iota((rows, LANES), 1) % 2 == 0), as_bf16(iota((rows, LANES), 1) % 2 == 1)


def even_rows(rows):
    return as_bf16(iota((rows, LANES), 0) % 2 == 0), as_bf16(iota((rows, LANES), 0) % 2 == 1)


def transposed_dot(left, right):
    return lax.dot_general(
        left, right, (((1,), (1,)), ((), ())), preferred_element_type=jnp.float32
    )


def left_factors(both_t, k, masks):
    q = masks[0].shape[0]
    parts = [both_t[(2 * k + p) * q : (2 * k + p + 1) * q] for p in range(2)]
    return jnp.concatenate([part * mask for part in parts for mask in masks], axis=0)


def weights_of(part):
    h = part.shape[1] // 2
    none = jnp.zeros((part.shape[0], h), part.dtype)
    made = []
    for k in range(2):
        one = part[:, k * h : (k + 1) * h]
        made.append(
            jnp.concatenate(
                [jnp.concatenate([one, none], axis=1), jnp.concatenate([none, one], axis=1)], axis=0
            )
        )
    return made


def halves(part):
    h = part.shape[1] // 2
    return part[:, :h], part[:, h:]


def places(route_ref, where_ref, table_ref, dims, blocks):
    aggregates, cap, rows = dims
    me = lax.axis_index("gx")
    lines = rows // cap
    rest = cap % SUB
    half = (cap - rest) * lines
    at_zero = me == 0
    for c in range(cap):
        if c < cap - rest:
            zero = (c, c + half // 2, c, c)
        else:
            h = c - (cap - rest)
            zero = (half + h, half + h + rest, SUB + h, SUB + h + rest)
        if c < rest:
            one = (half + c + rest, half + c, SUB + c, SUB + c + rest)
        else:
            h = c - rest
            one = (h, h + half // 2, h, h)
        for k in range(4):
            table_ref[k, c] = jnp.where(at_zero, zero[k], one[k])
    sent, kept = jnp.int32(0), jnp.int32(0)
    for i in range(aggregates):
        away = route_ref[0, i] != me
        one = away.astype(jnp.int32)
        c = jnp.where(away, sent, kept)
        sent = sent + one
        kept = kept + (1 - one)
        base = jnp.where(away, 0, blocks * rows)
        where_ref[0, i] = base + table_ref[0, c]
        where_ref[1, i] = base + table_ref[1, c]
        where_ref[2, i] = jnp.where(away, 0, 2 * SUB) + table_ref[2, c]
        where_ref[3, i] = jnp.where(away, 0, 2 * SUB) + table_ref[3, c]
    return sent, kept


def put(total_ref, where_ref, i, block, rows, value):
    n = value.shape[0] // 2
    one = where_ref[0, i] + block * rows
    two = where_ref[1, i] + block * rows
    total_ref[pl.ds(one, n, stride=SUB), :] = value[:n]
    total_ref[pl.ds(two, n, stride=SUB), :] = value[n:]


def finish(outs, total_ref, kind, dims, count):
    _, cap, rows = dims
    rest = cap % SUB
    full = (cap - rest) * (rows // cap)
    me = lax.axis_index("gx")
    line = iota((2 * SUB, LANES), 0)
    in_full = as_bf16(line % SUB + jnp.where(me == 0, 0, rest) < count) > 0.5
    in_half = as_bf16(line % rest + jnp.where(me == 0, cap - rest, 0) < count) > 0.5
    blocks = sum(n for _, n in outs)
    done = 0
    for out, n in outs:
        for k in range(n):
            for at, size, filled in ((0, full, in_full), (full, rows - full, in_half)):
                value = total_ref[pl.ds((kind * blocks + done + k) * rows + at, size), :]
                value = value.astype(jnp.bfloat16).reshape(-1, 2 * SUB, LANES)
                value = jnp.where(filled[None], value, jnp.zeros_like(value))
                out[k * rows + at : k * rows + at + size] = value.reshape(size, LANES)
        done += n


def face_kernel(p_hbm, face_ref, sem):
    last = p_hbm.shape[0] - 1
    at = jnp.where(lax.axis_index("gx") == 0, last, 0)
    copy = pltpu.make_async_copy(p_hbm.at[at], face_ref, sem.at[0])
    copy.start()
    copy.wait()


def inner_kernel(
    dims, grid, route_hbm, pair_hbm, p_ref, a_ref,
    send_ref, total_ref, keep_codes_ref, ya_ref, yb_ref, za_ref, zb_ref, zup_ref, zdn_ref, left_ref,
    route_ref, pair_ref, part_ref, codes_ref, where_ref, table_ref, sems,
):
    px, py, nz = grid
    aggregates, _, rows = dims
    nx, ny = 2 * px, 2 * py
    blk = p_ref.shape[2]
    q = blk // 2
    nb = 5
    copies = [
        pltpu.make_async_copy(one, two, sems.at[k])
        for k, (one, two) in enumerate(((route_hbm, route_ref), (pair_hbm, pair_ref)))
    ]
    for copy in copies:
        copy.start()
    clean, spread = constants(blk)
    masks = even_lanes(q)
    first, second = even_rows(blk)

    pairs = [(x, b) for x in range(nx) for b in range(py)]
    both = {e: pair(p_ref[e[0], 2 * e[1]], p_ref[e[0], 2 * e[1] + 1]) for e in pairs}
    tidy = {e: dot(clean, both[e]).astype(jnp.bfloat16) for e in pairs}
    for x, b in pairs:
        left_ref[x * py + b] = transposed_dot(spread, both[x, b]).astype(jnp.bfloat16)
        zdn_ref[x * py + b] = tidy[x, b][:blk]
        zup_ref[x * py + b] = tidy[x, b][blk:]
    y_even, z_even = lax.axis_index("gy") % 2 == 0, lax.axis_index("gz") % 2 == 0
    for a in range(px):
        one, two = tidy[2 * a, 0], tidy[2 * a + 1, 0]
        down = jnp.concatenate([one[:, :blk], two[:, :blk]], axis=1)
        one, two = tidy[2 * a, py - 1], tidy[2 * a + 1, py - 1]
        up = jnp.concatenate([one[:, blk:], two[:, blk:]], axis=1)
        ya_ref[a], yb_ref[a] = jnp.where(y_even, up, down), jnp.where(y_even, down, up)
    for x, b in pairs:
        down, up = tidy[x, b][:blk], tidy[x, b][blk:]
        za_ref[x * py + b] = jnp.where(z_even, up, down)
        zb_ref[x * py + b] = jnp.where(z_even, down, up)
    for x, y in [(x, y) for x in range(nx) for y in range(ny)]:
        here = a_ref.at[x, y]
        along_z = here[6] * first + here[5] * second
        right = jnp.concatenate(
            [pair(here[0], here[2 - x % 2]), pair(here[4 - y % 2], along_z)], axis=1
        )
        left = left_factors(left_ref[x * py + y // 2], y % 2, masks)
        got = dot(left, right).astype(jnp.bfloat16)
        parts = unpair(got[:, : 2 * blk]) + unpair(got[:, 2 * blk :])
        for k in range(4):
            part_ref[x, y, k] = parts[k]

    for copy in copies:
        copy.wait()
    sent, _ = places(route_ref, where_ref, table_ref, dims, nb)
    codes_ref[...] = jnp.full_like(codes_ref, -1.0)
    for i in range(aggregates):
        a, b, z, t = i // (py * nz * 2), (i // (nz * 2)) % py, (i // 2) % nz, i % 2
        code = (2 * (jnp.where(pair_ref[a, b, z] == 0, 2, 1) - t) + z).astype(jnp.float32)
        line = jnp.full((1, LANES), code, jnp.float32)
        codes_ref[pl.ds(where_ref[2, i], 1), :] = line
        codes_ref[pl.ds(where_ref[3, i], 1), :] = line

    for a, b in [(a, b) for a in range(px) for b in range(py)]:
        own, with_x, with_y, with_z = {}, {}, {}, {}
        for z, ref in enumerate((zdn_ref, zup_ref)):
            zs, zo = pl.ds(z * q, q), pl.ds((1 - z) * q, q)
            for u in range(2):
                x = 2 * a + u
                weight = weights_of(ref[x * py + b])
                for v in range(2):
                    y = 2 * b + v
                    stack = jnp.concatenate(
                        [
                            part_ref[x, y, 0, zs],
                            part_ref[2 * a + 1 - u, y, 1, zs],
                            part_ref[x, 2 * b + 1 - v, 2, zs],
                            part_ref[x, y, 3, zo],
                        ],
                        axis=0,
                    )
                    got = dot(stack, weight[v])
                    own[u, v, z] = got[:q]
                    with_x[1 - u, v, z] = got[q : 2 * q]
                    with_y[u, 1 - v, z] = got[2 * q : 3 * q]
                    with_z[u, v, 1 - z] = got[3 * q :]
        for z in range(nz):
            flat = pair_ref[a, b, z] == 0
            i = ((a * py + b) * nz + z) * 2
            sums = {}
            for u in range(2):
                for v in range(2):
                    t = u if u == v else jnp.where(flat, v, u)
                    m = u if u == v else jnp.where(flat, u, v)
                    e = (u, v, z)
                    sums[u, v] = own[e] + jnp.where(flat, with_x[e], with_y[e])
                    cross = jnp.where(flat, with_y[e], with_x[e])
                    put(total_ref, where_ref, i + t, 1 + m, rows, cross)
                    put(total_ref, where_ref, i + t, 3 + m, rows, with_z[e])
            put(total_ref, where_ref, i, 0, rows, sums[0, 0] + jnp.where(flat, sums[1, 0], sums[0, 1]))
            put(total_ref, where_ref, i + 1, 0, rows, sums[1, 1] + jnp.where(flat, sums[0, 1], sums[1, 0]))

    finish(((send_ref, nb),), total_ref, 0, dims, sent)
    send_ref[nb * rows :] = codes_ref[: 2 * SUB].astype(jnp.bfloat16)
    keep_codes_ref[...] = codes_ref[2 * SUB :].astype(jnp.bfloat16)


def outer_left_kernel(grid, left_ref, a_ref, face_ref, part_ref, xface_ref):
    px, py, _ = grid
    nx, ny = 2 * px, 2 * py
    blk = a_ref.shape[3]
    clean, _ = constants(blk)
    for b in range(py):
        both = pair(face_ref[2 * b], face_ref[2 * b + 1])
        xface_ref[b] = dot(clean, both).astype(jnp.bfloat16)
    masks = even_lanes(blk // 2)
    first, second = even_rows(blk)
    for x, y in [(x, y) for x in range(nx) for y in range(ny)]:
        here = a_ref.at[x, y]
        along_z = here[5] * first + here[6] * second
        low, high = halves(along_z)
        right = jnp.concatenate(
            [pair(here[1 + x % 2], here[3 + y % 2]), jnp.concatenate([low, high], axis=0)], axis=1
        )
        left = left_factors(left_ref[x * py + y // 2], y % 2, masks)
        got = dot(left, right).astype(jnp.bfloat16)
        part_ref[x, y, 0], part_ref[x, y, 1] = unpair(got[:, : 2 * blk])
        along = got[:, 2 * blk :]
        part_ref[x, y, 2] = jnp.concatenate([along[:blk], along[blk:]], axis=1)


def outer_kernel(
    dims, grid, route_ref, pair_ref, part_ref, zup_ref, zdn_ref,
    xface_ref, ya_ref, yb_ref, za_ref, zb_ref,
    send_xy_ref, send_z_ref, keep_xy_ref, keep_z_ref,
    total_ref, where_ref, table_ref,
):
    px, py, nz = grid
    _, _, rows = dims
    nx, ny = 2 * px, 2 * py
    blk = part_ref.shape[3]
    q = blk // 2
    nb = 6
    sent, kept = places(route_ref, where_ref, table_ref, dims, nb)
    me = lax.axis_index("gx")
    line = iota((blk, LANES), 0) * 0
    above = line + me > 0

    def from_sides(axis, first_ref, second_ref, at, high):
        index = lax.axis_index(axis)
        last = index == lax.axis_size(axis) - 1 if high else index == 0
        by_first = index % 2 == (0 if high else 1)
        kept = line + jnp.where(by_first | ~last, 1, 0) > 0
        value = jnp.where(by_first, first_ref[at], second_ref[at]).astype(jnp.float32)
        return jnp.where(kept, value, 0.0).astype(jnp.bfloat16)


    def beside_x(x, b, z, u):
        to = x - 1 if u == 0 else x + 1
        if 0 <= to < nx:
            return (zdn_ref, zup_ref)[z][to * py + b]
        part = xface_ref[b, z * blk : (z + 1) * blk].astype(jnp.float32)
        part = jnp.where(above, part, 0.0) if u == 0 else jnp.where(above, 0.0, part)
        return part.astype(jnp.bfloat16)

    def beside_y(x, y, z, v):
        to = y - 1 if v == 0 else y + 1
        if 0 <= to < ny:
            return (zdn_ref, zup_ref)[z][x * py + to // 2], to % 2
        at = (x // 2, slice(z * blk, (z + 1) * blk))
        return from_sides("gy", ya_ref, yb_ref, at, v == 1), x % 2

    for x in range(nx):
        made = []
        for b, z in [(b, z) for b in range(py) for z in range(nz)]:
            zs = pl.ds(z * q, q)
            u, a = x % 2, x // 2
            along_x = weights_of(beside_x(x, b, z, u))
            along_z = weights_of(from_sides("gz", za_ref, zb_ref, x * py + b, z == 1))
            flat = pair_ref[a, b, z] == 0
            for v in range(2):
                y = 2 * b + v
                t = u if u == v else jnp.where(flat, v, u)
                m = u if u == v else jnp.where(flat, u, v)
                i = ((a * py + b) * nz + z) * 2 + t
                other, k = beside_y(x, y, z, v)
                along_y = weights_of(other)[k]
                made.append((i, 2 * m, dot(part_ref[x, y, 0, zs], along_x[v])))
                made.append((i, 2 * m + 1, dot(part_ref[x, y, 1, zs], along_y)))
                made.append((i, 4 + m, dot(part_ref[x, y, 2, zs], along_z[v])))
        for i, block, got in made:
            put(total_ref, where_ref, i, block, rows, got)

    for kind, (xy, along, count) in enumerate((
        (send_xy_ref, send_z_ref, sent), (keep_xy_ref, keep_z_ref, kept),
    )):
        finish(((xy, 4), (along, 2)), total_ref, kind, dims, count)


def received(early_ref, rows):
    def early(k, at, size):
        return early_ref[k * rows + at : k * rows + at + size].reshape(-1, 2 * SUB, LANES)

    return early


def placed_blocks(early, xy_ref, z_ref, code, rows, at, size):
    near_low, near_high = (code < 1.5)[None], (code > 3.5)[None]
    upper = ((code == 1.0) | (code == 3.0) | (code == 5.0))[None]

    def tiles(ref, k):
        return ref[k * rows + at : k * rows + at + size].reshape(-1, 2 * SUB, LANES)

    if xy_ref is not None:
        yield 0, early(0, at, size)
        for m in range(2):
            cross, x_out, y_out = early(1 + m, at, size), tiles(xy_ref, 2 * m), tiles(xy_ref, 2 * m + 1)
            yield 1 + 5 * m, jnp.where(near_low, cross, x_out)
            yield 2 + 5 * m, jnp.where(near_low, x_out, jnp.where(near_high, y_out, cross))
            yield 3 + 5 * m, jnp.where(near_high, cross, y_out)
    if z_ref is not None:
        for m in range(2):
            z_in, z_out = early(3 + m, at, size), tiles(z_ref, m)
            yield 4 + 5 * m, jnp.where(upper, z_in, z_out)
            yield 5 + 5 * m, jnp.where(upper, z_out, z_in)


def twice(codes):
    return jnp.concatenate([codes, codes], axis=0)


def keep_kernel(dims, total_ref, codes_ref, xy_ref, z_ref, half_ref, out_hbm, full_ref, sem):
    cap, rows = dims
    full = (cap - cap % SUB) * (rows // cap)
    me = lax.axis_index("gx")

    def rounded(code):
        filled = (code > -0.5)[None]

        def early(k, at, size):
            value = total_ref[pl.ds((5 + k) * rows + at, size), :].astype(jnp.bfloat16)
            value = value.reshape(-1, 2 * SUB, LANES)
            return jnp.where(filled, value, jnp.zeros_like(value))

        return early

    copies = []
    code = twice(codes_ref[:SUB])
    for k, value in placed_blocks(rounded(code), xy_ref, z_ref, code, rows, 0, full):
        full_ref[k] = value.reshape(full, LANES)
        to = out_hbm.at[k, pl.ds(me * (2 * full), full), :]
        copies.append(pltpu.make_async_copy(full_ref.at[k], to, sem.at[k]))
        copies[-1].start()
    code = twice(codes_ref[SUB:])
    for k, value in placed_blocks(rounded(code), xy_ref, z_ref, code, rows, full, rows - full):
        half_ref[k] = value.reshape(rows - full, LANES)
    for copy in copies:
        copy.wait()


def take_kernel(dims, with_xy, early_ref, late_ref, half_ref, _, out_hbm, full_ref, mixed_ref, sem):
    cap, rows = dims
    full = (cap - cap % SUB) * (rows // cap)
    me = lax.axis_index("gx")
    codes = early_ref[5 * rows :]
    xy_ref, z_ref = (late_ref, None) if with_xy else (None, late_ref)
    early = received(early_ref, rows)
    copies = []
    for k, value in placed_blocks(early, xy_ref, z_ref, twice(codes[:SUB]), rows, 0, full):
        full_ref[k] = value.reshape(full, LANES)
        to = out_hbm.at[k, pl.ds((1 - me) * (2 * full), full), :]
        copies.append(pltpu.make_async_copy(full_ref.at[k], to, sem.at[0, k]))
        copies[-1].start()
    first_half = (iota((SUB, LANES), 0) < SUB // 2)[None]
    pick = first_half == (me == 0)
    for k, value in placed_blocks(early, xy_ref, z_ref, twice(codes[SUB:]), rows, full, rows - full):
        theirs = value.reshape(rows - full, LANES).astype(jnp.float32).reshape(-1, SUB, LANES)
        mine = half_ref[k].astype(jnp.float32).reshape(-1, SUB, LANES)
        low = jnp.where(pick, mine, theirs)
        high = pltpu.roll(jnp.where(pick, theirs, mine), SUB // 2, 1)
        mixed_ref[k, : rows - full] = low.reshape(rows - full, LANES).astype(jnp.bfloat16)
        mixed_ref[k, rows - full :] = high.reshape(rows - full, LANES).astype(jnp.bfloat16)
        to = out_hbm.at[k, full : 2 * full, :]
        copies.append(pltpu.make_async_copy(mixed_ref.at[k], to, sem.at[1, k]))
        copies[-1].start()
    for copy in copies:
        copy.wait()


SMEM = pl.BlockSpec(memory_space=pltpu.SMEM)
VMEM = pl.BlockSpec(memory_space=pltpu.VMEM)
ANY = pl.BlockSpec(memory_space=pl.ANY)


def bf16(*shape):
    return jax.ShapeDtypeStruct(shape, jnp.bfloat16)


def near(*shape):
    return pltpu.VMEM(shape, jnp.bfloat16)


def held(*arrays):
    return [pltpu.with_memory_space_constraint(one, pltpu.VMEM) for one in arrays]


def swaps(ny, nz):
    def first(i):
        return i + 1 if i % 2 == 0 else i - 1

    def second(i, n):
        j = i - 1 if i % 2 == 0 else i + 1
        return j if 0 <= j < n else None

    made = {"y_a": [], "y_b": [], "z_a": [], "z_b": []}
    for j in range(ny):
        for k in range(nz):
            to_y, to_z = second(j, ny), second(k, nz)
            made["y_a"].append((first(j), k))
            made["z_a"].append((j, first(k)))
            made["y_b"].append((j, first(k)) if to_y is None else (to_y, k))
            made["z_b"].append((first(j), k) if to_z is None else (j, to_z))
    return {name: [(i, j * nz + k) for i, (j, k) in enumerate(to)] for name, to in made.items()}


def local(a_blocks, prolong, pairing, route):
    devices_gx = lax.axis_size("gx")
    aggregates = route.shape[0]
    capacity = max(2, 3 * aggregates // (2 * devices_gx))
    nx, ny, nz, faces, entries = a_blocks.shape
    fits = (
        devices_gx == 2
        and lax.axis_size("gy") % 2 == 0
        and lax.axis_size("gz") % 2 == 0
        and nz == 2
        and nx % 2 == 0
        and ny % 2 == 0
        and faces == 7
        and entries == (LANES // 2) ** 2
        and capacity // SUB == 1
        and capacity % SUB == SUB // 2
    )
    if not fits:
        return general(a_blocks, prolong, pairing, route, capacity)
    px, py = nx // 2, ny // 2
    blk = math.isqrt(entries)
    lines = entries // LANES
    a_view = a_blocks.transpose(0, 1, 3, 2, 4).reshape(nx, ny, faces, nz, lines, LANES)
    a_view = a_view.transpose(0, 1, 2, 4, 3, 5).reshape(nx, ny, faces, nz * lines, LANES)
    p_view = prolong.reshape(nx, ny, nz, lines, LANES).transpose(0, 1, 3, 2, 4)
    p_view = p_view.reshape(nx, ny, nz * lines, LANES)
    route_row = route.reshape(1, aggregates)
    rows = capacity * lines
    dims, grid = (aggregates, capacity, rows), (px, py, nz)
    f32 = jnp.float32
    half_type = jnp.bfloat16
    face_x, face_y, face_z = (py, 2 * blk, LANES), (px, 2 * blk, LANES), (nx * py, blk, LANES)
    parts = (nx, ny, 3, blk, LANES)
    room = pltpu.CompilerParams(vmem_limit_bytes=24 * 2**20)
    cost = pl.CostEstimate(flops=10**9, bytes_accessed=4 * 10**6, transcendentals=0)

    swap = [(0, 1), (1, 0)]
    face = pl.pallas_call(
        face_kernel,
        out_shape=near(ny, blk, LANES),
        in_specs=[ANY],
        out_specs=VMEM,
        scratch_shapes=[pltpu.SemaphoreType.DMA((1,))],
        compiler_params=room,
        cost_estimate=cost,
        name="face",
    )(pltpu.with_memory_space_constraint(p_view, pltpu.HBM))
    face = lax.ppermute(face, "gx", swap)
    p_near, a_near = held(p_view, a_view)
    send_0, total, keep_codes, ya, yb, za, zb, zup, zdn, left = pl.pallas_call(
        functools.partial(inner_kernel, dims, grid),
        out_shape=(
            near(5 * rows + 2 * SUB, LANES),
            pltpu.VMEM((10 * rows, LANES), f32),
            near(2 * SUB, LANES),
            near(*face_y),
            near(*face_y),
            near(*face_z),
            near(*face_z),
            near(*face_z),
            near(*face_z),
            near(nx * py, 2 * blk, LANES),
        ),
        in_specs=[ANY, ANY, VMEM, VMEM],
        out_specs=[VMEM] * 10,
        scratch_shapes=[
            pltpu.SMEM(route_row.shape, jnp.int32),
            pltpu.SMEM(pairing.shape, jnp.int32),
            pltpu.VMEM((nx, ny, 4, blk, LANES), half_type),
            pltpu.VMEM((4 * SUB, LANES), f32),
            pltpu.SMEM((4, aggregates), jnp.int32),
            pltpu.SMEM((4, capacity), jnp.int32),
            pltpu.SemaphoreType.DMA((2,)),
        ],
        compiler_params=room,
        cost_estimate=cost,
        name="inner_blocks",
    )(
        *[pltpu.with_memory_space_constraint(one, pltpu.HBM) for one in (route_row, pairing)],
        p_near,
        a_near,
    )
    got_0 = lax.ppermute(send_0, "gx", swap)
    rounds = swaps(lax.axis_size("gy"), lax.axis_size("gz"))
    halos = []
    for name, value in (("y_a", ya), ("y_b", yb), ("z_a", za), ("z_b", zb)):
        halos.append(lax.ppermute(value, ("gy", "gz"), rounds[name]))

    part, xface = pl.pallas_call(
        functools.partial(outer_left_kernel, grid),
        out_shape=(near(*parts), near(*face_x)),
        in_specs=[VMEM] * 3,
        out_specs=[VMEM] * 2,
        compiler_params=room,
        cost_estimate=cost,
        name="outer_left",
    )(*held(left), a_near, *held(face))
    send_xy, send_z, keep_xy, keep_z = pl.pallas_call(
        functools.partial(outer_kernel, dims, grid),
        out_shape=(near(4 * rows, LANES), near(2 * rows, LANES)) * 2,
        in_specs=[SMEM, SMEM] + [VMEM] * 8,
        out_specs=[VMEM] * 4,
        scratch_shapes=[
            pltpu.VMEM((12 * rows, LANES), f32),
            pltpu.SMEM((4, aggregates), jnp.int32),
            pltpu.SMEM((4, capacity), jnp.int32),
        ],
        compiler_params=room,
        cost_estimate=cost,
        name="outer_blocks",
    )(route_row, pairing, *held(part, zup, zdn, xface, *halos))
    got_xy = lax.ppermute(send_xy, "gx", swap)
    got_z = lax.ppermute(send_z, "gx", swap)

    full = (capacity // SUB) * SUB * lines
    whole = 2 * rows
    half, out = pl.pallas_call(
        functools.partial(keep_kernel, (capacity, rows)),
        out_shape=(near(11, rows - full, LANES), bf16(11, whole, LANES)),
        in_specs=[VMEM] * 4,
        out_specs=[VMEM, ANY],
        scratch_shapes=[pltpu.VMEM((11, full, LANES), half_type), pltpu.SemaphoreType.DMA((11,))],
        compiler_params=room,
        cost_estimate=cost,
        name="place_kept",
    )(*held(total, keep_codes, keep_xy, keep_z))
    for with_xy, late in ((True, got_xy), (False, got_z)):
        out = pl.pallas_call(
            functools.partial(take_kernel, (capacity, rows), with_xy),
            out_shape=bf16(11, whole, LANES),
            in_specs=[VMEM] * 3 + [ANY],
            out_specs=ANY,
            input_output_aliases={3: 0},
            scratch_shapes=[
                pltpu.VMEM((11, full, LANES), half_type),
                pltpu.VMEM((11, full, LANES), half_type),
                pltpu.SemaphoreType.DMA((2, 11)),
            ],
            compiler_params=room,
            cost_estimate=cost,
            name="place_xy" if with_xy else "place_z",
        )(*held(got_0, late, half), out)
    out = out.reshape(11, whole // (SUB * lines), lines, SUB, LANES).transpose(1, 3, 0, 2, 4)
    return out.reshape(2 * capacity, 11, entries)


def solution(mesh):
    placed = (
        P("gx", "gy", "gz", None, None),
        P("gx", "gy", "gz", None),
        P("gx", "gy", "gz"),
        P(("gx", "gy", "gz"), None),
    )
    return jax.shard_map(
        local,
        mesh=mesh,
        in_specs=placed,
        out_specs=P(("gx", "gy", "gz"), None, None),
        check_vma=False,
    )
```

```python
import functools
import math

import jax
import jax.numpy as jnp
from jax import lax
from jax.experimental import pallas as pl
from jax.experimental.pallas import tpu as pltpu
from jax.sharding import PartitionSpec as P


x_first_order = [0, 2, 1, 3, 4, 5, 6]
x_second_order = [0, 1, 2, 3, 4, 5, 6]
y_first_order = [0, 4, 1, 2, 3, 5, 6]
y_second_order = [0, 3, 1, 2, 4, 5, 6]

LANES = 128
SUB = 8


def padded_2(array, sides, width):
    for axis, dim in sides:
        devices, length = (lax.axis_size(axis), array.shape[dim])
        up = [(i, (i + 1) % devices) for i in range(devices - 1)]
        down = [(j, i) for i, j in up]
        last = lax.slice_in_dim(array, length - width, length, axis=dim)
        initial = lax.slice_in_dim(array, 0, width, axis=dim)
        before = lax.ppermute(last, axis, up)
        after = lax.ppermute(initial, axis, down)
        array = jnp.concatenate([before, array, after], axis=dim)
    return array


def neighbours(padded):
    shifted = [
        padded[1:-1, 1:-1, 1:-1],
        padded[:-2, 1:-1, 1:-1],
        padded[2:, 1:-1, 1:-1],
        padded[1:-1, :-2, 1:-1],
        padded[1:-1, 2:, 1:-1],
        padded[1:-1, 1:-1, :-2],
        padded[1:-1, 1:-1, 2:],
    ]
    return jnp.stack(shifted, axis=3)


def triple(blocks, nearby):
    block_side = math.isqrt(blocks.shape[-1])
    leading = blocks.shape[:-1]
    left_mat = blocks.reshape(leading + (block_side, block_side))
    right_mat = nearby.reshape(leading + (block_side, block_side))
    own_block = jnp.swapaxes(right_mat[..., :1, :, :], -1, -2)
    product = jnp.matmul(left_mat, right_mat, preferred_element_type=jnp.float32).astype(
        jnp.bfloat16
    )
    result = jnp.matmul(own_block, product, preferred_element_type=jnp.float32)
    return result.reshape(leading + (block_side * block_side,))


def members(element_grid, pairs):
    size_x, size_y, size_z = element_grid.shape[:3]
    trailing = element_grid.shape[3:]
    patches = element_grid.reshape((size_x // 2, 2, size_y // 2, 2, size_z) + trailing)

    def pick(upper, lower, slot_order):
        return jnp.take(patches[:, upper, :, lower], jnp.array(slot_order, dtype=jnp.int32), axis=3)

    x_one = jnp.stack([pick(0, 0, x_first_order), pick(0, 1, x_first_order)], axis=3)
    x_two = jnp.stack([pick(1, 0, x_second_order), pick(1, 1, x_second_order)], axis=3)
    y_one = jnp.stack([pick(0, 0, y_first_order), pick(1, 0, y_first_order)], axis=3)
    y_two = jnp.stack([pick(0, 1, y_second_order), pick(1, 1, y_second_order)], axis=3)
    along_x = (pairs == 0).reshape(pairs.shape + (1,) * (x_one.ndim - 3))
    member_one = jnp.where(along_x, x_one, y_one)
    member_two = jnp.where(along_x, x_two, y_two)
    return (
        member_one.reshape((-1,) + member_one.shape[4:]),
        member_two.reshape((-1,) + member_two.shape[4:]),
    )


def arrange(member_one, member_two):
    diagonal = (
        member_one[..., 0, :]
        + member_two[..., 0, :]
        + member_one[..., 1, :]
        + member_two[..., 1, :]
    )
    return jnp.concatenate(
        [diagonal[..., None, :], member_one[..., 2:, :], member_two[..., 2:, :]], axis=-2
    )


def slot_sources(routes, n_dest, capacity):
    total = routes.shape[0]
    chosen = (routes[:, None] == jnp.arange(n_dest, dtype=jnp.int32)[None, :]).astype(jnp.int32)
    before = jnp.cumsum(chosen, axis=0) - chosen
    ranking = jnp.sum(before * chosen, axis=1)
    position = routes * capacity + ranking
    targets = jnp.arange(n_dest * capacity, dtype=jnp.int32)
    matches = position[None, :] == targets[:, None]
    anchor = jnp.sum(jnp.where(matches, jnp.arange(total, dtype=jnp.int32)[None, :], 0), axis=1)
    filled = jnp.any(matches, axis=1)
    return (anchor, filled)


def pack_slots(payload, anchor, filled):
    taken = jnp.take(payload, anchor, axis=0)
    keep_row = filled.reshape(filled.shape + (1,) * (payload.ndim - 1))
    return jnp.where(keep_row, taken, jnp.zeros_like(taken))


def general(a_blocks, prolong, pairing, route, capacity):
    padded = padded_2(prolong, (("gx", 0), ("gy", 1), ("gz", 2)), 1)
    nearby = neighbours(padded)
    anchor, filled = slot_sources(route[:, 0], lax.axis_size("gx"), capacity)
    galerkin = triple(a_blocks, nearby)
    member_one, member_two = members(galerkin, pairing)
    coarse = arrange(member_one, member_two).astype(jnp.bfloat16)
    return lax.all_to_all(
        pack_slots(coarse, anchor, filled), "gx", split_axis=0, concat_axis=0, tiled=True
    )


def dot(left, right):
    return jnp.dot(left, right, preferred_element_type=jnp.float32)


def iota(shape, axis):
    return lax.broadcasted_iota(jnp.int32, shape, axis)


def as_bf16(mask):
    return mask.astype(jnp.float32).astype(jnp.bfloat16)


def pair(one, two):
    h = one.shape[1] // 2
    low = jnp.concatenate([one[:, :h], two[:, :h]], axis=1)
    high = jnp.concatenate([one[:, h:], two[:, h:]], axis=1)
    return jnp.concatenate([low, high], axis=0)


def unpair(both):
    rows, h = both.shape[0] // 2, both.shape[1] // 2
    even, odd = both[:rows], both[rows:]
    return (
        jnp.concatenate([even[:, :h], odd[:, :h]], axis=1),
        jnp.concatenate([even[:, h:], odd[:, h:]], axis=1),
    )


def constants(blk):
    n = 2 * blk
    row, col = iota((n, n), 0), iota((n, n), 1)
    c, z = row % blk, row // blk
    clean = as_bf16(col == (c % 2) * blk + (c // 2) * 2 + z)
    q = blk // 2
    k, p = row // blk, (row // q) % 2
    spread = as_bf16(col == k * blk + 2 * (row % q) + p)
    return clean, spread


def even_lanes(rows):
    return as_bf16(iota((rows, LANES), 1) % 2 == 0), as_bf16(iota((rows, LANES), 1) % 2 == 1)


def even_rows(rows):
    return as_bf16(iota((rows, LANES), 0) % 2 == 0), as_bf16(iota((rows, LANES), 0) % 2 == 1)


def transposed_dot(left, right):
    return lax.dot_general(
        left, right, (((1,), (1,)), ((), ())), preferred_element_type=jnp.float32
    )


def left_factors(both_t, k, masks):
    q = masks[0].shape[0]
    parts = [both_t[(2 * k + p) * q : (2 * k + p + 1) * q] for p in range(2)]
    return jnp.concatenate([part * mask for part in parts for mask in masks], axis=0)


def weights_of(part):
    h = part.shape[1] // 2
    none = jnp.zeros((part.shape[0], h), part.dtype)
    made = []
    for k in range(2):
        one = part[:, k * h : (k + 1) * h]
        made.append(
            jnp.concatenate(
                [jnp.concatenate([one, none], axis=1), jnp.concatenate([none, one], axis=1)], axis=0
            )
        )
    return made


def halves(part):
    h = part.shape[1] // 2
    return part[:, :h], part[:, h:]


def places(route_ref, where_ref, table_ref, dims, blocks):
    aggregates, cap, rows = dims
    me = lax.axis_index("gx")
    lines = rows // cap
    rest = cap % SUB
    half = (cap - rest) * lines
    at_zero = me == 0
    for c in range(cap):
        if c < cap - rest:
            zero = (c, c + half // 2, c, c)
        else:
            h = c - (cap - rest)
            zero = (half + h, half + h + rest, SUB + h, SUB + h + rest)
        if c < rest:
            one = (half + c + rest, half + c, SUB + c, SUB + c + rest)
        else:
            h = c - rest
            one = (h, h + half // 2, h, h)
        for k in range(4):
            table_ref[k, c] = jnp.where(at_zero, zero[k], one[k])
    sent, kept = jnp.int32(0), jnp.int32(0)
    for i in range(aggregates):
        away = route_ref[0, i] != me
        one = away.astype(jnp.int32)
        c = jnp.where(away, sent, kept)
        sent = sent + one
        kept = kept + (1 - one)
        base = jnp.where(away, 0, blocks * rows)
        where_ref[0, i] = base + table_ref[0, c]
        where_ref[1, i] = base + table_ref[1, c]
        where_ref[2, i] = jnp.where(away, 0, 2 * SUB) + table_ref[2, c]
        where_ref[3, i] = jnp.where(away, 0, 2 * SUB) + table_ref[3, c]
    return sent, kept


def put(total_ref, where_ref, i, block, rows, value):
    n = value.shape[0] // 2
    one = where_ref[0, i] + block * rows
    two = where_ref[1, i] + block * rows
    total_ref[pl.ds(one, n, stride=SUB), :] = value[:n]
    total_ref[pl.ds(two, n, stride=SUB), :] = value[n:]


def finish(outs, total_ref, kind, dims, count):
    _, cap, rows = dims
    rest = cap % SUB
    full = (cap - rest) * (rows // cap)
    me = lax.axis_index("gx")
    line = iota((2 * SUB, LANES), 0)
    in_full = as_bf16(line % SUB + jnp.where(me == 0, 0, rest) < count) > 0.5
    in_half = as_bf16(line % rest + jnp.where(me == 0, cap - rest, 0) < count) > 0.5
    blocks = sum(n for _, n in outs)
    done = 0
    for out, n in outs:
        for k in range(n):
            for at, size, filled in ((0, full, in_full), (full, rows - full, in_half)):
                value = total_ref[pl.ds((kind * blocks + done + k) * rows + at, size), :]
                value = value.astype(jnp.bfloat16).reshape(-1, 2 * SUB, LANES)
                value = jnp.where(filled[None], value, jnp.zeros_like(value))
                out[k * rows + at : k * rows + at + size] = value.reshape(size, LANES)
        done += n


def face_kernel(p_hbm, face_ref, sem):
    last = p_hbm.shape[0] - 1
    at = jnp.where(lax.axis_index("gx") == 0, last, 0)
    copy = pltpu.make_async_copy(p_hbm.at[at], face_ref, sem.at[0])
    copy.start()
    copy.wait()


def in_groups(items, size):
    return [items[k : k + size] for k in range(0, len(items), size)]


def first_kernel(
    dims, grid, route_hbm, pair_hbm, p_ref, a_ref,
    send_ref, total_ref, zup_ref, zdn_ref, left_ref,
    route_ref, pair_ref, where_ref, table_ref, sems,
):
    px, py, nz = grid
    _, _, rows = dims
    nx = 2 * px
    blk = p_ref.shape[2]
    q = blk // 2
    nb = 2
    copies = [
        pltpu.make_async_copy(one, two, sems.at[k])
        for k, (one, two) in enumerate(((route_hbm, route_ref), (pair_hbm, pair_ref)))
    ]
    for copy in copies:
        copy.start()
    clean, spread = constants(blk)
    masks = even_lanes(q)
    first, second = even_rows(blk)
    lane = iota((blk, LANES), 1)
    low, high = as_bf16(lane < LANES // 2), as_bf16(lane >= LANES // 2)
    pairs = [(x, b) for x in range(nx) for b in range(py)]
    both = {e: pair(p_ref[e[0], 2 * e[1]], p_ref[e[0], 2 * e[1] + 1]) for e in pairs}
    left, tidy = {}, {}
    for e in pairs:
        at = e[0] * py + e[1]
        left[e] = transposed_dot(spread, both[e]).astype(jnp.bfloat16)
        left_ref[at] = left[e]
        got = dot(clean, both[e]).astype(jnp.bfloat16)
        tidy[e] = got[:blk], got[blk:]
        zdn_ref[at], zup_ref[at] = tidy[e]
    mixed = {}
    for x, b in pairs:
        right = pair(*[
            a_ref[x, 2 * b + v, 6] * first + a_ref[x, 2 * b + v, 5] * second for v in range(2)
        ])
        lefts = jnp.concatenate([left_factors(left[x, b], v, masks) for v in range(2)], axis=0)
        got = dot(lefts, right)
        chosen = iota((2 * blk, LANES), 1) < LANES // 2
        mixed[x, b] = jnp.where(chosen, got[: 2 * blk], got[2 * blk :]).astype(jnp.bfloat16)
    for copy in copies:
        copy.wait()
    sent, _ = places(route_ref, where_ref, table_ref, dims, nb)
    for group in in_groups(pairs, 4):
        made = []
        for x, b in group:
            for z in range(nz):
                stack = jnp.concatenate(
                    [mixed[x, b][z * q : (z + 1) * q], mixed[x, b][(2 + z) * q : (3 + z) * q]], axis=0
                )
                other = tidy[x, b][1 - z]
                weight = jnp.concatenate([other * low, other * high], axis=0)
                made.append((x, b, z, unpair(dot(stack, weight))))
        for x, b, z, parts in made:
            flat = pair_ref[x // 2, b, z] == 0
            i = ((x // 2 * py + b) * nz + z) * 2
            for v in range(2):
                u = x % 2
                t = u if u == v else jnp.where(flat, v, u)
                m = u if u == v else jnp.where(flat, u, v)
                put(total_ref, where_ref, i + t, m, rows, parts[v])
    finish(((send_ref, nb),), total_ref, 0, dims, sent)


def inner_kernel(
    dims, grid, route_hbm, pair_hbm, left_ref, zup_ref, zdn_ref, a_ref,
    send_ref, total_ref, keep_codes_ref, ya_ref, yb_ref, za_ref, zb_ref,
    route_ref, pair_ref, part_ref, codes_ref, where_ref, table_ref, sems,
):
    px, py, nz = grid
    aggregates, _, rows = dims
    nx, ny = 2 * px, 2 * py
    blk = a_ref.shape[3]
    q = blk // 2
    nb = 3
    copies = [
        pltpu.make_async_copy(one, two, sems.at[k])
        for k, (one, two) in enumerate(((route_hbm, route_ref), (pair_hbm, pair_ref)))
    ]
    for copy in copies:
        copy.start()
    masks = even_lanes(q)
    pairs = [(x, b) for x in range(nx) for b in range(py)]
    down_of = lambda x, b: zdn_ref[x * py + b]
    up_of = lambda x, b: zup_ref[x * py + b]

    def both_z(x, b, half):
        part = slice(half * blk, (half + 1) * blk)
        return jnp.concatenate([down_of(x, b)[:, part], up_of(x, b)[:, part]], axis=0)

    y_even, z_even = lax.axis_index("gy") % 2 == 0, lax.axis_index("gz") % 2 == 0
    for a in range(px):
        down = jnp.concatenate([both_z(2 * a, 0, 0), both_z(2 * a + 1, 0, 0)], axis=1)
        up = jnp.concatenate([both_z(2 * a, py - 1, 1), both_z(2 * a + 1, py - 1, 1)], axis=1)
        ya_ref[a], yb_ref[a] = jnp.where(y_even, up, down), jnp.where(y_even, down, up)
    for x, b in pairs:
        down, up = down_of(x, b), up_of(x, b)
        za_ref[x * py + b] = jnp.where(z_even, up, down)
        zb_ref[x * py + b] = jnp.where(z_even, down, up)
    for x, y in [(x, y) for x in range(nx) for y in range(ny)]:
        here = a_ref.at[x, y]
        low, high = halves(here[4 - y % 2])
        right = jnp.concatenate(
            [pair(here[0], here[2 - x % 2]), jnp.concatenate([low, high], axis=0)], axis=1
        )
        left = left_factors(left_ref[x * py + y // 2], y % 2, masks)
        got = dot(left, right).astype(jnp.bfloat16)
        part_ref[x, y, 0], part_ref[x, y, 1] = unpair(got[:, : 2 * blk])
        along = got[:, 2 * blk :]
        part_ref[x, y, 2] = jnp.concatenate([along[:blk], along[blk:]], axis=1)

    for copy in copies:
        copy.wait()
    sent, _ = places(route_ref, where_ref, table_ref, dims, nb)
    codes_ref[...] = jnp.full_like(codes_ref, -1.0)
    for i in range(aggregates):
        a, b, z, t = i // (py * nz * 2), (i // (nz * 2)) % py, (i // 2) % nz, i % 2
        code = (2 * (jnp.where(pair_ref[a, b, z] == 0, 2, 1) - t) + z).astype(jnp.float32)
        line = jnp.full((1, LANES), code, jnp.float32)
        codes_ref[pl.ds(where_ref[2, i], 1), :] = line
        codes_ref[pl.ds(where_ref[3, i], 1), :] = line

    for a, b in [(a, b) for a in range(px) for b in range(py)]:
        own, with_x, with_y = {}, {}, {}
        for z, ref in enumerate((zdn_ref, zup_ref)):
            zs = pl.ds(z * q, q)
            for u in range(2):
                x = 2 * a + u
                weight = weights_of(ref[x * py + b])
                for v in range(2):
                    y = 2 * b + v
                    stack = jnp.concatenate(
                        [
                            part_ref[x, y, 0, zs],
                            part_ref[2 * a + 1 - u, y, 1, zs],
                            part_ref[x, 2 * b + 1 - v, 2, zs],
                        ],
                        axis=0,
                    )
                    got = dot(stack, weight[v])
                    own[u, v, z] = got[:q]
                    with_x[1 - u, v, z] = got[q : 2 * q]
                    with_y[u, 1 - v, z] = got[2 * q :]
        for z in range(nz):
            flat = pair_ref[a, b, z] == 0
            i = ((a * py + b) * nz + z) * 2
            sums = {}
            for u in range(2):
                for v in range(2):
                    t = u if u == v else jnp.where(flat, v, u)
                    m = u if u == v else jnp.where(flat, u, v)
                    e = (u, v, z)
                    sums[u, v] = own[e] + jnp.where(flat, with_x[e], with_y[e])
                    cross = jnp.where(flat, with_y[e], with_x[e])
                    put(total_ref, where_ref, i + t, 1 + m, rows, cross)
            put(total_ref, where_ref, i, 0, rows, sums[0, 0] + jnp.where(flat, sums[1, 0], sums[0, 1]))
            put(total_ref, where_ref, i + 1, 0, rows, sums[1, 1] + jnp.where(flat, sums[0, 1], sums[1, 0]))

    finish(((send_ref, nb),), total_ref, 0, dims, sent)
    send_ref[nb * rows :] = codes_ref[: 2 * SUB].astype(jnp.bfloat16)
    keep_codes_ref[...] = codes_ref[2 * SUB :].astype(jnp.bfloat16)


def outer_left_kernel(grid, left_ref, a_ref, face_ref, part_ref, xface_ref):
    px, py, _ = grid
    nx, ny = 2 * px, 2 * py
    blk = a_ref.shape[3]
    clean, _ = constants(blk)
    for b in range(py):
        both = pair(face_ref[2 * b], face_ref[2 * b + 1])
        xface_ref[b] = dot(clean, both).astype(jnp.bfloat16)
    masks = even_lanes(blk // 2)
    first, second = even_rows(blk)
    for x, y in [(x, y) for x in range(nx) for y in range(ny)]:
        here = a_ref.at[x, y]
        along_z = here[5] * first + here[6] * second
        low, high = halves(along_z)
        right = jnp.concatenate(
            [pair(here[1 + x % 2], here[3 + y % 2]), jnp.concatenate([low, high], axis=0)], axis=1
        )
        left = left_factors(left_ref[x * py + y // 2], y % 2, masks)
        got = dot(left, right).astype(jnp.bfloat16)
        part_ref[x, y, 0], part_ref[x, y, 1] = unpair(got[:, : 2 * blk])
        along = got[:, 2 * blk :]
        part_ref[x, y, 2] = jnp.concatenate([along[:blk], along[blk:]], axis=1)


def outer_kernel(
    dims, grid, route_ref, pair_ref, part_ref, zup_ref, zdn_ref,
    xface_ref, ya_ref, yb_ref, za_ref, zb_ref,
    send_xy_ref, send_z_ref, keep_xy_ref, keep_z_ref,
    total_ref, where_ref, table_ref,
):
    px, py, nz = grid
    _, _, rows = dims
    nx, ny = 2 * px, 2 * py
    blk = part_ref.shape[3]
    q = blk // 2
    nb = 6
    sent, kept = places(route_ref, where_ref, table_ref, dims, nb)
    me = lax.axis_index("gx")
    line = iota((blk, LANES), 0) * 0
    above = line + me > 0

    def from_sides(axis, first_ref, second_ref, at, high):
        index = lax.axis_index(axis)
        last = index == lax.axis_size(axis) - 1 if high else index == 0
        by_first = index % 2 == (0 if high else 1)
        kept = line + jnp.where(by_first | ~last, 1, 0) > 0
        value = jnp.where(by_first, first_ref[at], second_ref[at]).astype(jnp.float32)
        return jnp.where(kept, value, 0.0).astype(jnp.bfloat16)


    def beside_x(x, b, z, u):
        to = x - 1 if u == 0 else x + 1
        if 0 <= to < nx:
            return (zdn_ref, zup_ref)[z][to * py + b]
        part = xface_ref[b, z * blk : (z + 1) * blk].astype(jnp.float32)
        part = jnp.where(above, part, 0.0) if u == 0 else jnp.where(above, 0.0, part)
        return part.astype(jnp.bfloat16)

    def beside_y(x, y, z, v):
        to = y - 1 if v == 0 else y + 1
        if 0 <= to < ny:
            return (zdn_ref, zup_ref)[z][x * py + to // 2], to % 2
        at = (x // 2, slice(z * blk, (z + 1) * blk))
        return from_sides("gy", ya_ref, yb_ref, at, v == 1), x % 2

    for x in range(nx):
        made = []
        for b, z in [(b, z) for b in range(py) for z in range(nz)]:
            zs = pl.ds(z * q, q)
            u, a = x % 2, x // 2
            along_x = weights_of(beside_x(x, b, z, u))
            along_z = weights_of(from_sides("gz", za_ref, zb_ref, x * py + b, z == 1))
            flat = pair_ref[a, b, z] == 0
            for v in range(2):
                y = 2 * b + v
                t = u if u == v else jnp.where(flat, v, u)
                m = u if u == v else jnp.where(flat, u, v)
                i = ((a * py + b) * nz + z) * 2 + t
                other, k = beside_y(x, y, z, v)
                along_y = weights_of(other)[k]
                made.append((i, 2 * m, dot(part_ref[x, y, 0, zs], along_x[v])))
                made.append((i, 2 * m + 1, dot(part_ref[x, y, 1, zs], along_y)))
                made.append((i, 4 + m, dot(part_ref[x, y, 2, zs], along_z[v])))
        for i, block, got in made:
            put(total_ref, where_ref, i, block, rows, got)

    for kind, (xy, along, count) in enumerate((
        (send_xy_ref, send_z_ref, sent), (keep_xy_ref, keep_z_ref, kept),
    )):
        finish(((xy, 4), (along, 2)), total_ref, kind, dims, count)


def received(z_ref, rest_ref, rows):
    def early(k, at, size):
        ref, k = (rest_ref, k) if k < 3 else (z_ref, k - 3)
        return ref[k * rows + at : k * rows + at + size].reshape(-1, 2 * SUB, LANES)

    return early


def placed_blocks(early, xy_ref, z_ref, code, rows, at, size):
    near_low, near_high = (code < 1.5)[None], (code > 3.5)[None]
    upper = ((code == 1.0) | (code == 3.0) | (code == 5.0))[None]

    def tiles(ref, k):
        return ref[k * rows + at : k * rows + at + size].reshape(-1, 2 * SUB, LANES)

    if xy_ref is not None:
        yield 0, early(0, at, size)
        for m in range(2):
            cross, x_out, y_out = early(1 + m, at, size), tiles(xy_ref, 2 * m), tiles(xy_ref, 2 * m + 1)
            yield 1 + 5 * m, jnp.where(near_low, cross, x_out)
            yield 2 + 5 * m, jnp.where(near_low, x_out, jnp.where(near_high, y_out, cross))
            yield 3 + 5 * m, jnp.where(near_high, cross, y_out)
    if z_ref is not None:
        for m in range(2):
            z_in, z_out = early(3 + m, at, size), tiles(z_ref, m)
            yield 4 + 5 * m, jnp.where(upper, z_in, z_out)
            yield 5 + 5 * m, jnp.where(upper, z_out, z_in)


def twice(codes):
    return jnp.concatenate([codes, codes], axis=0)


def keep_kernel(dims, z_total_ref, total_ref, codes_ref, xy_ref, z_ref, half_ref, out_hbm, full_ref, sem):
    cap, rows = dims
    full = (cap - cap % SUB) * (rows // cap)
    me = lax.axis_index("gx")

    def rounded(code):
        filled = (code > -0.5)[None]

        def early(k, at, size):
            ref, k = (total_ref, 3 + k) if k < 3 else (z_total_ref, 2 + k - 3)
            value = ref[pl.ds(k * rows + at, size), :].astype(jnp.bfloat16)
            value = value.reshape(-1, 2 * SUB, LANES)
            return jnp.where(filled, value, jnp.zeros_like(value))

        return early

    copies = []
    code = twice(codes_ref[:SUB])
    for k, value in placed_blocks(rounded(code), xy_ref, z_ref, code, rows, 0, full):
        full_ref[k] = value.reshape(full, LANES)
        to = out_hbm.at[k, pl.ds(me * (2 * full), full), :]
        copies.append(pltpu.make_async_copy(full_ref.at[k], to, sem.at[k]))
        copies[-1].start()
    code = twice(codes_ref[SUB:])
    for k, value in placed_blocks(rounded(code), xy_ref, z_ref, code, rows, full, rows - full):
        half_ref[k] = value.reshape(rows - full, LANES)
    for copy in copies:
        copy.wait()


def take_kernel(dims, with_xy, early_z_ref, early_ref, late_ref, half_ref, _, out_hbm, full_ref, mixed_ref, sem):
    cap, rows = dims
    full = (cap - cap % SUB) * (rows // cap)
    me = lax.axis_index("gx")
    codes = early_ref[3 * rows :]
    xy_ref, z_ref = (late_ref, None) if with_xy else (None, late_ref)
    early = received(early_z_ref, early_ref, rows)
    copies = []
    for k, value in placed_blocks(early, xy_ref, z_ref, twice(codes[:SUB]), rows, 0, full):
        full_ref[k] = value.reshape(full, LANES)
        to = out_hbm.at[k, pl.ds((1 - me) * (2 * full), full), :]
        copies.append(pltpu.make_async_copy(full_ref.at[k], to, sem.at[0, k]))
        copies[-1].start()
    first_half = (iota((SUB, LANES), 0) < SUB // 2)[None]
    pick = first_half == (me == 0)
    for k, value in placed_blocks(early, xy_ref, z_ref, twice(codes[SUB:]), rows, full, rows - full):
        theirs = value.reshape(rows - full, LANES).astype(jnp.float32).reshape(-1, SUB, LANES)
        mine = half_ref[k].astype(jnp.float32).reshape(-1, SUB, LANES)
        low = jnp.where(pick, mine, theirs)
        high = pltpu.roll(jnp.where(pick, theirs, mine), SUB // 2, 1)
        mixed_ref[k, : rows - full] = low.reshape(rows - full, LANES).astype(jnp.bfloat16)
        mixed_ref[k, rows - full :] = high.reshape(rows - full, LANES).astype(jnp.bfloat16)
        to = out_hbm.at[k, full : 2 * full, :]
        copies.append(pltpu.make_async_copy(mixed_ref.at[k], to, sem.at[1, k]))
        copies[-1].start()
    for copy in copies:
        copy.wait()


SMEM = pl.BlockSpec(memory_space=pltpu.SMEM)
VMEM = pl.BlockSpec(memory_space=pltpu.VMEM)
ANY = pl.BlockSpec(memory_space=pl.ANY)


def bf16(*shape):
    return jax.ShapeDtypeStruct(shape, jnp.bfloat16)


def near(*shape):
    return pltpu.VMEM(shape, jnp.bfloat16)


def held(*arrays):
    return [pltpu.with_memory_space_constraint(one, pltpu.VMEM) for one in arrays]


def swaps(ny, nz):
    def first(i):
        return i + 1 if i % 2 == 0 else i - 1

    def second(i, n):
        j = i - 1 if i % 2 == 0 else i + 1
        return j if 0 <= j < n else None

    made = {"y_a": [], "y_b": [], "z_a": [], "z_b": []}
    for j in range(ny):
        for k in range(nz):
            to_y, to_z = second(j, ny), second(k, nz)
            made["y_a"].append((first(j), k))
            made["z_a"].append((j, first(k)))
            made["y_b"].append((j, first(k)) if to_y is None else (to_y, k))
            made["z_b"].append((first(j), k) if to_z is None else (j, to_z))
    return {name: [(i, j * nz + k) for i, (j, k) in enumerate(to)] for name, to in made.items()}


def local(a_blocks, prolong, pairing, route):
    devices_gx = lax.axis_size("gx")
    aggregates = route.shape[0]
    capacity = max(2, 3 * aggregates // (2 * devices_gx))
    nx, ny, nz, faces, entries = a_blocks.shape
    fits = (
        devices_gx == 2
        and lax.axis_size("gy") % 2 == 0
        and lax.axis_size("gz") % 2 == 0
        and nz == 2
        and nx % 2 == 0
        and ny % 2 == 0
        and faces == 7
        and entries == (LANES // 2) ** 2
        and capacity // SUB == 1
        and capacity % SUB == SUB // 2
    )
    if not fits:
        return general(a_blocks, prolong, pairing, route, capacity)
    px, py = nx // 2, ny // 2
    blk = math.isqrt(entries)
    lines = entries // LANES
    a_view = a_blocks.transpose(0, 1, 3, 2, 4).reshape(nx, ny, faces, nz, lines, LANES)
    a_view = a_view.transpose(0, 1, 2, 4, 3, 5).reshape(nx, ny, faces, nz * lines, LANES)
    p_view = prolong.reshape(nx, ny, nz, lines, LANES).transpose(0, 1, 3, 2, 4)
    p_view = p_view.reshape(nx, ny, nz * lines, LANES)
    route_row = route.reshape(1, aggregates)
    rows = capacity * lines
    dims, grid = (aggregates, capacity, rows), (px, py, nz)
    f32 = jnp.float32
    half_type = jnp.bfloat16
    face_x, face_y, face_z = (py, 2 * blk, LANES), (px, 2 * blk, LANES), (nx * py, blk, LANES)
    parts = (nx, ny, 3, blk, LANES)
    room = pltpu.CompilerParams(vmem_limit_bytes=24 * 2**20)
    cost = pl.CostEstimate(flops=10**9, bytes_accessed=4 * 10**6, transcendentals=0)

    swap = [(0, 1), (1, 0)]
    face = pl.pallas_call(
        face_kernel,
        out_shape=near(ny, blk, LANES),
        in_specs=[ANY],
        out_specs=VMEM,
        scratch_shapes=[pltpu.SemaphoreType.DMA((1,))],
        compiler_params=room,
        cost_estimate=cost,
        name="face",
    )(pltpu.with_memory_space_constraint(p_view, pltpu.HBM))
    face = lax.ppermute(face, "gx", swap)
    p_near, a_near = held(p_view, a_view)
    scalars = [pltpu.with_memory_space_constraint(one, pltpu.HBM) for one in (route_row, pairing)]
    tables = [
        pltpu.SMEM(route_row.shape, jnp.int32),
        pltpu.SMEM(pairing.shape, jnp.int32),
        pltpu.SMEM((4, aggregates), jnp.int32),
        pltpu.SMEM((4, capacity), jnp.int32),
        pltpu.SemaphoreType.DMA((2,)),
    ]
    send_z, total_z, zup, zdn, left = pl.pallas_call(
        functools.partial(first_kernel, dims, grid),
        out_shape=(
            near(2 * rows, LANES),
            pltpu.VMEM((4 * rows, LANES), f32),
            near(*face_z),
            near(*face_z),
            near(nx * py, 2 * blk, LANES),
        ),
        in_specs=[ANY, ANY, VMEM, VMEM],
        out_specs=[VMEM] * 5,
        scratch_shapes=tables,
        compiler_params=room,
        cost_estimate=cost,
        name="first_blocks",
    )(*scalars, p_near, a_near)
    got_z = lax.ppermute(send_z, "gx", swap)
    near_z, left = held(zup, zdn), held(left)[0]
    send_0, total, keep_codes, ya, yb, za, zb = pl.pallas_call(
        functools.partial(inner_kernel, dims, grid),
        out_shape=(
            near(3 * rows + 2 * SUB, LANES),
            pltpu.VMEM((6 * rows, LANES), f32),
            near(2 * SUB, LANES),
            near(*face_y),
            near(*face_y),
            near(*face_z),
            near(*face_z),
        ),
        in_specs=[ANY, ANY] + [VMEM] * 4,
        out_specs=[VMEM] * 7,
        scratch_shapes=tables[:2]
        + [pltpu.VMEM((nx, ny, 3, blk, LANES), half_type), pltpu.VMEM((4 * SUB, LANES), f32)]
        + tables[2:],
        compiler_params=room,
        cost_estimate=cost,
        name="inner_blocks",
    )(*scalars, left, *near_z, a_near)
    got_0 = lax.ppermute(send_0, "gx", swap)
    rounds = swaps(lax.axis_size("gy"), lax.axis_size("gz"))
    halos = []
    for name, value in (("y_a", ya), ("y_b", yb), ("z_a", za), ("z_b", zb)):
        halos.append(lax.ppermute(value, ("gy", "gz"), rounds[name]))

    part, xface = pl.pallas_call(
        functools.partial(outer_left_kernel, grid),
        out_shape=(near(*parts), near(*face_x)),
        in_specs=[VMEM] * 3,
        out_specs=[VMEM] * 2,
        compiler_params=room,
        cost_estimate=cost,
        name="outer_left",
    )(left, a_near, *held(face))
    send_xy, send_late, keep_xy, keep_z = pl.pallas_call(
        functools.partial(outer_kernel, dims, grid),
        out_shape=(near(4 * rows, LANES), near(2 * rows, LANES)) * 2,
        in_specs=[SMEM, SMEM] + [VMEM] * 8,
        out_specs=[VMEM] * 4,
        scratch_shapes=[
            pltpu.VMEM((12 * rows, LANES), f32),
            pltpu.SMEM((4, aggregates), jnp.int32),
            pltpu.SMEM((4, capacity), jnp.int32),
        ],
        compiler_params=room,
        cost_estimate=cost,
        name="outer_blocks",
    )(route_row, pairing, *held(part), *near_z, *held(xface, *halos))
    got_xy = lax.ppermute(send_xy, "gx", swap)
    got_late = lax.ppermute(send_late, "gx", swap)

    full = (capacity // SUB) * SUB * lines
    whole = 2 * rows
    half, out = pl.pallas_call(
        functools.partial(keep_kernel, (capacity, rows)),
        out_shape=(near(11, rows - full, LANES), bf16(11, whole, LANES)),
        in_specs=[VMEM] * 5,
        out_specs=[VMEM, ANY],
        scratch_shapes=[pltpu.VMEM((11, full, LANES), half_type), pltpu.SemaphoreType.DMA((11,))],
        compiler_params=room,
        cost_estimate=cost,
        name="place_kept",
    )(*held(total_z, total, keep_codes, keep_xy, keep_z))
    for with_xy, late in ((True, got_xy), (False, got_late)):
        out = pl.pallas_call(
            functools.partial(take_kernel, (capacity, rows), with_xy),
            out_shape=bf16(11, whole, LANES),
            in_specs=[VMEM] * 4 + [ANY],
            out_specs=ANY,
            input_output_aliases={4: 0},
            scratch_shapes=[
                pltpu.VMEM((11, full, LANES), half_type),
                pltpu.VMEM((11, full, LANES), half_type),
                pltpu.SemaphoreType.DMA((2, 11)),
            ],
            compiler_params=room,
            cost_estimate=cost,
            name="place_xy" if with_xy else "place_z",
        )(*held(got_z, got_0, late, half), out)
    out = out.reshape(11, whole // (SUB * lines), lines, SUB, LANES).transpose(1, 3, 0, 2, 4)
    return out.reshape(2 * capacity, 11, entries)


def solution(mesh):
    placed = (
        P("gx", "gy", "gz", None, None),
        P("gx", "gy", "gz", None),
        P("gx", "gy", "gz"),
        P(("gx", "gy", "gz"), None),
    )
    return jax.shard_map(
        local,
        mesh=mesh,
        in_specs=placed,
        out_specs=P(("gx", "gy", "gz"), None, None),
        check_vma=False,
    )
```

```python
import functools
import math

import jax
import jax.numpy as jnp
from jax import lax
from jax.experimental import pallas as pl
from jax.experimental.pallas import tpu as pltpu
from jax.sharding import PartitionSpec as P


x_first_order = [0, 2, 1, 3, 4, 5, 6]
x_second_order = [0, 1, 2, 3, 4, 5, 6]
y_first_order = [0, 4, 1, 2, 3, 5, 6]
y_second_order = [0, 3, 1, 2, 4, 5, 6]

LANES = 128
SUB = 8


def padded_2(array, sides, width):
    for axis, dim in sides:
        devices, length = (lax.axis_size(axis), array.shape[dim])
        up = [(i, (i + 1) % devices) for i in range(devices - 1)]
        down = [(j, i) for i, j in up]
        last = lax.slice_in_dim(array, length - width, length, axis=dim)
        initial = lax.slice_in_dim(array, 0, width, axis=dim)
        before = lax.ppermute(last, axis, up)
        after = lax.ppermute(initial, axis, down)
        array = jnp.concatenate([before, array, after], axis=dim)
    return array


def neighbours(padded):
    shifted = [
        padded[1:-1, 1:-1, 1:-1],
        padded[:-2, 1:-1, 1:-1],
        padded[2:, 1:-1, 1:-1],
        padded[1:-1, :-2, 1:-1],
        padded[1:-1, 2:, 1:-1],
        padded[1:-1, 1:-1, :-2],
        padded[1:-1, 1:-1, 2:],
    ]
    return jnp.stack(shifted, axis=3)


def triple(blocks, nearby):
    block_side = math.isqrt(blocks.shape[-1])
    leading = blocks.shape[:-1]
    left_mat = blocks.reshape(leading + (block_side, block_side))
    right_mat = nearby.reshape(leading + (block_side, block_side))
    own_block = jnp.swapaxes(right_mat[..., :1, :, :], -1, -2)
    product = jnp.matmul(left_mat, right_mat, preferred_element_type=jnp.float32).astype(
        jnp.bfloat16
    )
    result = jnp.matmul(own_block, product, preferred_element_type=jnp.float32)
    return result.reshape(leading + (block_side * block_side,))


def members(element_grid, pairs):
    size_x, size_y, size_z = element_grid.shape[:3]
    trailing = element_grid.shape[3:]
    patches = element_grid.reshape((size_x // 2, 2, size_y // 2, 2, size_z) + trailing)

    def pick(upper, lower, slot_order):
        return jnp.take(patches[:, upper, :, lower], jnp.array(slot_order, dtype=jnp.int32), axis=3)

    x_one = jnp.stack([pick(0, 0, x_first_order), pick(0, 1, x_first_order)], axis=3)
    x_two = jnp.stack([pick(1, 0, x_second_order), pick(1, 1, x_second_order)], axis=3)
    y_one = jnp.stack([pick(0, 0, y_first_order), pick(1, 0, y_first_order)], axis=3)
    y_two = jnp.stack([pick(0, 1, y_second_order), pick(1, 1, y_second_order)], axis=3)
    along_x = (pairs == 0).reshape(pairs.shape + (1,) * (x_one.ndim - 3))
    member_one = jnp.where(along_x, x_one, y_one)
    member_two = jnp.where(along_x, x_two, y_two)
    return (
        member_one.reshape((-1,) + member_one.shape[4:]),
        member_two.reshape((-1,) + member_two.shape[4:]),
    )


def arrange(member_one, member_two):
    diagonal = (
        member_one[..., 0, :]
        + member_two[..., 0, :]
        + member_one[..., 1, :]
        + member_two[..., 1, :]
    )
    return jnp.concatenate(
        [diagonal[..., None, :], member_one[..., 2:, :], member_two[..., 2:, :]], axis=-2
    )


def slot_sources(routes, n_dest, capacity):
    total = routes.shape[0]
    chosen = (routes[:, None] == jnp.arange(n_dest, dtype=jnp.int32)[None, :]).astype(jnp.int32)
    before = jnp.cumsum(chosen, axis=0) - chosen
    ranking = jnp.sum(before * chosen, axis=1)
    position = routes * capacity + ranking
    targets = jnp.arange(n_dest * capacity, dtype=jnp.int32)
    matches = position[None, :] == targets[:, None]
    anchor = jnp.sum(jnp.where(matches, jnp.arange(total, dtype=jnp.int32)[None, :], 0), axis=1)
    filled = jnp.any(matches, axis=1)
    return (anchor, filled)


def pack_slots(payload, anchor, filled):
    taken = jnp.take(payload, anchor, axis=0)
    keep_row = filled.reshape(filled.shape + (1,) * (payload.ndim - 1))
    return jnp.where(keep_row, taken, jnp.zeros_like(taken))


def general(a_blocks, prolong, pairing, route, capacity):
    padded = padded_2(prolong, (("gx", 0), ("gy", 1), ("gz", 2)), 1)
    nearby = neighbours(padded)
    anchor, filled = slot_sources(route[:, 0], lax.axis_size("gx"), capacity)
    galerkin = triple(a_blocks, nearby)
    member_one, member_two = members(galerkin, pairing)
    coarse = arrange(member_one, member_two).astype(jnp.bfloat16)
    return lax.all_to_all(
        pack_slots(coarse, anchor, filled), "gx", split_axis=0, concat_axis=0, tiled=True
    )


def dot(left, right):
    return jnp.dot(left, right, preferred_element_type=jnp.float32)


def iota(shape, axis):
    return lax.broadcasted_iota(jnp.int32, shape, axis)


def as_bf16(mask):
    return mask.astype(jnp.float32).astype(jnp.bfloat16)


def pair(one, two):
    h = one.shape[1] // 2
    low = jnp.concatenate([one[:, :h], two[:, :h]], axis=1)
    high = jnp.concatenate([one[:, h:], two[:, h:]], axis=1)
    return jnp.concatenate([low, high], axis=0)


def unpair(both):
    rows, h = both.shape[0] // 2, both.shape[1] // 2
    even, odd = both[:rows], both[rows:]
    return (
        jnp.concatenate([even[:, :h], odd[:, :h]], axis=1),
        jnp.concatenate([even[:, h:], odd[:, h:]], axis=1),
    )


def constants(blk):
    n = 2 * blk
    row, col = iota((n, n), 0), iota((n, n), 1)
    c, z = row % blk, row // blk
    clean = as_bf16(col == (c % 2) * blk + (c // 2) * 2 + z)
    q = blk // 2
    k, p = row // blk, (row // q) % 2
    spread = as_bf16(col == k * blk + 2 * (row % q) + p)
    return clean, spread


def even_lanes(rows):
    return as_bf16(iota((rows, LANES), 1) % 2 == 0), as_bf16(iota((rows, LANES), 1) % 2 == 1)


def even_rows(rows):
    return as_bf16(iota((rows, LANES), 0) % 2 == 0), as_bf16(iota((rows, LANES), 0) % 2 == 1)


def transposed_dot(left, right):
    return lax.dot_general(
        left, right, (((1,), (1,)), ((), ())), preferred_element_type=jnp.float32
    )


def left_factors(both_t, k, masks):
    q = masks[0].shape[0]
    parts = [both_t[(2 * k + p) * q : (2 * k + p + 1) * q] for p in range(2)]
    return jnp.concatenate([part * mask for part in parts for mask in masks], axis=0)


def weights_of(part):
    h = part.shape[1] // 2
    none = jnp.zeros((part.shape[0], h), part.dtype)
    made = []
    for k in range(2):
        one = part[:, k * h : (k + 1) * h]
        made.append(
            jnp.concatenate(
                [jnp.concatenate([one, none], axis=1), jnp.concatenate([none, one], axis=1)], axis=0
            )
        )
    return made


def halves(part):
    h = part.shape[1] // 2
    return part[:, :h], part[:, h:]


def places(route_ref, where_ref, table_ref, dims, blocks):
    aggregates, cap, rows = dims
    me = lax.axis_index("gx")
    lines = rows // cap
    rest = cap % SUB
    half = (cap - rest) * lines
    at_zero = me == 0
    for c in range(cap):
        if c < cap - rest:
            zero = (c, c + half // 2, c, c)
        else:
            h = c - (cap - rest)
            zero = (half + h, half + h + rest, SUB + h, SUB + h + rest)
        if c < rest:
            one = (half + c + rest, half + c, SUB + c, SUB + c + rest)
        else:
            h = c - rest
            one = (h, h + half // 2, h, h)
        for k in range(4):
            table_ref[k, c] = jnp.where(at_zero, zero[k], one[k])
    sent, kept = jnp.int32(0), jnp.int32(0)
    for i in range(aggregates):
        away = route_ref[0, i] != me
        one = away.astype(jnp.int32)
        c = jnp.where(away, sent, kept)
        sent = sent + one
        kept = kept + (1 - one)
        base = jnp.where(away, 0, blocks * rows)
        where_ref[0, i] = base + table_ref[0, c]
        where_ref[1, i] = base + table_ref[1, c]
        where_ref[2, i] = jnp.where(away, 0, 2 * SUB) + table_ref[2, c]
        where_ref[3, i] = jnp.where(away, 0, 2 * SUB) + table_ref[3, c]
    return sent, kept


def put(total_ref, where_ref, i, block, rows, value):
    n = value.shape[0] // 2
    one = where_ref[0, i] + block * rows
    two = where_ref[1, i] + block * rows
    total_ref[pl.ds(one, n, stride=SUB), :] = value[:n]
    total_ref[pl.ds(two, n, stride=SUB), :] = value[n:]


def finish(outs, total_ref, kind, dims, count):
    _, cap, rows = dims
    rest = cap % SUB
    full = (cap - rest) * (rows // cap)
    me = lax.axis_index("gx")
    line = iota((2 * SUB, LANES), 0)
    in_full = as_bf16(line % SUB + jnp.where(me == 0, 0, rest) < count) > 0.5
    in_half = as_bf16(line % rest + jnp.where(me == 0, cap - rest, 0) < count) > 0.5
    blocks = sum(n for _, n in outs)
    done = 0
    for out, n in outs:
        for k in range(n):
            for at, size, filled in ((0, full, in_full), (full, rows - full, in_half)):
                value = total_ref[pl.ds((kind * blocks + done + k) * rows + at, size), :]
                value = value.astype(jnp.bfloat16).reshape(-1, 2 * SUB, LANES)
                value = jnp.where(filled[None], value, jnp.zeros_like(value))
                out[k * rows + at : k * rows + at + size] = value.reshape(size, LANES)
        done += n


def face_kernel(p_hbm, face_ref, sem):
    last = p_hbm.shape[0] - 1
    at = jnp.where(lax.axis_index("gx") == 0, last, 0)
    copy = pltpu.make_async_copy(p_hbm.at[at], face_ref, sem.at[0])
    copy.start()
    copy.wait()


def inner_kernel(
    dims, grid, route_hbm, pair_hbm, p_ref, a_ref,
    send_ref, total_ref, keep_codes_ref, zup_ref, zdn_ref, left_ref,
    route_ref, pair_ref, part_ref, codes_ref, where_ref, table_ref, sems,
):
    px, py, nz = grid
    aggregates, _, rows = dims
    nx, ny = 2 * px, 2 * py
    blk = p_ref.shape[2]
    q = blk // 2
    nb = 5
    copies = [
        pltpu.make_async_copy(one, two, sems.at[k])
        for k, (one, two) in enumerate(((route_hbm, route_ref), (pair_hbm, pair_ref)))
    ]
    for copy in copies:
        copy.start()
    for copy in copies:
        copy.wait()
    sent, _ = places(route_ref, where_ref, table_ref, dims, nb)
    codes_ref[...] = jnp.full_like(codes_ref, -1.0)
    for i in range(aggregates):
        a, b, z, t = i // (py * nz * 2), (i // (nz * 2)) % py, (i // 2) % nz, i % 2
        code = (2 * (jnp.where(pair_ref[a, b, z] == 0, 2, 1) - t) + z).astype(jnp.float32)
        line = jnp.full((1, LANES), code, jnp.float32)
        codes_ref[pl.ds(where_ref[2, i], 1), :] = line
        codes_ref[pl.ds(where_ref[3, i], 1), :] = line
    clean, spread = constants(blk)
    masks = even_lanes(q)
    first, second = even_rows(blk)

    pairs = [(x, b) for x in range(nx) for b in range(py)]
    both = {e: pair(p_ref[e[0], 2 * e[1]], p_ref[e[0], 2 * e[1] + 1]) for e in pairs}
    tidy = {e: dot(clean, both[e]).astype(jnp.bfloat16) for e in pairs}
    for x, b in pairs:
        left_ref[x * py + b] = transposed_dot(spread, both[x, b]).astype(jnp.bfloat16)
        zdn_ref[x * py + b] = tidy[x, b][:blk]
        zup_ref[x * py + b] = tidy[x, b][blk:]

    for x, y in [(x, y) for x in range(nx) for y in range(ny)]:
        here = a_ref.at[x, y]
        along_z = here[6] * first + here[5] * second
        right = jnp.concatenate(
            [pair(here[0], here[2 - x % 2]), pair(here[4 - y % 2], along_z)], axis=1
        )
        left = left_factors(left_ref[x * py + y // 2], y % 2, masks)
        got = dot(left, right).astype(jnp.bfloat16)
        parts = unpair(got[:, : 2 * blk]) + unpair(got[:, 2 * blk :])
        for k in range(4):
            part_ref[x, y, k] = parts[k]

    for a, b in [(a, b) for a in range(px) for b in range(py)]:
        own, with_x, with_y, with_z = {}, {}, {}, {}
        for z, ref in enumerate((zdn_ref, zup_ref)):
            zs, zo = pl.ds(z * q, q), pl.ds((1 - z) * q, q)
            for u in range(2):
                x = 2 * a + u
                weight = weights_of(ref[x * py + b])
                for v in range(2):
                    y = 2 * b + v
                    stack = jnp.concatenate(
                        [
                            part_ref[x, y, 0, zs],
                            part_ref[2 * a + 1 - u, y, 1, zs],
                            part_ref[x, 2 * b + 1 - v, 2, zs],
                            part_ref[x, y, 3, zo],
                        ],
                        axis=0,
                    )
                    got = dot(stack, weight[v])
                    own[u, v, z] = got[:q]
                    with_x[1 - u, v, z] = got[q : 2 * q]
                    with_y[u, 1 - v, z] = got[2 * q : 3 * q]
                    with_z[u, v, 1 - z] = got[3 * q :]
        for z in range(nz):
            flat = pair_ref[a, b, z] == 0
            i = ((a * py + b) * nz + z) * 2
            sums = {}
            for u in range(2):
                for v in range(2):
                    t = u if u == v else jnp.where(flat, v, u)
                    m = u if u == v else jnp.where(flat, u, v)
                    e = (u, v, z)
                    sums[u, v] = own[e] + jnp.where(flat, with_x[e], with_y[e])
                    cross = jnp.where(flat, with_y[e], with_x[e])
                    put(total_ref, where_ref, i + t, 1 + m, rows, cross)
                    put(total_ref, where_ref, i + t, 3 + m, rows, with_z[e])
            put(total_ref, where_ref, i, 0, rows, sums[0, 0] + jnp.where(flat, sums[1, 0], sums[0, 1]))
            put(total_ref, where_ref, i + 1, 0, rows, sums[1, 1] + jnp.where(flat, sums[0, 1], sums[1, 0]))

    finish(((send_ref, nb),), total_ref, 0, dims, sent)
    send_ref[nb * rows :] = codes_ref[: 2 * SUB].astype(jnp.bfloat16)
    keep_codes_ref[...] = codes_ref[2 * SUB :].astype(jnp.bfloat16)


def faces_kernel(grid, zup_ref, zdn_ref, ya_ref, yb_ref, za_ref, zb_ref):
    px, py, _ = grid
    blk = zup_ref.shape[1]
    y_even, z_even = lax.axis_index("gy") % 2 == 0, lax.axis_index("gz") % 2 == 0

    def plane(a, b, half):
        part = slice(half * blk, (half + 1) * blk)
        rows = [jnp.concatenate([zdn_ref[x * py + b], zup_ref[x * py + b]], axis=0) for x in (2 * a, 2 * a + 1)]
        return jnp.concatenate([row[:, part] for row in rows], axis=1)

    for a in range(px):
        down, up = plane(a, 0, 0), plane(a, py - 1, 1)
        ya_ref[a], yb_ref[a] = jnp.where(y_even, up, down), jnp.where(y_even, down, up)
    for at in range(2 * px * py):
        down, up = zdn_ref[at], zup_ref[at]
        za_ref[at] = jnp.where(z_even, up, down)
        zb_ref[at] = jnp.where(z_even, down, up)


def outer_left_kernel(grid, left_ref, a_ref, face_ref, part_ref, xface_ref):
    px, py, _ = grid
    nx, ny = 2 * px, 2 * py
    blk = a_ref.shape[3]
    clean, _ = constants(blk)
    for b in range(py):
        both = pair(face_ref[2 * b], face_ref[2 * b + 1])
        xface_ref[b] = dot(clean, both).astype(jnp.bfloat16)
    masks = even_lanes(blk // 2)
    first, second = even_rows(blk)
    for x, y in [(x, y) for x in range(nx) for y in range(ny)]:
        here = a_ref.at[x, y]
        along_z = here[5] * first + here[6] * second
        low, high = halves(along_z)
        right = jnp.concatenate(
            [pair(here[1 + x % 2], here[3 + y % 2]), jnp.concatenate([low, high], axis=0)], axis=1
        )
        left = left_factors(left_ref[x * py + y // 2], y % 2, masks)
        got = dot(left, right).astype(jnp.bfloat16)
        part_ref[x, y, 0], part_ref[x, y, 1] = unpair(got[:, : 2 * blk])
        along = got[:, 2 * blk :]
        part_ref[x, y, 2] = jnp.concatenate([along[:blk], along[blk:]], axis=1)


def outer_kernel(
    dims, grid, route_ref, pair_ref, part_ref, zup_ref, zdn_ref,
    xface_ref, ya_ref, yb_ref, za_ref, zb_ref,
    send_xy_ref, send_z_ref, keep_xy_ref, keep_z_ref,
    total_ref, where_ref, table_ref,
):
    px, py, nz = grid
    _, _, rows = dims
    nx, ny = 2 * px, 2 * py
    blk = part_ref.shape[3]
    q = blk // 2
    nb = 6
    sent, kept = places(route_ref, where_ref, table_ref, dims, nb)
    me = lax.axis_index("gx")
    line = iota((blk, LANES), 0) * 0
    above = line + me > 0

    def from_sides(axis, first_ref, second_ref, at, high):
        index = lax.axis_index(axis)
        last = index == lax.axis_size(axis) - 1 if high else index == 0
        by_first = index % 2 == (0 if high else 1)
        kept = line + jnp.where(by_first | ~last, 1, 0) > 0
        value = jnp.where(by_first, first_ref[at], second_ref[at]).astype(jnp.float32)
        return jnp.where(kept, value, 0.0).astype(jnp.bfloat16)


    def beside_x(x, b, z, u):
        to = x - 1 if u == 0 else x + 1
        if 0 <= to < nx:
            return (zdn_ref, zup_ref)[z][to * py + b]
        part = xface_ref[b, z * blk : (z + 1) * blk].astype(jnp.float32)
        part = jnp.where(above, part, 0.0) if u == 0 else jnp.where(above, 0.0, part)
        return part.astype(jnp.bfloat16)

    def beside_y(x, y, z, v):
        to = y - 1 if v == 0 else y + 1
        if 0 <= to < ny:
            return (zdn_ref, zup_ref)[z][x * py + to // 2], to % 2
        at = (x // 2, slice(z * blk, (z + 1) * blk))
        return from_sides("gy", ya_ref, yb_ref, at, v == 1), x % 2

    for x in range(nx):
        made = []
        for b, z in [(b, z) for b in range(py) for z in range(nz)]:
            zs = pl.ds(z * q, q)
            u, a = x % 2, x // 2
            along_x = weights_of(beside_x(x, b, z, u))
            along_z = weights_of(from_sides("gz", za_ref, zb_ref, x * py + b, z == 1))
            flat = pair_ref[a, b, z] == 0
            for v in range(2):
                y = 2 * b + v
                t = u if u == v else jnp.where(flat, v, u)
                m = u if u == v else jnp.where(flat, u, v)
                i = ((a * py + b) * nz + z) * 2 + t
                other, k = beside_y(x, y, z, v)
                along_y = weights_of(other)[k]
                made.append((i, 2 * m, dot(part_ref[x, y, 0, zs], along_x[v])))
                made.append((i, 2 * m + 1, dot(part_ref[x, y, 1, zs], along_y)))
                made.append((i, 4 + m, dot(part_ref[x, y, 2, zs], along_z[v])))
        for i, block, got in made:
            put(total_ref, where_ref, i, block, rows, got)

    for kind, (xy, along, count) in enumerate((
        (send_xy_ref, send_z_ref, sent), (keep_xy_ref, keep_z_ref, kept),
    )):
        finish(((xy, 4), (along, 2)), total_ref, kind, dims, count)


def received(early_ref, rows):
    def early(k, at, size):
        return early_ref[k * rows + at : k * rows + at + size].reshape(-1, 2 * SUB, LANES)

    return early


def placed_blocks(early, xy_ref, z_ref, code, rows, at, size):
    near_low, near_high = (code < 1.5)[None], (code > 3.5)[None]
    upper = ((code == 1.0) | (code == 3.0) | (code == 5.0))[None]

    def tiles(ref, k):
        return ref[k * rows + at : k * rows + at + size].reshape(-1, 2 * SUB, LANES)

    if xy_ref is not None:
        yield 0, early(0, at, size)
        for m in range(2):
            cross, x_out, y_out = early(1 + m, at, size), tiles(xy_ref, 2 * m), tiles(xy_ref, 2 * m + 1)
            yield 1 + 5 * m, jnp.where(near_low, cross, x_out)
            yield 2 + 5 * m, jnp.where(near_low, x_out, jnp.where(near_high, y_out, cross))
            yield 3 + 5 * m, jnp.where(near_high, cross, y_out)
    if z_ref is not None:
        for m in range(2):
            z_in, z_out = early(3 + m, at, size), tiles(z_ref, m)
            yield 4 + 5 * m, jnp.where(upper, z_in, z_out)
            yield 5 + 5 * m, jnp.where(upper, z_out, z_in)


def twice(codes):
    return jnp.concatenate([codes, codes], axis=0)


def keep_kernel(dims, total_ref, codes_ref, xy_ref, z_ref, half_ref, out_hbm, full_ref, sem):
    cap, rows = dims
    full = (cap - cap % SUB) * (rows // cap)
    me = lax.axis_index("gx")

    def rounded(code):
        filled = (code > -0.5)[None]

        def early(k, at, size):
            value = total_ref[pl.ds((5 + k) * rows + at, size), :].astype(jnp.bfloat16)
            value = value.reshape(-1, 2 * SUB, LANES)
            return jnp.where(filled, value, jnp.zeros_like(value))

        return early

    copies = []
    code = twice(codes_ref[:SUB])
    for k, value in placed_blocks(rounded(code), xy_ref, z_ref, code, rows, 0, full):
        full_ref[k] = value.reshape(full, LANES)
        to = out_hbm.at[k, pl.ds(me * (2 * full), full), :]
        copies.append(pltpu.make_async_copy(full_ref.at[k], to, sem.at[k]))
        copies[-1].start()
    code = twice(codes_ref[SUB:])
    for k, value in placed_blocks(rounded(code), xy_ref, z_ref, code, rows, full, rows - full):
        half_ref[k] = value.reshape(rows - full, LANES)
    for copy in copies:
        copy.wait()


def take_kernel(dims, with_xy, early_ref, late_ref, half_ref, _, out_hbm, full_ref, mixed_ref, sem):
    cap, rows = dims
    full = (cap - cap % SUB) * (rows // cap)
    me = lax.axis_index("gx")
    codes = early_ref[5 * rows :]
    xy_ref, z_ref = (late_ref, None) if with_xy else (None, late_ref)
    early = received(early_ref, rows)
    copies = []
    for k, value in placed_blocks(early, xy_ref, z_ref, twice(codes[:SUB]), rows, 0, full):
        full_ref[k] = value.reshape(full, LANES)
        to = out_hbm.at[k, pl.ds((1 - me) * (2 * full), full), :]
        copies.append(pltpu.make_async_copy(full_ref.at[k], to, sem.at[0, k]))
        copies[-1].start()
    first_half = (iota((SUB, LANES), 0) < SUB // 2)[None]
    pick = first_half == (me == 0)
    for k, value in placed_blocks(early, xy_ref, z_ref, twice(codes[SUB:]), rows, full, rows - full):
        theirs = value.reshape(rows - full, LANES).astype(jnp.float32).reshape(-1, SUB, LANES)
        mine = half_ref[k].astype(jnp.float32).reshape(-1, SUB, LANES)
        low = jnp.where(pick, mine, theirs)
        high = pltpu.roll(jnp.where(pick, theirs, mine), SUB // 2, 1)
        mixed_ref[k, : rows - full] = low.reshape(rows - full, LANES).astype(jnp.bfloat16)
        mixed_ref[k, rows - full :] = high.reshape(rows - full, LANES).astype(jnp.bfloat16)
        to = out_hbm.at[k, full : 2 * full, :]
        copies.append(pltpu.make_async_copy(mixed_ref.at[k], to, sem.at[1, k]))
        copies[-1].start()
    for copy in copies:
        copy.wait()


SMEM = pl.BlockSpec(memory_space=pltpu.SMEM)
VMEM = pl.BlockSpec(memory_space=pltpu.VMEM)
ANY = pl.BlockSpec(memory_space=pl.ANY)


def bf16(*shape):
    return jax.ShapeDtypeStruct(shape, jnp.bfloat16)


def near(*shape):
    return pltpu.VMEM(shape, jnp.bfloat16)


def held(*arrays):
    return [pltpu.with_memory_space_constraint(one, pltpu.VMEM) for one in arrays]


def swaps(ny, nz):
    def first(i):
        return i + 1 if i % 2 == 0 else i - 1

    def second(i, n):
        j = i - 1 if i % 2 == 0 else i + 1
        return j if 0 <= j < n else None

    made = {"y_a": [], "y_b": [], "z_a": [], "z_b": []}
    for j in range(ny):
        for k in range(nz):
            to_y, to_z = second(j, ny), second(k, nz)
            made["y_a"].append((first(j), k))
            made["z_a"].append((j, first(k)))
            made["y_b"].append((j, first(k)) if to_y is None else (to_y, k))
            made["z_b"].append((first(j), k) if to_z is None else (j, to_z))
    return {name: [(i, j * nz + k) for i, (j, k) in enumerate(to)] for name, to in made.items()}


def local(a_blocks, prolong, pairing, route):
    devices_gx = lax.axis_size("gx")
    aggregates = route.shape[0]
    capacity = max(2, 3 * aggregates // (2 * devices_gx))
    nx, ny, nz, faces, entries = a_blocks.shape
    fits = (
        devices_gx == 2
        and lax.axis_size("gy") % 2 == 0
        and lax.axis_size("gz") % 2 == 0
        and nz == 2
        and nx % 2 == 0
        and ny % 2 == 0
        and faces == 7
        and entries == (LANES // 2) ** 2
        and capacity // SUB == 1
        and capacity % SUB == SUB // 2
    )
    if not fits:
        return general(a_blocks, prolong, pairing, route, capacity)
    px, py = nx // 2, ny // 2
    blk = math.isqrt(entries)
    lines = entries // LANES
    a_view = a_blocks.transpose(0, 1, 3, 2, 4).reshape(nx, ny, faces, nz, lines, LANES)
    a_view = a_view.transpose(0, 1, 2, 4, 3, 5).reshape(nx, ny, faces, nz * lines, LANES)
    p_view = prolong.reshape(nx, ny, nz, lines, LANES).transpose(0, 1, 3, 2, 4)
    p_view = p_view.reshape(nx, ny, nz * lines, LANES)
    route_row = route.reshape(1, aggregates)
    rows = capacity * lines
    dims, grid = (aggregates, capacity, rows), (px, py, nz)
    f32 = jnp.float32
    half_type = jnp.bfloat16
    face_x, face_y, face_z = (py, 2 * blk, LANES), (px, 2 * blk, LANES), (nx * py, blk, LANES)
    parts = (nx, ny, 3, blk, LANES)
    room = pltpu.CompilerParams(vmem_limit_bytes=24 * 2**20)
    cost = pl.CostEstimate(flops=10**9, bytes_accessed=4 * 10**6, transcendentals=0)

    swap = [(0, 1), (1, 0)]
    face = pl.pallas_call(
        face_kernel,
        out_shape=near(ny, blk, LANES),
        in_specs=[ANY],
        out_specs=VMEM,
        scratch_shapes=[pltpu.SemaphoreType.DMA((1,))],
        compiler_params=room,
        cost_estimate=cost,
        name="face",
    )(pltpu.with_memory_space_constraint(p_view, pltpu.HBM))
    face = lax.ppermute(face, "gx", swap)
    p_near, a_near = held(p_view, a_view)
    send_0, total, keep_codes, zup, zdn, left = pl.pallas_call(
        functools.partial(inner_kernel, dims, grid),
        out_shape=(
            near(5 * rows + 2 * SUB, LANES),
            pltpu.VMEM((10 * rows, LANES), f32),
            near(2 * SUB, LANES),
            near(*face_z),
            near(*face_z),
            near(nx * py, 2 * blk, LANES),
        ),
        in_specs=[ANY, ANY, VMEM, VMEM],
        out_specs=[VMEM] * 6,
        scratch_shapes=[
            pltpu.SMEM(route_row.shape, jnp.int32),
            pltpu.SMEM(pairing.shape, jnp.int32),
            pltpu.VMEM((nx, ny, 4, blk, LANES), half_type),
            pltpu.VMEM((4 * SUB, LANES), f32),
            pltpu.SMEM((4, aggregates), jnp.int32),
            pltpu.SMEM((4, capacity), jnp.int32),
            pltpu.SemaphoreType.DMA((2,)),
        ],
        compiler_params=room,
        cost_estimate=cost,
        name="inner_blocks",
    )(route_row, pairing, p_near, a_near)
    got_0 = lax.ppermute(send_0, "gx", swap)
    zup, zdn = held(zup, zdn)
    ya, yb, za, zb = pl.pallas_call(
        functools.partial(faces_kernel, grid),
        out_shape=(near(*face_y), near(*face_y), near(*face_z), near(*face_z)),
        in_specs=[VMEM] * 2,
        out_specs=[VMEM] * 4,
        compiler_params=room,
        cost_estimate=cost,
        name="faces",
    )(zup, zdn)
    rounds = swaps(lax.axis_size("gy"), lax.axis_size("gz"))
    halos = []
    for name, value in (("y_a", ya), ("y_b", yb), ("z_a", za), ("z_b", zb)):
        halos.append(lax.ppermute(value, ("gy", "gz"), rounds[name]))

    part, xface = pl.pallas_call(
        functools.partial(outer_left_kernel, grid),
        out_shape=(near(*parts), near(*face_x)),
        in_specs=[VMEM] * 3,
        out_specs=[VMEM] * 2,
        compiler_params=room,
        cost_estimate=cost,
        name="outer_left",
    )(*held(left), a_near, *held(face))
    send_xy, send_z, keep_xy, keep_z = pl.pallas_call(
        functools.partial(outer_kernel, dims, grid),
        out_shape=(near(4 * rows, LANES), near(2 * rows, LANES)) * 2,
        in_specs=[SMEM, SMEM] + [VMEM] * 8,
        out_specs=[VMEM] * 4,
        scratch_shapes=[
            pltpu.VMEM((12 * rows, LANES), f32),
            pltpu.SMEM((4, aggregates), jnp.int32),
            pltpu.SMEM((4, capacity), jnp.int32),
        ],
        compiler_params=room,
        cost_estimate=cost,
        name="outer_blocks",
    )(route_row, pairing, *held(part), zup, zdn, *held(xface, *halos))
    got_xy = lax.ppermute(send_xy, "gx", swap)
    got_z = lax.ppermute(send_z, "gx", swap)

    full = (capacity // SUB) * SUB * lines
    whole = 2 * rows
    half, out = pl.pallas_call(
        functools.partial(keep_kernel, (capacity, rows)),
        out_shape=(near(11, rows - full, LANES), bf16(11, whole, LANES)),
        in_specs=[VMEM] * 4,
        out_specs=[VMEM, ANY],
        scratch_shapes=[pltpu.VMEM((11, full, LANES), half_type), pltpu.SemaphoreType.DMA((11,))],
        compiler_params=room,
        cost_estimate=cost,
        name="place_kept",
    )(*held(total, keep_codes, keep_xy, keep_z))
    for with_xy, late in ((True, got_xy), (False, got_z)):
        out = pl.pallas_call(
            functools.partial(take_kernel, (capacity, rows), with_xy),
            out_shape=bf16(11, whole, LANES),
            in_specs=[VMEM] * 3 + [ANY],
            out_specs=ANY,
            input_output_aliases={3: 0},
            scratch_shapes=[
                pltpu.VMEM((11, full, LANES), half_type),
                pltpu.VMEM((11, full, LANES), half_type),
                pltpu.SemaphoreType.DMA((2, 11)),
            ],
            compiler_params=room,
            cost_estimate=cost,
            name="place_xy" if with_xy else "place_z",
        )(*held(got_0, late, half), out)
    out = out.reshape(11, whole // (SUB * lines), lines, SUB, LANES).transpose(1, 3, 0, 2, 4)
    return out.reshape(2 * capacity, 11, entries)


def solution(mesh):
    placed = (
        P("gx", "gy", "gz", None, None),
        P("gx", "gy", "gz", None),
        P("gx", "gy", "gz"),
        P(("gx", "gy", "gz"), None),
    )
    return jax.shard_map(
        local,
        mesh=mesh,
        in_specs=placed,
        out_specs=P(("gx", "gy", "gz"), None, None),
        check_vma=False,
    )
```

```python
import functools
import math

import jax
import jax.numpy as jnp
from jax import lax
from jax.experimental import pallas as pl
from jax.experimental.pallas import tpu as pltpu
from jax.sharding import PartitionSpec as P


x_first_order = [0, 2, 1, 3, 4, 5, 6]
x_second_order = [0, 1, 2, 3, 4, 5, 6]
y_first_order = [0, 4, 1, 2, 3, 5, 6]
y_second_order = [0, 3, 1, 2, 4, 5, 6]

LANES = 128
SUB = 8


def padded_2(array, sides, width):
    for axis, dim in sides:
        devices, length = (lax.axis_size(axis), array.shape[dim])
        up = [(i, (i + 1) % devices) for i in range(devices - 1)]
        down = [(j, i) for i, j in up]
        last = lax.slice_in_dim(array, length - width, length, axis=dim)
        initial = lax.slice_in_dim(array, 0, width, axis=dim)
        before = lax.ppermute(last, axis, up)
        after = lax.ppermute(initial, axis, down)
        array = jnp.concatenate([before, array, after], axis=dim)
    return array


def neighbours(padded):
    shifted = [
        padded[1:-1, 1:-1, 1:-1],
        padded[:-2, 1:-1, 1:-1],
        padded[2:, 1:-1, 1:-1],
        padded[1:-1, :-2, 1:-1],
        padded[1:-1, 2:, 1:-1],
        padded[1:-1, 1:-1, :-2],
        padded[1:-1, 1:-1, 2:],
    ]
    return jnp.stack(shifted, axis=3)


def triple(blocks, nearby):
    block_side = math.isqrt(blocks.shape[-1])
    leading = blocks.shape[:-1]
    left_mat = blocks.reshape(leading + (block_side, block_side))
    right_mat = nearby.reshape(leading + (block_side, block_side))
    own_block = jnp.swapaxes(right_mat[..., :1, :, :], -1, -2)
    product = jnp.matmul(left_mat, right_mat, preferred_element_type=jnp.float32).astype(
        jnp.bfloat16
    )
    result = jnp.matmul(own_block, product, preferred_element_type=jnp.float32)
    return result.reshape(leading + (block_side * block_side,))


def members(element_grid, pairs):
    size_x, size_y, size_z = element_grid.shape[:3]
    trailing = element_grid.shape[3:]
    patches = element_grid.reshape((size_x // 2, 2, size_y // 2, 2, size_z) + trailing)

    def pick(upper, lower, slot_order):
        return jnp.take(patches[:, upper, :, lower], jnp.array(slot_order, dtype=jnp.int32), axis=3)

    x_one = jnp.stack([pick(0, 0, x_first_order), pick(0, 1, x_first_order)], axis=3)
    x_two = jnp.stack([pick(1, 0, x_second_order), pick(1, 1, x_second_order)], axis=3)
    y_one = jnp.stack([pick(0, 0, y_first_order), pick(1, 0, y_first_order)], axis=3)
    y_two = jnp.stack([pick(0, 1, y_second_order), pick(1, 1, y_second_order)], axis=3)
    along_x = (pairs == 0).reshape(pairs.shape + (1,) * (x_one.ndim - 3))
    member_one = jnp.where(along_x, x_one, y_one)
    member_two = jnp.where(along_x, x_two, y_two)
    return (
        member_one.reshape((-1,) + member_one.shape[4:]),
        member_two.reshape((-1,) + member_two.shape[4:]),
    )


def arrange(member_one, member_two):
    diagonal = (
        member_one[..., 0, :]
        + member_two[..., 0, :]
        + member_one[..., 1, :]
        + member_two[..., 1, :]
    )
    return jnp.concatenate(
        [diagonal[..., None, :], member_one[..., 2:, :], member_two[..., 2:, :]], axis=-2
    )


def slot_sources(routes, n_dest, capacity):
    total = routes.shape[0]
    chosen = (routes[:, None] == jnp.arange(n_dest, dtype=jnp.int32)[None, :]).astype(jnp.int32)
    before = jnp.cumsum(chosen, axis=0) - chosen
    ranking = jnp.sum(before * chosen, axis=1)
    position = routes * capacity + ranking
    targets = jnp.arange(n_dest * capacity, dtype=jnp.int32)
    matches = position[None, :] == targets[:, None]
    anchor = jnp.sum(jnp.where(matches, jnp.arange(total, dtype=jnp.int32)[None, :], 0), axis=1)
    filled = jnp.any(matches, axis=1)
    return (anchor, filled)


def pack_slots(payload, anchor, filled):
    taken = jnp.take(payload, anchor, axis=0)
    keep_row = filled.reshape(filled.shape + (1,) * (payload.ndim - 1))
    return jnp.where(keep_row, taken, jnp.zeros_like(taken))


def general(a_blocks, prolong, pairing, route, capacity):
    padded = padded_2(prolong, (("gx", 0), ("gy", 1), ("gz", 2)), 1)
    nearby = neighbours(padded)
    anchor, filled = slot_sources(route[:, 0], lax.axis_size("gx"), capacity)
    galerkin = triple(a_blocks, nearby)
    member_one, member_two = members(galerkin, pairing)
    coarse = arrange(member_one, member_two).astype(jnp.bfloat16)
    return lax.all_to_all(
        pack_slots(coarse, anchor, filled), "gx", split_axis=0, concat_axis=0, tiled=True
    )


def dot(left, right):
    return jnp.dot(left, right, preferred_element_type=jnp.float32)


def iota(shape, axis):
    return lax.broadcasted_iota(jnp.int32, shape, axis)


def as_bf16(mask):
    return mask.astype(jnp.float32).astype(jnp.bfloat16)


def pair(one, two):
    h = one.shape[1] // 2
    low = jnp.concatenate([one[:, :h], two[:, :h]], axis=1)
    high = jnp.concatenate([one[:, h:], two[:, h:]], axis=1)
    return jnp.concatenate([low, high], axis=0)


def unpair(both):
    rows, h = both.shape[0] // 2, both.shape[1] // 2
    even, odd = both[:rows], both[rows:]
    return (
        jnp.concatenate([even[:, :h], odd[:, :h]], axis=1),
        jnp.concatenate([even[:, h:], odd[:, h:]], axis=1),
    )


def constants(blk):
    n = 2 * blk
    row, col = iota((n, n), 0), iota((n, n), 1)
    c, z = row % blk, row // blk
    clean = as_bf16(col == (c % 2) * blk + (c // 2) * 2 + z)
    q = blk // 2
    k, p = row // blk, (row // q) % 2
    spread = as_bf16(col == k * blk + 2 * (row % q) + p)
    return clean, spread


def even_lanes(rows):
    return as_bf16(iota((rows, LANES), 1) % 2 == 0), as_bf16(iota((rows, LANES), 1) % 2 == 1)


def even_rows(rows):
    return as_bf16(iota((rows, LANES), 0) % 2 == 0), as_bf16(iota((rows, LANES), 0) % 2 == 1)


def transposed_dot(left, right):
    return lax.dot_general(
        left, right, (((1,), (1,)), ((), ())), preferred_element_type=jnp.float32
    )


def left_factors(both_t, k, masks):
    q = masks[0].shape[0]
    parts = [both_t[(2 * k + p) * q : (2 * k + p + 1) * q] for p in range(2)]
    return jnp.concatenate([part * mask for part in parts for mask in masks], axis=0)


def weights_of(part):
    h = part.shape[1] // 2
    none = jnp.zeros((part.shape[0], h), part.dtype)
    made = []
    for k in range(2):
        one = part[:, k * h : (k + 1) * h]
        made.append(
            jnp.concatenate(
                [jnp.concatenate([one, none], axis=1), jnp.concatenate([none, one], axis=1)], axis=0
            )
        )
    return made


def halves(part):
    h = part.shape[1] // 2
    return part[:, :h], part[:, h:]


def places(route_ref, where_ref, table_ref, dims, blocks):
    aggregates, cap, rows = dims
    me = lax.axis_index("gx")
    lines = rows // cap
    rest = cap % SUB
    half = (cap - rest) * lines
    at_zero = me == 0
    for c in range(cap):
        if c < cap - rest:
            zero = (c, c + half // 2, c, c)
        else:
            h = c - (cap - rest)
            zero = (half + h, half + h + rest, SUB + h, SUB + h + rest)
        if c < rest:
            one = (half + c + rest, half + c, SUB + c, SUB + c + rest)
        else:
            h = c - rest
            one = (h, h + half // 2, h, h)
        for k in range(4):
            table_ref[k, c] = jnp.where(at_zero, zero[k], one[k])
    sent, kept = jnp.int32(0), jnp.int32(0)
    for i in range(aggregates):
        away = route_ref[0, i] != me
        one = away.astype(jnp.int32)
        c = jnp.where(away, sent, kept)
        sent = sent + one
        kept = kept + (1 - one)
        base = jnp.where(away, 0, blocks * rows)
        where_ref[0, i] = base + table_ref[0, c]
        where_ref[1, i] = base + table_ref[1, c]
        where_ref[2, i] = jnp.where(away, 0, 2 * SUB) + table_ref[2, c]
        where_ref[3, i] = jnp.where(away, 0, 2 * SUB) + table_ref[3, c]
    return sent, kept


def put(total_ref, where_ref, i, block, rows, value):
    n = value.shape[0] // 2
    one = where_ref[0, i] + block * rows
    two = where_ref[1, i] + block * rows
    total_ref[pl.ds(one, n, stride=SUB), :] = value[:n]
    total_ref[pl.ds(two, n, stride=SUB), :] = value[n:]


def finish(outs, total_ref, kind, dims, count):
    _, cap, rows = dims
    rest = cap % SUB
    full = (cap - rest) * (rows // cap)
    me = lax.axis_index("gx")
    line = iota((2 * SUB, LANES), 0)
    in_full = as_bf16(line % SUB + jnp.where(me == 0, 0, rest) < count) > 0.5
    in_half = as_bf16(line % rest + jnp.where(me == 0, cap - rest, 0) < count) > 0.5
    blocks = sum(n for _, n in outs)
    done = 0
    for out, n in outs:
        for k in range(n):
            for at, size, filled in ((0, full, in_full), (full, rows - full, in_half)):
                value = total_ref[pl.ds((kind * blocks + done + k) * rows + at, size), :]
                value = value.astype(jnp.bfloat16).reshape(-1, 2 * SUB, LANES)
                value = jnp.where(filled[None], value, jnp.zeros_like(value))
                out[k * rows + at : k * rows + at + size] = value.reshape(size, LANES)
        done += n


def inner_kernel(
    dims, grid, route_hbm, pair_hbm, p_hbm, a_hbm,
    send_ref, total_ref, keep_codes_ref, zup_ref, zdn_ref, left_ref, a_ref,
    p_ref, route_ref, pair_ref, part_ref, codes_ref, where_ref, table_ref, sems,
):
    px, py, nz = grid
    aggregates, _, rows = dims
    nx, ny = 2 * px, 2 * py
    blk = p_ref.shape[2]
    q = blk // 2
    nb = 5
    copies = [
        pltpu.make_async_copy(one, two, sems.at[k])
        for k, (one, two) in enumerate((
            (p_hbm, p_ref), (route_hbm, route_ref), (pair_hbm, pair_ref), (a_hbm, a_ref),
        ))
    ]
    for copy in copies:
        copy.start()
    for copy in copies[:3]:
        copy.wait()
    sent, _ = places(route_ref, where_ref, table_ref, dims, nb)
    codes_ref[...] = jnp.full_like(codes_ref, -1.0)
    for i in range(aggregates):
        a, b, z, t = i // (py * nz * 2), (i // (nz * 2)) % py, (i // 2) % nz, i % 2
        code = (2 * (jnp.where(pair_ref[a, b, z] == 0, 2, 1) - t) + z).astype(jnp.float32)
        line = jnp.full((1, LANES), code, jnp.float32)
        codes_ref[pl.ds(where_ref[2, i], 1), :] = line
        codes_ref[pl.ds(where_ref[3, i], 1), :] = line
    clean, spread = constants(blk)
    masks = even_lanes(q)
    first, second = even_rows(blk)

    pairs = [(x, b) for x in range(nx) for b in range(py)]
    both = {e: pair(p_ref[e[0], 2 * e[1]], p_ref[e[0], 2 * e[1] + 1]) for e in pairs}
    tidy = {e: dot(clean, both[e]).astype(jnp.bfloat16) for e in pairs}
    for x, b in pairs:
        left_ref[x * py + b] = transposed_dot(spread, both[x, b]).astype(jnp.bfloat16)
        zdn_ref[x * py + b] = tidy[x, b][:blk]
        zup_ref[x * py + b] = tidy[x, b][blk:]

    face = p_ref[jnp.where(lax.axis_index("gx") == 0, nx - 1, 0)]
    send_ref[nb * rows + 2 * SUB :] = face.reshape(ny * blk, LANES)
    copies[3].wait()

    for x, y in [(x, y) for x in range(nx) for y in range(ny)]:
        here = a_ref.at[x, y]
        along_z = here[6] * first + here[5] * second
        right = jnp.concatenate(
            [pair(here[0], here[2 - x % 2]), pair(here[4 - y % 2], along_z)], axis=1
        )
        left = left_factors(left_ref[x * py + y // 2], y % 2, masks)
        got = dot(left, right).astype(jnp.bfloat16)
        parts = unpair(got[:, : 2 * blk]) + unpair(got[:, 2 * blk :])
        for k in range(4):
            part_ref[x, y, k] = parts[k]

    for a, b in [(a, b) for a in range(px) for b in range(py)]:
        own, with_x, with_y, with_z = {}, {}, {}, {}
        for z, ref in enumerate((zdn_ref, zup_ref)):
            zs, zo = pl.ds(z * q, q), pl.ds((1 - z) * q, q)
            for u in range(2):
                x = 2 * a + u
                weight = weights_of(ref[x * py + b])
                for v in range(2):
                    y = 2 * b + v
                    stack = jnp.concatenate(
                        [
                            part_ref[x, y, 0, zs],
                            part_ref[2 * a + 1 - u, y, 1, zs],
                            part_ref[x, 2 * b + 1 - v, 2, zs],
                            part_ref[x, y, 3, zo],
                        ],
                        axis=0,
                    )
                    got = dot(stack, weight[v])
                    own[u, v, z] = got[:q]
                    with_x[1 - u, v, z] = got[q : 2 * q]
                    with_y[u, 1 - v, z] = got[2 * q : 3 * q]
                    with_z[u, v, 1 - z] = got[3 * q :]
        for z in range(nz):
            flat = pair_ref[a, b, z] == 0
            i = ((a * py + b) * nz + z) * 2
            sums = {}
            for u in range(2):
                for v in range(2):
                    t = u if u == v else jnp.where(flat, v, u)
                    m = u if u == v else jnp.where(flat, u, v)
                    e = (u, v, z)
                    sums[u, v] = own[e] + jnp.where(flat, with_x[e], with_y[e])
                    cross = jnp.where(flat, with_y[e], with_x[e])
                    put(total_ref, where_ref, i + t, 1 + m, rows, cross)
                    put(total_ref, where_ref, i + t, 3 + m, rows, with_z[e])
            put(total_ref, where_ref, i, 0, rows, sums[0, 0] + jnp.where(flat, sums[1, 0], sums[0, 1]))
            put(total_ref, where_ref, i + 1, 0, rows, sums[1, 1] + jnp.where(flat, sums[0, 1], sums[1, 0]))

    finish(((send_ref, nb),), total_ref, 0, dims, sent)
    send_ref[nb * rows : nb * rows + 2 * SUB] = codes_ref[: 2 * SUB].astype(jnp.bfloat16)
    keep_codes_ref[...] = codes_ref[2 * SUB :].astype(jnp.bfloat16)


def faces_kernel(grid, zup_ref, zdn_ref, ya_ref, yb_ref, za_ref, zb_ref):
    px, py, _ = grid
    blk = zup_ref.shape[1]
    y_even, z_even = lax.axis_index("gy") % 2 == 0, lax.axis_index("gz") % 2 == 0

    def plane(a, b, half):
        part = slice(half * blk, (half + 1) * blk)
        rows = [jnp.concatenate([zdn_ref[x * py + b], zup_ref[x * py + b]], axis=0) for x in (2 * a, 2 * a + 1)]
        return jnp.concatenate([row[:, part] for row in rows], axis=1)

    for a in range(px):
        down, up = plane(a, 0, 0), plane(a, py - 1, 1)
        ya_ref[a], yb_ref[a] = jnp.where(y_even, up, down), jnp.where(y_even, down, up)
    for at in range(2 * px * py):
        down, up = zdn_ref[at], zup_ref[at]
        za_ref[at] = jnp.where(z_even, up, down)
        zb_ref[at] = jnp.where(z_even, down, up)


def outer_left_kernel(grid, left_ref, a_ref, part_ref):
    px, py, _ = grid
    nx, ny = 2 * px, 2 * py
    blk = a_ref.shape[3]
    masks = even_lanes(blk // 2)
    first, second = even_rows(blk)
    for x, y in [(x, y) for x in range(nx) for y in range(ny)]:
        here = a_ref.at[x, y]
        along_z = here[5] * first + here[6] * second
        low, high = halves(along_z)
        right = jnp.concatenate(
            [pair(here[1 + x % 2], here[3 + y % 2]), jnp.concatenate([low, high], axis=0)], axis=1
        )
        left = left_factors(left_ref[x * py + y // 2], y % 2, masks)
        got = dot(left, right).astype(jnp.bfloat16)
        part_ref[x, y, 0], part_ref[x, y, 1] = unpair(got[:, : 2 * blk])
        along = got[:, 2 * blk :]
        part_ref[x, y, 2] = jnp.concatenate([along[:blk], along[blk:]], axis=1)


def outer_yz_kernel(
    dims, grid, route_ref, pair_ref, part_ref, zup_ref, zdn_ref, ya_ref, yb_ref, za_ref, zb_ref,
    send_ref, keep_ref, total_ref, where_ref, table_ref,
):
    px, py, nz = grid
    _, _, rows = dims
    nx, ny = 2 * px, 2 * py
    blk = part_ref.shape[3]
    q = blk // 2
    nb = 4
    sent, kept = places(route_ref, where_ref, table_ref, dims, nb)
    line = iota((blk, LANES), 0) * 0

    def from_sides(axis, first_ref, second_ref, at, high):
        index = lax.axis_index(axis)
        last = index == lax.axis_size(axis) - 1 if high else index == 0
        by_first = index % 2 == (0 if high else 1)
        kept = line + jnp.where(by_first | ~last, 1, 0) > 0
        value = jnp.where(by_first, first_ref[at], second_ref[at]).astype(jnp.float32)
        return jnp.where(kept, value, 0.0).astype(jnp.bfloat16)

    def beside_y(x, y, z, v):
        to = y - 1 if v == 0 else y + 1
        if 0 <= to < ny:
            return (zdn_ref, zup_ref)[z][x * py + to // 2], to % 2
        at = (x // 2, slice(z * blk, (z + 1) * blk))
        return from_sides("gy", ya_ref, yb_ref, at, v == 1), x % 2

    for x in range(nx):
        made = []
        for b, z in [(b, z) for b in range(py) for z in range(nz)]:
            zs = pl.ds(z * q, q)
            along_z = weights_of(from_sides("gz", za_ref, zb_ref, x * py + b, z == 1))
            for v in range(2):
                y = 2 * b + v
                i, m = of_element(pair_ref, grid, x, y, z)
                other, k = beside_y(x, y, z, v)
                along_y = weights_of(other)[k]
                made.append((i, m, dot(part_ref[x, y, 1, zs], along_y)))
                made.append((i, 2 + m, dot(part_ref[x, y, 2, zs], along_z[v])))
        for i, block, got in made:
            put(total_ref, where_ref, i, block, rows, got)

    for kind, (out, count) in enumerate(((send_ref, sent), (keep_ref, kept))):
        finish(((out, nb),), total_ref, kind, dims, count)


def outer_x_kernel(
    dims, grid, route_ref, pair_ref, part_ref, zup_ref, zdn_ref, early_ref,
    send_ref, keep_ref, total_ref, where_ref, table_ref,
):
    px, py, nz = grid
    _, _, rows = dims
    nx, ny = 2 * px, 2 * py
    blk = part_ref.shape[3]
    q = blk // 2
    nb = 2
    sent, kept = places(route_ref, where_ref, table_ref, dims, nb)
    above = iota((2 * blk, LANES), 0) * 0 + lax.axis_index("gx") > 0
    clean, _ = constants(blk)
    face = early_ref.shape[0] - ny * blk
    low, high = [], []
    for b in range(py):
        at = face + 2 * b * blk
        tidy = dot(clean, pair(early_ref[at : at + blk], early_ref[at + blk : at + 2 * blk]))
        low.append(jnp.where(above, tidy, 0.0).astype(jnp.bfloat16))
        high.append(jnp.where(above, 0.0, tidy).astype(jnp.bfloat16))

    for x in range(nx):
        made = []
        for b, z in [(b, z) for b in range(py) for z in range(nz)]:
            zs = pl.ds(z * q, q)
            to = x - 1 if x % 2 == 0 else x + 1
            if 0 <= to < nx:
                part = (zdn_ref, zup_ref)[z][to * py + b]
            else:
                part = (low if to < 0 else high)[b][z * blk : (z + 1) * blk]
            along_x = weights_of(part)
            for v in range(2):
                i, m = of_element(pair_ref, grid, x, 2 * b + v, z)
                made.append((i, m, dot(part_ref[x, 2 * b + v, 0, zs], along_x[v])))
        for i, block, got in made:
            put(total_ref, where_ref, i, block, rows, got)

    for kind, (out, count) in enumerate(((send_ref, sent), (keep_ref, kept))):
        finish(((out, nb),), total_ref, kind, dims, count)


def of_element(pair_ref, grid, x, y, z):
    _, py, nz = grid
    a, b, u, v = x // 2, y // 2, x % 2, y % 2
    flat = pair_ref[a, b, z] == 0
    t = u if u == v else jnp.where(flat, v, u)
    m = u if u == v else jnp.where(flat, u, v)
    return ((a * py + b) * nz + z) * 2 + t, m


def received(early_ref, rows):
    def early(k, at, size):
        return early_ref[k * rows + at : k * rows + at + size].reshape(-1, 2 * SUB, LANES)

    return early


def placed_blocks(early, x_ref, yz_ref, code, rows, at, size, without_x=True):
    near_low, near_high = (code < 1.5)[None], (code > 3.5)[None]
    upper = ((code == 1.0) | (code == 3.0) | (code == 5.0))[None]

    def tiles(ref, k):
        return ref[k * rows + at : k * rows + at + size].reshape(-1, 2 * SUB, LANES)

    if without_x:
        yield 0, early(0, at, size)
    for m in range(2):
        cross, y_out = early(1 + m, at, size), tiles(yz_ref, m)
        if x_ref is not None:
            x_out = tiles(x_ref, m)
            yield 1 + 5 * m, jnp.where(near_low, cross, x_out)
            yield 2 + 5 * m, jnp.where(near_low, x_out, jnp.where(near_high, y_out, cross))
        if without_x:
            z_in, z_out = early(3 + m, at, size), tiles(yz_ref, 2 + m)
            yield 3 + 5 * m, jnp.where(near_high, cross, y_out)
            yield 4 + 5 * m, jnp.where(upper, z_in, z_out)
            yield 5 + 5 * m, jnp.where(upper, z_out, z_in)


def twice(codes):
    return jnp.concatenate([codes, codes], axis=0)


def keep_kernel(dims, total_ref, codes_ref, x_ref, yz_ref, half_ref, out_hbm, full_ref, sem):
    cap, rows = dims
    full = (cap - cap % SUB) * (rows // cap)
    me = lax.axis_index("gx")

    def rounded(code):
        filled = (code > -0.5)[None]

        def early(k, at, size):
            value = total_ref[pl.ds((5 + k) * rows + at, size), :].astype(jnp.bfloat16)
            value = value.reshape(-1, 2 * SUB, LANES)
            return jnp.where(filled, value, jnp.zeros_like(value))

        return early

    copies = []
    code = twice(codes_ref[:SUB])
    for k, value in placed_blocks(rounded(code), x_ref, yz_ref, code, rows, 0, full):
        full_ref[k] = value.reshape(full, LANES)
        to = out_hbm.at[k, pl.ds(me * (2 * full), full), :]
        copies.append(pltpu.make_async_copy(full_ref.at[k], to, sem.at[k]))
        copies[-1].start()
    code = twice(codes_ref[SUB:])
    for k, value in placed_blocks(rounded(code), x_ref, yz_ref, code, rows, full, rows - full):
        half_ref[k] = value.reshape(rows - full, LANES)
    for copy in copies:
        copy.wait()


def take_kernel(dims, with_x, early_ref, *refs):
    late, (half_ref, _, out_hbm, full_ref, mixed_ref, sem) = refs[: -6], refs[-6:]
    cap, rows = dims
    full = (cap - cap % SUB) * (rows // cap)
    me = lax.axis_index("gx")
    codes = early_ref[5 * rows : 5 * rows + 2 * SUB]
    x_ref, yz_ref = late if with_x else (None, late[0])
    early = received(early_ref, rows)
    copies = []
    for k, value in placed_blocks(early, x_ref, yz_ref, twice(codes[:SUB]), rows, 0, full, not with_x):
        full_ref[k] = value.reshape(full, LANES)
        to = out_hbm.at[k, pl.ds((1 - me) * (2 * full), full), :]
        copies.append(pltpu.make_async_copy(full_ref.at[k], to, sem.at[0, k]))
        copies[-1].start()
    first_half = (iota((SUB, LANES), 0) < SUB // 2)[None]
    pick = first_half == (me == 0)
    for k, value in placed_blocks(
        early, x_ref, yz_ref, twice(codes[SUB:]), rows, full, rows - full, not with_x
    ):
        theirs = value.reshape(rows - full, LANES).astype(jnp.float32).reshape(-1, SUB, LANES)
        mine = half_ref[k].astype(jnp.float32).reshape(-1, SUB, LANES)
        low = jnp.where(pick, mine, theirs)
        high = pltpu.roll(jnp.where(pick, theirs, mine), SUB // 2, 1)
        mixed_ref[k, : rows - full] = low.reshape(rows - full, LANES).astype(jnp.bfloat16)
        mixed_ref[k, rows - full :] = high.reshape(rows - full, LANES).astype(jnp.bfloat16)
        to = out_hbm.at[k, full : 2 * full, :]
        copies.append(pltpu.make_async_copy(mixed_ref.at[k], to, sem.at[1, k]))
        copies[-1].start()
    for copy in copies:
        copy.wait()


SMEM = pl.BlockSpec(memory_space=pltpu.SMEM)
VMEM = pl.BlockSpec(memory_space=pltpu.VMEM)
ANY = pl.BlockSpec(memory_space=pl.ANY)


def bf16(*shape):
    return jax.ShapeDtypeStruct(shape, jnp.bfloat16)


def near(*shape):
    return pltpu.VMEM(shape, jnp.bfloat16)


def held(*arrays):
    return [pltpu.with_memory_space_constraint(one, pltpu.VMEM) for one in arrays]


def swaps(ny, nz):
    def first(i):
        return i + 1 if i % 2 == 0 else i - 1

    def second(i, n):
        j = i - 1 if i % 2 == 0 else i + 1
        return j if 0 <= j < n else None

    made = {"y_a": [], "y_b": [], "z_a": [], "z_b": []}
    for j in range(ny):
        for k in range(nz):
            to_y, to_z = second(j, ny), second(k, nz)
            made["y_a"].append((first(j), k))
            made["z_a"].append((j, first(k)))
            made["y_b"].append((j, first(k)) if to_y is None else (to_y, k))
            made["z_b"].append((first(j), k) if to_z is None else (j, to_z))
    return {name: [(i, j * nz + k) for i, (j, k) in enumerate(to)] for name, to in made.items()}


def local(a_blocks, prolong, pairing, route):
    devices_gx = lax.axis_size("gx")
    aggregates = route.shape[0]
    capacity = max(2, 3 * aggregates // (2 * devices_gx))
    nx, ny, nz, faces, entries = a_blocks.shape
    fits = (
        devices_gx == 2
        and lax.axis_size("gy") % 2 == 0
        and lax.axis_size("gz") % 2 == 0
        and nz == 2
        and nx % 2 == 0
        and ny % 2 == 0
        and faces == 7
        and entries == (LANES // 2) ** 2
        and capacity // SUB == 1
        and capacity % SUB == SUB // 2
    )
    if not fits:
        return general(a_blocks, prolong, pairing, route, capacity)
    px, py = nx // 2, ny // 2
    blk = math.isqrt(entries)
    lines = entries // LANES
    a_view = a_blocks.transpose(0, 1, 3, 2, 4).reshape(nx, ny, faces, nz, lines, LANES)
    a_view = a_view.transpose(0, 1, 2, 4, 3, 5).reshape(nx, ny, faces, nz * lines, LANES)
    p_view = prolong.reshape(nx, ny, nz, lines, LANES).transpose(0, 1, 3, 2, 4)
    p_view = p_view.reshape(nx, ny, nz * lines, LANES)
    route_row = route.reshape(1, aggregates)
    rows = capacity * lines
    dims, grid = (aggregates, capacity, rows), (px, py, nz)
    f32 = jnp.float32
    half_type = jnp.bfloat16
    face_y, face_z = (px, 2 * blk, LANES), (nx * py, blk, LANES)
    parts = (nx, ny, 3, blk, LANES)
    room = pltpu.CompilerParams(vmem_limit_bytes=24 * 2**20)
    cost = pl.CostEstimate(flops=10**9, bytes_accessed=4 * 10**6, transcendentals=0)

    swap = [(0, 1), (1, 0)]
    send_0, total, keep_codes, zup, zdn, left, a_near = pl.pallas_call(
        functools.partial(inner_kernel, dims, grid),
        out_shape=(
            near(5 * rows + 2 * SUB + ny * blk, LANES),
            pltpu.VMEM((10 * rows, LANES), f32),
            near(2 * SUB, LANES),
            near(*face_z),
            near(*face_z),
            near(nx * py, 2 * blk, LANES),
            near(*a_view.shape),
        ),
        in_specs=[ANY] * 4,
        out_specs=[VMEM] * 7,
        scratch_shapes=[
            pltpu.VMEM(p_view.shape, half_type),
            pltpu.SMEM(route_row.shape, jnp.int32),
            pltpu.SMEM(pairing.shape, jnp.int32),
            pltpu.VMEM((nx, ny, 4, blk, LANES), half_type),
            pltpu.VMEM((4 * SUB, LANES), f32),
            pltpu.SMEM((4, aggregates), jnp.int32),
            pltpu.SMEM((4, capacity), jnp.int32),
            pltpu.SemaphoreType.DMA((4,)),
        ],
        compiler_params=room,
        cost_estimate=cost,
        name="inner_blocks",
    )(*[pltpu.with_memory_space_constraint(one, pltpu.HBM) for one in (route_row, pairing, p_view, a_view)])
    got_0 = lax.ppermute(send_0, "gx", swap)
    zup, zdn = held(zup, zdn)
    ya, yb, za, zb = pl.pallas_call(
        functools.partial(faces_kernel, grid),
        out_shape=(near(*face_y), near(*face_y), near(*face_z), near(*face_z)),
        in_specs=[VMEM] * 2,
        out_specs=[VMEM] * 4,
        compiler_params=room,
        cost_estimate=cost,
        name="faces",
    )(zup, zdn)
    rounds = swaps(lax.axis_size("gy"), lax.axis_size("gz"))
    halos = []
    for name, value in (("y_a", ya), ("y_b", yb), ("z_a", za), ("z_b", zb)):
        halos.append(lax.ppermute(value, ("gy", "gz"), rounds[name]))

    left, a_near = held(left, a_near)
    part = pl.pallas_call(
        functools.partial(outer_left_kernel, grid),
        out_shape=near(*parts),
        in_specs=[VMEM] * 2,
        out_specs=VMEM,
        compiler_params=room,
        cost_estimate=cost,
        name="outer_left",
    )(left, a_near)
    part = held(part)[0]

    def outer(kernel, blocks, *arrays):
        return pl.pallas_call(
            functools.partial(kernel, dims, grid),
            out_shape=(near(blocks * rows, LANES),) * 2,
            in_specs=[SMEM, SMEM] + [VMEM] * (3 + len(arrays)),
            out_specs=[VMEM] * 2,
            scratch_shapes=[
                pltpu.VMEM((2 * blocks * rows, LANES), f32),
                pltpu.SMEM((4, aggregates), jnp.int32),
                pltpu.SMEM((4, capacity), jnp.int32),
            ],
            compiler_params=room,
            cost_estimate=cost,
        )(route_row, pairing, part, zup, zdn, *held(*arrays))

    send_yz, keep_yz = outer(outer_yz_kernel, 4, *halos)
    got_yz = lax.ppermute(send_yz, "gx", swap)
    send_x, keep_x = outer(outer_x_kernel, 2, got_0)
    got_x = lax.ppermute(send_x, "gx", swap)

    full = (capacity // SUB) * SUB * lines
    whole = 2 * rows
    half, out = pl.pallas_call(
        functools.partial(keep_kernel, (capacity, rows)),
        out_shape=(near(11, rows - full, LANES), bf16(11, whole, LANES)),
        in_specs=[VMEM] * 4,
        out_specs=[VMEM, ANY],
        scratch_shapes=[pltpu.VMEM((11, full, LANES), half_type), pltpu.SemaphoreType.DMA((11,))],
        compiler_params=room,
        cost_estimate=cost,
        name="place_kept",
    )(*held(total, keep_codes, keep_x, keep_yz))
    for with_x, late in ((False, (got_yz,)), (True, (got_x, got_yz))):
        out = pl.pallas_call(
            functools.partial(take_kernel, (capacity, rows), with_x),
            out_shape=bf16(11, whole, LANES),
            in_specs=[VMEM] * (2 + len(late)) + [ANY],
            out_specs=ANY,
            input_output_aliases={2 + len(late): 0},
            scratch_shapes=[
                pltpu.VMEM((11, full, LANES), half_type),
                pltpu.VMEM((11, full, LANES), half_type),
                pltpu.SemaphoreType.DMA((2, 11)),
            ],
            compiler_params=room,
            cost_estimate=cost,
            name="place_x" if with_x else "place_yz",
        )(*held(got_0, *late, half), out)
    out = out.reshape(11, whole // (SUB * lines), lines, SUB, LANES).transpose(1, 3, 0, 2, 4)
    return out.reshape(2 * capacity, 11, entries)


def solution(mesh):
    placed = (
        P("gx", "gy", "gz", None, None),
        P("gx", "gy", "gz", None),
        P("gx", "gy", "gz"),
        P(("gx", "gy", "gz"), None),
    )
    return jax.shard_map(
        local,
        mesh=mesh,
        in_specs=placed,
        out_specs=P(("gx", "gy", "gz"), None, None),
        check_vma=False,
    )
```

```python
import functools
import math

import jax
import jax.numpy as jnp
from jax import lax
from jax.experimental import pallas as pl
from jax.experimental.pallas import tpu as pltpu
from jax.sharding import PartitionSpec as P


x_first_order = [0, 2, 1, 3, 4, 5, 6]
x_second_order = [0, 1, 2, 3, 4, 5, 6]
y_first_order = [0, 4, 1, 2, 3, 5, 6]
y_second_order = [0, 3, 1, 2, 4, 5, 6]

LANES = 128
SUB = 8


def padded_2(array, sides, width):
    for axis, dim in sides:
        devices, length = (lax.axis_size(axis), array.shape[dim])
        up = [(i, (i + 1) % devices) for i in range(devices - 1)]
        down = [(j, i) for i, j in up]
        last = lax.slice_in_dim(array, length - width, length, axis=dim)
        initial = lax.slice_in_dim(array, 0, width, axis=dim)
        before = lax.ppermute(last, axis, up)
        after = lax.ppermute(initial, axis, down)
        array = jnp.concatenate([before, array, after], axis=dim)
    return array


def neighbours(padded):
    shifted = [
        padded[1:-1, 1:-1, 1:-1],
        padded[:-2, 1:-1, 1:-1],
        padded[2:, 1:-1, 1:-1],
        padded[1:-1, :-2, 1:-1],
        padded[1:-1, 2:, 1:-1],
        padded[1:-1, 1:-1, :-2],
        padded[1:-1, 1:-1, 2:],
    ]
    return jnp.stack(shifted, axis=3)


def triple(blocks, nearby):
    block_side = math.isqrt(blocks.shape[-1])
    leading = blocks.shape[:-1]
    left_mat = blocks.reshape(leading + (block_side, block_side))
    right_mat = nearby.reshape(leading + (block_side, block_side))
    own_block = jnp.swapaxes(right_mat[..., :1, :, :], -1, -2)
    product = jnp.matmul(left_mat, right_mat, preferred_element_type=jnp.float32).astype(
        jnp.bfloat16
    )
    result = jnp.matmul(own_block, product, preferred_element_type=jnp.float32)
    return result.reshape(leading + (block_side * block_side,))


def members(element_grid, pairs):
    size_x, size_y, size_z = element_grid.shape[:3]
    trailing = element_grid.shape[3:]
    patches = element_grid.reshape((size_x // 2, 2, size_y // 2, 2, size_z) + trailing)

    def pick(upper, lower, slot_order):
        return jnp.take(patches[:, upper, :, lower], jnp.array(slot_order, dtype=jnp.int32), axis=3)

    x_one = jnp.stack([pick(0, 0, x_first_order), pick(0, 1, x_first_order)], axis=3)
    x_two = jnp.stack([pick(1, 0, x_second_order), pick(1, 1, x_second_order)], axis=3)
    y_one = jnp.stack([pick(0, 0, y_first_order), pick(1, 0, y_first_order)], axis=3)
    y_two = jnp.stack([pick(0, 1, y_second_order), pick(1, 1, y_second_order)], axis=3)
    along_x = (pairs == 0).reshape(pairs.shape + (1,) * (x_one.ndim - 3))
    member_one = jnp.where(along_x, x_one, y_one)
    member_two = jnp.where(along_x, x_two, y_two)
    return (
        member_one.reshape((-1,) + member_one.shape[4:]),
        member_two.reshape((-1,) + member_two.shape[4:]),
    )


def arrange(member_one, member_two):
    diagonal = (
        member_one[..., 0, :]
        + member_two[..., 0, :]
        + member_one[..., 1, :]
        + member_two[..., 1, :]
    )
    return jnp.concatenate(
        [diagonal[..., None, :], member_one[..., 2:, :], member_two[..., 2:, :]], axis=-2
    )


def slot_sources(routes, n_dest, capacity):
    total = routes.shape[0]
    chosen = (routes[:, None] == jnp.arange(n_dest, dtype=jnp.int32)[None, :]).astype(jnp.int32)
    before = jnp.cumsum(chosen, axis=0) - chosen
    ranking = jnp.sum(before * chosen, axis=1)
    position = routes * capacity + ranking
    targets = jnp.arange(n_dest * capacity, dtype=jnp.int32)
    matches = position[None, :] == targets[:, None]
    anchor = jnp.sum(jnp.where(matches, jnp.arange(total, dtype=jnp.int32)[None, :], 0), axis=1)
    filled = jnp.any(matches, axis=1)
    return (anchor, filled)


def pack_slots(payload, anchor, filled):
    taken = jnp.take(payload, anchor, axis=0)
    keep_row = filled.reshape(filled.shape + (1,) * (payload.ndim - 1))
    return jnp.where(keep_row, taken, jnp.zeros_like(taken))


def general(a_blocks, prolong, pairing, route, capacity):
    padded = padded_2(prolong, (("gx", 0), ("gy", 1), ("gz", 2)), 1)
    nearby = neighbours(padded)
    anchor, filled = slot_sources(route[:, 0], lax.axis_size("gx"), capacity)
    galerkin = triple(a_blocks, nearby)
    member_one, member_two = members(galerkin, pairing)
    coarse = arrange(member_one, member_two).astype(jnp.bfloat16)
    return lax.all_to_all(
        pack_slots(coarse, anchor, filled), "gx", split_axis=0, concat_axis=0, tiled=True
    )


def dot(left, right):
    return jnp.dot(left, right, preferred_element_type=jnp.float32)


def iota(shape, axis):
    return lax.broadcasted_iota(jnp.int32, shape, axis)


def as_bf16(mask):
    return mask.astype(jnp.float32).astype(jnp.bfloat16)


def pair(one, two):
    h = one.shape[1] // 2
    low = jnp.concatenate([one[:, :h], two[:, :h]], axis=1)
    high = jnp.concatenate([one[:, h:], two[:, h:]], axis=1)
    return jnp.concatenate([low, high], axis=0)


def unpair(both):
    rows, h = both.shape[0] // 2, both.shape[1] // 2
    even, odd = both[:rows], both[rows:]
    return (
        jnp.concatenate([even[:, :h], odd[:, :h]], axis=1),
        jnp.concatenate([even[:, h:], odd[:, h:]], axis=1),
    )


def constants(blk):
    n = 2 * blk
    row, col = iota((n, n), 0), iota((n, n), 1)
    c, z = row % blk, row // blk
    clean = as_bf16(col == (c % 2) * blk + (c // 2) * 2 + z)
    q = blk // 2
    k, p = row // blk, (row // q) % 2
    spread = as_bf16(col == k * blk + 2 * (row % q) + p)
    return clean, spread


def even_lanes(rows):
    return as_bf16(iota((rows, LANES), 1) % 2 == 0), as_bf16(iota((rows, LANES), 1) % 2 == 1)


def even_rows(rows):
    return as_bf16(iota((rows, LANES), 0) % 2 == 0), as_bf16(iota((rows, LANES), 0) % 2 == 1)


def transposed_dot(left, right):
    return lax.dot_general(
        left, right, (((1,), (1,)), ((), ())), preferred_element_type=jnp.float32
    )


def left_factors(both_t, k, masks):
    q = masks[0].shape[0]
    parts = [both_t[(2 * k + p) * q : (2 * k + p + 1) * q] for p in range(2)]
    return jnp.concatenate([part * mask for part in parts for mask in masks], axis=0)


def weights_of(part):
    h = part.shape[1] // 2
    none = jnp.zeros((part.shape[0], h), part.dtype)
    made = []
    for k in range(2):
        one = part[:, k * h : (k + 1) * h]
        made.append(
            jnp.concatenate(
                [jnp.concatenate([one, none], axis=1), jnp.concatenate([none, one], axis=1)], axis=0
            )
        )
    return made


def halves(part):
    h = part.shape[1] // 2
    return part[:, :h], part[:, h:]


def make_table(table_ref, dims):
    _, cap, rows = dims
    me = lax.axis_index("gx")
    lines = rows // cap
    rest = cap % SUB
    half = (cap - rest) * lines
    at_zero = me == 0
    for c in range(cap):
        if c < cap - rest:
            zero = (c, c + half // 2, c, c)
        else:
            h = c - (cap - rest)
            zero = (half + h, half + h + rest, SUB + h, SUB + h + rest)
        if c < rest:
            one = (half + c + rest, half + c, SUB + c, SUB + c + rest)
        else:
            h = c - rest
            one = (h, h + half // 2, h, h)
        for k in range(4):
            table_ref[k, c] = jnp.where(at_zero, zero[k], one[k])


def places(route_ref, where_ref, table_ref, dims, blocks):
    aggregates, _, rows = dims
    me = lax.axis_index("gx")
    sent, kept = jnp.int32(0), jnp.int32(0)
    for i in range(aggregates):
        away = route_ref[0, i] != me
        one = away.astype(jnp.int32)
        c = jnp.where(away, sent, kept)
        sent = sent + one
        kept = kept + (1 - one)
        base = jnp.where(away, 0, blocks * rows)
        where_ref[0, i] = base + table_ref[0, c]
        where_ref[1, i] = base + table_ref[1, c]
        where_ref[2, i] = jnp.where(away, 0, 2 * SUB) + table_ref[2, c]
        where_ref[3, i] = jnp.where(away, 0, 2 * SUB) + table_ref[3, c]
    return sent, kept


def put(total_ref, where_ref, i, block, rows, value):
    n = value.shape[0] // 2
    one = where_ref[0, i] + block * rows
    two = where_ref[1, i] + block * rows
    total_ref[pl.ds(one, n, stride=SUB), :] = value[:n]
    total_ref[pl.ds(two, n, stride=SUB), :] = value[n:]


def finish(outs, total_ref, kind, dims, count):
    _, cap, rows = dims
    rest = cap % SUB
    full = (cap - rest) * (rows // cap)
    me = lax.axis_index("gx")
    line = iota((2 * SUB, LANES), 0)
    in_full = as_bf16(line % SUB + jnp.where(me == 0, 0, rest) < count) > 0.5
    in_half = as_bf16(line % rest + jnp.where(me == 0, cap - rest, 0) < count) > 0.5
    blocks = sum(n for _, n in outs)
    done = 0
    for out, n in outs:
        for k in range(n):
            for at, size, filled in ((0, full, in_full), (full, rows - full, in_half)):
                value = total_ref[pl.ds((kind * blocks + done + k) * rows + at, size), :]
                value = value.astype(jnp.bfloat16).reshape(-1, 2 * SUB, LANES)
                value = jnp.where(filled[None], value, jnp.zeros_like(value))
                out[k * rows + at : k * rows + at + size] = value.reshape(size, LANES)
        done += n


def inner_kernel(
    dims, grid, route_hbm, pair_hbm, p_hbm, a_hbm,
    send_ref, total_ref, keep_codes_ref, zup_ref, zdn_ref, left_ref, a_ref,
    p_ref, route_ref, pair_ref, part_ref, codes_ref, where_ref, table_ref, sems,
):
    px, py, nz = grid
    aggregates, _, rows = dims
    nx, ny = 2 * px, 2 * py
    blk = p_ref.shape[2]
    q = blk // 2
    nb = 5
    copies = [
        pltpu.make_async_copy(one, two, sems.at[k])
        for k, (one, two) in enumerate((
            (p_hbm, p_ref), (route_hbm, route_ref), (pair_hbm, pair_ref),
        ))
    ]
    blocks = [
        pltpu.make_async_copy(a_hbm.at[x], a_ref.at[x], sems.at[3 + x]) for x in range(nx)
    ]
    for copy in copies + blocks:
        copy.start()
    clean, spread = constants(blk)
    masks = even_lanes(q)
    first, second = even_rows(blk)
    codes_ref[...] = jnp.full_like(codes_ref, -1.0)
    make_table(table_ref, dims)
    for copy in copies:
        copy.wait()
    sent, _ = places(route_ref, where_ref, table_ref, dims, nb)
    for i in range(aggregates):
        a, b, z, t = i // (py * nz * 2), (i // (nz * 2)) % py, (i // 2) % nz, i % 2
        code = (2 * (jnp.where(pair_ref[a, b, z] == 0, 2, 1) - t) + z).astype(jnp.float32)
        line = jnp.full((1, LANES), code, jnp.float32)
        codes_ref[pl.ds(where_ref[2, i], 1), :] = line
        codes_ref[pl.ds(where_ref[3, i], 1), :] = line

    pairs = [(x, b) for x in range(nx) for b in range(py)]
    both = {e: pair(p_ref[e[0], 2 * e[1]], p_ref[e[0], 2 * e[1] + 1]) for e in pairs}
    tidy = {e: dot(clean, both[e]).astype(jnp.bfloat16) for e in pairs}
    for x, b in pairs:
        left_ref[x * py + b] = transposed_dot(spread, both[x, b]).astype(jnp.bfloat16)
        zdn_ref[x * py + b] = tidy[x, b][:blk]
        zup_ref[x * py + b] = tidy[x, b][blk:]

    face = p_ref[jnp.where(lax.axis_index("gx") == 0, nx - 1, 0)]
    send_ref[nb * rows + 2 * SUB :] = face.reshape(ny * blk, LANES)
    for copy in blocks:
        copy.wait()

    for x, y in [(x, y) for x in range(nx) for y in range(ny)]:
        here = a_ref.at[x, y]
        along_z = here[6] * first + here[5] * second
        right = jnp.concatenate(
            [pair(here[0], here[2 - x % 2]), pair(here[4 - y % 2], along_z)], axis=1
        )
        left = left_factors(left_ref[x * py + y // 2], y % 2, masks)
        got = dot(left, right).astype(jnp.bfloat16)
        parts = unpair(got[:, : 2 * blk]) + unpair(got[:, 2 * blk :])
        for k in range(4):
            part_ref[x, y, k] = parts[k]

    for a, b in [(a, b) for a in range(px) for b in range(py)]:
        own, with_x, with_y, with_z = {}, {}, {}, {}
        for z, ref in enumerate((zdn_ref, zup_ref)):
            zs, zo = pl.ds(z * q, q), pl.ds((1 - z) * q, q)
            for u in range(2):
                x = 2 * a + u
                weight = weights_of(ref[x * py + b])
                for v in range(2):
                    y = 2 * b + v
                    stack = jnp.concatenate(
                        [
                            part_ref[x, y, 0, zs],
                            part_ref[2 * a + 1 - u, y, 1, zs],
                            part_ref[x, 2 * b + 1 - v, 2, zs],
                            part_ref[x, y, 3, zo],
                        ],
                        axis=0,
                    )
                    got = dot(stack, weight[v])
                    own[u, v, z] = got[:q]
                    with_x[1 - u, v, z] = got[q : 2 * q]
                    with_y[u, 1 - v, z] = got[2 * q : 3 * q]
                    with_z[u, v, 1 - z] = got[3 * q :]
        for z in range(nz):
            flat = pair_ref[a, b, z] == 0
            i = ((a * py + b) * nz + z) * 2
            sums = {}
            for u in range(2):
                for v in range(2):
                    t = u if u == v else jnp.where(flat, v, u)
                    m = u if u == v else jnp.where(flat, u, v)
                    e = (u, v, z)
                    sums[u, v] = own[e] + jnp.where(flat, with_x[e], with_y[e])
                    cross = jnp.where(flat, with_y[e], with_x[e])
                    put(total_ref, where_ref, i + t, 1 + m, rows, cross)
                    put(total_ref, where_ref, i + t, 3 + m, rows, with_z[e])
            put(total_ref, where_ref, i, 0, rows, sums[0, 0] + jnp.where(flat, sums[1, 0], sums[0, 1]))
            put(total_ref, where_ref, i + 1, 0, rows, sums[1, 1] + jnp.where(flat, sums[0, 1], sums[1, 0]))

    finish(((send_ref, nb),), total_ref, 0, dims, sent)
    send_ref[nb * rows : nb * rows + 2 * SUB] = codes_ref[: 2 * SUB].astype(jnp.bfloat16)
    keep_codes_ref[...] = codes_ref[2 * SUB :].astype(jnp.bfloat16)


def faces_kernel(grid, zup_ref, zdn_ref, ya_ref, yb_ref, za_ref, zb_ref):
    px, py, _ = grid
    blk = zup_ref.shape[1]
    y_even, z_even = lax.axis_index("gy") % 2 == 0, lax.axis_index("gz") % 2 == 0

    def plane(a, b, half):
        part = slice(half * blk, (half + 1) * blk)
        rows = [jnp.concatenate([zdn_ref[x * py + b], zup_ref[x * py + b]], axis=0) for x in (2 * a, 2 * a + 1)]
        return jnp.concatenate([row[:, part] for row in rows], axis=1)

    for a in range(px):
        down, up = plane(a, 0, 0), plane(a, py - 1, 1)
        ya_ref[a], yb_ref[a] = jnp.where(y_even, up, down), jnp.where(y_even, down, up)
    for at in range(2 * px * py):
        down, up = zdn_ref[at], zup_ref[at]
        za_ref[at] = jnp.where(z_even, up, down)
        zb_ref[at] = jnp.where(z_even, down, up)


def outer_left_kernel(grid, left_ref, a_ref, part_ref):
    px, py, _ = grid
    nx, ny = 2 * px, 2 * py
    blk = a_ref.shape[3]
    masks = even_lanes(blk // 2)
    first, second = even_rows(blk)
    for x, y in [(x, y) for x in range(nx) for y in range(ny)]:
        here = a_ref.at[x, y]
        along_z = here[5] * first + here[6] * second
        low, high = halves(along_z)
        right = jnp.concatenate(
            [pair(here[1 + x % 2], here[3 + y % 2]), jnp.concatenate([low, high], axis=0)], axis=1
        )
        left = left_factors(left_ref[x * py + y // 2], y % 2, masks)
        got = dot(left, right).astype(jnp.bfloat16)
        part_ref[x, y, 0], part_ref[x, y, 1] = unpair(got[:, : 2 * blk])
        along = got[:, 2 * blk :]
        part_ref[x, y, 2] = jnp.concatenate([along[:blk], along[blk:]], axis=1)


def outer_yz_kernel(
    dims, grid, route_ref, pair_ref, part_ref, zup_ref, zdn_ref, ya_ref, yb_ref, za_ref, zb_ref,
    send_ref, keep_ref, total_ref, where_ref, table_ref,
):
    px, py, nz = grid
    _, _, rows = dims
    nx, ny = 2 * px, 2 * py
    blk = part_ref.shape[3]
    q = blk // 2
    nb = 4
    make_table(table_ref, dims)
    sent, kept = places(route_ref, where_ref, table_ref, dims, nb)
    line = iota((blk, LANES), 0) * 0

    def from_sides(axis, first_ref, second_ref, at, high):
        index = lax.axis_index(axis)
        last = index == lax.axis_size(axis) - 1 if high else index == 0
        by_first = index % 2 == (0 if high else 1)
        kept = line + jnp.where(by_first | ~last, 1, 0) > 0
        value = jnp.where(by_first, first_ref[at], second_ref[at]).astype(jnp.float32)
        return jnp.where(kept, value, 0.0).astype(jnp.bfloat16)

    def beside_y(x, y, z, v):
        to = y - 1 if v == 0 else y + 1
        if 0 <= to < ny:
            return (zdn_ref, zup_ref)[z][x * py + to // 2], to % 2
        at = (x // 2, slice(z * blk, (z + 1) * blk))
        return from_sides("gy", ya_ref, yb_ref, at, v == 1), x % 2

    for x in range(nx):
        made = []
        for b, z in [(b, z) for b in range(py) for z in range(nz)]:
            zs = pl.ds(z * q, q)
            along_z = weights_of(from_sides("gz", za_ref, zb_ref, x * py + b, z == 1))
            for v in range(2):
                y = 2 * b + v
                i, m = of_element(pair_ref, grid, x, y, z)
                other, k = beside_y(x, y, z, v)
                along_y = weights_of(other)[k]
                made.append((i, m, dot(part_ref[x, y, 1, zs], along_y)))
                made.append((i, 2 + m, dot(part_ref[x, y, 2, zs], along_z[v])))
        for i, block, got in made:
            put(total_ref, where_ref, i, block, rows, got)

    for kind, (out, count) in enumerate(((send_ref, sent), (keep_ref, kept))):
        finish(((out, nb),), total_ref, kind, dims, count)


def outer_x_kernel(
    dims, grid, route_ref, pair_ref, part_ref, zup_ref, zdn_ref, early_ref,
    send_one_ref, send_two_ref, keep_ref, total_ref, where_ref, table_ref,
):
    px, py, nz = grid
    _, _, rows = dims
    nx, ny = 2 * px, 2 * py
    blk = part_ref.shape[3]
    q = blk // 2
    nb = 2
    make_table(table_ref, dims)
    sent, kept = places(route_ref, where_ref, table_ref, dims, nb)
    above = iota((2 * blk, LANES), 0) * 0 + lax.axis_index("gx") > 0
    clean, _ = constants(blk)
    face = early_ref.shape[0] - ny * blk
    low, high = [], []
    for b in range(py):
        at = face + 2 * b * blk
        tidy = dot(clean, pair(early_ref[at : at + blk], early_ref[at + blk : at + 2 * blk]))
        low.append(jnp.where(above, tidy, 0.0).astype(jnp.bfloat16))
        high.append(jnp.where(above, 0.0, tidy).astype(jnp.bfloat16))

    for x in range(nx):
        made = []
        for b, z in [(b, z) for b in range(py) for z in range(nz)]:
            zs = pl.ds(z * q, q)
            to = x - 1 if x % 2 == 0 else x + 1
            if 0 <= to < nx:
                part = (zdn_ref, zup_ref)[z][to * py + b]
            else:
                part = (low if to < 0 else high)[b][z * blk : (z + 1) * blk]
            along_x = weights_of(part)
            for v in range(2):
                i, m = of_element(pair_ref, grid, x, 2 * b + v, z)
                made.append((i, m, dot(part_ref[x, 2 * b + v, 0, zs], along_x[v])))
        for i, block, got in made:
            put(total_ref, where_ref, i, block, rows, got)

    finish(((send_one_ref, 1), (send_two_ref, 1)), total_ref, 0, dims, sent)
    finish(((keep_ref, nb),), total_ref, 1, dims, kept)


def of_element(pair_ref, grid, x, y, z):
    _, py, nz = grid
    a, b, u, v = x // 2, y // 2, x % 2, y % 2
    flat = pair_ref[a, b, z] == 0
    t = u if u == v else jnp.where(flat, v, u)
    m = u if u == v else jnp.where(flat, u, v)
    return ((a * py + b) * nz + z) * 2 + t, m


def received(early_ref, rows):
    def early(k, at, size):
        return early_ref[k * rows + at : k * rows + at + size].reshape(-1, 2 * SUB, LANES)

    return early


def placed_blocks(early, x_refs, yz_ref, code, rows, at, size, without_x=True):
    near_low, near_high = (code < 1.5)[None], (code > 3.5)[None]
    upper = ((code == 1.0) | (code == 3.0) | (code == 5.0))[None]

    def tiles(ref, k):
        return ref[k * rows + at : k * rows + at + size].reshape(-1, 2 * SUB, LANES)

    if without_x:
        yield 0, early(0, at, size)
    for m in range(2):
        if m not in x_refs and not without_x:
            continue
        cross, y_out = early(1 + m, at, size), tiles(yz_ref, m)
        if m in x_refs:
            x_out = tiles(*x_refs[m])
            yield 1 + 5 * m, jnp.where(near_low, cross, x_out)
            yield 2 + 5 * m, jnp.where(near_low, x_out, jnp.where(near_high, y_out, cross))
        if without_x:
            z_in, z_out = early(3 + m, at, size), tiles(yz_ref, 2 + m)
            yield 3 + 5 * m, jnp.where(near_high, cross, y_out)
            yield 4 + 5 * m, jnp.where(upper, z_in, z_out)
            yield 5 + 5 * m, jnp.where(upper, z_out, z_in)


def twice(codes):
    return jnp.concatenate([codes, codes], axis=0)


def keep_kernel(dims, total_ref, codes_ref, x_ref, yz_ref, half_ref, out_hbm, full_ref, sem):
    cap, rows = dims
    full = (cap - cap % SUB) * (rows // cap)
    me = lax.axis_index("gx")

    def rounded(code):
        filled = (code > -0.5)[None]

        def early(k, at, size):
            value = total_ref[pl.ds((5 + k) * rows + at, size), :].astype(jnp.bfloat16)
            value = value.reshape(-1, 2 * SUB, LANES)
            return jnp.where(filled, value, jnp.zeros_like(value))

        return early

    copies = []
    code = twice(codes_ref[:SUB])
    for k, value in placed_blocks(rounded(code), {0: (x_ref, 0), 1: (x_ref, 1)}, yz_ref, code, rows, 0, full):
        full_ref[k] = value.reshape(full, LANES)
        to = out_hbm.at[k, pl.ds(me * (2 * full), full), :]
        copies.append(pltpu.make_async_copy(full_ref.at[k], to, sem.at[k]))
        copies[-1].start()
    code = twice(codes_ref[SUB:])
    for k, value in placed_blocks(rounded(code), {0: (x_ref, 0), 1: (x_ref, 1)}, yz_ref, code, rows, full, rows - full):
        half_ref[k] = value.reshape(rows - full, LANES)
    for copy in copies:
        copy.wait()


def take_kernel(dims, member, early_ref, yz_ref, *refs):
    late, (half_ref, _, out_hbm, full_ref, mixed_ref, sem) = refs[: -6], refs[-6:]
    cap, rows = dims
    full = (cap - cap % SUB) * (rows // cap)
    me = lax.axis_index("gx")
    codes = early_ref[5 * rows : 5 * rows + 2 * SUB]
    x_refs = {} if member is None else {member: (late[0], 0)}
    early = received(early_ref, rows)
    copies = []
    for k, value in placed_blocks(
        early, x_refs, yz_ref, twice(codes[:SUB]), rows, 0, full, member is None
    ):
        full_ref[k] = value.reshape(full, LANES)
        to = out_hbm.at[k, pl.ds((1 - me) * (2 * full), full), :]
        copies.append(pltpu.make_async_copy(full_ref.at[k], to, sem.at[0, k]))
        copies[-1].start()
    first_half = (iota((SUB, LANES), 0) < SUB // 2)[None]
    pick = first_half == (me == 0)
    for k, value in placed_blocks(
        early, x_refs, yz_ref, twice(codes[SUB:]), rows, full, rows - full, member is None
    ):
        theirs = value.reshape(rows - full, LANES).astype(jnp.float32).reshape(-1, SUB, LANES)
        mine = half_ref[k].astype(jnp.float32).reshape(-1, SUB, LANES)
        low = jnp.where(pick, mine, theirs)
        high = pltpu.roll(jnp.where(pick, theirs, mine), SUB // 2, 1)
        mixed_ref[k, : rows - full] = low.reshape(rows - full, LANES).astype(jnp.bfloat16)
        mixed_ref[k, rows - full :] = high.reshape(rows - full, LANES).astype(jnp.bfloat16)
        to = out_hbm.at[k, full : 2 * full, :]
        copies.append(pltpu.make_async_copy(mixed_ref.at[k], to, sem.at[1, k]))
        copies[-1].start()
    for copy in copies:
        copy.wait()


SMEM = pl.BlockSpec(memory_space=pltpu.SMEM)
VMEM = pl.BlockSpec(memory_space=pltpu.VMEM)
ANY = pl.BlockSpec(memory_space=pl.ANY)


def bf16(*shape):
    return jax.ShapeDtypeStruct(shape, jnp.bfloat16)


def near(*shape):
    return pltpu.VMEM(shape, jnp.bfloat16)


def held(*arrays):
    return [pltpu.with_memory_space_constraint(one, pltpu.VMEM) for one in arrays]


def swaps(ny, nz):
    def first(i):
        return i + 1 if i % 2 == 0 else i - 1

    def second(i, n):
        j = i - 1 if i % 2 == 0 else i + 1
        return j if 0 <= j < n else None

    made = {"y_a": [], "y_b": [], "z_a": [], "z_b": []}
    for j in range(ny):
        for k in range(nz):
            to_y, to_z = second(j, ny), second(k, nz)
            made["y_a"].append((first(j), k))
            made["z_a"].append((j, first(k)))
            made["y_b"].append((j, first(k)) if to_y is None else (to_y, k))
            made["z_b"].append((first(j), k) if to_z is None else (j, to_z))
    return {name: [(i, j * nz + k) for i, (j, k) in enumerate(to)] for name, to in made.items()}


def local(a_blocks, prolong, pairing, route):
    devices_gx = lax.axis_size("gx")
    aggregates = route.shape[0]
    capacity = max(2, 3 * aggregates // (2 * devices_gx))
    nx, ny, nz, faces, entries = a_blocks.shape
    fits = (
        devices_gx == 2
        and lax.axis_size("gy") % 2 == 0
        and lax.axis_size("gz") % 2 == 0
        and nz == 2
        and nx % 2 == 0
        and ny % 2 == 0
        and faces == 7
        and entries == (LANES // 2) ** 2
        and capacity // SUB == 1
        and capacity % SUB == SUB // 2
    )
    if not fits:
        return general(a_blocks, prolong, pairing, route, capacity)
    px, py = nx // 2, ny // 2
    blk = math.isqrt(entries)
    lines = entries // LANES
    a_view = a_blocks.transpose(0, 1, 3, 2, 4).reshape(nx, ny, faces, nz, lines, LANES)
    a_view = a_view.transpose(0, 1, 2, 4, 3, 5).reshape(nx, ny, faces, nz * lines, LANES)
    p_view = prolong.reshape(nx, ny, nz, lines, LANES).transpose(0, 1, 3, 2, 4)
    p_view = p_view.reshape(nx, ny, nz * lines, LANES)
    route_row = route.reshape(1, aggregates)
    rows = capacity * lines
    dims, grid = (aggregates, capacity, rows), (px, py, nz)
    f32 = jnp.float32
    half_type = jnp.bfloat16
    face_y, face_z = (px, 2 * blk, LANES), (nx * py, blk, LANES)
    parts = (nx, ny, 3, blk, LANES)
    room = pltpu.CompilerParams(vmem_limit_bytes=24 * 2**20)
    cost = pl.CostEstimate(flops=10**9, bytes_accessed=4 * 10**6, transcendentals=0)

    swap = [(0, 1), (1, 0)]
    send_0, total, keep_codes, zup, zdn, left, a_near = pl.pallas_call(
        functools.partial(inner_kernel, dims, grid),
        out_shape=(
            near(5 * rows + 2 * SUB + ny * blk, LANES),
            pltpu.VMEM((10 * rows, LANES), f32),
            near(2 * SUB, LANES),
            near(*face_z),
            near(*face_z),
            near(nx * py, 2 * blk, LANES),
            near(*a_view.shape),
        ),
        in_specs=[ANY] * 4,
        out_specs=[VMEM] * 7,
        scratch_shapes=[
            pltpu.VMEM(p_view.shape, half_type),
            pltpu.SMEM(route_row.shape, jnp.int32),
            pltpu.SMEM(pairing.shape, jnp.int32),
            pltpu.VMEM((nx, ny, 4, blk, LANES), half_type),
            pltpu.VMEM((4 * SUB, LANES), f32),
            pltpu.SMEM((4, aggregates), jnp.int32),
            pltpu.SMEM((4, capacity), jnp.int32),
            pltpu.SemaphoreType.DMA((3 + nx,)),
        ],
        compiler_params=room,
        cost_estimate=cost,
        name="inner_blocks",
    )(*[pltpu.with_memory_space_constraint(one, pltpu.HBM) for one in (route_row, pairing, p_view, a_view)])
    got_0 = lax.ppermute(send_0, "gx", swap)
    zup, zdn = held(zup, zdn)
    ya, yb, za, zb = pl.pallas_call(
        functools.partial(faces_kernel, grid),
        out_shape=(near(*face_y), near(*face_y), near(*face_z), near(*face_z)),
        in_specs=[VMEM] * 2,
        out_specs=[VMEM] * 4,
        compiler_params=room,
        cost_estimate=cost,
        name="faces",
    )(zup, zdn)
    rounds = swaps(lax.axis_size("gy"), lax.axis_size("gz"))
    halos = []
    for name, value in (("y_a", ya), ("y_b", yb), ("z_a", za), ("z_b", zb)):
        halos.append(lax.ppermute(value, ("gy", "gz"), rounds[name]))

    left, a_near = held(left, a_near)
    part = pl.pallas_call(
        functools.partial(outer_left_kernel, grid),
        out_shape=near(*parts),
        in_specs=[VMEM] * 2,
        out_specs=VMEM,
        compiler_params=room,
        cost_estimate=cost,
        name="outer_left",
    )(left, a_near)
    part = held(part)[0]

    def outer(kernel, blocks, sends, *arrays):
        return pl.pallas_call(
            functools.partial(kernel, dims, grid),
            out_shape=(near(blocks // sends * rows, LANES),) * sends
            + (near(blocks * rows, LANES),),
            in_specs=[SMEM, SMEM] + [VMEM] * (3 + len(arrays)),
            out_specs=[VMEM] * (sends + 1),
            scratch_shapes=[
                pltpu.VMEM((2 * blocks * rows, LANES), f32),
                pltpu.SMEM((4, aggregates), jnp.int32),
                pltpu.SMEM((4, capacity), jnp.int32),
            ],
            compiler_params=room,
            cost_estimate=cost,
        )(route_row, pairing, part, zup, zdn, *held(*arrays))

    send_yz, keep_yz = outer(outer_yz_kernel, 4, 1, *halos)
    got_yz = lax.ppermute(send_yz, "gx", swap)
    send_one, send_two, keep_x = outer(outer_x_kernel, 2, 2, got_0)
    got_one = lax.ppermute(send_one, "gx", swap)
    got_two = lax.ppermute(send_two, "gx", swap)

    full = (capacity // SUB) * SUB * lines
    whole = 2 * rows
    half, out = pl.pallas_call(
        functools.partial(keep_kernel, (capacity, rows)),
        out_shape=(near(11, rows - full, LANES), bf16(11, whole, LANES)),
        in_specs=[VMEM] * 4,
        out_specs=[VMEM, ANY],
        scratch_shapes=[pltpu.VMEM((11, full, LANES), half_type), pltpu.SemaphoreType.DMA((11,))],
        compiler_params=room,
        cost_estimate=cost,
        name="place_kept",
    )(*held(total, keep_codes, keep_x, keep_yz))
    for member, late in ((None, (got_yz,)), (0, (got_yz, got_one)), (1, (got_yz, got_two))):
        out = pl.pallas_call(
            functools.partial(take_kernel, (capacity, rows), member),
            out_shape=bf16(11, whole, LANES),
            in_specs=[VMEM] * (2 + len(late)) + [ANY],
            out_specs=ANY,
            input_output_aliases={2 + len(late): 0},
            scratch_shapes=[
                pltpu.VMEM((11, full, LANES), half_type),
                pltpu.VMEM((11, full, LANES), half_type),
                pltpu.SemaphoreType.DMA((2, 11)),
            ],
            compiler_params=room,
            cost_estimate=cost,
        )(*held(got_0, *late, half), out)
    out = out.reshape(11, whole // (SUB * lines), lines, SUB, LANES).transpose(1, 3, 0, 2, 4)
    return out.reshape(2 * capacity, 11, entries)


def solution(mesh):
    placed = (
        P("gx", "gy", "gz", None, None),
        P("gx", "gy", "gz", None),
        P("gx", "gy", "gz"),
        P(("gx", "gy", "gz"), None),
    )
    return jax.shard_map(
        local,
        mesh=mesh,
        in_specs=placed,
        out_specs=P(("gx", "gy", "gz"), None, None),
        check_vma=False,
    )
```

```python
import functools
import math

import jax
import jax.numpy as jnp
from jax import lax
from jax.experimental import pallas as pl
from jax.experimental.pallas import tpu as pltpu
from jax.sharding import PartitionSpec as P


x_first_order = [0, 2, 1, 3, 4, 5, 6]
x_second_order = [0, 1, 2, 3, 4, 5, 6]
y_first_order = [0, 4, 1, 2, 3, 5, 6]
y_second_order = [0, 3, 1, 2, 4, 5, 6]

LANES = 128
SUB = 8


def padded_2(array, sides, width):
    for axis, dim in sides:
        devices, length = (lax.axis_size(axis), array.shape[dim])
        up = [(i, (i + 1) % devices) for i in range(devices - 1)]
        down = [(j, i) for i, j in up]
        last = lax.slice_in_dim(array, length - width, length, axis=dim)
        initial = lax.slice_in_dim(array, 0, width, axis=dim)
        before = lax.ppermute(last, axis, up)
        after = lax.ppermute(initial, axis, down)
        array = jnp.concatenate([before, array, after], axis=dim)
    return array


def neighbours(padded):
    shifted = [
        padded[1:-1, 1:-1, 1:-1],
        padded[:-2, 1:-1, 1:-1],
        padded[2:, 1:-1, 1:-1],
        padded[1:-1, :-2, 1:-1],
        padded[1:-1, 2:, 1:-1],
        padded[1:-1, 1:-1, :-2],
        padded[1:-1, 1:-1, 2:],
    ]
    return jnp.stack(shifted, axis=3)


def triple(blocks, nearby):
    block_side = math.isqrt(blocks.shape[-1])
    leading = blocks.shape[:-1]
    left_mat = blocks.reshape(leading + (block_side, block_side))
    right_mat = nearby.reshape(leading + (block_side, block_side))
    own_block = jnp.swapaxes(right_mat[..., :1, :, :], -1, -2)
    product = jnp.matmul(left_mat, right_mat, preferred_element_type=jnp.float32).astype(
        jnp.bfloat16
    )
    result = jnp.matmul(own_block, product, preferred_element_type=jnp.float32)
    return result.reshape(leading + (block_side * block_side,))


def members(element_grid, pairs):
    size_x, size_y, size_z = element_grid.shape[:3]
    trailing = element_grid.shape[3:]
    patches = element_grid.reshape((size_x // 2, 2, size_y // 2, 2, size_z) + trailing)

    def pick(upper, lower, slot_order):
        return jnp.take(patches[:, upper, :, lower], jnp.array(slot_order, dtype=jnp.int32), axis=3)

    x_one = jnp.stack([pick(0, 0, x_first_order), pick(0, 1, x_first_order)], axis=3)
    x_two = jnp.stack([pick(1, 0, x_second_order), pick(1, 1, x_second_order)], axis=3)
    y_one = jnp.stack([pick(0, 0, y_first_order), pick(1, 0, y_first_order)], axis=3)
    y_two = jnp.stack([pick(0, 1, y_second_order), pick(1, 1, y_second_order)], axis=3)
    along_x = (pairs == 0).reshape(pairs.shape + (1,) * (x_one.ndim - 3))
    member_one = jnp.where(along_x, x_one, y_one)
    member_two = jnp.where(along_x, x_two, y_two)
    return (
        member_one.reshape((-1,) + member_one.shape[4:]),
        member_two.reshape((-1,) + member_two.shape[4:]),
    )


def arrange(member_one, member_two):
    diagonal = (
        member_one[..., 0, :]
        + member_two[..., 0, :]
        + member_one[..., 1, :]
        + member_two[..., 1, :]
    )
    return jnp.concatenate(
        [diagonal[..., None, :], member_one[..., 2:, :], member_two[..., 2:, :]], axis=-2
    )


def slot_sources(routes, n_dest, capacity):
    total = routes.shape[0]
    chosen = (routes[:, None] == jnp.arange(n_dest, dtype=jnp.int32)[None, :]).astype(jnp.int32)
    before = jnp.cumsum(chosen, axis=0) - chosen
    ranking = jnp.sum(before * chosen, axis=1)
    position = routes * capacity + ranking
    targets = jnp.arange(n_dest * capacity, dtype=jnp.int32)
    matches = position[None, :] == targets[:, None]
    anchor = jnp.sum(jnp.where(matches, jnp.arange(total, dtype=jnp.int32)[None, :], 0), axis=1)
    filled = jnp.any(matches, axis=1)
    return (anchor, filled)


def pack_slots(payload, anchor, filled):
    taken = jnp.take(payload, anchor, axis=0)
    keep_row = filled.reshape(filled.shape + (1,) * (payload.ndim - 1))
    return jnp.where(keep_row, taken, jnp.zeros_like(taken))


def general(a_blocks, prolong, pairing, route, capacity):
    padded = padded_2(prolong, (("gx", 0), ("gy", 1), ("gz", 2)), 1)
    nearby = neighbours(padded)
    anchor, filled = slot_sources(route[:, 0], lax.axis_size("gx"), capacity)
    galerkin = triple(a_blocks, nearby)
    member_one, member_two = members(galerkin, pairing)
    coarse = arrange(member_one, member_two).astype(jnp.bfloat16)
    return lax.all_to_all(
        pack_slots(coarse, anchor, filled), "gx", split_axis=0, concat_axis=0, tiled=True
    )


def dot(left, right):
    return jnp.dot(left, right, preferred_element_type=jnp.float32)


def iota(shape, axis):
    return lax.broadcasted_iota(jnp.int32, shape, axis)


def as_bf16(mask):
    return mask.astype(jnp.float32).astype(jnp.bfloat16)


def pair(one, two):
    h = one.shape[1] // 2
    low = jnp.concatenate([one[:, :h], two[:, :h]], axis=1)
    high = jnp.concatenate([one[:, h:], two[:, h:]], axis=1)
    return jnp.concatenate([low, high], axis=0)


def unpair(both):
    rows, h = both.shape[0] // 2, both.shape[1] // 2
    even, odd = both[:rows], both[rows:]
    return (
        jnp.concatenate([even[:, :h], odd[:, :h]], axis=1),
        jnp.concatenate([even[:, h:], odd[:, h:]], axis=1),
    )


def constants(blk):
    n = 2 * blk
    row, col = iota((n, n), 0), iota((n, n), 1)
    c, z = row % blk, row // blk
    clean = as_bf16(col == (c % 2) * blk + (c // 2) * 2 + z)
    q = blk // 2
    k, p = row // blk, (row // q) % 2
    spread = as_bf16(col == k * blk + 2 * (row % q) + p)
    return clean, spread


def even_lanes(rows):
    return as_bf16(iota((rows, LANES), 1) % 2 == 0), as_bf16(iota((rows, LANES), 1) % 2 == 1)


def even_rows(rows):
    return as_bf16(iota((rows, LANES), 0) % 2 == 0), as_bf16(iota((rows, LANES), 0) % 2 == 1)


def transposed_dot(left, right):
    return lax.dot_general(
        left, right, (((1,), (1,)), ((), ())), preferred_element_type=jnp.float32
    )


def left_factors(both_t, k, masks):
    q = masks[0].shape[0]
    parts = [both_t[(2 * k + p) * q : (2 * k + p + 1) * q] for p in range(2)]
    return jnp.concatenate([part * mask for part in parts for mask in masks], axis=0)


def weights_of(part):
    h = part.shape[1] // 2
    none = jnp.zeros((part.shape[0], h), part.dtype)
    made = []
    for k in range(2):
        one = part[:, k * h : (k + 1) * h]
        made.append(
            jnp.concatenate(
                [jnp.concatenate([one, none], axis=1), jnp.concatenate([none, one], axis=1)], axis=0
            )
        )
    return made


def halves(part):
    h = part.shape[1] // 2
    return part[:, :h], part[:, h:]


def make_table(table_ref, dims):
    _, cap, rows = dims
    me = lax.axis_index("gx")
    lines = rows // cap
    rest = cap % SUB
    half = (cap - rest) * lines
    at_zero = me == 0
    for c in range(cap):
        if c < cap - rest:
            zero = (c, c + half // 2, c, c)
        else:
            h = c - (cap - rest)
            zero = (half + h, half + h + rest, SUB + h, SUB + h + rest)
        if c < rest:
            one = (half + c + rest, half + c, SUB + c, SUB + c + rest)
        else:
            h = c - rest
            one = (h, h + half // 2, h, h)
        for k in range(4):
            table_ref[k, c] = jnp.where(at_zero, zero[k], one[k])


def places(route_ref, where_ref, table_ref, dims, blocks):
    aggregates, _, rows = dims
    me = lax.axis_index("gx")
    sent, kept = jnp.int32(0), jnp.int32(0)
    for i in range(aggregates):
        away = route_ref[0, i] != me
        one = away.astype(jnp.int32)
        c = jnp.where(away, sent, kept)
        sent = sent + one
        kept = kept + (1 - one)
        base = jnp.where(away, 0, blocks * rows)
        where_ref[0, i] = base + table_ref[0, c]
        where_ref[1, i] = base + table_ref[1, c]
        where_ref[2, i] = jnp.where(away, 0, 2 * SUB) + table_ref[2, c]
        where_ref[3, i] = jnp.where(away, 0, 2 * SUB) + table_ref[3, c]
    return sent, kept


def put(total_ref, where_ref, i, block, rows, value):
    n = value.shape[0] // 2
    one = where_ref[0, i] + block * rows
    two = where_ref[1, i] + block * rows
    total_ref[pl.ds(one, n, stride=SUB), :] = value[:n]
    total_ref[pl.ds(two, n, stride=SUB), :] = value[n:]


def finish(outs, total_ref, kind, dims, count):
    _, cap, rows = dims
    rest = cap % SUB
    full = (cap - rest) * (rows // cap)
    me = lax.axis_index("gx")
    line = iota((2 * SUB, LANES), 0)
    in_full = as_bf16(line % SUB + jnp.where(me == 0, 0, rest) < count) > 0.5
    in_half = as_bf16(line % rest + jnp.where(me == 0, cap - rest, 0) < count) > 0.5
    blocks = sum(n for _, n in outs)
    done = 0
    for out, n in outs:
        for k in range(n):
            for at, size, filled in ((0, full, in_full), (full, rows - full, in_half)):
                value = total_ref[pl.ds((kind * blocks + done + k) * rows + at, size), :]
                value = value.astype(jnp.bfloat16).reshape(-1, 2 * SUB, LANES)
                value = jnp.where(filled[None], value, jnp.zeros_like(value))
                out[k * rows + at : k * rows + at + size] = value.reshape(size, LANES)
        done += n


def inner_kernel(
    dims, grid, route_hbm, pair_hbm, p_hbm, a_hbm,
    send_ref, total_ref, keep_codes_ref, zup_ref, zdn_ref, left_ref, a_ref,
    p_ref, route_ref, pair_ref, part_ref, codes_ref, where_ref, table_ref, sems,
):
    px, py, nz = grid
    aggregates, _, rows = dims
    nx, ny = 2 * px, 2 * py
    blk = p_ref.shape[2]
    q = blk // 2
    nb = 5
    copies = [
        pltpu.make_async_copy(one, two, sems.at[k])
        for k, (one, two) in enumerate((
            (p_hbm, p_ref), (route_hbm, route_ref), (pair_hbm, pair_ref),
        ))
    ]
    blocks = [
        pltpu.make_async_copy(a_hbm.at[x], a_ref.at[x], sems.at[3 + x]) for x in range(nx)
    ]
    for copy in copies + blocks:
        copy.start()
    clean, spread = constants(blk)
    masks = even_lanes(q)
    first, second = even_rows(blk)
    codes_ref[...] = jnp.full_like(codes_ref, -1.0)
    make_table(table_ref, dims)
    copies[0].wait()
    pairs = [(x, b) for x in range(nx) for b in range(py)]
    both = {e: pair(p_ref[e[0], 2 * e[1]], p_ref[e[0], 2 * e[1] + 1]) for e in pairs}
    tidy = {e: dot(clean, both[e]).astype(jnp.bfloat16) for e in pairs}
    for x, b in pairs:
        left_ref[x * py + b] = transposed_dot(spread, both[x, b]).astype(jnp.bfloat16)
        zdn_ref[x * py + b] = tidy[x, b][:blk]
        zup_ref[x * py + b] = tidy[x, b][blk:]

    face = p_ref[jnp.where(lax.axis_index("gx") == 0, nx - 1, 0)]
    send_ref[nb * rows + 2 * SUB :] = face.reshape(ny * blk, LANES)
    for copy in copies[1:] + blocks:
        copy.wait()
    sent, _ = places(route_ref, where_ref, table_ref, dims, nb)
    for i in range(aggregates):
        a, b, z, t = i // (py * nz * 2), (i // (nz * 2)) % py, (i // 2) % nz, i % 2
        code = (2 * (jnp.where(pair_ref[a, b, z] == 0, 2, 1) - t) + z).astype(jnp.float32)
        line = jnp.full((1, LANES), code, jnp.float32)
        codes_ref[pl.ds(where_ref[2, i], 1), :] = line
        codes_ref[pl.ds(where_ref[3, i], 1), :] = line

    for x, y in [(x, y) for x in range(nx) for y in range(ny)]:
        here = a_ref.at[x, y]
        along_z = here[6] * first + here[5] * second
        right = jnp.concatenate(
            [pair(here[0], here[2 - x % 2]), pair(here[4 - y % 2], along_z)], axis=1
        )
        left = left_factors(left_ref[x * py + y // 2], y % 2, masks)
        got = dot(left, right).astype(jnp.bfloat16)
        parts = unpair(got[:, : 2 * blk]) + unpair(got[:, 2 * blk :])
        for k in range(4):
            part_ref[x, y, k] = parts[k]

    for a, b in [(a, b) for a in range(px) for b in range(py)]:
        own, with_x, with_y, with_z = {}, {}, {}, {}
        for z, ref in enumerate((zdn_ref, zup_ref)):
            zs, zo = pl.ds(z * q, q), pl.ds((1 - z) * q, q)
            for u in range(2):
                x = 2 * a + u
                weight = weights_of(ref[x * py + b])
                for v in range(2):
                    y = 2 * b + v
                    stack = jnp.concatenate(
                        [
                            part_ref[x, y, 0, zs],
                            part_ref[2 * a + 1 - u, y, 1, zs],
                            part_ref[x, 2 * b + 1 - v, 2, zs],
                            part_ref[x, y, 3, zo],
                        ],
                        axis=0,
                    )
                    got = dot(stack, weight[v])
                    own[u, v, z] = got[:q]
                    with_x[1 - u, v, z] = got[q : 2 * q]
                    with_y[u, 1 - v, z] = got[2 * q : 3 * q]
                    with_z[u, v, 1 - z] = got[3 * q :]
        for z in range(nz):
            flat = pair_ref[a, b, z] == 0
            i = ((a * py + b) * nz + z) * 2
            sums = {}
            for u in range(2):
                for v in range(2):
                    t = u if u == v else jnp.where(flat, v, u)
                    m = u if u == v else jnp.where(flat, u, v)
                    e = (u, v, z)
                    sums[u, v] = own[e] + jnp.where(flat, with_x[e], with_y[e])
                    cross = jnp.where(flat, with_y[e], with_x[e])
                    put(total_ref, where_ref, i + t, 1 + m, rows, cross)
                    put(total_ref, where_ref, i + t, 3 + m, rows, with_z[e])
            put(total_ref, where_ref, i, 0, rows, sums[0, 0] + jnp.where(flat, sums[1, 0], sums[0, 1]))
            put(total_ref, where_ref, i + 1, 0, rows, sums[1, 1] + jnp.where(flat, sums[0, 1], sums[1, 0]))

    finish(((send_ref, nb),), total_ref, 0, dims, sent)
    send_ref[nb * rows : nb * rows + 2 * SUB] = codes_ref[: 2 * SUB].astype(jnp.bfloat16)
    keep_codes_ref[...] = codes_ref[2 * SUB :].astype(jnp.bfloat16)


def faces_kernel(grid, zup_ref, zdn_ref, ya_ref, yb_ref, za_ref, zb_ref):
    px, py, _ = grid
    blk = zup_ref.shape[1]
    y_even, z_even = lax.axis_index("gy") % 2 == 0, lax.axis_index("gz") % 2 == 0

    def plane(a, b, half):
        part = slice(half * blk, (half + 1) * blk)
        rows = [jnp.concatenate([zdn_ref[x * py + b], zup_ref[x * py + b]], axis=0) for x in (2 * a, 2 * a + 1)]
        return jnp.concatenate([row[:, part] for row in rows], axis=1)

    for a in range(px):
        down, up = plane(a, 0, 0), plane(a, py - 1, 1)
        ya_ref[a], yb_ref[a] = jnp.where(y_even, up, down), jnp.where(y_even, down, up)
    for at in range(2 * px * py):
        down, up = zdn_ref[at], zup_ref[at]
        za_ref[at] = jnp.where(z_even, up, down)
        zb_ref[at] = jnp.where(z_even, down, up)


def outer_left_kernel(grid, left_ref, a_ref, part_ref):
    px, py, _ = grid
    nx, ny = 2 * px, 2 * py
    blk = a_ref.shape[3]
    masks = even_lanes(blk // 2)
    first, second = even_rows(blk)
    for x, y in [(x, y) for x in range(nx) for y in range(ny)]:
        here = a_ref.at[x, y]
        along_z = here[5] * first + here[6] * second
        low, high = halves(along_z)
        right = jnp.concatenate(
            [pair(here[1 + x % 2], here[3 + y % 2]), jnp.concatenate([low, high], axis=0)], axis=1
        )
        left = left_factors(left_ref[x * py + y // 2], y % 2, masks)
        got = dot(left, right).astype(jnp.bfloat16)
        part_ref[x, y, 0], part_ref[x, y, 1] = unpair(got[:, : 2 * blk])
        along = got[:, 2 * blk :]
        part_ref[x, y, 2] = jnp.concatenate([along[:blk], along[blk:]], axis=1)


def outer_yz_kernel(
    dims, grid, route_ref, pair_ref, part_ref, zup_ref, zdn_ref, ya_ref, yb_ref, za_ref, zb_ref,
    send_ref, keep_ref, total_ref, where_ref, table_ref,
):
    px, py, nz = grid
    _, _, rows = dims
    nx, ny = 2 * px, 2 * py
    blk = part_ref.shape[3]
    q = blk // 2
    nb = 4
    make_table(table_ref, dims)
    sent, kept = places(route_ref, where_ref, table_ref, dims, nb)
    line = iota((blk, LANES), 0) * 0

    def from_sides(axis, first_ref, second_ref, at, high):
        index = lax.axis_index(axis)
        last = index == lax.axis_size(axis) - 1 if high else index == 0
        by_first = index % 2 == (0 if high else 1)
        kept = line + jnp.where(by_first | ~last, 1, 0) > 0
        value = jnp.where(by_first, first_ref[at], second_ref[at]).astype(jnp.float32)
        return jnp.where(kept, value, 0.0).astype(jnp.bfloat16)

    def beside_y(x, y, z, v):
        to = y - 1 if v == 0 else y + 1
        if 0 <= to < ny:
            return (zdn_ref, zup_ref)[z][x * py + to // 2], to % 2
        at = (x // 2, slice(z * blk, (z + 1) * blk))
        return from_sides("gy", ya_ref, yb_ref, at, v == 1), x % 2

    for x in range(nx):
        made = []
        for b, z in [(b, z) for b in range(py) for z in range(nz)]:
            zs = pl.ds(z * q, q)
            along_z = weights_of(from_sides("gz", za_ref, zb_ref, x * py + b, z == 1))
            for v in range(2):
                y = 2 * b + v
                i, m = of_element(pair_ref, grid, x, y, z)
                other, k = beside_y(x, y, z, v)
                along_y = weights_of(other)[k]
                made.append((i, m, dot(part_ref[x, y, 1, zs], along_y)))
                made.append((i, 2 + m, dot(part_ref[x, y, 2, zs], along_z[v])))
        for i, block, got in made:
            put(total_ref, where_ref, i, block, rows, got)

    for kind, (out, count) in enumerate(((send_ref, sent), (keep_ref, kept))):
        finish(((out, nb),), total_ref, kind, dims, count)


def outer_x_kernel(
    dims, grid, route_ref, pair_ref, part_ref, zup_ref, zdn_ref, early_ref,
    send_ref, keep_ref, total_ref, where_ref, table_ref,
):
    px, py, nz = grid
    _, _, rows = dims
    nx, ny = 2 * px, 2 * py
    blk = part_ref.shape[3]
    q = blk // 2
    nb = 2
    make_table(table_ref, dims)
    sent, kept = places(route_ref, where_ref, table_ref, dims, nb)
    above = iota((2 * blk, LANES), 0) * 0 + lax.axis_index("gx") > 0
    clean, _ = constants(blk)
    face = early_ref.shape[0] - ny * blk
    low, high = [], []
    for b in range(py):
        at = face + 2 * b * blk
        tidy = dot(clean, pair(early_ref[at : at + blk], early_ref[at + blk : at + 2 * blk]))
        low.append(jnp.where(above, tidy, 0.0).astype(jnp.bfloat16))
        high.append(jnp.where(above, 0.0, tidy).astype(jnp.bfloat16))

    for x in range(nx):
        made = []
        for b, z in [(b, z) for b in range(py) for z in range(nz)]:
            zs = pl.ds(z * q, q)
            to = x - 1 if x % 2 == 0 else x + 1
            if 0 <= to < nx:
                part = (zdn_ref, zup_ref)[z][to * py + b]
            else:
                part = (low if to < 0 else high)[b][z * blk : (z + 1) * blk]
            along_x = weights_of(part)
            for v in range(2):
                i, m = of_element(pair_ref, grid, x, 2 * b + v, z)
                made.append((i, m, dot(part_ref[x, 2 * b + v, 0, zs], along_x[v])))
        for i, block, got in made:
            put(total_ref, where_ref, i, block, rows, got)

    for kind, (out, count) in enumerate(((send_ref, sent), (keep_ref, kept))):
        finish(((out, nb),), total_ref, kind, dims, count)


def of_element(pair_ref, grid, x, y, z):
    _, py, nz = grid
    a, b, u, v = x // 2, y // 2, x % 2, y % 2
    flat = pair_ref[a, b, z] == 0
    t = u if u == v else jnp.where(flat, v, u)
    m = u if u == v else jnp.where(flat, u, v)
    return ((a * py + b) * nz + z) * 2 + t, m


def received(early_ref, rows):
    def early(k, at, size):
        return early_ref[k * rows + at : k * rows + at + size].reshape(-1, 2 * SUB, LANES)

    return early


def placed_blocks(early, x_ref, yz_ref, code, rows, at, size, without_x=True):
    near_low, near_high = (code < 1.5)[None], (code > 3.5)[None]
    upper = ((code == 1.0) | (code == 3.0) | (code == 5.0))[None]

    def tiles(ref, k):
        return ref[k * rows + at : k * rows + at + size].reshape(-1, 2 * SUB, LANES)

    if without_x:
        yield 0, early(0, at, size)
    for m in range(2):
        cross, y_out = early(1 + m, at, size), tiles(yz_ref, m)
        if x_ref is not None:
            x_out = tiles(x_ref, m)
            yield 1 + 5 * m, jnp.where(near_low, cross, x_out)
            yield 2 + 5 * m, jnp.where(near_low, x_out, jnp.where(near_high, y_out, cross))
        if without_x:
            z_in, z_out = early(3 + m, at, size), tiles(yz_ref, 2 + m)
            yield 3 + 5 * m, jnp.where(near_high, cross, y_out)
            yield 4 + 5 * m, jnp.where(upper, z_in, z_out)
            yield 5 + 5 * m, jnp.where(upper, z_out, z_in)


def twice(codes):
    return jnp.concatenate([codes, codes], axis=0)


def keep_kernel(dims, total_ref, codes_ref, x_ref, yz_ref, half_ref, out_hbm, full_ref, sem):
    cap, rows = dims
    full = (cap - cap % SUB) * (rows // cap)
    me = lax.axis_index("gx")

    def rounded(code):
        filled = (code > -0.5)[None]

        def early(k, at, size):
            value = total_ref[pl.ds((5 + k) * rows + at, size), :].astype(jnp.bfloat16)
            value = value.reshape(-1, 2 * SUB, LANES)
            return jnp.where(filled, value, jnp.zeros_like(value))

        return early

    copies = []
    code = twice(codes_ref[:SUB])
    for k, value in placed_blocks(rounded(code), x_ref, yz_ref, code, rows, 0, full):
        full_ref[k] = value.reshape(full, LANES)
        to = out_hbm.at[k, pl.ds(me * (2 * full), full), :]
        copies.append(pltpu.make_async_copy(full_ref.at[k], to, sem.at[k]))
        copies[-1].start()
    code = twice(codes_ref[SUB:])
    for k, value in placed_blocks(rounded(code), x_ref, yz_ref, code, rows, full, rows - full):
        half_ref[k] = value.reshape(rows - full, LANES)
    for copy in copies:
        copy.wait()


def take_kernel(dims, with_x, early_ref, *refs):
    late, (half_ref, _, out_hbm, full_ref, mixed_ref, sem) = refs[: -6], refs[-6:]
    cap, rows = dims
    full = (cap - cap % SUB) * (rows // cap)
    me = lax.axis_index("gx")
    codes = early_ref[5 * rows : 5 * rows + 2 * SUB]
    x_ref, yz_ref = late if with_x else (None, late[0])
    early = received(early_ref, rows)
    copies = []
    for k, value in placed_blocks(early, x_ref, yz_ref, twice(codes[:SUB]), rows, 0, full, not with_x):
        full_ref[k] = value.reshape(full, LANES)
        to = out_hbm.at[k, pl.ds((1 - me) * (2 * full), full), :]
        copies.append(pltpu.make_async_copy(full_ref.at[k], to, sem.at[0, k]))
        copies[-1].start()
    first_half = (iota((SUB, LANES), 0) < SUB // 2)[None]
    pick = first_half == (me == 0)
    for k, value in placed_blocks(
        early, x_ref, yz_ref, twice(codes[SUB:]), rows, full, rows - full, not with_x
    ):
        theirs = value.reshape(rows - full, LANES).astype(jnp.float32).reshape(-1, SUB, LANES)
        mine = half_ref[k].astype(jnp.float32).reshape(-1, SUB, LANES)
        low = jnp.where(pick, mine, theirs)
        high = pltpu.roll(jnp.where(pick, theirs, mine), SUB // 2, 1)
        mixed_ref[k, : rows - full] = low.reshape(rows - full, LANES).astype(jnp.bfloat16)
        mixed_ref[k, rows - full :] = high.reshape(rows - full, LANES).astype(jnp.bfloat16)
        to = out_hbm.at[k, full : 2 * full, :]
        copies.append(pltpu.make_async_copy(mixed_ref.at[k], to, sem.at[1, k]))
        copies[-1].start()
    for copy in copies:
        copy.wait()


SMEM = pl.BlockSpec(memory_space=pltpu.SMEM)
VMEM = pl.BlockSpec(memory_space=pltpu.VMEM)
ANY = pl.BlockSpec(memory_space=pl.ANY)


def bf16(*shape):
    return jax.ShapeDtypeStruct(shape, jnp.bfloat16)


def near(*shape):
    return pltpu.VMEM(shape, jnp.bfloat16)


def held(*arrays):
    return [pltpu.with_memory_space_constraint(one, pltpu.VMEM) for one in arrays]


def swaps(ny, nz):
    def first(i):
        return i + 1 if i % 2 == 0 else i - 1

    def second(i, n):
        j = i - 1 if i % 2 == 0 else i + 1
        return j if 0 <= j < n else None

    made = {"y_a": [], "y_b": [], "z_a": [], "z_b": []}
    for j in range(ny):
        for k in range(nz):
            to_y, to_z = second(j, ny), second(k, nz)
            made["y_a"].append((first(j), k))
            made["z_a"].append((j, first(k)))
            made["y_b"].append((j, first(k)) if to_y is None else (to_y, k))
            made["z_b"].append((first(j), k) if to_z is None else (j, to_z))
    return {name: [(i, j * nz + k) for i, (j, k) in enumerate(to)] for name, to in made.items()}


def local(a_blocks, prolong, pairing, route):
    devices_gx = lax.axis_size("gx")
    aggregates = route.shape[0]
    capacity = max(2, 3 * aggregates // (2 * devices_gx))
    nx, ny, nz, faces, entries = a_blocks.shape
    fits = (
        devices_gx == 2
        and lax.axis_size("gy") % 2 == 0
        and lax.axis_size("gz") % 2 == 0
        and nz == 2
        and nx % 2 == 0
        and ny % 2 == 0
        and faces == 7
        and entries == (LANES // 2) ** 2
        and capacity // SUB == 1
        and capacity % SUB == SUB // 2
    )
    if not fits:
        return general(a_blocks, prolong, pairing, route, capacity)
    px, py = nx // 2, ny // 2
    blk = math.isqrt(entries)
    lines = entries // LANES
    a_view = a_blocks.transpose(0, 1, 3, 2, 4).reshape(nx, ny, faces, nz, lines, LANES)
    a_view = a_view.transpose(0, 1, 2, 4, 3, 5).reshape(nx, ny, faces, nz * lines, LANES)
    p_view = prolong.reshape(nx, ny, nz, lines, LANES).transpose(0, 1, 3, 2, 4)
    p_view = p_view.reshape(nx, ny, nz * lines, LANES)
    route_row = route.reshape(1, aggregates)
    rows = capacity * lines
    dims, grid = (aggregates, capacity, rows), (px, py, nz)
    f32 = jnp.float32
    half_type = jnp.bfloat16
    face_y, face_z = (px, 2 * blk, LANES), (nx * py, blk, LANES)
    parts = (nx, ny, 3, blk, LANES)
    room = pltpu.CompilerParams(vmem_limit_bytes=24 * 2**20)
    cost = pl.CostEstimate(flops=10**9, bytes_accessed=4 * 10**6, transcendentals=0)

    swap = [(0, 1), (1, 0)]
    send_0, total, keep_codes, zup, zdn, left, a_near = pl.pallas_call(
        functools.partial(inner_kernel, dims, grid),
        out_shape=(
            near(5 * rows + 2 * SUB + ny * blk, LANES),
            pltpu.VMEM((10 * rows, LANES), f32),
            near(2 * SUB, LANES),
            near(*face_z),
            near(*face_z),
            near(nx * py, 2 * blk, LANES),
            near(*a_view.shape),
        ),
        in_specs=[ANY] * 4,
        out_specs=[VMEM] * 7,
        scratch_shapes=[
            pltpu.VMEM(p_view.shape, half_type),
            pltpu.SMEM(route_row.shape, jnp.int32),
            pltpu.SMEM(pairing.shape, jnp.int32),
            pltpu.VMEM((nx, ny, 4, blk, LANES), half_type),
            pltpu.VMEM((4 * SUB, LANES), f32),
            pltpu.SMEM((4, aggregates), jnp.int32),
            pltpu.SMEM((4, capacity), jnp.int32),
            pltpu.SemaphoreType.DMA((3 + nx,)),
        ],
        compiler_params=room,
        cost_estimate=cost,
        name="inner_blocks",
    )(*[pltpu.with_memory_space_constraint(one, pltpu.HBM) for one in (route_row, pairing, p_view, a_view)])
    got_0 = lax.ppermute(send_0, "gx", swap)
    zup, zdn = held(zup, zdn)
    ya, yb, za, zb = pl.pallas_call(
        functools.partial(faces_kernel, grid),
        out_shape=(near(*face_y), near(*face_y), near(*face_z), near(*face_z)),
        in_specs=[VMEM] * 2,
        out_specs=[VMEM] * 4,
        compiler_params=room,
        cost_estimate=cost,
        name="faces",
    )(zup, zdn)
    rounds = swaps(lax.axis_size("gy"), lax.axis_size("gz"))
    halos = []
    for name, value in (("y_a", ya), ("y_b", yb), ("z_a", za), ("z_b", zb)):
        halos.append(lax.ppermute(value, ("gy", "gz"), rounds[name]))

    left, a_near = held(left, a_near)
    part = pl.pallas_call(
        functools.partial(outer_left_kernel, grid),
        out_shape=near(*parts),
        in_specs=[VMEM] * 2,
        out_specs=VMEM,
        compiler_params=room,
        cost_estimate=cost,
        name="outer_left",
    )(left, a_near)
    part = held(part)[0]

    def outer(kernel, blocks, *arrays):
        return pl.pallas_call(
            functools.partial(kernel, dims, grid),
            out_shape=(near(blocks * rows, LANES),) * 2,
            in_specs=[SMEM, SMEM] + [VMEM] * (3 + len(arrays)),
            out_specs=[VMEM] * 2,
            scratch_shapes=[
                pltpu.VMEM((2 * blocks * rows, LANES), f32),
                pltpu.SMEM((4, aggregates), jnp.int32),
                pltpu.SMEM((4, capacity), jnp.int32),
            ],
            compiler_params=room,
            cost_estimate=cost,
        )(route_row, pairing, part, zup, zdn, *held(*arrays))

    send_yz, keep_yz = outer(outer_yz_kernel, 4, *halos)
    got_yz = lax.ppermute(send_yz, "gx", swap)
    send_x, keep_x = outer(outer_x_kernel, 2, got_0)
    got_x = lax.ppermute(send_x, "gx", swap)

    full = (capacity // SUB) * SUB * lines
    whole = 2 * rows
    half, out = pl.pallas_call(
        functools.partial(keep_kernel, (capacity, rows)),
        out_shape=(near(11, rows - full, LANES), bf16(11, whole, LANES)),
        in_specs=[VMEM] * 4,
        out_specs=[VMEM, ANY],
        scratch_shapes=[pltpu.VMEM((11, full, LANES), half_type), pltpu.SemaphoreType.DMA((11,))],
        compiler_params=room,
        cost_estimate=cost,
        name="place_kept",
    )(*held(total, keep_codes, keep_x, keep_yz))
    for with_x, late in ((False, (got_yz,)), (True, (got_x, got_yz))):
        out = pl.pallas_call(
            functools.partial(take_kernel, (capacity, rows), with_x),
            out_shape=bf16(11, whole, LANES),
            in_specs=[VMEM] * (2 + len(late)) + [ANY],
            out_specs=ANY,
            input_output_aliases={2 + len(late): 0},
            scratch_shapes=[
                pltpu.VMEM((11, full, LANES), half_type),
                pltpu.VMEM((11, full, LANES), half_type),
                pltpu.SemaphoreType.DMA((2, 11)),
            ],
            compiler_params=room,
            cost_estimate=cost,
            name="place_x" if with_x else "place_yz",
        )(*held(got_0, *late, half), out)
    out = out.reshape(11, whole // (SUB * lines), lines, SUB, LANES).transpose(1, 3, 0, 2, 4)
    return out.reshape(2 * capacity, 11, entries)


def solution(mesh):
    placed = (
        P("gx", "gy", "gz", None, None),
        P("gx", "gy", "gz", None),
        P("gx", "gy", "gz"),
        P(("gx", "gy", "gz"), None),
    )
    return jax.shard_map(
        local,
        mesh=mesh,
        in_specs=placed,
        out_specs=P(("gx", "gy", "gz"), None, None),
        check_vma=False,
    )
```

```python
import functools
import math

import jax
import jax.numpy as jnp
from jax import lax
from jax.experimental import pallas as pl
from jax.experimental.pallas import tpu as pltpu
from jax.sharding import PartitionSpec as P


x_first_order = [0, 2, 1, 3, 4, 5, 6]
x_second_order = [0, 1, 2, 3, 4, 5, 6]
y_first_order = [0, 4, 1, 2, 3, 5, 6]
y_second_order = [0, 3, 1, 2, 4, 5, 6]

LANES = 128
SUB = 8


def padded_2(array, sides, width):
    for axis, dim in sides:
        devices, length = (lax.axis_size(axis), array.shape[dim])
        up = [(i, (i + 1) % devices) for i in range(devices - 1)]
        down = [(j, i) for i, j in up]
        last = lax.slice_in_dim(array, length - width, length, axis=dim)
        initial = lax.slice_in_dim(array, 0, width, axis=dim)
        before = lax.ppermute(last, axis, up)
        after = lax.ppermute(initial, axis, down)
        array = jnp.concatenate([before, array, after], axis=dim)
    return array


def neighbours(padded):
    shifted = [
        padded[1:-1, 1:-1, 1:-1],
        padded[:-2, 1:-1, 1:-1],
        padded[2:, 1:-1, 1:-1],
        padded[1:-1, :-2, 1:-1],
        padded[1:-1, 2:, 1:-1],
        padded[1:-1, 1:-1, :-2],
        padded[1:-1, 1:-1, 2:],
    ]
    return jnp.stack(shifted, axis=3)


def triple(blocks, nearby):
    block_side = math.isqrt(blocks.shape[-1])
    leading = blocks.shape[:-1]
    left_mat = blocks.reshape(leading + (block_side, block_side))
    right_mat = nearby.reshape(leading + (block_side, block_side))
    own_block = jnp.swapaxes(right_mat[..., :1, :, :], -1, -2)
    product = jnp.matmul(left_mat, right_mat, preferred_element_type=jnp.float32).astype(
        jnp.bfloat16
    )
    result = jnp.matmul(own_block, product, preferred_element_type=jnp.float32)
    return result.reshape(leading + (block_side * block_side,))


def members(element_grid, pairs):
    size_x, size_y, size_z = element_grid.shape[:3]
    trailing = element_grid.shape[3:]
    patches = element_grid.reshape((size_x // 2, 2, size_y // 2, 2, size_z) + trailing)

    def pick(upper, lower, slot_order):
        return jnp.take(patches[:, upper, :, lower], jnp.array(slot_order, dtype=jnp.int32), axis=3)

    x_one = jnp.stack([pick(0, 0, x_first_order), pick(0, 1, x_first_order)], axis=3)
    x_two = jnp.stack([pick(1, 0, x_second_order), pick(1, 1, x_second_order)], axis=3)
    y_one = jnp.stack([pick(0, 0, y_first_order), pick(1, 0, y_first_order)], axis=3)
    y_two = jnp.stack([pick(0, 1, y_second_order), pick(1, 1, y_second_order)], axis=3)
    along_x = (pairs == 0).reshape(pairs.shape + (1,) * (x_one.ndim - 3))
    member_one = jnp.where(along_x, x_one, y_one)
    member_two = jnp.where(along_x, x_two, y_two)
    return (
        member_one.reshape((-1,) + member_one.shape[4:]),
        member_two.reshape((-1,) + member_two.shape[4:]),
    )


def arrange(member_one, member_two):
    diagonal = (
        member_one[..., 0, :]
        + member_two[..., 0, :]
        + member_one[..., 1, :]
        + member_two[..., 1, :]
    )
    return jnp.concatenate(
        [diagonal[..., None, :], member_one[..., 2:, :], member_two[..., 2:, :]], axis=-2
    )


def slot_sources(routes, n_dest, capacity):
    total = routes.shape[0]
    chosen = (routes[:, None] == jnp.arange(n_dest, dtype=jnp.int32)[None, :]).astype(jnp.int32)
    before = jnp.cumsum(chosen, axis=0) - chosen
    ranking = jnp.sum(before * chosen, axis=1)
    position = routes * capacity + ranking
    targets = jnp.arange(n_dest * capacity, dtype=jnp.int32)
    matches = position[None, :] == targets[:, None]
    anchor = jnp.sum(jnp.where(matches, jnp.arange(total, dtype=jnp.int32)[None, :], 0), axis=1)
    filled = jnp.any(matches, axis=1)
    return (anchor, filled)


def pack_slots(payload, anchor, filled):
    taken = jnp.take(payload, anchor, axis=0)
    keep_row = filled.reshape(filled.shape + (1,) * (payload.ndim - 1))
    return jnp.where(keep_row, taken, jnp.zeros_like(taken))


def general(a_blocks, prolong, pairing, route, capacity):
    padded = padded_2(prolong, (("gx", 0), ("gy", 1), ("gz", 2)), 1)
    nearby = neighbours(padded)
    anchor, filled = slot_sources(route[:, 0], lax.axis_size("gx"), capacity)
    galerkin = triple(a_blocks, nearby)
    member_one, member_two = members(galerkin, pairing)
    coarse = arrange(member_one, member_two).astype(jnp.bfloat16)
    return lax.all_to_all(
        pack_slots(coarse, anchor, filled), "gx", split_axis=0, concat_axis=0, tiled=True
    )


def dot(left, right):
    return jnp.dot(left, right, preferred_element_type=jnp.float32)


def iota(shape, axis):
    return lax.broadcasted_iota(jnp.int32, shape, axis)


def as_bf16(mask):
    return mask.astype(jnp.float32).astype(jnp.bfloat16)


def pair(one, two):
    h = one.shape[1] // 2
    low = jnp.concatenate([one[:, :h], two[:, :h]], axis=1)
    high = jnp.concatenate([one[:, h:], two[:, h:]], axis=1)
    return jnp.concatenate([low, high], axis=0)


def unpair(both):
    rows, h = both.shape[0] // 2, both.shape[1] // 2
    even, odd = both[:rows], both[rows:]
    return (
        jnp.concatenate([even[:, :h], odd[:, :h]], axis=1),
        jnp.concatenate([even[:, h:], odd[:, h:]], axis=1),
    )


def constants(blk):
    n = 2 * blk
    row, col = iota((n, n), 0), iota((n, n), 1)
    c, z = row % blk, row // blk
    clean = as_bf16(col == (c % 2) * blk + (c // 2) * 2 + z)
    q = blk // 2
    k, p = row // blk, (row // q) % 2
    spread = as_bf16(col == k * blk + 2 * (row % q) + p)
    return clean, spread


def even_lanes(rows):
    return as_bf16(iota((rows, LANES), 1) % 2 == 0), as_bf16(iota((rows, LANES), 1) % 2 == 1)


def even_rows(rows):
    return as_bf16(iota((rows, LANES), 0) % 2 == 0), as_bf16(iota((rows, LANES), 0) % 2 == 1)


def transposed_dot(left, right):
    return lax.dot_general(
        left, right, (((1,), (1,)), ((), ())), preferred_element_type=jnp.float32
    )


def left_factors(both_t, k, masks):
    q = masks[0].shape[0]
    parts = [both_t[(2 * k + p) * q : (2 * k + p + 1) * q] for p in range(2)]
    return jnp.concatenate([part * mask for part in parts for mask in masks], axis=0)


def weights_of(part):
    h = part.shape[1] // 2
    none = jnp.zeros((part.shape[0], h), part.dtype)
    made = []
    for k in range(2):
        one = part[:, k * h : (k + 1) * h]
        made.append(
            jnp.concatenate(
                [jnp.concatenate([one, none], axis=1), jnp.concatenate([none, one], axis=1)], axis=0
            )
        )
    return made


def halves(part):
    h = part.shape[1] // 2
    return part[:, :h], part[:, h:]


def make_table(table_ref, dims):
    _, cap, rows = dims
    me = lax.axis_index("gx")
    lines = rows // cap
    rest = cap % SUB
    half = (cap - rest) * lines
    at_zero = me == 0
    for c in range(cap):
        if c < cap - rest:
            zero = (c, c + half // 2, c, c)
        else:
            h = c - (cap - rest)
            zero = (half + h, half + h + rest, SUB + h, SUB + h + rest)
        if c < rest:
            one = (half + c + rest, half + c, SUB + c, SUB + c + rest)
        else:
            h = c - rest
            one = (h, h + half // 2, h, h)
        for k in range(4):
            table_ref[k, c] = jnp.where(at_zero, zero[k], one[k])


def places(route_ref, where_ref, table_ref, dims, blocks):
    aggregates, _, rows = dims
    me = lax.axis_index("gx")
    sent, kept = jnp.int32(0), jnp.int32(0)
    for i in range(aggregates):
        away = route_ref[0, i] != me
        one = away.astype(jnp.int32)
        c = jnp.where(away, sent, kept)
        sent = sent + one
        kept = kept + (1 - one)
        base = jnp.where(away, 0, blocks * rows)
        where_ref[0, i] = base + table_ref[0, c]
        where_ref[1, i] = base + table_ref[1, c]
        where_ref[2, i] = jnp.where(away, 0, 2 * SUB) + table_ref[2, c]
        where_ref[3, i] = jnp.where(away, 0, 2 * SUB) + table_ref[3, c]
    return sent, kept


def put(total_ref, where_ref, i, block, rows, value):
    n = value.shape[0] // 2
    one = where_ref[0, i] + block * rows
    two = where_ref[1, i] + block * rows
    total_ref[pl.ds(one, n, stride=SUB), :] = value[:n]
    total_ref[pl.ds(two, n, stride=SUB), :] = value[n:]


def finish(outs, total_ref, kind, dims, count):
    _, cap, rows = dims
    rest = cap % SUB
    full = (cap - rest) * (rows // cap)
    me = lax.axis_index("gx")
    line = iota((2 * SUB, LANES), 0)
    in_full = as_bf16(line % SUB + jnp.where(me == 0, 0, rest) < count) > 0.5
    in_half = as_bf16(line % rest + jnp.where(me == 0, cap - rest, 0) < count) > 0.5
    blocks = sum(n for _, n in outs)
    done = 0
    for out, n in outs:
        for k in range(n):
            for at, size, filled in ((0, full, in_full), (full, rows - full, in_half)):
                value = total_ref[pl.ds((kind * blocks + done + k) * rows + at, size), :]
                value = value.astype(jnp.bfloat16).reshape(-1, 2 * SUB, LANES)
                value = jnp.where(filled[None], value, jnp.zeros_like(value))
                out[k * rows + at : k * rows + at + size] = value.reshape(size, LANES)
        done += n


def inner_kernel(
    dims, grid, route_hbm, pair_hbm, p_hbm, a_hbm,
    send_ref, total_ref, keep_codes_ref, zup_ref, zdn_ref, left_ref, a_ref,
    p_ref, route_ref, pair_ref, part_ref, codes_ref, where_ref, table_ref, sems,
):
    px, py, nz = grid
    aggregates, _, rows = dims
    nx, ny = 2 * px, 2 * py
    blk = p_ref.shape[2]
    q = blk // 2
    nb = 5
    copies = [
        pltpu.make_async_copy(one, two, sems.at[k])
        for k, (one, two) in enumerate((
            (p_hbm, p_ref), (route_hbm, route_ref), (pair_hbm, pair_ref),
        ))
    ]
    blocks = [
        pltpu.make_async_copy(a_hbm.at[x], a_ref.at[x], sems.at[3 + x]) for x in range(nx)
    ]
    for copy in copies + blocks:
        copy.start()
    clean, spread = constants(blk)
    masks = even_lanes(q)
    first, second = even_rows(blk)
    codes_ref[...] = jnp.full_like(codes_ref, -1.0)
    make_table(table_ref, dims)
    for copy in copies:
        copy.wait()
    sent, _ = places(route_ref, where_ref, table_ref, dims, nb)
    for i in range(aggregates):
        a, b, z, t = i // (py * nz * 2), (i // (nz * 2)) % py, (i // 2) % nz, i % 2
        code = (2 * (jnp.where(pair_ref[a, b, z] == 0, 2, 1) - t) + z).astype(jnp.float32)
        line = jnp.full((1, LANES), code, jnp.float32)
        codes_ref[pl.ds(where_ref[2, i], 1), :] = line
        codes_ref[pl.ds(where_ref[3, i], 1), :] = line

    pairs = [(x, b) for x in range(nx) for b in range(py)]
    both = {e: pair(p_ref[e[0], 2 * e[1]], p_ref[e[0], 2 * e[1] + 1]) for e in pairs}
    tidy = {e: dot(clean, both[e]).astype(jnp.bfloat16) for e in pairs}
    for x, b in pairs:
        left_ref[x * py + b] = transposed_dot(spread, both[x, b]).astype(jnp.bfloat16)
        zdn_ref[x * py + b] = tidy[x, b][:blk]
        zup_ref[x * py + b] = tidy[x, b][blk:]

    face = p_ref[jnp.where(lax.axis_index("gx") == 0, nx - 1, 0)]
    send_ref[nb * rows + 2 * SUB :] = face.reshape(ny * blk, LANES)

    for x, y in [(x, y) for x in range(nx) for y in range(ny)]:
        if y == 0 and x % px == 0:
            for copy in blocks[x : x + px]:
                copy.wait()
        here = a_ref.at[x, y]
        along_z = here[6] * first + here[5] * second
        right = jnp.concatenate(
            [pair(here[0], here[2 - x % 2]), pair(here[4 - y % 2], along_z)], axis=1
        )
        left = left_factors(left_ref[x * py + y // 2], y % 2, masks)
        got = dot(left, right).astype(jnp.bfloat16)
        parts = unpair(got[:, : 2 * blk]) + unpair(got[:, 2 * blk :])
        for k in range(4):
            part_ref[x, y, k] = parts[k]

    for a, b in [(a, b) for a in range(px) for b in range(py)]:
        own, with_x, with_y, with_z = {}, {}, {}, {}
        for z, ref in enumerate((zdn_ref, zup_ref)):
            zs, zo = pl.ds(z * q, q), pl.ds((1 - z) * q, q)
            for u in range(2):
                x = 2 * a + u
                weight = weights_of(ref[x * py + b])
                for v in range(2):
                    y = 2 * b + v
                    stack = jnp.concatenate(
                        [
                            part_ref[x, y, 0, zs],
                            part_ref[2 * a + 1 - u, y, 1, zs],
                            part_ref[x, 2 * b + 1 - v, 2, zs],
                            part_ref[x, y, 3, zo],
                        ],
                        axis=0,
                    )
                    got = dot(stack, weight[v])
                    own[u, v, z] = got[:q]
                    with_x[1 - u, v, z] = got[q : 2 * q]
                    with_y[u, 1 - v, z] = got[2 * q : 3 * q]
                    with_z[u, v, 1 - z] = got[3 * q :]
        for z in range(nz):
            flat = pair_ref[a, b, z] == 0
            i = ((a * py + b) * nz + z) * 2
            sums = {}
            for u in range(2):
                for v in range(2):
                    t = u if u == v else jnp.where(flat, v, u)
                    m = u if u == v else jnp.where(flat, u, v)
                    e = (u, v, z)
                    sums[u, v] = own[e] + jnp.where(flat, with_x[e], with_y[e])
                    cross = jnp.where(flat, with_y[e], with_x[e])
                    put(total_ref, where_ref, i + t, 1 + m, rows, cross)
                    put(total_ref, where_ref, i + t, 3 + m, rows, with_z[e])
            put(total_ref, where_ref, i, 0, rows, sums[0, 0] + jnp.where(flat, sums[1, 0], sums[0, 1]))
            put(total_ref, where_ref, i + 1, 0, rows, sums[1, 1] + jnp.where(flat, sums[0, 1], sums[1, 0]))

    finish(((send_ref, nb),), total_ref, 0, dims, sent)
    send_ref[nb * rows : nb * rows + 2 * SUB] = codes_ref[: 2 * SUB].astype(jnp.bfloat16)
    keep_codes_ref[...] = codes_ref[2 * SUB :].astype(jnp.bfloat16)


def faces_kernel(grid, zup_ref, zdn_ref, ya_ref, yb_ref, za_ref, zb_ref):
    px, py, _ = grid
    blk = zup_ref.shape[1]
    y_even, z_even = lax.axis_index("gy") % 2 == 0, lax.axis_index("gz") % 2 == 0

    def plane(a, b, half):
        part = slice(half * blk, (half + 1) * blk)
        rows = [jnp.concatenate([zdn_ref[x * py + b], zup_ref[x * py + b]], axis=0) for x in (2 * a, 2 * a + 1)]
        return jnp.concatenate([row[:, part] for row in rows], axis=1)

    for a in range(px):
        down, up = plane(a, 0, 0), plane(a, py - 1, 1)
        ya_ref[a], yb_ref[a] = jnp.where(y_even, up, down), jnp.where(y_even, down, up)
    for at in range(2 * px * py):
        down, up = zdn_ref[at], zup_ref[at]
        za_ref[at] = jnp.where(z_even, up, down)
        zb_ref[at] = jnp.where(z_even, down, up)


def outer_left_kernel(grid, left_ref, a_ref, part_ref):
    px, py, _ = grid
    nx, ny = 2 * px, 2 * py
    blk = a_ref.shape[3]
    masks = even_lanes(blk // 2)
    first, second = even_rows(blk)
    for x, y in [(x, y) for x in range(nx) for y in range(ny)]:
        here = a_ref.at[x, y]
        along_z = here[5] * first + here[6] * second
        low, high = halves(along_z)
        right = jnp.concatenate(
            [pair(here[1 + x % 2], here[3 + y % 2]), jnp.concatenate([low, high], axis=0)], axis=1
        )
        left = left_factors(left_ref[x * py + y // 2], y % 2, masks)
        got = dot(left, right).astype(jnp.bfloat16)
        part_ref[x, y, 0], part_ref[x, y, 1] = unpair(got[:, : 2 * blk])
        along = got[:, 2 * blk :]
        part_ref[x, y, 2] = jnp.concatenate([along[:blk], along[blk:]], axis=1)


def outer_yz_kernel(
    dims, grid, route_ref, pair_ref, part_ref, zup_ref, zdn_ref, ya_ref, yb_ref, za_ref, zb_ref,
    send_ref, keep_ref, total_ref, where_ref, table_ref,
):
    px, py, nz = grid
    _, _, rows = dims
    nx, ny = 2 * px, 2 * py
    blk = part_ref.shape[3]
    q = blk // 2
    nb = 4
    make_table(table_ref, dims)
    sent, kept = places(route_ref, where_ref, table_ref, dims, nb)
    line = iota((blk, LANES), 0) * 0

    def from_sides(axis, first_ref, second_ref, at, high):
        index = lax.axis_index(axis)
        last = index == lax.axis_size(axis) - 1 if high else index == 0
        by_first = index % 2 == (0 if high else 1)
        kept = line + jnp.where(by_first | ~last, 1, 0) > 0
        value = jnp.where(by_first, first_ref[at], second_ref[at]).astype(jnp.float32)
        return jnp.where(kept, value, 0.0).astype(jnp.bfloat16)

    def beside_y(x, y, z, v):
        to = y - 1 if v == 0 else y + 1
        if 0 <= to < ny:
            return (zdn_ref, zup_ref)[z][x * py + to // 2], to % 2
        at = (x // 2, slice(z * blk, (z + 1) * blk))
        return from_sides("gy", ya_ref, yb_ref, at, v == 1), x % 2

    for x in range(nx):
        made = []
        for b, z in [(b, z) for b in range(py) for z in range(nz)]:
            zs = pl.ds(z * q, q)
            along_z = weights_of(from_sides("gz", za_ref, zb_ref, x * py + b, z == 1))
            for v in range(2):
                y = 2 * b + v
                i, m = of_element(pair_ref, grid, x, y, z)
                other, k = beside_y(x, y, z, v)
                along_y = weights_of(other)[k]
                made.append((i, m, dot(part_ref[x, y, 1, zs], along_y)))
                made.append((i, 2 + m, dot(part_ref[x, y, 2, zs], along_z[v])))
        for i, block, got in made:
            put(total_ref, where_ref, i, block, rows, got)

    for kind, (out, count) in enumerate(((send_ref, sent), (keep_ref, kept))):
        finish(((out, nb),), total_ref, kind, dims, count)


def outer_x_kernel(
    dims, grid, route_ref, pair_ref, part_ref, zup_ref, zdn_ref, early_ref,
    send_ref, keep_ref, total_ref, where_ref, table_ref,
):
    px, py, nz = grid
    _, _, rows = dims
    nx, ny = 2 * px, 2 * py
    blk = part_ref.shape[3]
    q = blk // 2
    nb = 2
    make_table(table_ref, dims)
    sent, kept = places(route_ref, where_ref, table_ref, dims, nb)
    above = iota((2 * blk, LANES), 0) * 0 + lax.axis_index("gx") > 0
    clean, _ = constants(blk)
    face = early_ref.shape[0] - ny * blk
    low, high = [], []
    for b in range(py):
        at = face + 2 * b * blk
        tidy = dot(clean, pair(early_ref[at : at + blk], early_ref[at + blk : at + 2 * blk]))
        low.append(jnp.where(above, tidy, 0.0).astype(jnp.bfloat16))
        high.append(jnp.where(above, 0.0, tidy).astype(jnp.bfloat16))

    for x in range(nx):
        made = []
        for b, z in [(b, z) for b in range(py) for z in range(nz)]:
            zs = pl.ds(z * q, q)
            to = x - 1 if x % 2 == 0 else x + 1
            if 0 <= to < nx:
                part = (zdn_ref, zup_ref)[z][to * py + b]
            else:
                part = (low if to < 0 else high)[b][z * blk : (z + 1) * blk]
            along_x = weights_of(part)
            for v in range(2):
                i, m = of_element(pair_ref, grid, x, 2 * b + v, z)
                made.append((i, m, dot(part_ref[x, 2 * b + v, 0, zs], along_x[v])))
        for i, block, got in made:
            put(total_ref, where_ref, i, block, rows, got)

    for kind, (out, count) in enumerate(((send_ref, sent), (keep_ref, kept))):
        finish(((out, nb),), total_ref, kind, dims, count)


def of_element(pair_ref, grid, x, y, z):
    _, py, nz = grid
    a, b, u, v = x // 2, y // 2, x % 2, y % 2
    flat = pair_ref[a, b, z] == 0
    t = u if u == v else jnp.where(flat, v, u)
    m = u if u == v else jnp.where(flat, u, v)
    return ((a * py + b) * nz + z) * 2 + t, m


def received(early_ref, rows):
    def early(k, at, size):
        return early_ref[k * rows + at : k * rows + at + size].reshape(-1, 2 * SUB, LANES)

    return early


def placed_blocks(early, x_ref, yz_ref, code, rows, at, size, without_x=True):
    near_low, near_high = (code < 1.5)[None], (code > 3.5)[None]
    upper = ((code == 1.0) | (code == 3.0) | (code == 5.0))[None]

    def tiles(ref, k):
        return ref[k * rows + at : k * rows + at + size].reshape(-1, 2 * SUB, LANES)

    if without_x:
        yield 0, early(0, at, size)
    for m in range(2):
        cross, y_out = early(1 + m, at, size), tiles(yz_ref, m)
        if x_ref is not None:
            x_out = tiles(x_ref, m)
            yield 1 + 5 * m, jnp.where(near_low, cross, x_out)
            yield 2 + 5 * m, jnp.where(near_low, x_out, jnp.where(near_high, y_out, cross))
        if without_x:
            z_in, z_out = early(3 + m, at, size), tiles(yz_ref, 2 + m)
            yield 3 + 5 * m, jnp.where(near_high, cross, y_out)
            yield 4 + 5 * m, jnp.where(upper, z_in, z_out)
            yield 5 + 5 * m, jnp.where(upper, z_out, z_in)


def twice(codes):
    return jnp.concatenate([codes, codes], axis=0)


def keep_kernel(dims, total_ref, codes_ref, x_ref, yz_ref, half_ref, out_hbm, full_ref, sem):
    cap, rows = dims
    full = (cap - cap % SUB) * (rows // cap)
    me = lax.axis_index("gx")

    def rounded(code):
        filled = (code > -0.5)[None]

        def early(k, at, size):
            value = total_ref[pl.ds((5 + k) * rows + at, size), :].astype(jnp.bfloat16)
            value = value.reshape(-1, 2 * SUB, LANES)
            return jnp.where(filled, value, jnp.zeros_like(value))

        return early

    copies = []
    code = twice(codes_ref[:SUB])
    for k, value in placed_blocks(rounded(code), x_ref, yz_ref, code, rows, 0, full):
        full_ref[k] = value.reshape(full, LANES)
        to = out_hbm.at[k, pl.ds(me * (2 * full), full), :]
        copies.append(pltpu.make_async_copy(full_ref.at[k], to, sem.at[k]))
        copies[-1].start()
    code = twice(codes_ref[SUB:])
    for k, value in placed_blocks(rounded(code), x_ref, yz_ref, code, rows, full, rows - full):
        half_ref[k] = value.reshape(rows - full, LANES)
    for copy in copies:
        copy.wait()


def take_kernel(dims, with_x, early_ref, *refs):
    late, (half_ref, _, out_hbm, full_ref, mixed_ref, sem) = refs[: -6], refs[-6:]
    cap, rows = dims
    full = (cap - cap % SUB) * (rows // cap)
    me = lax.axis_index("gx")
    codes = early_ref[5 * rows : 5 * rows + 2 * SUB]
    x_ref, yz_ref = late if with_x else (None, late[0])
    early = received(early_ref, rows)
    copies = []
    for k, value in placed_blocks(early, x_ref, yz_ref, twice(codes[:SUB]), rows, 0, full, not with_x):
        full_ref[k] = value.reshape(full, LANES)
        to = out_hbm.at[k, pl.ds((1 - me) * (2 * full), full), :]
        copies.append(pltpu.make_async_copy(full_ref.at[k], to, sem.at[0, k]))
        copies[-1].start()
    first_half = (iota((SUB, LANES), 0) < SUB // 2)[None]
    pick = first_half == (me == 0)
    for k, value in placed_blocks(
        early, x_ref, yz_ref, twice(codes[SUB:]), rows, full, rows - full, not with_x
    ):
        theirs = value.reshape(rows - full, LANES).astype(jnp.float32).reshape(-1, SUB, LANES)
        mine = half_ref[k].astype(jnp.float32).reshape(-1, SUB, LANES)
        low = jnp.where(pick, mine, theirs)
        high = pltpu.roll(jnp.where(pick, theirs, mine), SUB // 2, 1)
        mixed_ref[k, : rows - full] = low.reshape(rows - full, LANES).astype(jnp.bfloat16)
        mixed_ref[k, rows - full :] = high.reshape(rows - full, LANES).astype(jnp.bfloat16)
        to = out_hbm.at[k, full : 2 * full, :]
        copies.append(pltpu.make_async_copy(mixed_ref.at[k], to, sem.at[1, k]))
        copies[-1].start()
    for copy in copies:
        copy.wait()


SMEM = pl.BlockSpec(memory_space=pltpu.SMEM)
VMEM = pl.BlockSpec(memory_space=pltpu.VMEM)
ANY = pl.BlockSpec(memory_space=pl.ANY)


def bf16(*shape):
    return jax.ShapeDtypeStruct(shape, jnp.bfloat16)


def near(*shape):
    return pltpu.VMEM(shape, jnp.bfloat16)


def held(*arrays):
    return [pltpu.with_memory_space_constraint(one, pltpu.VMEM) for one in arrays]


def swaps(ny, nz):
    def first(i):
        return i + 1 if i % 2 == 0 else i - 1

    def second(i, n):
        j = i - 1 if i % 2 == 0 else i + 1
        return j if 0 <= j < n else None

    made = {"y_a": [], "y_b": [], "z_a": [], "z_b": []}
    for j in range(ny):
        for k in range(nz):
            to_y, to_z = second(j, ny), second(k, nz)
            made["y_a"].append((first(j), k))
            made["z_a"].append((j, first(k)))
            made["y_b"].append((j, first(k)) if to_y is None else (to_y, k))
            made["z_b"].append((first(j), k) if to_z is None else (j, to_z))
    return {name: [(i, j * nz + k) for i, (j, k) in enumerate(to)] for name, to in made.items()}


def local(a_blocks, prolong, pairing, route):
    devices_gx = lax.axis_size("gx")
    aggregates = route.shape[0]
    capacity = max(2, 3 * aggregates // (2 * devices_gx))
    nx, ny, nz, faces, entries = a_blocks.shape
    fits = (
        devices_gx == 2
        and lax.axis_size("gy") % 2 == 0
        and lax.axis_size("gz") % 2 == 0
        and nz == 2
        and nx % 2 == 0
        and ny % 2 == 0
        and faces == 7
        and entries == (LANES // 2) ** 2
        and capacity // SUB == 1
        and capacity % SUB == SUB // 2
    )
    if not fits:
        return general(a_blocks, prolong, pairing, route, capacity)
    px, py = nx // 2, ny // 2
    blk = math.isqrt(entries)
    lines = entries // LANES
    a_view = a_blocks.transpose(0, 1, 3, 2, 4).reshape(nx, ny, faces, nz, lines, LANES)
    a_view = a_view.transpose(0, 1, 2, 4, 3, 5).reshape(nx, ny, faces, nz * lines, LANES)
    p_view = prolong.reshape(nx, ny, nz, lines, LANES).transpose(0, 1, 3, 2, 4)
    p_view = p_view.reshape(nx, ny, nz * lines, LANES)
    route_row = route.reshape(1, aggregates)
    rows = capacity * lines
    dims, grid = (aggregates, capacity, rows), (px, py, nz)
    f32 = jnp.float32
    half_type = jnp.bfloat16
    face_y, face_z = (px, 2 * blk, LANES), (nx * py, blk, LANES)
    parts = (nx, ny, 3, blk, LANES)
    room = pltpu.CompilerParams(vmem_limit_bytes=24 * 2**20)
    cost = pl.CostEstimate(flops=10**9, bytes_accessed=4 * 10**6, transcendentals=0)

    swap = [(0, 1), (1, 0)]
    send_0, total, keep_codes, zup, zdn, left, a_near = pl.pallas_call(
        functools.partial(inner_kernel, dims, grid),
        out_shape=(
            near(5 * rows + 2 * SUB + ny * blk, LANES),
            pltpu.VMEM((10 * rows, LANES), f32),
            near(2 * SUB, LANES),
            near(*face_z),
            near(*face_z),
            near(nx * py, 2 * blk, LANES),
            near(*a_view.shape),
        ),
        in_specs=[ANY] * 4,
        out_specs=[VMEM] * 7,
        scratch_shapes=[
            pltpu.VMEM(p_view.shape, half_type),
            pltpu.SMEM(route_row.shape, jnp.int32),
            pltpu.SMEM(pairing.shape, jnp.int32),
            pltpu.VMEM((nx, ny, 4, blk, LANES), half_type),
            pltpu.VMEM((4 * SUB, LANES), f32),
            pltpu.SMEM((4, aggregates), jnp.int32),
            pltpu.SMEM((4, capacity), jnp.int32),
            pltpu.SemaphoreType.DMA((3 + nx,)),
        ],
        compiler_params=room,
        cost_estimate=cost,
        name="inner_blocks",
    )(*[pltpu.with_memory_space_constraint(one, pltpu.HBM) for one in (route_row, pairing, p_view, a_view)])
    got_0 = lax.ppermute(send_0, "gx", swap)
    zup, zdn = held(zup, zdn)
    ya, yb, za, zb = pl.pallas_call(
        functools.partial(faces_kernel, grid),
        out_shape=(near(*face_y), near(*face_y), near(*face_z), near(*face_z)),
        in_specs=[VMEM] * 2,
        out_specs=[VMEM] * 4,
        compiler_params=room,
        cost_estimate=cost,
        name="faces",
    )(zup, zdn)
    rounds = swaps(lax.axis_size("gy"), lax.axis_size("gz"))
    halos = []
    for name, value in (("y_a", ya), ("y_b", yb), ("z_a", za), ("z_b", zb)):
        halos.append(lax.ppermute(value, ("gy", "gz"), rounds[name]))

    left, a_near = held(left, a_near)
    part = pl.pallas_call(
        functools.partial(outer_left_kernel, grid),
        out_shape=near(*parts),
        in_specs=[VMEM] * 2,
        out_specs=VMEM,
        compiler_params=room,
        cost_estimate=cost,
        name="outer_left",
    )(left, a_near)
    part = held(part)[0]

    def outer(kernel, blocks, *arrays):
        return pl.pallas_call(
            functools.partial(kernel, dims, grid),
            out_shape=(near(blocks * rows, LANES),) * 2,
            in_specs=[SMEM, SMEM] + [VMEM] * (3 + len(arrays)),
            out_specs=[VMEM] * 2,
            scratch_shapes=[
                pltpu.VMEM((2 * blocks * rows, LANES), f32),
                pltpu.SMEM((4, aggregates), jnp.int32),
                pltpu.SMEM((4, capacity), jnp.int32),
            ],
            compiler_params=room,
            cost_estimate=cost,
        )(route_row, pairing, part, zup, zdn, *held(*arrays))

    send_yz, keep_yz = outer(outer_yz_kernel, 4, *halos)
    got_yz = lax.ppermute(send_yz, "gx", swap)
    send_x, keep_x = outer(outer_x_kernel, 2, got_0)
    got_x = lax.ppermute(send_x, "gx", swap)

    full = (capacity // SUB) * SUB * lines
    whole = 2 * rows
    half, out = pl.pallas_call(
        functools.partial(keep_kernel, (capacity, rows)),
        out_shape=(near(11, rows - full, LANES), bf16(11, whole, LANES)),
        in_specs=[VMEM] * 4,
        out_specs=[VMEM, ANY],
        scratch_shapes=[pltpu.VMEM((11, full, LANES), half_type), pltpu.SemaphoreType.DMA((11,))],
        compiler_params=room,
        cost_estimate=cost,
        name="place_kept",
    )(*held(total, keep_codes, keep_x, keep_yz))
    for with_x, late in ((False, (got_yz,)), (True, (got_x, got_yz))):
        out = pl.pallas_call(
            functools.partial(take_kernel, (capacity, rows), with_x),
            out_shape=bf16(11, whole, LANES),
            in_specs=[VMEM] * (2 + len(late)) + [ANY],
            out_specs=ANY,
            input_output_aliases={2 + len(late): 0},
            scratch_shapes=[
                pltpu.VMEM((11, full, LANES), half_type),
                pltpu.VMEM((11, full, LANES), half_type),
                pltpu.SemaphoreType.DMA((2, 11)),
            ],
            compiler_params=room,
            cost_estimate=cost,
            name="place_x" if with_x else "place_yz",
        )(*held(got_0, *late, half), out)
    out = out.reshape(11, whole // (SUB * lines), lines, SUB, LANES).transpose(1, 3, 0, 2, 4)
    return out.reshape(2 * capacity, 11, entries)


def solution(mesh):
    placed = (
        P("gx", "gy", "gz", None, None),
        P("gx", "gy", "gz", None),
        P("gx", "gy", "gz"),
        P(("gx", "gy", "gz"), None),
    )
    return jax.shard_map(
        local,
        mesh=mesh,
        in_specs=placed,
        out_specs=P(("gx", "gy", "gz"), None, None),
        check_vma=False,
    )
```

```python
import functools
import math

import jax
import jax.numpy as jnp
from jax import lax
from jax.experimental import pallas as pl
from jax.experimental.pallas import tpu as pltpu
from jax.sharding import PartitionSpec as P


x_first_order = [0, 2, 1, 3, 4, 5, 6]
x_second_order = [0, 1, 2, 3, 4, 5, 6]
y_first_order = [0, 4, 1, 2, 3, 5, 6]
y_second_order = [0, 3, 1, 2, 4, 5, 6]

LANES = 128
SUB = 8


def padded_2(array, sides, width):
    for axis, dim in sides:
        devices, length = (lax.axis_size(axis), array.shape[dim])
        up = [(i, (i + 1) % devices) for i in range(devices - 1)]
        down = [(j, i) for i, j in up]
        last = lax.slice_in_dim(array, length - width, length, axis=dim)
        initial = lax.slice_in_dim(array, 0, width, axis=dim)
        before = lax.ppermute(last, axis, up)
        after = lax.ppermute(initial, axis, down)
        array = jnp.concatenate([before, array, after], axis=dim)
    return array


def neighbours(padded):
    shifted = [
        padded[1:-1, 1:-1, 1:-1],
        padded[:-2, 1:-1, 1:-1],
        padded[2:, 1:-1, 1:-1],
        padded[1:-1, :-2, 1:-1],
        padded[1:-1, 2:, 1:-1],
        padded[1:-1, 1:-1, :-2],
        padded[1:-1, 1:-1, 2:],
    ]
    return jnp.stack(shifted, axis=3)


def triple(blocks, nearby):
    block_side = math.isqrt(blocks.shape[-1])
    leading = blocks.shape[:-1]
    left_mat = blocks.reshape(leading + (block_side, block_side))
    right_mat = nearby.reshape(leading + (block_side, block_side))
    own_block = jnp.swapaxes(right_mat[..., :1, :, :], -1, -2)
    product = jnp.matmul(left_mat, right_mat, preferred_element_type=jnp.float32).astype(
        jnp.bfloat16
    )
    result = jnp.matmul(own_block, product, preferred_element_type=jnp.float32)
    return result.reshape(leading + (block_side * block_side,))


def members(element_grid, pairs):
    size_x, size_y, size_z = element_grid.shape[:3]
    trailing = element_grid.shape[3:]
    patches = element_grid.reshape((size_x // 2, 2, size_y // 2, 2, size_z) + trailing)

    def pick(upper, lower, slot_order):
        return jnp.take(patches[:, upper, :, lower], jnp.array(slot_order, dtype=jnp.int32), axis=3)

    x_one = jnp.stack([pick(0, 0, x_first_order), pick(0, 1, x_first_order)], axis=3)
    x_two = jnp.stack([pick(1, 0, x_second_order), pick(1, 1, x_second_order)], axis=3)
    y_one = jnp.stack([pick(0, 0, y_first_order), pick(1, 0, y_first_order)], axis=3)
    y_two = jnp.stack([pick(0, 1, y_second_order), pick(1, 1, y_second_order)], axis=3)
    along_x = (pairs == 0).reshape(pairs.shape + (1,) * (x_one.ndim - 3))
    member_one = jnp.where(along_x, x_one, y_one)
    member_two = jnp.where(along_x, x_two, y_two)
    return (
        member_one.reshape((-1,) + member_one.shape[4:]),
        member_two.reshape((-1,) + member_two.shape[4:]),
    )


def arrange(member_one, member_two):
    diagonal = (
        member_one[..., 0, :]
        + member_two[..., 0, :]
        + member_one[..., 1, :]
        + member_two[..., 1, :]
    )
    return jnp.concatenate(
        [diagonal[..., None, :], member_one[..., 2:, :], member_two[..., 2:, :]], axis=-2
    )


def slot_sources(routes, n_dest, capacity):
    total = routes.shape[0]
    chosen = (routes[:, None] == jnp.arange(n_dest, dtype=jnp.int32)[None, :]).astype(jnp.int32)
    before = jnp.cumsum(chosen, axis=0) - chosen
    ranking = jnp.sum(before * chosen, axis=1)
    position = routes * capacity + ranking
    targets = jnp.arange(n_dest * capacity, dtype=jnp.int32)
    matches = position[None, :] == targets[:, None]
    anchor = jnp.sum(jnp.where(matches, jnp.arange(total, dtype=jnp.int32)[None, :], 0), axis=1)
    filled = jnp.any(matches, axis=1)
    return (anchor, filled)


def pack_slots(payload, anchor, filled):
    taken = jnp.take(payload, anchor, axis=0)
    keep_row = filled.reshape(filled.shape + (1,) * (payload.ndim - 1))
    return jnp.where(keep_row, taken, jnp.zeros_like(taken))


def general(a_blocks, prolong, pairing, route, capacity):
    padded = padded_2(prolong, (("gx", 0), ("gy", 1), ("gz", 2)), 1)
    nearby = neighbours(padded)
    anchor, filled = slot_sources(route[:, 0], lax.axis_size("gx"), capacity)
    galerkin = triple(a_blocks, nearby)
    member_one, member_two = members(galerkin, pairing)
    coarse = arrange(member_one, member_two).astype(jnp.bfloat16)
    return lax.all_to_all(
        pack_slots(coarse, anchor, filled), "gx", split_axis=0, concat_axis=0, tiled=True
    )


def dot(left, right):
    return jnp.dot(left, right, preferred_element_type=jnp.float32)


def iota(shape, axis):
    return lax.broadcasted_iota(jnp.int32, shape, axis)


def as_bf16(mask):
    return mask.astype(jnp.float32).astype(jnp.bfloat16)


def pair(one, two):
    h = one.shape[1] // 2
    low = jnp.concatenate([one[:, :h], two[:, :h]], axis=1)
    high = jnp.concatenate([one[:, h:], two[:, h:]], axis=1)
    return jnp.concatenate([low, high], axis=0)


def unpair(both):
    rows, h = both.shape[0] // 2, both.shape[1] // 2
    even, odd = both[:rows], both[rows:]
    return (
        jnp.concatenate([even[:, :h], odd[:, :h]], axis=1),
        jnp.concatenate([even[:, h:], odd[:, h:]], axis=1),
    )


def constants(blk):
    n = 2 * blk
    row, col = iota((n, n), 0), iota((n, n), 1)
    c, z = row % blk, row // blk
    clean = as_bf16(col == (c % 2) * blk + (c // 2) * 2 + z)
    q = blk // 2
    k, p = row // blk, (row // q) % 2
    spread = as_bf16(col == k * blk + 2 * (row % q) + p)
    return clean, spread


def even_lanes(rows):
    return as_bf16(iota((rows, LANES), 1) % 2 == 0), as_bf16(iota((rows, LANES), 1) % 2 == 1)


def even_rows(rows):
    return as_bf16(iota((rows, LANES), 0) % 2 == 0), as_bf16(iota((rows, LANES), 0) % 2 == 1)


def transposed_dot(left, right):
    return lax.dot_general(
        left, right, (((1,), (1,)), ((), ())), preferred_element_type=jnp.float32
    )


def left_factors(both_t, k, masks):
    q = masks[0].shape[0]
    parts = [both_t[(2 * k + p) * q : (2 * k + p + 1) * q] for p in range(2)]
    return jnp.concatenate([part * mask for part in parts for mask in masks], axis=0)


def weights_of(part):
    h = part.shape[1] // 2
    none = jnp.zeros((part.shape[0], h), part.dtype)
    made = []
    for k in range(2):
        one = part[:, k * h : (k + 1) * h]
        made.append(
            jnp.concatenate(
                [jnp.concatenate([one, none], axis=1), jnp.concatenate([none, one], axis=1)], axis=0
            )
        )
    return made


def halves(part):
    h = part.shape[1] // 2
    return part[:, :h], part[:, h:]


def make_table(table_ref, dims):
    _, cap, rows = dims
    me = lax.axis_index("gx")
    lines = rows // cap
    rest = cap % SUB
    half = (cap - rest) * lines
    at_zero = me == 0
    for c in range(cap):
        if c < cap - rest:
            zero = (c, c + half // 2, c, c)
        else:
            h = c - (cap - rest)
            zero = (half + h, half + h + rest, SUB + h, SUB + h + rest)
        if c < rest:
            one = (half + c + rest, half + c, SUB + c, SUB + c + rest)
        else:
            h = c - rest
            one = (h, h + half // 2, h, h)
        for k in range(4):
            table_ref[k, c] = jnp.where(at_zero, zero[k], one[k])


def places(route_ref, where_ref, table_ref, dims, blocks):
    aggregates, _, rows = dims
    me = lax.axis_index("gx")
    sent, kept = jnp.int32(0), jnp.int32(0)
    for i in range(aggregates):
        away = route_ref[0, i] != me
        one = away.astype(jnp.int32)
        c = jnp.where(away, sent, kept)
        sent = sent + one
        kept = kept + (1 - one)
        base = jnp.where(away, 0, blocks * rows)
        where_ref[0, i] = base + table_ref[0, c]
        where_ref[1, i] = base + table_ref[1, c]
        where_ref[2, i] = jnp.where(away, 0, 2 * SUB) + table_ref[2, c]
        where_ref[3, i] = jnp.where(away, 0, 2 * SUB) + table_ref[3, c]
    return sent, kept


def put(total_ref, where_ref, i, block, rows, value):
    n = value.shape[0] // 2
    one = where_ref[0, i] + block * rows
    two = where_ref[1, i] + block * rows
    total_ref[pl.ds(one, n, stride=SUB), :] = value[:n]
    total_ref[pl.ds(two, n, stride=SUB), :] = value[n:]


def finish(outs, total_ref, kind, dims, count):
    _, cap, rows = dims
    rest = cap % SUB
    full = (cap - rest) * (rows // cap)
    me = lax.axis_index("gx")
    line = iota((2 * SUB, LANES), 0)
    in_full = as_bf16(line % SUB + jnp.where(me == 0, 0, rest) < count) > 0.5
    in_half = as_bf16(line % rest + jnp.where(me == 0, cap - rest, 0) < count) > 0.5
    blocks = sum(n for _, n in outs)
    done = 0
    for out, n in outs:
        for k in range(n):
            for at, size, filled in ((0, full, in_full), (full, rows - full, in_half)):
                value = total_ref[pl.ds((kind * blocks + done + k) * rows + at, size), :]
                value = value.astype(jnp.bfloat16).reshape(-1, 2 * SUB, LANES)
                value = jnp.where(filled[None], value, jnp.zeros_like(value))
                out[k * rows + at : k * rows + at + size] = value.reshape(size, LANES)
        done += n


def inner_kernel(
    dims, grid, route_hbm, pair_hbm, p_hbm, a_hbm,
    send_ref, total_ref, keep_codes_ref, zup_ref, zdn_ref, left_ref, a_ref,
    p_ref, route_ref, pair_ref, part_ref, codes_ref, where_ref, table_ref, sems,
):
    px, py, nz = grid
    aggregates, _, rows = dims
    nx, ny = 2 * px, 2 * py
    blk = p_ref.shape[2]
    q = blk // 2
    nb = 5
    copies = [
        pltpu.make_async_copy(one, two, sems.at[k])
        for k, (one, two) in enumerate((
            (p_hbm, p_ref), (route_hbm, route_ref), (pair_hbm, pair_ref),
        ))
    ]
    blocks = [
        pltpu.make_async_copy(a_hbm.at[x], a_ref.at[x], sems.at[3 + x]) for x in range(nx)
    ]
    for copy in copies + blocks:
        copy.start()
    clean, spread = constants(blk)
    masks = even_lanes(q)
    first, second = even_rows(blk)
    codes_ref[...] = jnp.full_like(codes_ref, -1.0)
    make_table(table_ref, dims)
    for copy in copies:
        copy.wait()
    sent, _ = places(route_ref, where_ref, table_ref, dims, nb)
    for i in range(aggregates):
        a, b, z, t = i // (py * nz * 2), (i // (nz * 2)) % py, (i // 2) % nz, i % 2
        code = (2 * (jnp.where(pair_ref[a, b, z] == 0, 2, 1) - t) + z).astype(jnp.float32)
        line = jnp.full((1, LANES), code, jnp.float32)
        codes_ref[pl.ds(where_ref[2, i], 1), :] = line
        codes_ref[pl.ds(where_ref[3, i], 1), :] = line

    pairs = [(x, b) for x in range(nx) for b in range(py)]
    both = {e: pair(p_ref[e[0], 2 * e[1]], p_ref[e[0], 2 * e[1] + 1]) for e in pairs}
    tidy = {e: dot(clean, both[e]).astype(jnp.bfloat16) for e in pairs}
    for x, b in pairs:
        left_ref[x * py + b] = transposed_dot(spread, both[x, b]).astype(jnp.bfloat16)
        zdn_ref[x * py + b] = tidy[x, b][:blk]
        zup_ref[x * py + b] = tidy[x, b][blk:]

    face = p_ref[jnp.where(lax.axis_index("gx") == 0, nx - 1, 0)]
    send_ref[nb * rows + 2 * SUB :] = face.reshape(ny * blk, LANES)
    for copy in blocks:
        copy.wait()

    for x, y in [(x, y) for x in range(nx) for y in range(ny)]:
        here = a_ref.at[x, y]
        along_z = here[6] * first + here[5] * second
        right = jnp.concatenate(
            [pair(here[0], here[2 - x % 2]), pair(here[4 - y % 2], along_z)], axis=1
        )
        left = left_factors(left_ref[x * py + y // 2], y % 2, masks)
        got = dot(left, right).astype(jnp.bfloat16)
        parts = unpair(got[:, : 2 * blk]) + unpair(got[:, 2 * blk :])
        for k in range(4):
            part_ref[x, y, k] = parts[k]

    for a, b in [(a, b) for a in range(px) for b in range(py)]:
        own, with_x, with_y, with_z = {}, {}, {}, {}
        for z, ref in enumerate((zdn_ref, zup_ref)):
            zs, zo = pl.ds(z * q, q), pl.ds((1 - z) * q, q)
            for u in range(2):
                x = 2 * a + u
                weight = weights_of(ref[x * py + b])
                for v in range(2):
                    y = 2 * b + v
                    stack = jnp.concatenate(
                        [
                            part_ref[x, y, 0, zs],
                            part_ref[2 * a + 1 - u, y, 1, zs],
                            part_ref[x, 2 * b + 1 - v, 2, zs],
                            part_ref[x, y, 3, zo],
                        ],
                        axis=0,
                    )
                    got = dot(stack, weight[v])
                    own[u, v, z] = got[:q]
                    with_x[1 - u, v, z] = got[q : 2 * q]
                    with_y[u, 1 - v, z] = got[2 * q : 3 * q]
                    with_z[u, v, 1 - z] = got[3 * q :]
        for z in range(nz):
            flat = pair_ref[a, b, z] == 0
            i = ((a * py + b) * nz + z) * 2
            sums = {}
            for u in range(2):
                for v in range(2):
                    t = u if u == v else jnp.where(flat, v, u)
                    m = u if u == v else jnp.where(flat, u, v)
                    e = (u, v, z)
                    sums[u, v] = own[e] + jnp.where(flat, with_x[e], with_y[e])
                    cross = jnp.where(flat, with_y[e], with_x[e])
                    put(total_ref, where_ref, i + t, 1 + m, rows, cross)
                    put(total_ref, where_ref, i + t, 3 + m, rows, with_z[e])
            put(total_ref, where_ref, i, 0, rows, sums[0, 0] + jnp.where(flat, sums[1, 0], sums[0, 1]))
            put(total_ref, where_ref, i + 1, 0, rows, sums[1, 1] + jnp.where(flat, sums[0, 1], sums[1, 0]))

    finish(((send_ref, nb),), total_ref, 0, dims, sent)
    send_ref[nb * rows : nb * rows + 2 * SUB] = codes_ref[: 2 * SUB].astype(jnp.bfloat16)
    keep_codes_ref[...] = codes_ref[2 * SUB :].astype(jnp.bfloat16)


def faces_kernel(grid, zup_ref, zdn_ref, ya_ref, yb_ref, za_ref, zb_ref):
    px, py, _ = grid
    blk = zup_ref.shape[1]
    y_even, z_even = lax.axis_index("gy") % 2 == 0, lax.axis_index("gz") % 2 == 0

    def plane(a, b, half):
        part = slice(half * blk, (half + 1) * blk)
        rows = [jnp.concatenate([zdn_ref[x * py + b], zup_ref[x * py + b]], axis=0) for x in (2 * a, 2 * a + 1)]
        return jnp.concatenate([row[:, part] for row in rows], axis=1)

    for a in range(px):
        down, up = plane(a, 0, 0), plane(a, py - 1, 1)
        ya_ref[a], yb_ref[a] = jnp.where(y_even, up, down), jnp.where(y_even, down, up)
    for at in range(2 * px * py):
        down, up = zdn_ref[at], zup_ref[at]
        za_ref[at] = jnp.where(z_even, up, down)
        zb_ref[at] = jnp.where(z_even, down, up)


def outer_left_kernel(grid, left_ref, a_ref, part_ref):
    px, py, _ = grid
    nx, ny = 2 * px, 2 * py
    blk = a_ref.shape[3]
    masks = even_lanes(blk // 2)
    first, second = even_rows(blk)
    for x, y in [(x, y) for x in range(nx) for y in range(ny)]:
        here = a_ref.at[x, y]
        along_z = here[5] * first + here[6] * second
        low, high = halves(along_z)
        right = jnp.concatenate(
            [pair(here[1 + x % 2], here[3 + y % 2]), jnp.concatenate([low, high], axis=0)], axis=1
        )
        left = left_factors(left_ref[x * py + y // 2], y % 2, masks)
        got = dot(left, right).astype(jnp.bfloat16)
        part_ref[x, y, 0], part_ref[x, y, 1] = unpair(got[:, : 2 * blk])
        along = got[:, 2 * blk :]
        part_ref[x, y, 2] = jnp.concatenate([along[:blk], along[blk:]], axis=1)


def outer_yz_kernel(
    dims, grid, route_ref, pair_ref, part_ref, zup_ref, zdn_ref, ya_ref, yb_ref, za_ref, zb_ref,
    send_ref, keep_ref, total_ref, where_ref, table_ref,
):
    px, py, nz = grid
    _, _, rows = dims
    nx, ny = 2 * px, 2 * py
    blk = part_ref.shape[3]
    q = blk // 2
    nb = 4
    make_table(table_ref, dims)
    sent, kept = places(route_ref, where_ref, table_ref, dims, nb)
    line = iota((blk, LANES), 0) * 0

    def from_sides(axis, first_ref, second_ref, at, high):
        index = lax.axis_index(axis)
        last = index == lax.axis_size(axis) - 1 if high else index == 0
        by_first = index % 2 == (0 if high else 1)
        kept = line + jnp.where(by_first | ~last, 1, 0) > 0
        value = jnp.where(by_first, first_ref[at], second_ref[at]).astype(jnp.float32)
        return jnp.where(kept, value, 0.0).astype(jnp.bfloat16)

    def beside_y(x, y, z, v):
        to = y - 1 if v == 0 else y + 1
        if 0 <= to < ny:
            return (zdn_ref, zup_ref)[z][x * py + to // 2], to % 2
        at = (x // 2, slice(z * blk, (z + 1) * blk))
        return from_sides("gy", ya_ref, yb_ref, at, v == 1), x % 2

    for x in range(nx):
        made = []
        for b, z in [(b, z) for b in range(py) for z in range(nz)]:
            zs = pl.ds(z * q, q)
            along_z = weights_of(from_sides("gz", za_ref, zb_ref, x * py + b, z == 1))
            for v in range(2):
                y = 2 * b + v
                i, m = of_element(pair_ref, grid, x, y, z)
                other, k = beside_y(x, y, z, v)
                along_y = weights_of(other)[k]
                made.append((i, m, dot(part_ref[x, y, 1, zs], along_y)))
                made.append((i, 2 + m, dot(part_ref[x, y, 2, zs], along_z[v])))
        for i, block, got in made:
            put(total_ref, where_ref, i, block, rows, got)

    for kind, (out, count) in enumerate(((send_ref, sent), (keep_ref, kept))):
        finish(((out, nb),), total_ref, kind, dims, count)


def outer_x_kernel(
    dims, grid, route_ref, pair_ref, part_ref, zup_ref, zdn_ref, early_ref,
    send_ref, keep_ref, total_ref, where_ref, table_ref,
):
    px, py, nz = grid
    _, _, rows = dims
    nx, ny = 2 * px, 2 * py
    blk = part_ref.shape[3]
    q = blk // 2
    nb = 2
    make_table(table_ref, dims)
    sent, kept = places(route_ref, where_ref, table_ref, dims, nb)
    above = iota((2 * blk, LANES), 0) * 0 + lax.axis_index("gx") > 0
    clean, _ = constants(blk)
    face = early_ref.shape[0] - ny * blk
    low, high = [], []
    for b in range(py):
        at = face + 2 * b * blk
        tidy = dot(clean, pair(early_ref[at : at + blk], early_ref[at + blk : at + 2 * blk]))
        low.append(jnp.where(above, tidy, 0.0).astype(jnp.bfloat16))
        high.append(jnp.where(above, 0.0, tidy).astype(jnp.bfloat16))

    for x in range(nx):
        made = []
        for b, z in [(b, z) for b in range(py) for z in range(nz)]:
            zs = pl.ds(z * q, q)
            to = x - 1 if x % 2 == 0 else x + 1
            if 0 <= to < nx:
                part = (zdn_ref, zup_ref)[z][to * py + b]
            else:
                part = (low if to < 0 else high)[b][z * blk : (z + 1) * blk]
            along_x = weights_of(part)
            for v in range(2):
                i, m = of_element(pair_ref, grid, x, 2 * b + v, z)
                made.append((i, m, dot(part_ref[x, 2 * b + v, 0, zs], along_x[v])))
        for i, block, got in made:
            put(total_ref, where_ref, i, block, rows, got)

    for kind, (out, count) in enumerate(((send_ref, sent), (keep_ref, kept))):
        finish(((out, nb),), total_ref, kind, dims, count)


def of_element(pair_ref, grid, x, y, z):
    _, py, nz = grid
    a, b, u, v = x // 2, y // 2, x % 2, y % 2
    flat = pair_ref[a, b, z] == 0
    t = u if u == v else jnp.where(flat, v, u)
    m = u if u == v else jnp.where(flat, u, v)
    return ((a * py + b) * nz + z) * 2 + t, m


def received(early_ref, rows):
    def early(k, at, size):
        return early_ref[k * rows + at : k * rows + at + size].reshape(-1, 2 * SUB, LANES)

    return early


def placed_blocks(early, x_ref, yz_ref, code, rows, at, size, without_x=True):
    near_low, near_high = (code < 1.5)[None], (code > 3.5)[None]
    upper = ((code == 1.0) | (code == 3.0) | (code == 5.0))[None]

    def tiles(ref, k):
        return ref[k * rows + at : k * rows + at + size].reshape(-1, 2 * SUB, LANES)

    if without_x:
        yield 0, early(0, at, size)
    for m in range(2):
        cross, y_out = early(1 + m, at, size), tiles(yz_ref, m)
        if x_ref is not None:
            x_out = tiles(x_ref, m)
            yield 1 + 5 * m, jnp.where(near_low, cross, x_out)
            yield 2 + 5 * m, jnp.where(near_low, x_out, jnp.where(near_high, y_out, cross))
        if without_x:
            z_in, z_out = early(3 + m, at, size), tiles(yz_ref, 2 + m)
            yield 3 + 5 * m, jnp.where(near_high, cross, y_out)
            yield 4 + 5 * m, jnp.where(upper, z_in, z_out)
            yield 5 + 5 * m, jnp.where(upper, z_out, z_in)


def twice(codes):
    return jnp.concatenate([codes, codes], axis=0)


def keep_kernel(dims, total_ref, codes_ref, x_ref, yz_ref, half_ref, out_hbm, full_ref, sem):
    cap, rows = dims
    full = (cap - cap % SUB) * (rows // cap)
    me = lax.axis_index("gx")

    def rounded(code):
        filled = (code > -0.5)[None]

        def early(k, at, size):
            value = total_ref[pl.ds((5 + k) * rows + at, size), :].astype(jnp.bfloat16)
            value = value.reshape(-1, 2 * SUB, LANES)
            return jnp.where(filled, value, jnp.zeros_like(value))

        return early

    copies = []
    code = twice(codes_ref[:SUB])
    for k, value in placed_blocks(rounded(code), x_ref, yz_ref, code, rows, 0, full):
        full_ref[k] = value.reshape(full, LANES)
        to = out_hbm.at[k, pl.ds(me * (2 * full), full), :]
        copies.append(pltpu.make_async_copy(full_ref.at[k], to, sem.at[k]))
        copies[-1].start()
    code = twice(codes_ref[SUB:])
    for k, value in placed_blocks(rounded(code), x_ref, yz_ref, code, rows, full, rows - full):
        half_ref[k] = value.reshape(rows - full, LANES)
    for copy in copies:
        copy.wait()


def take_kernel(dims, with_x, early_ref, *refs):
    late, (half_ref, _, out_hbm, full_ref, mixed_ref, sem) = refs[: -6], refs[-6:]
    cap, rows = dims
    full = (cap - cap % SUB) * (rows // cap)
    me = lax.axis_index("gx")
    codes = early_ref[5 * rows : 5 * rows + 2 * SUB]
    x_ref, yz_ref = late if with_x else (None, late[0])
    early = received(early_ref, rows)
    copies = []
    for k, value in placed_blocks(early, x_ref, yz_ref, twice(codes[:SUB]), rows, 0, full, not with_x):
        full_ref[k] = value.reshape(full, LANES)
        to = out_hbm.at[k, pl.ds((1 - me) * (2 * full), full), :]
        copies.append(pltpu.make_async_copy(full_ref.at[k], to, sem.at[0, k]))
        copies[-1].start()
    first_half = (iota((SUB, LANES), 0) < SUB // 2)[None]
    pick = first_half == (me == 0)
    for k, value in placed_blocks(
        early, x_ref, yz_ref, twice(codes[SUB:]), rows, full, rows - full, not with_x
    ):
        theirs = value.reshape(rows - full, LANES).astype(jnp.float32).reshape(-1, SUB, LANES)
        mine = half_ref[k].astype(jnp.float32).reshape(-1, SUB, LANES)
        low = jnp.where(pick, mine, theirs)
        high = pltpu.roll(jnp.where(pick, theirs, mine), SUB // 2, 1)
        mixed_ref[k, : rows - full] = low.reshape(rows - full, LANES).astype(jnp.bfloat16)
        mixed_ref[k, rows - full :] = high.reshape(rows - full, LANES).astype(jnp.bfloat16)
        to = out_hbm.at[k, full : 2 * full, :]
        copies.append(pltpu.make_async_copy(mixed_ref.at[k], to, sem.at[1, k]))
        copies[-1].start()
    for copy in copies:
        copy.wait()


SMEM = pl.BlockSpec(memory_space=pltpu.SMEM)
VMEM = pl.BlockSpec(memory_space=pltpu.VMEM)
ANY = pl.BlockSpec(memory_space=pl.ANY)


def bf16(*shape):
    return jax.ShapeDtypeStruct(shape, jnp.bfloat16)


def near(*shape):
    return pltpu.VMEM(shape, jnp.bfloat16)


def held(*arrays):
    return [pltpu.with_memory_space_constraint(one, pltpu.VMEM) for one in arrays]


def swaps(ny, nz):
    def first(i):
        return i + 1 if i % 2 == 0 else i - 1

    def second(i, n):
        j = i - 1 if i % 2 == 0 else i + 1
        return j if 0 <= j < n else None

    made = {"y_a": [], "y_b": [], "z_a": [], "z_b": []}
    for j in range(ny):
        for k in range(nz):
            to_y, to_z = second(j, ny), second(k, nz)
            made["y_a"].append((first(j), k))
            made["z_a"].append((j, first(k)))
            made["y_b"].append((j, first(k)) if to_y is None else (to_y, k))
            made["z_b"].append((first(j), k) if to_z is None else (j, to_z))
    return {name: [(i, j * nz + k) for i, (j, k) in enumerate(to)] for name, to in made.items()}


def local(a_blocks, prolong, pairing, route):
    devices_gx = lax.axis_size("gx")
    aggregates = route.shape[0]
    capacity = max(2, 3 * aggregates // (2 * devices_gx))
    nx, ny, nz, faces, entries = a_blocks.shape
    fits = (
        devices_gx == 2
        and lax.axis_size("gy") % 2 == 0
        and lax.axis_size("gz") % 2 == 0
        and nz == 2
        and nx % 2 == 0
        and ny % 2 == 0
        and faces == 7
        and entries == (LANES // 2) ** 2
        and capacity // SUB == 1
        and capacity % SUB == SUB // 2
    )
    if not fits:
        return general(a_blocks, prolong, pairing, route, capacity)
    px, py = nx // 2, ny // 2
    blk = math.isqrt(entries)
    lines = entries // LANES
    a_view = a_blocks.transpose(0, 1, 3, 2, 4).reshape(nx, ny, faces, nz, lines, LANES)
    a_view = a_view.transpose(0, 1, 2, 4, 3, 5).reshape(nx, ny, faces, nz * lines, LANES)
    p_view = prolong.reshape(nx, ny, nz, lines, LANES).transpose(0, 1, 3, 2, 4)
    p_view = p_view.reshape(nx, ny, nz * lines, LANES)
    route_row = route.reshape(1, aggregates)
    rows = capacity * lines
    dims, grid = (aggregates, capacity, rows), (px, py, nz)
    f32 = jnp.float32
    half_type = jnp.bfloat16
    face_y, face_z = (px, 2 * blk, LANES), (nx * py, blk, LANES)
    parts = (nx, ny, 3, blk, LANES)
    room = pltpu.CompilerParams(vmem_limit_bytes=24 * 2**20)
    cost = pl.CostEstimate(flops=10**9, bytes_accessed=4 * 10**6, transcendentals=0)

    swap = [(0, 1), (1, 0)]
    send_0, total, keep_codes, zup, zdn, left, a_near = pl.pallas_call(
        functools.partial(inner_kernel, dims, grid),
        out_shape=(
            near(5 * rows + 2 * SUB + ny * blk, LANES),
            pltpu.VMEM((10 * rows, LANES), f32),
            near(2 * SUB, LANES),
            near(*face_z),
            near(*face_z),
            near(nx * py, 2 * blk, LANES),
            near(*a_view.shape),
        ),
        in_specs=[ANY] * 4,
        out_specs=[VMEM] * 7,
        scratch_shapes=[
            pltpu.VMEM(p_view.shape, half_type),
            pltpu.SMEM(route_row.shape, jnp.int32),
            pltpu.SMEM(pairing.shape, jnp.int32),
            pltpu.VMEM((nx, ny, 4, blk, LANES), half_type),
            pltpu.VMEM((4 * SUB, LANES), f32),
            pltpu.SMEM((4, aggregates), jnp.int32),
            pltpu.SMEM((4, capacity), jnp.int32),
            pltpu.SemaphoreType.DMA((3 + nx,)),
        ],
        compiler_params=pltpu.CompilerParams(vmem_limit_bytes=24 * 2**20),
        cost_estimate=cost,
        name="inner_blocks",
    )(*[pltpu.with_memory_space_constraint(one, pltpu.HBM) for one in (route_row, pairing, p_view, a_view)])
    got_0 = lax.ppermute(send_0, "gx", swap)
    zup, zdn = held(zup, zdn)
    ya, yb, za, zb = pl.pallas_call(
        functools.partial(faces_kernel, grid),
        out_shape=(near(*face_y), near(*face_y), near(*face_z), near(*face_z)),
        in_specs=[VMEM] * 2,
        out_specs=[VMEM] * 4,
        compiler_params=room,
        cost_estimate=cost,
        name="faces",
    )(zup, zdn)
    rounds = swaps(lax.axis_size("gy"), lax.axis_size("gz"))
    halos = []
    for name, value in (("y_a", ya), ("y_b", yb), ("z_a", za), ("z_b", zb)):
        halos.append(lax.ppermute(value, ("gy", "gz"), rounds[name]))

    left, a_near = held(left, a_near)
    part = pl.pallas_call(
        functools.partial(outer_left_kernel, grid),
        out_shape=near(*parts),
        in_specs=[VMEM] * 2,
        out_specs=VMEM,
        compiler_params=room,
        cost_estimate=cost,
        name="outer_left",
    )(left, a_near)
    part = held(part)[0]

    def outer(kernel, blocks, *arrays):
        return pl.pallas_call(
            functools.partial(kernel, dims, grid),
            out_shape=(near(blocks * rows, LANES),) * 2,
            in_specs=[SMEM, SMEM] + [VMEM] * (3 + len(arrays)),
            out_specs=[VMEM] * 2,
            scratch_shapes=[
                pltpu.VMEM((2 * blocks * rows, LANES), f32),
                pltpu.SMEM((4, aggregates), jnp.int32),
                pltpu.SMEM((4, capacity), jnp.int32),
            ],
            compiler_params=room,
            cost_estimate=cost,
        )(route_row, pairing, part, zup, zdn, *held(*arrays))

    send_yz, keep_yz = outer(outer_yz_kernel, 4, *halos)
    got_yz = lax.ppermute(send_yz, "gx", swap)
    send_x, keep_x = outer(outer_x_kernel, 2, got_0)
    got_x = lax.ppermute(send_x, "gx", swap)

    full = (capacity // SUB) * SUB * lines
    whole = 2 * rows
    half, out = pl.pallas_call(
        functools.partial(keep_kernel, (capacity, rows)),
        out_shape=(near(11, rows - full, LANES), bf16(11, whole, LANES)),
        in_specs=[VMEM] * 4,
        out_specs=[VMEM, ANY],
        scratch_shapes=[pltpu.VMEM((11, full, LANES), half_type), pltpu.SemaphoreType.DMA((11,))],
        compiler_params=room,
        cost_estimate=cost,
        name="place_kept",
    )(*held(total, keep_codes, keep_x, keep_yz))
    for with_x, late in ((False, (got_yz,)), (True, (got_x, got_yz))):
        out = pl.pallas_call(
            functools.partial(take_kernel, (capacity, rows), with_x),
            out_shape=bf16(11, whole, LANES),
            in_specs=[VMEM] * (2 + len(late)) + [ANY],
            out_specs=ANY,
            input_output_aliases={2 + len(late): 0},
            scratch_shapes=[
                pltpu.VMEM((11, full, LANES), half_type),
                pltpu.VMEM((11, full, LANES), half_type),
                pltpu.SemaphoreType.DMA((2, 11)),
            ],
            compiler_params=pltpu.CompilerParams(vmem_limit_bytes=24 * 2**20),
            cost_estimate=cost,
            name="place_x" if with_x else "place_yz",
        )(*held(got_0, *late, half), out)
    out = out.reshape(11, whole // (SUB * lines), lines, SUB, LANES).transpose(1, 3, 0, 2, 4)
    return out.reshape(2 * capacity, 11, entries)


def solution(mesh):
    placed = (
        P("gx", "gy", "gz", None, None),
        P("gx", "gy", "gz", None),
        P("gx", "gy", "gz"),
        P(("gx", "gy", "gz"), None),
    )
    return jax.shard_map(
        local,
        mesh=mesh,
        in_specs=placed,
        out_specs=P(("gx", "gy", "gz"), None, None),
        check_vma=False,
    )
```
